32 devices in a mesh: dp: 4 (over z), fsdp: 8 (over y, x, core).
Axes of the slice: x: 2, y: 2, z: 4, core: 2. Of those that a mesh axis runs over, the one named last changes fastest.
Arguments:
- tokens: bfloat16 [4096, 1280], P(('dp', 'fsdp')), may hold values from -6 to 6
- lengths: int32 [32, 2], P(('dp', 'fsdp')), may hold values from 1 to 96, 128 in all within a row
- padding: int32 [4096], P(('dp', 'fsdp')), may hold values 0 or 1
- ln1_gain: bfloat16 [1280], P('fsdp'), may hold values from 0.099609375 to 1.8984375
- ln1_bias: bfloat16 [1280], P('fsdp'), may hold values from -4 to 4
- w_qkv: bfloat16 [1280, 3840], P('fsdp'), may hold values from -0.15625 to 0.15625
- b_query: bfloat16 [1280], P('fsdp'), may hold values from -4 to 4
- b_value: bfloat16 [1280], P('fsdp'), may hold values from -4 to 4
- w_out: bfloat16 [1280, 1280], P('fsdp'), may hold values from -0.625 to 0.625
- b_out: bfloat16 [1280], P('fsdp'), may hold values from -4 to 4
- ln2_gain: bfloat16 [1280], P('fsdp'), may hold values from 0.099609375 to 1.8984375
- ln2_bias: bfloat16 [1280], P('fsdp'), may hold values from -4 to 4
- w_up: bfloat16 [1280, 5120], P('fsdp'), may hold values from -0.15625 to 0.15625
- b_up: bfloat16 [5120], P('fsdp'), may hold values from -6 to 6
- w_down: bfloat16 [5120, 1280], P('fsdp'), may hold values from -0.078125 to 0.078125
- b_down: bfloat16 [1280], P('fsdp'), may hold values from -4 to 4
- cotangent: bfloat16 [4096, 1280], P(('dp', 'fsdp')), may hold values from -6 to 6
Outputs:
- layer_out: bfloat16 [4096, 1280], P(('dp', 'fsdp'))
- grad_tokens: float32 [4096, 1280], P(('dp', 'fsdp'))
- grad_ln1_gain: float32 [1280], P('fsdp')
- grad_ln1_bias: float32 [1280], P('fsdp')
- grad_w_qkv: float32 [1280, 3840], P('fsdp')
- grad_b_query: float32 [1280], P('fsdp')
- grad_b_value: float32 [1280], P('fsdp')
- grad_w_out: float32 [1280, 1280], P('fsdp')
- grad_b_out: float32 [1280], P('fsdp')
- grad_ln2_gain: float32 [1280], P('fsdp')
- grad_ln2_bias: float32 [1280], P('fsdp')
- grad_w_up: float32 [1280, 5120], P('fsdp')
- grad_b_up: float32 [5120], P('fsdp')
- grad_w_down: float32 [5120, 1280], P('fsdp')
- grad_b_down: float32 [1280], P('fsdp')
- cls_mean: float32 [1280], replicated
- cls_var: float32 [1280], replicated
The draws below stay inside these ranges and needn't reach their ends.
Inputs may be any that keep to these rules, and one draw needn't show every extreme that they name: `lengths`: each row sums to 128; each length lies between 32 and 96. `padding`: A CLS token is a key whatever its mark.
All inputs are finite; a program needn't handle non-finite values. No bound on the sum of `padding` on one device may be relied on, other than what follows from the above.
Results may differ from the reference program's by a relative error of at most 0.015.
Values may be sent and summed in bfloat16 or wider, within the bound.
No kernel may reach another device: no remote copies, remote signals or barrier semaphores. Data moves between devices by JAX's collectives and lax.ppermute only.
A program may use at most 256 MiB of HBM per device.

```python
import math
import jax
import jax.numpy as jnp
import numpy as np
from jax import lax

D = 1280
HEADS = 20
HEAD_DIM = 64
FF = 5120
TOK_DEV = 128
CELLS_DEV = 2
CELL_MAX = 96
TOKENS = 4096
N_DP = 4
N_FSDP = 8


def set_ends(drawn, own_key, least, top_value):
    index_at = [jax.random.randint(jax.random.fold_in(own_key, axis), (), 0, length) for axis, length in enumerate(drawn.shape)]
    widest = drawn.shape.index(max(drawn.shape))
    neighbour = index_at[:widest] + [(index_at[widest] + 1) % drawn.shape[widest]] + index_at[widest + 1:]
    return drawn.at[tuple(index_at)].set(least).at[tuple(neighbour)].set(top_value)


def with_spikes(array, own_key, source, target, shards_of, factor):
    owner, partner = [(jnp.arange(array.shape[dim]) // (array.shape[dim] // shards_of)).reshape([-1 if axis == dim else 1 for axis in range(array.ndim)]) for dim in (source, target)]
    chosen = jax.random.permutation(own_key, shards_of)[partner]
    strong = (owner == chosen) | (owner == (partner + shards_of // 2) % shards_of)
    return jnp.where(strong, factor * array, array)


def steps_of(stream_key, shape, cuts, low, top_value):
    gain = 1.0
    for position, shards_of in cuts:
        steps = jax.random.uniform(jax.random.fold_in(jax.random.fold_in(stream_key, 6), position), (shards_of,), jnp.float32, low / len(cuts), top_value / len(cuts))
        gain = gain * jnp.repeat(jnp.exp(steps), shape[position] // shards_of).reshape((-1,) + (1,) * (len(shape) - 1 - position))
    return gain


def profile(amount, total, most, slope):
    loads = [(1 << 20) // math.isqrt(grade ** slope) + 1 for grade in range(2, amount + 1)]
    spare, given = total - most - (amount - 1), [1] * (amount - 1)
    while spare > 0:
        free = [i for i in range(amount - 1) if given[i] < most]
        whole, left = sum([loads[i] for i in free]), spare
        for i in free:
            more = min(most - given[i], max(1, left * loads[i] // whole), spare)
            given[i] = given[i] + more
            spare = spare - more
    return np.array([most] + given)


def ragged_sizes(key, number_of, total, limit, skew):
    if number_of == 2:
        one = jax.random.randint(key, (), max(1, total - limit), min(limit, total - 1) + 1)
        return jnp.stack([one, total - one])
    sizes = jnp.asarray(profile(number_of, total, limit, skew), jnp.int32)
    twos = (number_of - 1) // 2
    donor, receiver = sizes[1:1 + 2 * twos:2], sizes[2:2 + 2 * twos:2]
    room = jnp.minimum(donor - 1, limit - receiver)
    passed = jax.random.randint(jax.random.fold_in(key, 1), (twos,), 0, 1 << 20) % (room + 1)
    sizes = sizes.at[1:1 + 2 * twos:2].set(donor - passed).at[2:2 + 2 * twos:2].set(receiver + passed)
    return sizes[jax.random.permutation(jax.random.fold_in(key, 2), number_of)]


def bell_draw(stream_key, shape, deviation, bound, cuts=(), kind=jnp.bfloat16):
    array = jax.random.normal(stream_key, shape, jnp.float32) * deviation
    if len(cuts) > 0:
        array = steps_of(stream_key, shape, cuts, -0.22, 0.18) * array
    return jnp.clip(array, min=-bound, max=bound).astype(kind)


def noise_with(stream_key, shape, deviation, bound, pieces, heavy, kind=jnp.bfloat16):
    array = deviation * jax.random.normal(stream_key, shape, jnp.float32)
    if pieces:
        array = array * steps_of(stream_key, shape, pieces, -0.22, 0.18)
    return jnp.clip(with_spikes(array, jax.random.fold_in(stream_key, 3), *heavy), -bound, bound).astype(kind)


def setup_inputs(seed: int = 0) -> dict:
    key_of = jax.random.split(jax.random.key(seed), 18)
    tokens = bell_draw(key_of[0], (TOKENS, D), 1.0, 6.0, ((0, 32),))
    lengths = jax.vmap(lambda own: ragged_sizes(own, CELLS_DEV, TOK_DEV, CELL_MAX, 0))(jax.random.split(key_of[1], (N_DP * N_FSDP))).reshape((N_DP * N_FSDP, CELLS_DEV)).astype(jnp.int32)
    padding = set_ends((jax.random.randint(key_of[2], (TOKENS,), 0, 8) < 7).astype(jnp.int32), jax.random.fold_in(key_of[2], 1), 0, 1)
    ln1_gain = jnp.clip(1.0 + 0.18 * jax.random.normal(key_of[3], (D,), jnp.float32), 0.099609375, 1.8984375).astype(jnp.bfloat16)
    ln1_bias = bell_draw(key_of[4], (D,), 0.3, 4.0, ((0, 8),))
    w_qkv = bell_draw(key_of[5], (D, 3 * D), D ** -0.5, 0.15625, ((0, 8),))
    b_query = bell_draw(key_of[6], (D,), 0.3, 4.0, ((0, 8),))
    b_value = bell_draw(key_of[7], (D,), 0.3, 4.0, ((0, 8),))
    w_out = bell_draw(key_of[8], (D, D), (D // 16) ** -0.5, 0.625, ((0, 8),))
    b_out = bell_draw(key_of[9], (D,), 0.3, 4.0, ((0, 8),))
    ln2_gain = jnp.clip(1.0 + 0.18 * jax.random.normal(key_of[10], (D,), jnp.float32), 0.099609375, 1.8984375).astype(jnp.bfloat16)
    ln2_bias = bell_draw(key_of[11], (D,), 0.3, 4.0, ((0, 8),))
    w_up = bell_draw(key_of[12], (D, FF), D ** -0.5, 0.15625, ((0, 8),))
    b_up = bell_draw(key_of[13], (FF,), 0.5, 6.0, ((0, 8),))
    w_down = bell_draw(key_of[14], (FF, D), FF ** -0.5, 0.078125, ((0, 8),))
    b_down = bell_draw(key_of[15], (D,), 0.3, 4.0, ((0, 8),))
    cotangent = noise_with(key_of[16], (TOKENS, D), 1.0, 6.0, ((0, 32),), (0, 1, 32, 2.75))
    return dict(tokens=tokens, lengths=lengths, padding=padding, ln1_gain=ln1_gain, ln1_bias=ln1_bias, w_qkv=w_qkv, b_query=b_query, b_value=b_value, w_out=w_out, b_out=b_out, ln2_gain=ln2_gain, ln2_bias=ln2_bias, w_up=w_up, b_up=b_up, w_down=w_down, b_down=b_down, cotangent=cotangent)


@jax.custom_vjp
def low(v):
    return lax.optimization_barrier(v.astype(jnp.bfloat16)).astype(jnp.float32)

@jax.custom_vjp
def low_back(v):
    return v

def low_keep(v):
    return (low(v), None)

def low_pass(kept, grad):
    return (grad,)

def back_keep(v):
    return (v, None)

def back_low(kept, grad):
    return (low(grad),)
low.defvjp(low_keep, low_pass)
low_back.defvjp(back_keep, back_low)

def both_round(values):
    return low(low_back(values))

def dense(left, right):
    return jnp.dot(left, right, precision=lax.Precision.HIGHEST)

def layer_norm(values, norm_gain, norm_bias):
    center = lax.optimization_barrier(jnp.mean(values, axis=-1, keepdims=True))
    centred = values - center
    spread = lax.optimization_barrier(jnp.mean(centred * centred, axis=-1, keepdims=True))
    return centred * lax.rsqrt(spread + 1e-05) * norm_gain + norm_bias

def cell_layout(lengths_row, padding_row):
    places = jnp.arange(padding_row.shape[0], dtype=jnp.int32)
    finish = jnp.cumsum(lengths_row).astype(jnp.int32)
    starts = (finish - lengths_row).astype(jnp.int32)
    member = lax.optimization_barrier(jnp.sum((places[:, None] >= finish[None, :]).astype(jnp.int32), axis=1))
    leading = jnp.any(places[:, None] == starts[None, :], axis=1)
    usable = (padding_row > 0) | leading
    return (member[:, None] == member[None, :]) & usable[None, :]

def layer_block(inputs, lengths_row, padding_row, weights):
    first_gain, first_bias, whole_qkv, query_bias, value_bias, whole_out, out_bias, second_gain, second_bias, whole_up, up_bias, whole_down, down_bias = weights
    row_total = inputs.shape[0]
    allowed = cell_layout(lengths_row, padding_row)
    normed_first = low(layer_norm(inputs, first_gain, first_bias))
    projected = dense(normed_first, whole_qkv)
    query = both_round(projected[:, :D] + query_bias).reshape(row_total, HEADS, HEAD_DIM)
    key_rows = both_round(projected[:, D:2 * D]).reshape(row_total, HEADS, HEAD_DIM)
    value_rows = both_round(projected[:, 2 * D:] + value_bias).reshape(row_total, HEADS, HEAD_DIM)
    raw = jnp.einsum('thd,shd->hts', query, key_rows, precision=lax.Precision.HIGHEST)
    scores = low_back(raw) * HEAD_DIM ** (-0.5)
    masked = jnp.where(allowed[None], scores, -1e+30)
    probs = jax.nn.softmax(masked, axis=-1)
    context = jnp.einsum('hts,shd->thd', low(probs), value_rows, precision=lax.Precision.HIGHEST)
    context = both_round(context.reshape(row_total, D))
    mixed = inputs + low_back(dense(context, whole_out) + out_bias)
    normed_second = low(layer_norm(mixed, second_gain, second_bias))
    hidden_pre = low_back(dense(normed_second, whole_up) + up_bias)
    activated = low(jax.nn.gelu(hidden_pre, approximate=False))
    return mixed + dense(activated, whole_down) + down_bias

def reference(tokens, lengths, padding, ln1_gain, ln1_bias, w_qkv, b_query, b_value, w_out, b_out, ln2_gain, ln2_bias, w_up, b_up, w_down, b_down, cotangent):
    blocks = N_DP * N_FSDP
    params = (ln1_gain, ln1_bias, w_qkv, b_query, b_value, w_out, b_out, ln2_gain, ln2_bias, w_up, b_up, w_down, b_down)
    params = tuple((entry.astype(jnp.float32) for entry in params))
    pad_rows = padding.reshape(blocks, TOK_DEV)
    checked = jax.checkpoint(layer_block)

    def forward(inputs, *weights):
        shaped = inputs.reshape(blocks, TOK_DEV, D)

        def apply_block(packed):
            return checked(packed[0], packed[1], packed[2], weights)
        outputs = lax.map(apply_block, (shaped, lengths, pad_rows))
        return outputs.reshape(TOKENS, D)
    result, pullback = jax.vjp(forward, tokens.astype(jnp.float32), *params)
    grads = pullback(cotangent.astype(jnp.float32))
    starts = (jnp.cumsum(lengths, axis=1) - lengths).astype(jnp.int32)
    offsets = (jnp.arange(blocks, dtype=jnp.int32) * TOK_DEV).astype(jnp.int32)
    picks = (starts + offsets[:, None]).astype(jnp.int32).reshape(-1)
    picked = result[picks]
    cls_mean = lax.optimization_barrier(jnp.mean(picked, axis=0))
    cls_var = lax.optimization_barrier(jnp.mean(picked * picked, axis=0)) - cls_mean * cls_mean
    return (result.astype(jnp.bfloat16), grads[0], grads[1], grads[2], grads[3], grads[4], grads[5], grads[6], grads[7], grads[8], grads[9], grads[10], grads[11], grads[12], grads[13], cls_mean, cls_var)
```

```python
from functools import partial

import jax
import jax.numpy as jnp
from jax import lax
from jax.experimental import pallas as pl
from jax.experimental.pallas import tpu as pltpu
from jax.sharding import PartitionSpec as P

D = 1280
HEADS = 20
HEAD_DIM = 64
FF = 5120
CELLS_DEV = 2
EPS = 1e-05

TEAM = 8
CHIPS = 4
HEADS_CHIP = HEADS // CHIPS
D_CHIP = D // CHIPS
FF_CHIP = FF // CHIPS

f32 = jnp.float32
bf16 = jnp.bfloat16


def dot(a, b, dims):
    return lax.dot_general(a, b, (dims, ((), ())), preferred_element_type=f32)


def mm(a, b):
    return dot(a, b, ((1,), (0,)))


def mm_t(a, b):
    return dot(a, b, ((1,), (1,)))


def t_mm(a, b):
    return dot(a, b, ((0,), (0,)))


def normalize(values):
    center = jnp.mean(values, axis=-1, keepdims=True)
    centred = values - center
    spread = jnp.mean(centred * centred, axis=-1, keepdims=True)
    inverse = lax.rsqrt(spread + EPS)
    return centred * inverse, inverse


def norm_backward(grad_out, normed, inverse, norm_gain):
    grad_normed = grad_out * norm_gain
    first_mean = jnp.mean(grad_normed, axis=-1, keepdims=True)
    second_mean = jnp.mean(grad_normed * normed, axis=-1, keepdims=True)
    grad_in = inverse * (grad_normed - first_mean - normed * second_mean)
    return grad_in, jnp.sum(grad_out * normed, axis=0), jnp.sum(grad_out, axis=0)


def softmax_rows(query, key, keep):
    raw = dot(query, key, ((1,), (1,))) * (HEAD_DIM ** (-0.5))
    masked = jnp.where(keep, raw, -1e30)
    grown = jnp.exp(masked - jnp.max(masked, axis=-1, keepdims=True))
    return grown / jnp.sum(grown, axis=-1, keepdims=True)


def attention_kernel(projected, mask, context):
    keep = mask[...].astype(f32) > 0.5
    for head in range(HEADS_CHIP):
        lo = head * HEAD_DIM
        query = projected[:, lo : lo + HEAD_DIM]
        key = projected[:, D_CHIP + lo : D_CHIP + lo + HEAD_DIM]
        value = projected[:, 2 * D_CHIP + lo : 2 * D_CHIP + lo + HEAD_DIM]
        probs = softmax_rows(query, key, keep).astype(bf16)
        context[:, lo : lo + HEAD_DIM] = mm(probs, value).astype(bf16)


def attention_back_kernel(projected, mask, grad_context, grad_projected):
    keep = mask[...].astype(f32) > 0.5
    for head in range(HEADS_CHIP):
        lo = head * HEAD_DIM
        query = projected[:, lo : lo + HEAD_DIM]
        key = projected[:, D_CHIP + lo : D_CHIP + lo + HEAD_DIM]
        value = projected[:, 2 * D_CHIP + lo : 2 * D_CHIP + lo + HEAD_DIM]
        grad = grad_context[:, lo : lo + HEAD_DIM]
        probs = softmax_rows(query, key, keep)
        grad_probs = mm_t(grad, value)
        along = jnp.sum(grad_probs * probs, axis=-1, keepdims=True)
        grad_scores = (probs * (grad_probs - along) * (HEAD_DIM ** (-0.5))).astype(bf16)
        grad_projected[:, lo : lo + HEAD_DIM] = mm(grad_scores, key).astype(bf16)
        grad_projected[:, D_CHIP + lo : D_CHIP + lo + HEAD_DIM] = t_mm(grad_scores, query).astype(bf16)
        grad_projected[:, 2 * D_CHIP + lo : 2 * D_CHIP + lo + HEAD_DIM] = t_mm(
            probs.astype(bf16), grad
        ).astype(bf16)


def attention(projected, mask):
    rows = mask.shape[1]
    return pl.pallas_call(
        attention_kernel,
        grid=(projected.shape[0] // rows,),
        in_specs=[
            pl.BlockSpec((rows, 3 * D_CHIP), lambda i: (i, 0)),
            pl.BlockSpec((rows, rows), lambda i: (i, 0)),
        ],
        out_specs=pl.BlockSpec((rows, D_CHIP), lambda i: (i, 0)),
        out_shape=jax.ShapeDtypeStruct((projected.shape[0], D_CHIP), bf16),
        cost_estimate=pl.CostEstimate(flops=10**9, bytes_accessed=2 * 10**6, transcendentals=330000),
        name="attention",
    )(projected, mask)


def attention_back(projected, mask, grad_context):
    rows = mask.shape[1]
    return pl.pallas_call(
        attention_back_kernel,
        grid=(projected.shape[0] // rows,),
        in_specs=[
            pl.BlockSpec((rows, 3 * D_CHIP), lambda i: (i, 0)),
            pl.BlockSpec((rows, rows), lambda i: (i, 0)),
            pl.BlockSpec((rows, D_CHIP), lambda i: (i, 0)),
        ],
        out_specs=pl.BlockSpec((rows, 3 * D_CHIP), lambda i: (i, 0)),
        out_shape=jax.ShapeDtypeStruct(projected.shape, bf16),
        cost_estimate=pl.CostEstimate(flops=3 * 10**9, bytes_accessed=4 * 10**6, transcendentals=330000),
        name="attention_back",
    )(projected, mask, grad_context)


def local(
    tokens,
    lengths,
    padding,
    ln1_gain,
    ln1_bias,
    w_qkv,
    b_query,
    b_value,
    w_out,
    b_out,
    ln2_gain,
    ln2_bias,
    w_up,
    b_up,
    w_down,
    b_down,
    cotangent,
):
    fsdp_count = lax.axis_size("fsdp")
    dp_count = lax.axis_size("dp")
    groups = fsdp_count // TEAM
    place = lax.axis_index("fsdp") // groups
    chip = place // 2
    core = place % 2
    depth = lax.axis_index("dp")
    rows = tokens.shape[0]

    def swap(value, mask):
        pairs = [
            (team * groups + group, (team ^ mask) * groups + group)
            for team in range(TEAM)
            for group in range(groups)
        ]
        return lax.ppermute(value, "fsdp", pairs)

    shard_groups = [[team * groups + group for group in range(groups)] for team in range(TEAM)]

    def gather_shards(value):
        if groups == 1:
            return value
        return lax.all_gather(value, "fsdp", axis=0, tiled=True, axis_index_groups=shard_groups)

    def scatter_shards(value):
        if groups == 1:
            return value
        return lax.psum_scatter(
            value, "fsdp", scatter_dimension=0, tiled=True, axis_index_groups=shard_groups
        )

    def by_core(mine, other):
        return jnp.where(core == 0, mine, other), jnp.where(core == 0, other, mine)

    def pick(stack, index):
        return lax.dynamic_index_in_dim(stack, index, 0, keepdims=False)

    def from_chips(send_to):
        return [send_to(0)] + [swap(send_to(i), 2 * i) for i in range(1, CHIPS)]

    def gather_chips(value):
        return jnp.concatenate(from_chips(lambda i: value), axis=0)

    def scatter_chips(partial_sum):
        low = partial_sum.astype(bf16)
        parts = from_chips(
            lambda i: partial_sum[:rows] if i == 0 else low[i * rows : (i + 1) * rows]
        )
        return parts[0] + parts[1].astype(f32) + parts[2].astype(f32) + parts[3].astype(f32)

    def along_z(pairs, value):
        return lax.ppermute(value, "dp", pairs)

    def sum_dp(low):
        if dp_count != 4:
            return lax.psum(low, "dp")
        inward = along_z([(0, 1), (3, 2)], low)
        half = (low.astype(f32) + inward.astype(f32)).astype(bf16)
        across = along_z([(1, 2), (2, 1)], half)
        whole = (half.astype(f32) + across.astype(f32)).astype(bf16)
        outward = along_z([(1, 0), (2, 3)], whole)
        return jnp.where((depth == 1) | (depth == 2), whole, outward)

    def sum_everywhere(value):
        for mask in (1, 2, 4):
            value = value + swap(value, mask)
        if groups > 1:
            value = lax.psum(
                value,
                "fsdp",
                axis_index_groups=shard_groups,
            )
        return sum_dp_wide(value)

    def sum_dp_wide(value):
        if dp_count != 4:
            return lax.psum(value, "dp")
        for mask in (1, 2):
            value = value + along_z([(z, z ^ mask) for z in range(4)], value)
        return value

    w_qkv, w_out, w_up, w_down = (gather_shards(w) for w in (w_qkv, w_out, w_up, w_down))
    share = D // TEAM
    finish = jnp.cumsum(lengths[0])
    places = jnp.arange(rows, dtype=jnp.int32)
    member = jnp.sum((places[:, None] >= finish[None, :]).astype(jnp.int32), axis=1)
    leading = jnp.any(places[:, None] == (finish - lengths[0])[None, :], axis=1)
    usable = (padding > 0) | leading
    code = (2 * member + usable.astype(jnp.int32)).astype(bf16)
    vectors = [
        gather_shards(v)
        for v in (ln1_gain, ln1_bias, b_query, b_value, b_out, ln2_gain, ln2_bias, b_down, b_up)
    ]
    small = jnp.concatenate(vectors + [code]).reshape(1, -1)
    for bit, mask in ((core, 1), (chip % 2, 2), (chip // 2, 4)):
        other = swap(small, mask)
        small = jnp.concatenate(
            [jnp.where(bit == 0, small, other), jnp.where(bit == 0, other, small)], axis=0
        )
    wide = small.astype(f32)
    first_gain, first_bias, query_bias, value_bias, out_bias, second_gain, second_bias, down_bias = (
        wide[:, i * share : (i + 1) * share].reshape(D) for i in range(8)
    )
    up_bias = lax.dynamic_slice(wide, (2 * chip, 8 * share), (2, FF // TEAM)).reshape(FF_CHIP)
    query_bias = lax.dynamic_slice(query_bias, (chip * D_CHIP,), (D_CHIP,))
    value_bias = lax.dynamic_slice(value_bias, (chip * D_CHIP,), (D_CHIP,))
    codes = jnp.stack(
        [pick(wide, 2 * (chip ^ i) + core)[8 * share + FF // TEAM :] for i in range(CHIPS)]
    )
    of_cell = jnp.floor(codes * 0.5)
    open_key = codes - 2.0 * of_cell
    mask = (of_cell[:, :, None] == of_cell[:, None, :]) & (open_key[:, None, :] > 0.5)
    mask = mask.astype(bf16).reshape(CHIPS * rows, rows)

    by_chip = w_qkv.reshape(share, 3, CHIPS, D_CHIP).transpose(2, 0, 1, 3).reshape(CHIPS, share, 3 * D_CHIP)

    def all_rows(parts):
        mine = jnp.stack(parts)
        lower, upper = by_core(mine, swap(mine, 1))
        both = jnp.stack([lower, upper], axis=1)
        ordered = jnp.stack([pick(both, chip ^ i) for i in range(CHIPS)])
        return ordered.reshape(D, -1)

    whole_tokens = gather_chips(tokens)
    qkv_cols = all_rows(from_chips(lambda i: pick(by_chip, chip ^ i)))
    up_cols = all_rows(
        from_chips(lambda i: lax.dynamic_slice(w_up, (0, (chip ^ i) * FF_CHIP), (share, FF_CHIP)))
    )
    out_rows = jnp.concatenate(by_core(w_out, swap(w_out, 1)), axis=0)
    down_rows = jnp.concatenate(by_core(w_down, swap(w_down, 1)), axis=0)
    whole_cotangent = gather_chips(cotangent)

    inputs = tokens.astype(f32)
    normed_all, _ = normalize(whole_tokens.astype(f32))
    first_low = (normed_all * first_gain + first_bias).astype(bf16)
    qkv_bias = jnp.concatenate([query_bias, jnp.zeros((D_CHIP,), f32), value_bias])
    projected = (mm(first_low, qkv_cols) + qkv_bias).astype(bf16)
    context = attention(projected, mask)
    mixed = inputs + scatter_chips(mm(context, out_rows)) + out_bias
    second_normed, second_inverse = normalize(mixed)
    second_low = gather_chips((second_normed * second_gain + second_bias).astype(bf16))
    hidden_pre = mm(second_low, up_cols) + up_bias
    below = 0.5 * (1.0 + lax.erf(hidden_pre * (0.5**0.5)))
    bell = jnp.exp(-0.5 * hidden_pre * hidden_pre) * 0.3989422804014327
    act_low = (hidden_pre * below).astype(bf16)
    result = mixed + scatter_chips(mm(act_low, down_rows)) + down_bias
    picked = jnp.where(leading[:, None], result, 0.0)
    moments = sum_everywhere(jnp.stack([jnp.sum(picked, axis=0), jnp.sum(picked * picked, axis=0)]))
    moments = moments / (CELLS_DEV * dp_count * fsdp_count)
    cls_mean = moments[0]
    cls_var = moments[1] - cls_mean * cls_mean

    grad_result = cotangent.astype(f32)
    grad_down_bias = jnp.sum(grad_result, axis=0)

    def own_core(grad, parts):
        halves = grad.reshape(parts, 2, -1, grad.shape[-1])
        kept = lax.dynamic_index_in_dim(halves, core, 1, keepdims=False)
        sent = lax.dynamic_index_in_dim(halves, 1 - core, 1, keepdims=False)
        return (kept + swap(sent.astype(bf16), 1).astype(f32)).astype(bf16)

    def own_rows(grad):
        kept = own_core(grad, CHIPS)
        return jnp.stack(from_chips(lambda i: pick(kept, chip ^ i)))

    down_sum = sum_dp(own_core(t_mm(act_low, whole_cotangent), 1)[0])
    grad_act = mm_t(whole_cotangent, down_rows)
    grad_pre = (grad_act * (below + hidden_pre * bell)).astype(bf16)
    grad_up_bias = jnp.sum(grad_pre.astype(f32), axis=0)
    up_sum = sum_dp(own_rows(t_mm(second_low, grad_pre)))
    grad_second = scatter_chips(mm_t(grad_pre, up_cols))
    grad_from_second, grad_second_gain, grad_second_bias = norm_backward(
        grad_second, second_normed, second_inverse, second_gain
    )
    grad_mixed = grad_result + grad_from_second
    grad_branch = grad_mixed.astype(bf16)
    grad_out_bias = jnp.sum(grad_branch.astype(f32), axis=0)
    whole_branch = gather_chips(grad_branch)
    out_sum = sum_dp(own_core(t_mm(context, whole_branch), 1)[0])
    grad_context = mm_t(whole_branch, out_rows).astype(bf16)
    grad_projected = attention_back(projected, mask, grad_context)
    grad_qkv_bias = jnp.sum(grad_projected.astype(f32), axis=0)
    qkv_sum = sum_dp(own_rows(t_mm(first_low, grad_projected)))
    grad_first = scatter_chips(mm_t(grad_projected, qkv_cols))
    first_normed, first_inverse = normalize(inputs)
    grad_from_first, grad_first_gain, grad_first_bias = norm_backward(
        grad_first, first_normed, first_inverse, first_gain
    )
    grad_inputs = grad_mixed + grad_from_first

    full = jnp.stack(
        [
            grad_first_gain,
            grad_first_bias,
            grad_out_bias,
            grad_second_gain,
            grad_second_bias,
            grad_down_bias,
        ]
    ).reshape(6, CHIPS, 2, share)
    full = full.transpose(1, 2, 0, 3).reshape(CHIPS, 2, 6 * share)
    parts = from_chips(lambda i: pick(full, chip ^ i))
    of_chip = jnp.concatenate(
        [
            grad_qkv_bias[:D_CHIP].reshape(2, share),
            grad_qkv_bias[2 * D_CHIP :].reshape(2, share),
            grad_up_bias.reshape(2, FF // TEAM),
        ],
        axis=1,
    )
    both = jnp.concatenate([parts[0] + parts[1] + parts[2] + parts[3], of_chip], axis=1)
    vector = pick(both, core) + swap(pick(both, 1 - core), 1)
    vector = sum_dp_wide(vector)
    cuts = [vector[i * share : (i + 1) * share] for i in range(8)] + [vector[8 * share :]]
    (
        first_gain_sum,
        first_bias_sum,
        out_bias_sum,
        second_gain_sum,
        second_bias_sum,
        down_bias_sum,
        query_bias_sum,
        value_bias_sum,
        up_bias_sum,
    ) = (scatter_shards(v) for v in cuts)

    qkv_total = jnp.stack([pick(qkv_sum, chip ^ i) for i in range(CHIPS)])
    qkv_total = (
        qkv_total.reshape(CHIPS, share, 3, D_CHIP).transpose(1, 2, 0, 3).reshape(share, 3 * D)
    ).astype(f32)
    up_total = jnp.concatenate([pick(up_sum, chip ^ i) for i in range(CHIPS)], axis=1).astype(f32)

    return (
        result.astype(bf16),
        grad_inputs,
        first_gain_sum,
        first_bias_sum,
        scatter_shards(qkv_total),
        query_bias_sum,
        value_bias_sum,
        scatter_shards(out_sum.astype(f32)),
        out_bias_sum,
        second_gain_sum,
        second_bias_sum,
        scatter_shards(up_total),
        up_bias_sum,
        scatter_shards(down_sum.astype(f32)),
        down_bias_sum,
        cls_mean,
        cls_var,
    )


def solution(mesh):
    tokens_spec = P(("dp", "fsdp"), None)
    vector = P("fsdp")
    matrix = P("fsdp", None)
    in_specs = (
        tokens_spec,
        P(("dp", "fsdp"), None),
        P(("dp", "fsdp")),
        vector,
        vector,
        matrix,
        vector,
        vector,
        matrix,
        vector,
        vector,
        vector,
        matrix,
        vector,
        matrix,
        vector,
        tokens_spec,
    )
    out_specs = (
        tokens_spec,
        tokens_spec,
        vector,
        vector,
        matrix,
        vector,
        vector,
        matrix,
        vector,
        vector,
        vector,
        matrix,
        vector,
        matrix,
        vector,
        P(),
        P(),
    )
    return jax.shard_map(local, mesh=mesh, in_specs=in_specs, out_specs=out_specs, check_vma=False)
```

```python
import jax
import jax.numpy as jnp
from jax import lax
from jax.experimental import pallas as pl
from jax.experimental.pallas import tpu as pltpu
from jax.sharding import PartitionSpec as P

D = 1280
HEADS = 20
HEAD_DIM = 64
FF = 5120
CELLS_DEV = 2
EPS = 1e-05

TEAM = 8
CHIPS = 4
HEADS_CHIP = HEADS // CHIPS
D_CHIP = D // CHIPS
FF_CHIP = FF // CHIPS
SHARE = D // TEAM
FF_SHARE = FF // TEAM
SCALE = HEAD_DIM ** (-0.5)

GAIN1, BIAS1, BIAS_OUT, GAIN2, BIAS2, BIAS_DOWN, BIAS_UP, BIAS_QKV = range(8)
TABLE_ROWS = 8

COST = pl.CostEstimate(flops=1, bytes_accessed=1, transcendentals=0)
ANY = pl.BlockSpec(memory_space=pl.ANY)
SMEM = pl.BlockSpec(memory_space=pltpu.SMEM)
VMEM = pl.BlockSpec(memory_space=pltpu.VMEM)

f32 = jnp.float32
bf16 = jnp.bfloat16


def dot(a, b, dims):
    return lax.dot_general(a, b, (dims, ((), ())), preferred_element_type=f32)


def mm(a, b):
    return dot(a, b, ((1,), (0,)))


def mm_t(a, b):
    return dot(a, b, ((1,), (1,)))


def t_mm(a, b):
    return dot(a, b, ((0,), (0,)))


def normalize(values):
    center = jnp.mean(values, axis=-1, keepdims=True)
    centred = values - center
    spread = jnp.mean(centred * centred, axis=-1, keepdims=True)
    inverse = lax.rsqrt(spread + EPS)
    return centred * inverse, inverse


def norm_backward(grad_out, normed, inverse, norm_gain):
    grad_normed = grad_out * norm_gain
    first_mean = jnp.mean(grad_normed, axis=-1, keepdims=True)
    second_mean = jnp.mean(grad_normed * normed, axis=-1, keepdims=True)
    grad_in = inverse * (grad_normed - first_mean - normed * second_mean)
    gain_sum = jnp.sum(grad_out * normed, axis=0, keepdims=True)
    return grad_in, gain_sum, jnp.sum(grad_out, axis=0, keepdims=True)


def heads_of(projected, offset):
    return [
        projected[:, offset + i * HEAD_DIM : offset + (i + 1) * HEAD_DIM] for i in range(HEADS_CHIP)
    ]


def softmax_rows(queries, keys, keep):
    raw = jnp.concatenate([mm_t(q, k) for q, k in zip(queries, keys)], axis=0)
    masked = jnp.where(keep, raw * SCALE, -1e30)
    grown = jnp.exp(masked - jnp.max(masked, axis=-1, keepdims=True))
    return grown * (1.0 / jnp.sum(grown, axis=-1, keepdims=True))


def keep_of(mask):
    return jnp.concatenate([mask.astype(f32)] * HEADS_CHIP, axis=0) > 0.5


def attend(projected, mask):
    rows = mask.shape[0]
    probs = softmax_rows(heads_of(projected, 0), heads_of(projected, D_CHIP), keep_of(mask))
    probs = probs.astype(bf16)
    out = [
        mm(probs[i * rows : (i + 1) * rows], value)
        for i, value in enumerate(heads_of(projected, 2 * D_CHIP))
    ]
    return jnp.concatenate(out, axis=1).astype(bf16)


def attend_back(projected, mask, grad_context):
    rows = mask.shape[0]
    queries, keys, values = (heads_of(projected, i * D_CHIP) for i in range(3))
    grads = heads_of(grad_context, 0)
    probs = softmax_rows(queries, keys, keep_of(mask))
    grad_probs = jnp.concatenate([mm_t(g, v) for g, v in zip(grads, values)], axis=0)
    along = jnp.sum(grad_probs * probs, axis=-1, keepdims=True)
    grad_scores = (probs * (grad_probs - along) * SCALE).astype(bf16)
    probs = probs.astype(bf16)

    def cut(stack, i):
        return stack[i * rows : (i + 1) * rows]

    out = (
        [mm(cut(grad_scores, i), keys[i]) for i in range(HEADS_CHIP)]
        + [t_mm(cut(grad_scores, i), queries[i]) for i in range(HEADS_CHIP)]
        + [t_mm(cut(probs, i), grads[i]) for i in range(HEADS_CHIP)]
    )
    return jnp.concatenate(out, axis=1).astype(bf16)


HALF = SHARE // 2
EXTRA = 16
ROWS_Z = 2 * SHARE


def call(kernel, name, kinds, out_shapes, scratch=(), vmem=16):
    specs = {"s": SMEM, "a": ANY, "v": VMEM}
    return pl.pallas_call(
        kernel,
        in_specs=[specs[kind] for kind in kinds],
        out_specs=[VMEM] * len(out_shapes),
        out_shape=[jax.ShapeDtypeStruct(shape, kind) for shape, kind in out_shapes],
        scratch_shapes=list(scratch),
        compiler_params=pltpu.CompilerParams(vmem_limit_bytes=vmem * 2**20),
        cost_estimate=COST,
        name=name,
    )


def sems(count):
    return pltpu.SemaphoreType.DMA((count,))


def row_at(i, size):
    return pl.ds(pl.multiple_of(i * size, size), size)


def tiled(width, tile, body):
    @pl.loop(0, width // tile)
    def _(i):
        body(row_at(i, tile))


def stack_blocks(blocks, whole):
    rows = blocks[0].shape[0]
    for i, block in enumerate(blocks):
        whole[i * rows : (i + 1) * rows, :] = block[...]


def row_of(spot, i, of_core, half=None):
    row = (2 * (spot[0] ^ i) + of_core) * SHARE
    if half is None:
        return pl.ds(pl.multiple_of(row, SHARE), SHARE)
    return pl.ds(pl.multiple_of(row + half * HALF, HALF), HALF)


def stack_columns(spot, mine, other, whole):
    core, side = spot[1], spot[2]
    for of_core, (near, far) in ((core, mine), (1 - core, other)):
        whole[row_of(spot, 0, of_core), :] = near[:SHARE, :]
        for i in range(1, CHIPS):
            lo = SHARE + (i - 1) * HALF
            whole[row_of(spot, i, of_core, side), :] = near[lo : lo + HALF, :]
            lo = (i - 1) * HALF
            whole[row_of(spot, i, of_core, 1 - side), :] = far[lo : lo + HALF, :]


def by_core_copies(core, mine, other, whole, sem):
    size = mine.shape[0]
    return [
        pltpu.make_async_copy(mine, whole.at[row_at(core, size)], sem.at[0]),
        pltpu.make_async_copy(other, whole.at[row_at(1 - core, size)], sem.at[1]),
    ]


def start_all(copies):
    for copy in copies:
        copy.start()


def wait_all(copies):
    for copy in copies:
        copy.wait()


def chip_columns(weights, rows, chip):
    start = pl.multiple_of((chip * 5 // 2) * 128, 128)
    odd = lax.rem(chip, 2) == 1
    out = []
    for kind in range(3):
        window = weights[rows, pl.ds(kind * D + start, 384)]
        out.append(jnp.where(odd, window[:, 64 : 64 + D_CHIP], window[:, :D_CHIP]))
    return jnp.concatenate(out, axis=1)


def qkv_blocks_kernel(spot, lengths, padding, weights, *refs):
    vectors, own, sent = refs[:9], refs[9], refs[10 : 9 + CHIPS]
    held, marks, whole, vector_sems, sem = refs[9 + CHIPS : 18 + CHIPS], *refs[18 + CHIPS :]
    copies = [
        pltpu.make_async_copy(vector, here, vector_sems.at[i])
        for i, (vector, here) in enumerate(zip(vectors, held))
    ]
    copies.append(pltpu.make_async_copy(padding, marks, sem.at[0]))
    copies.append(pltpu.make_async_copy(weights, whole, sem.at[1]))
    start_all(copies)
    wait_all(copies)
    rows = padding.shape[-1]
    place = lax.broadcasted_iota(jnp.int32, (1, rows), 1)
    first = lengths[0, 0]
    member = (place >= first).astype(f32)
    leading = (place == 0) | (place == first)
    usable = jnp.where(leading | (marks[...].reshape(1, rows) > 0), 1.0, 0.0)
    code = 2.0 * member + usable
    width = 3 * D_CHIP
    lines = [v[...].astype(f32).reshape(1, -1) for v in held]
    extra = jnp.concatenate(
        [
            jnp.concatenate(lines[:6], axis=1),
            jnp.concatenate(lines[6:], axis=1),
            jnp.concatenate([code, jnp.zeros((1, width - rows), f32)], axis=1),
            jnp.zeros((EXTRA - 3, width), f32),
        ],
        axis=0,
    ).astype(bf16)
    own[:SHARE, :] = chip_columns(whole, slice(None), spot[0])
    own[SHARE:, :] = extra
    for i, block in enumerate(sent):
        block[:HALF, :] = chip_columns(whole, row_at(spot[2], HALF), spot[0] ^ (i + 1))
        block[HALF:, :] = extra


def qkv_blocks(spot, lengths, padding, weights, vectors):
    half = ((HALF + EXTRA, 3 * D_CHIP), bf16)
    return call(
        qkv_blocks_kernel,
        "qkv_blocks",
        "ss" + "a" * 11,
        [((SHARE + EXTRA, 3 * D_CHIP), bf16)] + [half] * (CHIPS - 1),
        [pltpu.VMEM(v.shape, v.dtype) for v in vectors]
        + [
            pltpu.VMEM(padding.shape, padding.dtype),
            pltpu.VMEM(weights.shape, weights.dtype),
            sems(9),
            sems(2),
        ],
    )(spot, lengths, padding, weights, *vectors)


def qkv_join_kernel(own, q1, q2, q3, near, near_half, extras):
    near[:SHARE, :] = own[:SHARE, :]
    extras[:EXTRA, :] = own[SHARE:, :]
    for i, block in enumerate((q1, q2, q3)):
        near[SHARE + i * HALF : SHARE + (i + 1) * HALF, :] = block[:HALF, :]
        near_half[i * HALF : (i + 1) * HALF, :] = block[:HALF, :]
        extras[(i + 1) * EXTRA : (i + 2) * EXTRA, :] = block[HALF:, :]


def qkv_join(blocks):
    width = blocks[0].shape[-1]
    return call(
        qkv_join_kernel,
        "qkv_join",
        "vvvv",
        [
            ((SHARE + 3 * HALF, width), bf16),
            ((3 * HALF, width), bf16),
            ((CHIPS * EXTRA, width), bf16),
        ],
    )(*blocks)


def up_blocks_kernel(spot, weights, cotangent, own, *sent):
    def columns(chip):
        return pl.ds(pl.multiple_of(chip * FF_CHIP, FF_CHIP), FF_CHIP)

    rows = cotangent.shape[0]
    own[...] = weights[:, columns(spot[0])]
    for i, block in enumerate(sent):
        block[:rows, :] = cotangent[...]
        block[rows:, :] = weights[row_at(spot[2], HALF), columns(spot[0] ^ (i + 1))]


def up_blocks(spot, weights, cotangent):
    half = ((cotangent.shape[0] + HALF, FF_CHIP), bf16)
    return call(
        up_blocks_kernel, "up_blocks", "svv", [((SHARE, FF_CHIP), bf16)] + [half] * (CHIPS - 1)
    )(spot, weights, cotangent)


def up_join_kernel(own, cotangent, u1, u2, u3, near, near_half, whole):
    rows = cotangent.shape[0]
    near[:SHARE, :] = own[...]
    whole[:rows, :] = cotangent[...]
    for i, block in enumerate((u1, u2, u3)):
        near[SHARE + i * HALF : SHARE + (i + 1) * HALF, :] = block[rows:, :]
        near_half[i * HALF : (i + 1) * HALF, :] = block[rows:, :]
        whole[(i + 1) * rows : (i + 2) * rows, :] = block[:rows, :]


def up_join(own, cotangent, blocks):
    return call(
        up_join_kernel,
        "up_join",
        "vvvvv",
        [
            ((SHARE + 3 * HALF, FF_CHIP), bf16),
            ((3 * HALF, FF_CHIP), bf16),
            ((CHIPS * cotangent.shape[0], D), bf16),
        ],
    )(own, cotangent, *blocks)


def fill_table(spot, extras, table, mask):
    chip, core = spot[0], spot[1]
    rows = mask.shape[1]
    table[...] = jnp.zeros_like(table)
    for team in range(TEAM):
        for i in range(6):
            table[i : i + 1, team * SHARE : (team + 1) * SHARE] = extras[
                team, 0:1, i * SHARE : (i + 1) * SHARE
            ]
    for half in range(2):
        line = extras[2 * chip + half, 1:2, :]
        lo = half * SHARE
        table[BIAS_QKV : BIAS_QKV + 1, lo : lo + SHARE] = line[:, :SHARE]
        table[BIAS_QKV : BIAS_QKV + 1, 2 * D_CHIP + lo : 2 * D_CHIP + lo + SHARE] = line[
            :, SHARE : 2 * SHARE
        ]
        table[BIAS_UP : BIAS_UP + 1, half * FF_SHARE : (half + 1) * FF_SHARE] = line[:, 2 * SHARE :]
    for i in range(CHIPS):
        code = extras[2 * (chip ^ i) + core, 2:3, :rows]
        of_key = jnp.broadcast_to(code, (rows, rows))
        cell_of_key = jnp.floor(of_key * 0.5)
        open_key = of_key - 2.0 * cell_of_key
        keep = jnp.where(cell_of_key == cell_of_key.T, open_key, 0.0)
        mask[i * rows : (i + 1) * rows, :] = keep.astype(bf16)


def token_norm_kernel(x0, x1, x2, x3, normed):
    rows = x0.shape[0]
    for i, x in enumerate((x0, x1, x2, x3)):
        normed[i * rows : (i + 1) * rows, :] = normalize(x[...].astype(f32))[0]


def token_norm(blocks):
    rows, width = blocks[0].shape
    return call(token_norm_kernel, "token_norm", "vvvv", [((CHIPS * rows, width), f32)])(*blocks)[0]


def enter_kernel(spot, normed, *refs):
    mine, other, refs = refs[:3], refs[3:6], refs[6:]
    out_mine, out_other, refs = *refs[:2], refs[2:]
    table, mask, qkv, out, first_low, projected, context = refs[:7]
    partials = refs[7 : 7 + CHIPS]
    extras, out_sems = refs[7 + CHIPS :]
    rows = mask.shape[1]
    out_copies = by_core_copies(spot[1], out_mine, out_other, out, out_sems)
    start_all(out_copies)
    for of_core, lines in ((spot[1], mine[2]), (1 - spot[1], other[2])):
        for i in range(CHIPS):
            extras[2 * (spot[0] ^ i) + of_core] = lines[i * EXTRA : (i + 1) * EXTRA, :].astype(f32)
    fill_table(spot, extras, table, mask)
    stack_columns(spot, mine[:2], other[:2], qkv)
    gain = table[GAIN1 : GAIN1 + 1, :]
    bias = table[BIAS1 : BIAS1 + 1, :]
    first_low[...] = (normed[...] * gain + bias).astype(bf16)
    for lo, hi in ((0, 384), (384, 768), (768, 960)):
        shift = table[BIAS_QKV : BIAS_QKV + 1, lo:hi]
        projected[:, lo:hi] = (mm(first_low[...], qkv[:, lo:hi]) + shift).astype(bf16)

    @pl.loop(0, CHIPS)
    def _(i):
        at = row_at(i, rows)
        context[at, :] = attend(projected[at, :], mask[at, :])

    wait_all(out_copies)

    def partial(at):
        whole = mm(context[...], out[:, at]).astype(bf16)
        for i, part in enumerate(partials):
            part[:, at] = whole[i * rows : (i + 1) * rows]

    tiled(D, 256, partial)


def enter(spot, normed, mine, other, out_mine, out_other):
    total = normed.shape[0]
    rows = total // CHIPS
    outs = call(
        enter_kernel,
        "enter",
        "sv" + "v" * 6 + "aa",
        [
            ((TABLE_ROWS, D), f32),
            ((total, rows), bf16),
            ((D, 3 * D_CHIP), bf16),
            ((D_CHIP, D), bf16),
            ((total, D), bf16),
            ((total, 3 * D_CHIP), bf16),
            ((total, D_CHIP), bf16),
        ]
        + [((rows, D), bf16)] * CHIPS,
        [pltpu.VMEM((TEAM, EXTRA, 3 * D_CHIP), f32), sems(2)],
    )(spot, normed, *mine, *other, out_mine, out_other)
    return outs[:7], outs[7:]


def leave_kernel(
    b0, b1, b2, b3, qkv, out, projected, mask, branch, grad_projected, bias_sum, *refs
):
    partials, grad_context = refs[:CHIPS], refs[CHIPS]
    rows = b0.shape[0]
    stack_blocks((b0, b1, b2, b3), branch)
    grad_context[...] = mm_t(branch[...], out[...]).astype(bf16)
    bias_sum[...] = jnp.zeros_like(bias_sum)

    @pl.loop(0, CHIPS)
    def _(i):
        at = row_at(i, rows)
        grad = attend_back(projected[at, :], mask[at, :], grad_context[at, :])
        grad_projected[at, :] = grad
        bias_sum[...] += jnp.sum(grad.astype(f32), axis=0, keepdims=True)

    def partial(at):
        whole = mm_t(grad_projected[...], qkv[at, :]).astype(bf16)
        for i, part in enumerate(partials):
            part[:, at] = whole[i * rows : (i + 1) * rows]

    tiled(D, 256, partial)


def leave(blocks, qkv, out, projected, mask):
    rows = blocks[0].shape[0]
    total = CHIPS * rows
    outs = call(
        leave_kernel,
        "leave",
        "v" * 8,
        [((total, D), bf16), ((total, 3 * D_CHIP), bf16), ((1, 3 * D_CHIP), f32)]
        + [((rows, D), bf16)] * CHIPS,
        [pltpu.VMEM((total, D_CHIP), bf16)],
    )(*blocks, qkv, out, projected, mask)
    return outs[:3], outs[3:]


def total_of(parts):
    total = parts[0][...].astype(f32)
    for part in parts[1:]:
        total = total + part[...].astype(f32)
    return total


def mix_kernel(p0, p1, p2, p3, tokens, table, mixed, second):
    total = total_of((p0, p1, p2, p3)) + tokens[...].astype(f32)
    total = total + table[BIAS_OUT : BIAS_OUT + 1, :]
    mixed[...] = total
    normed, _ = normalize(total)
    second[...] = (normed * table[GAIN2 : GAIN2 + 1, :] + table[BIAS2 : BIAS2 + 1, :]).astype(bf16)


def mix(parts, tokens, table):
    shape = tokens.shape
    return call(mix_kernel, "mix", "v" * 6, [(shape, f32), (shape, bf16)])(*parts, tokens, table)


def unmix_kernel(p0, p1, p2, p3, mixed, table, cotangent, grad_mixed, branch, sums):
    grad = total_of((p0, p1, p2, p3))
    normed, inverse = normalize(mixed[...])
    grad_in, gain_sum, bias_sum = norm_backward(grad, normed, inverse, table[GAIN2 : GAIN2 + 1, :])
    grad_out = cotangent[...].astype(f32)
    grad_in = grad_in + grad_out
    grad_mixed[...] = grad_in
    low = grad_in.astype(bf16)
    branch[...] = low
    sums[...] = jnp.zeros_like(sums)
    sums[0:1, :] = jnp.sum(low.astype(f32), axis=0, keepdims=True)
    sums[1:2, :] = gain_sum
    sums[2:3, :] = bias_sum
    sums[3:4, :] = jnp.sum(grad_out, axis=0, keepdims=True)


def unmix(parts, mixed, table, cotangent):
    shape = cotangent.shape
    return call(
        unmix_kernel, "unmix", "v" * 7, [(shape, f32), (shape, bf16), ((8, D), f32)]
    )(*parts, mixed, table, cotangent)


def act_grad_kernel(spot, whole, mine, other, grad_act, down, down_sems):
    copies = by_core_copies(spot[1], mine, other, down, down_sems)
    start_all(copies)
    wait_all(copies)

    def columns(at):
        grad_act[:, at] = mm_t(whole[...], down[at, :])

    tiled(FF_CHIP, 256, columns)


def act_grad(spot, cotangent, down_mine, down_other):
    return call(
        act_grad_kernel,
        "act_grad",
        "svaa",
        [((cotangent.shape[0], FF_CHIP), f32), ((FF_CHIP, D), bf16)],
        [sems(2)],
    )(spot, cotangent, down_mine, down_other)


def hidden_kernel(spot, s0, s1, s2, s3, grad_act, cotangent, table, *refs):
    mine, other, refs = refs[:2], refs[2:4], refs[4:]
    second, act, grad_pre, down_sent, bias_sum = refs[:5]
    partials = refs[5 : 5 + CHIPS]
    up, pre_act = refs[5 + CHIPS :]
    rows = s0.shape[0]
    stack_columns(spot, mine, other, up)
    stack_blocks((s0, s1, s2, s3), second)

    def columns(at):
        pre_act[:, at] = mm(second[...], up[:, at]) + table[BIAS_UP : BIAS_UP + 1, at]

    tiled(FF_CHIP, 256, columns)
    bias_sum[...] = jnp.zeros_like(bias_sum)

    def activate(at):
        pre = pre_act[at, :]
        below = 0.5 * (1.0 + lax.erf(pre * (0.5**0.5)))
        bell = jnp.exp(-0.5 * pre * pre) * 0.3989422804014327
        act[at, :] = (pre * below).astype(bf16)
        grad = (grad_act[at, :] * (below + pre * bell)).astype(bf16)
        grad_pre[at, :] = grad
        bias_sum[...] += jnp.sum(grad.astype(f32), axis=0, keepdims=True)

    tiled(second.shape[0], 64, activate)
    first = (1 - spot[1]) * FF_SHARE

    @pl.loop(0, FF_SHARE // 128)
    def _(i):
        columns_at = pl.ds(pl.multiple_of(first + i * 128, 128), 128)
        down_sent[row_at(i, 128), :] = t_mm(act[:, columns_at], cotangent[...]).astype(bf16)

    def partial(at):
        whole = mm_t(grad_pre[...], up[at, :]).astype(bf16)
        for i, part in enumerate(partials):
            part[:, at] = whole[i * rows : (i + 1) * rows]

    tiled(D, 256, partial)


def hidden(spot, blocks, grad_act, cotangent, table, mine, other):
    rows = blocks[0].shape[0]
    total = CHIPS * rows
    outs = call(
        hidden_kernel,
        "hidden",
        "svvvvvvv" + "v" * 4,
        [
            ((total, D), bf16),
            ((total, FF_CHIP), bf16),
            ((total, FF_CHIP), bf16),
            ((FF_SHARE, D), bf16),
            ((1, FF_CHIP), f32),
        ]
        + [((rows, D), bf16)] * CHIPS,
        [pltpu.VMEM((D, FF_CHIP), bf16), pltpu.VMEM((total, FF_CHIP), f32)],
    )(spot, *blocks, grad_act, cotangent, table, *mine, *other)
    return outs[:5], outs[5:]


def down_grad_kernel(spot, act, cotangent, got, first, second):
    kept = pl.ds(pl.multiple_of(spot[1] * FF_SHARE, 128), FF_SHARE)
    half = FF_SHARE // 2
    total = t_mm(act[:, kept], cotangent[...]) + got[...].astype(f32)
    first[...] = total[:half].astype(bf16)
    second[...] = total[half:].astype(bf16)


def down_grad_of(spot, act, cotangent, got):
    half = FF_SHARE // 2
    return call(
        down_grad_kernel, "down_grad", "svvv", [((half, D), bf16), ((half, D), bf16)]
    )(spot, act, cotangent, got)


def split_rows(core, whole, sent, kept):
    for k in range(CHIPS):
        targets = ((sent[k // 2], k % 2, 1 - core), (kept, k, core))
        for target, at, of_core in targets:
            start = pl.multiple_of((2 * k + of_core) * SHARE, SHARE)
            target[at] = whole[pl.ds(start, SHARE), :].astype(bf16)


def up_grad_kernel(spot, second, grad_pre, sent_a, sent_b, kept, whole):
    def columns(at):
        whole[at, :] = t_mm(second[:, at], grad_pre[...])

    tiled(D, 256, columns)
    split_rows(spot[1], whole, (sent_a, sent_b), kept)


def up_grad_of(spot, second, grad_pre):
    half = ((CHIPS // 2, SHARE, FF_CHIP), bf16)
    return call(
        up_grad_kernel,
        "up_grad",
        "svv",
        [half, half, ((CHIPS, SHARE, FF_CHIP), bf16)],
        [pltpu.VMEM((D, FF_CHIP), f32)],
    )(spot, second, grad_pre)


def result_kernel(act, down, *partials):
    rows = partials[0].shape[0]

    def columns(at):
        whole = mm(act[...], down[:, at]).astype(bf16)
        for i, part in enumerate(partials):
            part[:, at] = whole[i * rows : (i + 1) * rows]

    tiled(D, 256, columns)


def result_of(act, down):
    rows = act.shape[0] // CHIPS
    return call(result_kernel, "result", "vv", [((rows, D), bf16)] * CHIPS)(act, down)


def qkv_grad_kernel(
    spot,
    first_low,
    grad_projected,
    context,
    branch,
    sent_a,
    sent_b,
    kept,
    out_sent,
    out_kept,
    whole,
    out,
):
    core = spot[1]

    def columns(at):
        whole[at, :] = t_mm(first_low[:, at], grad_projected[...])

    tiled(D, 256, columns)
    split_rows(core, whole, (sent_a, sent_b), kept)
    out[...] = t_mm(context[...], branch[...])
    for target, of_core in ((out_sent, 1 - core), (out_kept, core)):
        target[...] = out[row_at(of_core, SHARE), :].astype(bf16)


def qkv_grad_of(spot, first_low, grad_projected, context, branch):
    half = ((CHIPS // 2, SHARE, 3 * D_CHIP), bf16)
    rows = ((SHARE, D), bf16)
    return call(
        qkv_grad_kernel,
        "qkv_grad",
        "svvvv",
        [half, half, ((CHIPS, SHARE, 3 * D_CHIP), bf16), rows, rows],
        [pltpu.VMEM((D, 3 * D_CHIP), f32), pltpu.VMEM((D_CHIP, D), f32)],
    )(spot, first_low, grad_projected, context, branch)


def add_kernel(*refs):
    count = len(refs) // 3
    for a, b, c in zip(refs[:count], refs[count : 2 * count], refs[2 * count :]):
        c[...] = (a[...].astype(f32) + b[...].astype(f32)).astype(c.dtype)


def add_all(left, right):
    shapes = [(a.shape, a.dtype) for a in left]
    return call(add_kernel, "add", "v" * (2 * len(left)), shapes)(*left, *right)


def split_add_kernel(kept, got_a, got_b, *halves):
    for i, (half, got) in enumerate(zip(halves, (got_a, got_b))):
        for j in range(CHIPS // 2):
            total = kept[i * CHIPS // 2 + j].astype(f32) + got[j].astype(f32)
            half[j * SHARE : (j + 1) * SHARE, :] = total.astype(bf16)


def split_add(kept, got_a, got_b):
    shape = (ROWS_Z, kept.shape[-1])
    return call(split_add_kernel, "split_add", "vvv", [(shape, bf16)] * 2)(kept, got_a, got_b)


PACKED = SHARE * 3 // 4
STEP = SHARE // 4


def pack_kernel(kept, got_a, got_b, out_kept, out_got, *chunks):
    for i, chunk in enumerate(chunks):
        for j in range(2):
            got = got_b if i else got_a
            total = (kept[2 * i + j].astype(f32) + got[j].astype(f32)).astype(bf16)
            lo = j * PACKED
            chunk[lo : lo + PACKED, : 3 * D_CHIP] = total[:PACKED]
            for part in range(3):
                at = lo + part * STEP
                chunk[at : at + STEP, 3 * D_CHIP :] = total[
                    PACKED:, part * D_CHIP : (part + 1) * D_CHIP
                ]
        rows = slice(i * HALF, (i + 1) * HALF)
        total = out_kept[rows, :].astype(f32) + out_got[rows, :].astype(f32)
        chunk[2 * PACKED :, :] = total.astype(bf16)


def pack(kept, got_a, got_b, out_kept, out_got):
    return call(pack_kernel, "pack", "vvvvv", [((ROWS_Z, D), bf16)] * 2)(
        kept, got_a, got_b, out_kept, out_got
    )


def unpacked(chunk, j):
    lo = j * PACKED
    tail = [
        chunk[lo + part * STEP : lo + (part + 1) * STEP, 3 * D_CHIP :] for part in range(3)
    ]
    return jnp.concatenate(
        [chunk[lo : lo + PACKED, : 3 * D_CHIP], jnp.concatenate(tail, axis=1)], axis=0
    )


def z_kernel(names, spot, *refs):
    ref = dict(zip(names, refs))
    middle = spot[3] > 0
    if "half" in ref:
        ref["half"][...] = (ref["low"][...].astype(f32) + ref["got_side"][...].astype(f32)).astype(
            bf16
        )
    if "send" in ref:
        sent = None
        if "half_before" in ref:
            sent = (
                ref["half_before"][...].astype(f32) + ref["got_middle"][...].astype(f32)
            ).astype(bf16)
        if "low_next" in ref:
            low_next = ref["low_next"][...]
            sent = low_next if sent is None else jnp.where(middle, sent, low_next)
        ref["send"][...] = sent
    if "final" in ref:
        ref["final"][...] = jnp.where(middle, ref["sent_before"][...], ref["got_side"][...])


def z_step(spot, inputs, outputs):
    inputs = {name: value for name, value in inputs.items() if value is not None}
    names = tuple(inputs) + tuple(outputs)
    shape = ((ROWS_Z, D), bf16)

    def kernel(*refs):
        z_kernel(names, *refs)

    done = call(kernel, "z_step", "s" + "v" * len(inputs), [shape] * len(outputs))(
        spot, *inputs.values()
    )
    return dict(zip(outputs, done))


def last_kernel(spot, down_a, sent, got, b0, b1, b2, b3, down, qkv, stack):
    down[:ROWS_Z, :] = down_a[...].astype(f32)
    down[ROWS_Z:, :] = jnp.where(spot[3] > 0, sent[...], got[...]).astype(f32)
    qkv_rows(spot, (b0, b1, b2, b3), qkv, stack)


def last(spot, down_a, sent, got, blocks):
    shape = blocks[0].shape
    return call(
        last_kernel,
        "last",
        "s" + "v" * 7,
        [((2 * ROWS_Z, D), f32), ((shape[0], 3 * D), f32)],
        [pltpu.VMEM((CHIPS,) + shape, bf16)],
    )(spot, down_a, sent, got, *blocks)


def up_exchange_kernel(spot, a, b, *blocks):
    chunks = (a, b)
    for i, block in enumerate(blocks):
        chip = spot[0] ^ i
        at = row_at(lax.rem(chip, 2), SHARE)
        block[...] = jnp.where(chip >= 2, chunks[1][at, :], chunks[0][at, :])


def up_exchange(spot, a, b):
    return call(up_exchange_kernel, "up_exchange", "svv", [((SHARE, FF_CHIP), bf16)] * CHIPS)(
        spot, a, b
    )


def qkv_exchange_kernel(spot, a, b, *refs):
    blocks, out_rows, stack = refs[:CHIPS], refs[CHIPS], refs[CHIPS + 1]
    for i, chunk in enumerate((a, b)):
        for j in range(2):
            stack[2 * i + j] = unpacked(chunk, j)
        out_rows[i * HALF : (i + 1) * HALF, :] = chunk[2 * PACKED :, :].astype(f32)
    for i, block in enumerate(blocks):
        block[...] = stack[spot[0] ^ i]


def qkv_exchange(spot, a, b):
    shape = (SHARE, 3 * D_CHIP)
    outs = call(
        qkv_exchange_kernel,
        "qkv_exchange",
        "svv",
        [(shape, bf16)] * CHIPS + [((SHARE, D), f32)],
        [pltpu.VMEM((CHIPS,) + shape, bf16)],
    )(spot, a, b)
    return outs[:CHIPS], outs[CHIPS]


def qkv_rows(spot, blocks, weights, stack):
    for i, block in enumerate(blocks):
        stack[spot[0] ^ i] = block[...]
    for chip in range(CHIPS):
        for kind in range(3):
            lo = kind * D + chip * D_CHIP
            weights[:, lo : lo + D_CHIP] = stack[
                chip, :, kind * D_CHIP : (kind + 1) * D_CHIP
            ].astype(f32)


def up_rows_kernel(spot, b0, b1, b2, b3, weights):
    for i, block in enumerate((b0, b1, b2, b3)):
        start = pl.multiple_of((spot[0] ^ i) * FF_CHIP, FF_CHIP)
        weights[:, pl.ds(start, FF_CHIP)] = block[...].astype(f32)


def up_rows(spot, blocks):
    return call(up_rows_kernel, "up_rows", "svvvv", [((SHARE, FF), f32)])(spot, *blocks)[0]


def end_kernel(
    spot,
    lengths,
    p0,
    p1,
    p2,
    p3,
    r0,
    r1,
    r2,
    r3,
    grad_mixed,
    tokens,
    table,
    mixed,
    mix_sums,
    qkv_sum,
    up_sum,
    layer_out,
    grad_tokens,
    sums,
):
    grad = total_of((p0, p1, p2, p3))
    normed, inverse = normalize(tokens[...].astype(f32))
    grad_in, gain_sum, bias_sum = norm_backward(grad, normed, inverse, table[GAIN1 : GAIN1 + 1, :])
    grad_tokens[...] = grad_mixed[...] + grad_in
    result = mixed[...] + total_of((r0, r1, r2, r3)) + table[BIAS_DOWN : BIAS_DOWN + 1, :]
    layer_out[...] = result.astype(bf16)
    place = lax.broadcasted_iota(jnp.int32, (result.shape[0], 1), 0)
    picked = jnp.where((place == 0) | (place == lengths[0, 0]), result, 0.0)
    sums[...] = jnp.zeros_like(sums)
    sums[0:1, :] = gain_sum
    sums[1:2, :] = bias_sum
    sums[2:6, :] = mix_sums[0:4, :]
    sums[6:7, :] = jnp.sum(picked, axis=0, keepdims=True)
    sums[7:8, :] = jnp.sum(picked * picked, axis=0, keepdims=True)
    for k in range(CHIPS):
        here = spot[0] == k
        sums[8 + k : 9 + k, :D_CHIP] = jnp.where(here, qkv_sum[:, :D_CHIP], 0.0)
        sums[12 + k : 13 + k, :D_CHIP] = jnp.where(here, qkv_sum[:, 2 * D_CHIP :], 0.0)
        sums[16 + k : 17 + k, :] = jnp.where(here, up_sum[...], 0.0)


def end(spot, lengths, parts, results, *rest):
    shape = parts[0].shape
    return call(
        end_kernel,
        "end",
        "ss" + "v" * 15,
        [(shape, bf16), (shape, f32), ((24, D), f32)],
    )(spot, lengths, *parts, *results, *rest)


def fence(*values):
    return lax.optimization_barrier(values)


def local(
    tokens,
    lengths,
    padding,
    ln1_gain,
    ln1_bias,
    w_qkv,
    b_query,
    b_value,
    w_out,
    b_out,
    ln2_gain,
    ln2_bias,
    w_up,
    b_up,
    w_down,
    b_down,
    cotangent,
):
    fsdp_count = lax.axis_size("fsdp")
    dp_count = lax.axis_size("dp")
    groups = fsdp_count // TEAM
    place = lax.axis_index("fsdp") // groups
    chip = place // 2
    core = place % 2
    depth = lax.axis_index("dp")
    middle = (depth == 1) | (depth == 2)
    spot = jnp.stack([chip, core, depth % 2, middle.astype(jnp.int32)]).astype(jnp.int32)

    def swap(value, mask):
        pairs = [
            (team * groups + group, (team ^ mask) * groups + group)
            for team in range(TEAM)
            for group in range(groups)
        ]
        return lax.ppermute(value, "fsdp", pairs)

    shard_groups = [[team * groups + group for group in range(groups)] for team in range(TEAM)]
    def gather_shards(value):
        if groups == 1:
            return value
        return lax.all_gather(value, "fsdp", axis=0, tiled=True, axis_index_groups=shard_groups)

    def scatter_shards(value):
        if groups == 1:
            return value
        return lax.psum_scatter(
            value, "fsdp", scatter_dimension=0, tiled=True, axis_index_groups=shard_groups
        )

    def along_z(pairs, value):
        return lax.ppermute(value, "dp", pairs)

    def z_swap(value):
        return along_z([(0, 1), (1, 0), (2, 3), (3, 2)], value)

    def z_middle(value):
        return along_z([(1, 2), (2, 1)], value)

    def from_chips(blocks):
        return [blocks[0]] + [swap(block, 2 * i) for i, block in enumerate(blocks) if i > 0]

    def fence_list(first, *others):
        done = fence(*first, *others)
        return list(done[: len(first)]), *done[len(first) :]

    w_qkv, w_out, w_up, w_down = (gather_shards(w) for w in (w_qkv, w_out, w_up, w_down))
    given = (ln1_gain, ln1_bias, b_out, ln2_gain, ln2_bias, b_down, b_query, b_value, b_up)
    qkv_sent = qkv_blocks(spot, lengths, padding, w_qkv, [gather_shards(v) for v in given])
    qkv_near, qkv_half, extras = qkv_join(from_chips(qkv_sent))
    qkv_far = z_swap(qkv_half)
    qkv_near_other, extras_other = swap(qkv_near, 1), swap(extras, 1)
    tokens_sent, extras = fence(tokens, extras)
    blocks = [tokens] + [swap(tokens_sent, 2 * i) for i in range(1, CHIPS)]
    normed = token_norm(blocks)
    normed, qkv_far, extras_other = fence(normed, qkv_far, extras_other)
    qkv_far_other = swap(qkv_far, 1)
    out_sent, normed = fence(w_out, normed)
    out_other = swap(out_sent, 1)
    up_own, *up_sent = up_blocks(spot, w_up, cotangent)
    up_sent, normed = fence_list(up_sent, normed)
    loads = [swap(block, 2 * i + 2) for i, block in enumerate(up_sent)]

    (table, mask, qkv, out, first_low, projected, context), partial_out = enter(
        spot,
        normed,
        [qkv_near, qkv_far, extras],
        [qkv_near_other, qkv_far_other, extras_other],
        w_out,
        out_other,
    )
    loads, *partial_out = fence_list(loads, *partial_out)
    out_parts = from_chips(partial_out)
    up_near, up_half, whole_cotangent = up_join(up_own, cotangent, loads)
    up_far = z_swap(up_half)
    down_sent, up_half = fence(w_down, up_half)
    down_other = swap(down_sent, 1)
    out_parts, down_other = fence_list(out_parts, down_other)
    mixed, second_own = mix(out_parts, tokens, table)
    second_blocks = from_chips([second_own] * CHIPS)
    up_near, up_far, second_own = fence(up_near, up_far, second_own)
    up_near_other, up_far_other = swap(up_near, 1), swap(up_far, 1)
    whole_cotangent, second_own = fence(whole_cotangent, second_own)
    grad_act, down = act_grad(spot, whole_cotangent, w_down, down_other)

    second_blocks, grad_act = fence_list(second_blocks, grad_act)
    (second_low, act_low, grad_pre, down_sent, up_bias_sum), partial_second = hidden(
        spot,
        second_blocks,
        grad_act,
        whole_cotangent,
        table,
        [up_near, up_far],
        [up_near_other, up_far_other],
    )
    down_got = swap(down_sent, 1)
    second_parts = from_chips(partial_second)
    down_a, down_b = down_grad_of(spot, act_low, whole_cotangent, down_got)
    side0 = z_swap(down_a)

    second_low, down_a = fence(second_low, down_a)
    up_sent_a, up_sent_b, up_kept = up_grad_of(spot, second_low, grad_pre)
    up_a, up_b = split_add(up_kept, swap(up_sent_a, 1), swap(up_sent_b, 1))

    second_parts, side0, up_a = fence_list(second_parts, side0, up_a)
    z = z_step(spot, dict(got_side=side0, low=down_a, low_next=up_a), ("half", "send"))
    half0, send1 = z["half"], z["send"]
    side1, middle1 = z_swap(send1), z_middle(half0)
    second_parts, half0 = fence_list(second_parts, half0)
    grad_mixed, branch_own, mix_sums = unmix(second_parts, mixed, table, cotangent)
    branch_blocks = from_chips([branch_own] * CHIPS)
    act_low, branch_own = fence(act_low, branch_own)
    partial_result = result_of(act_low, down)

    branch_blocks, side1, middle1, *partial_result = fence_list(
        branch_blocks, side1, middle1, *partial_result
    )
    z = z_step(
        spot,
        dict(got_side=side1, got_middle=middle1, low=up_a, half_before=half0, low_next=up_b),
        ("half", "send"),
    )
    half1, send2 = z["half"], z["send"]
    side2, middle2 = z_swap(send2), z_middle(half1)
    branch_blocks, half1 = fence_list(branch_blocks, half1)
    (whole_branch, grad_projected, qkv_bias_sum), partial_first = leave(
        branch_blocks, qkv, out, projected, mask
    )
    first_low, grad_projected = fence(first_low, grad_projected)
    qkv_sent_a, qkv_sent_b, qkv_kept, out_sent, out_kept = qkv_grad_of(
        spot, first_low, grad_projected, context, whole_branch
    )
    qkv_a, qkv_b = pack(
        qkv_kept, swap(qkv_sent_a, 1), swap(qkv_sent_b, 1), out_kept, swap(out_sent, 1)
    )

    side2, middle2, qkv_a = fence(side2, middle2, qkv_a)
    z = z_step(
        spot,
        dict(got_side=side2, got_middle=middle2, low=up_b, half_before=half1, low_next=qkv_a),
        ("half", "send"),
    )
    half2, send3 = z["half"], z["send"]
    side3, middle3 = z_swap(send3), z_middle(half2)
    *partial_first, half2 = fence(*partial_first, half2)
    first_parts = from_chips(partial_first)
    down_a_final = z_step(spot, dict(got_side=side2, sent_before=send2), ("final",))["final"]

    first_parts, side3, middle3 = fence_list(first_parts, side3, middle3)
    z = z_step(
        spot,
        dict(
            got_side=side3,
            got_middle=middle3,
            low=qkv_a,
            half_before=half2,
            low_next=qkv_b,
            sent_before=send3,
        ),
        ("half", "send", "final"),
    )
    half3, send4, up_a_final = z["half"], z["send"], z["final"]
    side4, middle4 = z_swap(send4), z_middle(half3)
    *partial_result, half3 = fence(*partial_result, half3)
    result_parts = from_chips(partial_result)

    result_parts, side4, middle4 = fence_list(result_parts, side4, middle4)
    z = z_step(
        spot,
        dict(
            got_side=side4,
            got_middle=middle4,
            low=qkv_b,
            half_before=half3,
            low_next=down_b,
            sent_before=send4,
        ),
        ("half", "send", "final"),
    )
    half4, send5, up_b_final = z["half"], z["send"], z["final"]
    side5, middle5 = z_swap(send5), z_middle(half4)
    result_parts, half4 = fence_list(result_parts, half4)
    layer_out, grad_tokens, sums = end(
        spot,
        lengths,
        first_parts,
        result_parts,
        grad_mixed,
        tokens,
        table,
        mixed,
        mix_sums,
        qkv_bias_sum,
        up_bias_sum,
    )
    for mask_bit in (1, 2, 4):
        (sums,) = add_all([sums], [swap(sums, mask_bit)])
    if groups > 1:
        sums = lax.psum(sums, "fsdp", axis_index_groups=shard_groups)
    sums_got = z_swap(sums)

    side5, middle5, sums_got = fence(side5, middle5, sums_got)
    z = z_step(
        spot,
        dict(
            got_side=side5,
            got_middle=middle5,
            low=down_b,
            half_before=half4,
            sent_before=send5,
        ),
        ("half", "send", "final"),
    )
    half5, send6, qkv_a_final = z["half"], z["send"], z["final"]
    side6, middle6 = z_swap(send6), z_middle(half5)
    up_a_final, half5 = fence(up_a_final, half5)
    up_total = from_chips(up_exchange(spot, up_a_final, up_b_final))
    (sums,) = add_all([sums], [sums_got])

    up_total, side6, middle6, sums = fence_list(up_total, side6, middle6, sums)
    z = z_step(
        spot,
        dict(got_side=side6, got_middle=middle6, half_before=half5, sent_before=send6),
        ("send", "final"),
    )
    send7, qkv_b_final = z["send"], z["final"]
    side7 = along_z([(1, 0), (2, 3)], send7)
    qkv_a_final, send7, sums = fence(qkv_a_final, send7, sums)
    qkv_last, out_grad = qkv_exchange(spot, qkv_a_final, qkv_b_final)
    qkv_total = from_chips(qkv_last)
    sums_got = along_z([(z, z ^ 2) for z in range(4)], sums)
    up_grad = up_rows(spot, up_total)
    qkv_total, side7, up_grad = fence_list(qkv_total, side7, up_grad)
    down_grad, qkv_grad = last(spot, down_a_final, send7, side7, qkv_total)
    (sums,) = add_all([sums], [sums_got])

    index = lax.axis_index("fsdp")
    size = D // fsdp_count

    def owned(row):
        return lax.dynamic_slice(sums, (row, index * size), (1, size)).reshape(size)

    def owned_at(row, width, share):
        start = index * share
        return lax.dynamic_slice(sums, (row + start // width, start % width), (1, share)).reshape(
            share
        )

    moments = sums[6:8] / (CELLS_DEV * dp_count * fsdp_count)
    cls_mean = moments[0]
    cls_var = moments[1] - cls_mean * cls_mean

    return (
        layer_out,
        grad_tokens,
        owned(0),
        owned(1),
        scatter_shards(qkv_grad),
        owned_at(8, D_CHIP, size),
        owned_at(12, D_CHIP, size),
        scatter_shards(out_grad),
        owned(2),
        owned(3),
        owned(4),
        scatter_shards(up_grad),
        owned_at(16, FF_CHIP, FF // fsdp_count),
        scatter_shards(down_grad),
        owned(5),
        cls_mean,
        cls_var,
    )


def solution(mesh):
    tokens_spec = P(("dp", "fsdp"), None)
    vector = P("fsdp")
    matrix = P("fsdp", None)
    in_specs = (
        tokens_spec,
        P(("dp", "fsdp"), None),
        P(("dp", "fsdp")),
        vector,
        vector,
        matrix,
        vector,
        vector,
        matrix,
        vector,
        vector,
        vector,
        matrix,
        vector,
        matrix,
        vector,
        tokens_spec,
    )
    out_specs = (
        tokens_spec,
        tokens_spec,
        vector,
        vector,
        matrix,
        vector,
        vector,
        matrix,
        vector,
        vector,
        vector,
        matrix,
        vector,
        matrix,
        vector,
        P(),
        P(),
    )
    return jax.shard_map(local, mesh=mesh, in_specs=in_specs, out_specs=out_specs, check_vma=False)
```

```python
import jax
import jax.numpy as jnp
from jax import lax
from jax.experimental import pallas as pl
from jax.experimental.pallas import tpu as pltpu
from jax.sharding import PartitionSpec as P

D = 1280
HEADS = 20
HEAD_DIM = 64
FF = 5120
CELLS_DEV = 2
EPS = 1e-05

TEAM = 8
CHIPS = 4
HEADS_CHIP = HEADS // CHIPS
D_CHIP = D // CHIPS
FF_CHIP = FF // CHIPS
SHARE = D // TEAM
FF_SHARE = FF // TEAM
SCALE = HEAD_DIM ** (-0.5)

GAIN1, BIAS1, BIAS_OUT, GAIN2, BIAS2, BIAS_DOWN, BIAS_UP, BIAS_QKV = range(8)
TABLE_ROWS = 8
SUM_ROWS = 16

COST = pl.CostEstimate(flops=1, bytes_accessed=1, transcendentals=0)
SMEM = pl.BlockSpec(memory_space=pltpu.SMEM)
HBM = pl.BlockSpec(memory_space=pltpu.HBM)
VMEM = pl.BlockSpec(memory_space=pltpu.VMEM)

f32 = jnp.float32
bf16 = jnp.bfloat16


def dot(a, b, dims):
    return lax.dot_general(a, b, (dims, ((), ())), preferred_element_type=f32)


def mm(a, b):
    return dot(a, b, ((1,), (0,)))


def mm_t(a, b):
    return dot(a, b, ((1,), (1,)))


def t_mm(a, b):
    return dot(a, b, ((0,), (0,)))


def normalize(values):
    center = jnp.mean(values, axis=-1, keepdims=True)
    centred = values - center
    spread = jnp.mean(centred * centred, axis=-1, keepdims=True)
    inverse = lax.rsqrt(spread + EPS)
    return centred * inverse, inverse


def norm_backward(grad_out, normed, inverse, norm_gain):
    grad_normed = grad_out * norm_gain
    first_mean = jnp.mean(grad_normed, axis=-1, keepdims=True)
    second_mean = jnp.mean(grad_normed * normed, axis=-1, keepdims=True)
    grad_in = inverse * (grad_normed - first_mean - normed * second_mean)
    gain_sum = jnp.sum(grad_out * normed, axis=0, keepdims=True)
    return grad_in, gain_sum, jnp.sum(grad_out, axis=0, keepdims=True)


def heads_of(projected, offset):
    return [
        projected[:, offset + i * HEAD_DIM : offset + (i + 1) * HEAD_DIM] for i in range(HEADS_CHIP)
    ]


def softmax_rows(queries, keys, keep):
    raw = jnp.concatenate([mm_t(q, k) for q, k in zip(queries, keys)], axis=0)
    masked = jnp.where(keep, raw * SCALE, -1e30)
    grown = jnp.exp(masked - jnp.max(masked, axis=-1, keepdims=True))
    return grown * (1.0 / jnp.sum(grown, axis=-1, keepdims=True))


def keep_of(mask):
    return jnp.concatenate([mask.astype(f32)] * HEADS_CHIP, axis=0) > 0.5


def attend(projected, mask):
    rows = mask.shape[0]
    probs = softmax_rows(heads_of(projected, 0), heads_of(projected, D_CHIP), keep_of(mask))
    probs = probs.astype(bf16)
    out = [
        mm(probs[i * rows : (i + 1) * rows], value)
        for i, value in enumerate(heads_of(projected, 2 * D_CHIP))
    ]
    return jnp.concatenate(out, axis=1).astype(bf16)


def attend_back(projected, mask, grad_context):
    rows = mask.shape[0]
    queries, keys, values = (heads_of(projected, i * D_CHIP) for i in range(3))
    grads = heads_of(grad_context, 0)
    probs = softmax_rows(queries, keys, keep_of(mask))
    grad_probs = jnp.concatenate([mm_t(g, v) for g, v in zip(grads, values)], axis=0)
    along = jnp.sum(grad_probs * probs, axis=-1, keepdims=True)
    grad_scores = (probs * (grad_probs - along) * SCALE).astype(bf16)
    probs = probs.astype(bf16)

    def cut(stack, i):
        return stack[i * rows : (i + 1) * rows]

    out = (
        [mm(cut(grad_scores, i), keys[i]) for i in range(HEADS_CHIP)]
        + [t_mm(cut(grad_scores, i), queries[i]) for i in range(HEADS_CHIP)]
        + [t_mm(cut(probs, i), grads[i]) for i in range(HEADS_CHIP)]
    )
    return jnp.concatenate(out, axis=1).astype(bf16)


HALF = SHARE // 2
EXTRA = 16
ROWS_Z = 2 * SHARE


def call(kernel, name, kinds, out_shapes, scratch=(), vmem=16):
    specs = {"s": SMEM, "h": HBM, "v": VMEM}
    made = pl.pallas_call(
        kernel,
        in_specs=[specs[kind] for kind in kinds],
        out_specs=[VMEM] * len(out_shapes),
        out_shape=[jax.ShapeDtypeStruct(shape, kind) for shape, kind in out_shapes],
        scratch_shapes=list(scratch),
        compiler_params=pltpu.CompilerParams(vmem_limit_bytes=vmem * 2**20),
        cost_estimate=COST,
        name=name,
    )

    def run(*args):
        placed = [
            pltpu.with_memory_space_constraint(arg, pltpu.HBM) if kind == "h" else arg
            for kind, arg in zip(kinds, args, strict=True)
        ]
        return made(*placed)

    return run


def sems(count):
    return pltpu.SemaphoreType.DMA((count,))


def row_at(i, size):
    return pl.ds(pl.multiple_of(i * size, size), size)


def tiled(width, tile, body):
    @pl.loop(0, width // tile)
    def _(i):
        body(row_at(i, tile))


def stack_blocks(blocks, whole):
    rows = blocks[0].shape[0]
    for i, block in enumerate(blocks):
        whole[i * rows : (i + 1) * rows, :] = block[...]


def row_of(spot, i, of_core, half=None):
    row = (2 * (spot[0] ^ i) + of_core) * SHARE
    if half is None:
        return pl.ds(pl.multiple_of(row, SHARE), SHARE)
    return pl.ds(pl.multiple_of(row + half * HALF, HALF), HALF)


def stack_columns(spot, mine, other, whole):
    core, side = spot[1], spot[2]
    for of_core, (own, near, far) in ((core, mine), (1 - core, other)):
        whole[row_of(spot, 0, of_core), :] = own[:SHARE, :]
        for i in range(1, CHIPS):
            rows = slice((i - 1) * HALF, i * HALF)
            whole[row_of(spot, i, of_core, side), :] = near[rows, :]
            whole[row_of(spot, i, of_core, 1 - side), :] = far[rows, :]


def by_core_copies(core, mine, other, whole, sem):
    size = mine.shape[0]
    return [
        pltpu.make_async_copy(mine, whole.at[row_at(core, size)], sem.at[0]),
        pltpu.make_async_copy(other, whole.at[row_at(1 - core, size)], sem.at[1]),
    ]


def start_all(copies):
    for copy in copies:
        copy.start()


def wait_all(copies):
    for copy in copies:
        copy.wait()


def chip_columns(weights, rows, chip):
    start = pl.multiple_of((chip * 5 // 2) * 128, 128)
    odd = lax.rem(chip, 2) == 1
    out = []
    for kind in range(3):
        window = weights[rows, pl.ds(kind * D + start, 384)]
        out.append(jnp.where(odd, window[:, 64 : 64 + D_CHIP], window[:, :D_CHIP]))
    return jnp.concatenate(out, axis=1)


def qkv_blocks_kernel(spot, lengths, padding, weights, *refs):
    vectors, own, sent = refs[:9], refs[9], refs[10 : 9 + CHIPS]
    held, marks, whole, vector_sems, sem = refs[9 + CHIPS : 18 + CHIPS], *refs[18 + CHIPS :]
    copies = [
        pltpu.make_async_copy(vector, here, vector_sems.at[i])
        for i, (vector, here) in enumerate(zip(vectors, held))
    ]
    copies.append(pltpu.make_async_copy(padding, marks, sem.at[0]))
    copies.append(pltpu.make_async_copy(weights, whole, sem.at[1]))
    start_all(copies)
    wait_all(copies)
    rows = padding.shape[-1]
    place = lax.broadcasted_iota(jnp.int32, (1, rows), 1)
    first = lengths[0, 0]
    member = (place >= first).astype(f32)
    leading = (place == 0) | (place == first)
    usable = jnp.where(leading | (marks[...].reshape(1, rows) > 0), 1.0, 0.0)
    code = 2.0 * member + usable
    width = 3 * D_CHIP
    lines = [v[...].astype(f32).reshape(1, -1) for v in held]
    extra = jnp.concatenate(
        [
            jnp.concatenate(lines[:6], axis=1),
            jnp.concatenate(lines[6:], axis=1),
            jnp.concatenate([code, jnp.zeros((1, width - rows), f32)], axis=1),
            jnp.zeros((EXTRA - 3, width), f32),
        ],
        axis=0,
    ).astype(bf16)
    own[:SHARE, :] = chip_columns(whole, slice(None), spot[0])
    own[SHARE:, :] = extra
    for i, block in enumerate(sent):
        block[:HALF, :] = chip_columns(whole, row_at(spot[2], HALF), spot[0] ^ (i + 1))
        block[HALF:, :] = extra


def qkv_blocks(spot, lengths, padding, weights, vectors):
    half = ((HALF + EXTRA, 3 * D_CHIP), bf16)
    return call(
        qkv_blocks_kernel,
        "qkv_blocks",
        "ss" + "h" * 11,
        [((SHARE + EXTRA, 3 * D_CHIP), bf16)] + [half] * (CHIPS - 1),
        [pltpu.VMEM(v.shape, v.dtype) for v in vectors]
        + [
            pltpu.VMEM(padding.shape, padding.dtype),
            pltpu.VMEM(weights.shape, weights.dtype),
            sems(9),
            sems(2),
        ],
    )(spot, lengths, padding, weights, *vectors)


def qkv_join_kernel(own, q1, q2, q3, near, near_half, extras):
    near[:SHARE, :] = own[:SHARE, :]
    extras[:EXTRA, :] = own[SHARE:, :]
    for i, block in enumerate((q1, q2, q3)):
        near[SHARE + i * HALF : SHARE + (i + 1) * HALF, :] = block[:HALF, :]
        near_half[i * HALF : (i + 1) * HALF, :] = block[:HALF, :]
        extras[(i + 1) * EXTRA : (i + 2) * EXTRA, :] = block[HALF:, :]


def qkv_join(blocks):
    width = blocks[0].shape[-1]
    return call(
        qkv_join_kernel,
        "qkv_join",
        "vvvv",
        [
            ((SHARE + 3 * HALF, width), bf16),
            ((3 * HALF, width), bf16),
            ((CHIPS * EXTRA, width), bf16),
        ],
    )(*blocks)


def up_blocks_kernel(spot, weights, cotangent, own, *sent):
    def columns(chip):
        return pl.ds(pl.multiple_of(chip * FF_CHIP, FF_CHIP), FF_CHIP)

    rows = cotangent.shape[0]
    own[...] = weights[:, columns(spot[0])]
    for i, block in enumerate(sent):
        block[:rows, :] = cotangent[...]
        block[rows:, :] = weights[row_at(spot[2], HALF), columns(spot[0] ^ (i + 1))]


def up_blocks(spot, weights, cotangent):
    half = ((cotangent.shape[0] + HALF, FF_CHIP), bf16)
    return call(
        up_blocks_kernel, "up_blocks", "svv", [((SHARE, FF_CHIP), bf16)] + [half] * (CHIPS - 1)
    )(spot, weights, cotangent)


def up_join_kernel(cotangent, u1, u2, u3, half_a, half_b, whole):
    rows = cotangent.shape[0]
    whole[:rows, :] = cotangent[...]
    size = half_a.shape[0]
    near = []
    for i, block in enumerate((u1, u2, u3)):
        near.append(block[rows:, :])
        whole[(i + 1) * rows : (i + 2) * rows, :] = block[:rows, :]
    near = jnp.concatenate(near, axis=0)
    half_a[...] = near[:size]
    half_b[...] = near[size:]


def up_join(cotangent, blocks):
    half = ((3 * HALF // 2, FF_CHIP), bf16)
    return call(
        up_join_kernel,
        "up_join",
        "vvvv",
        [half, half, ((CHIPS * cotangent.shape[0], D), bf16)],
    )(cotangent, *blocks)


def halves_kernel(whole, first, second):
    size = first.shape[0]
    first[...] = whole[:size, :]
    second[...] = whole[size:, :]


def halves(whole):
    shape = (whole.shape[0] // 2, whole.shape[1])
    return call(halves_kernel, "halves", "v", [(shape, whole.dtype)] * 2)(whole)


def join_kernel(*refs):
    stack_blocks(refs[:-1], refs[-1])


def join(blocks):
    rows, width = blocks[0].shape
    count = len(blocks)
    return call(join_kernel, "join", "v" * count, [((count * rows, width), blocks[0].dtype)])(
        *blocks
    )[0]


def fill_table(spot, extras, table, mask):
    chip, core = spot[0], spot[1]
    rows = mask.shape[1]
    table[...] = jnp.zeros_like(table)
    for team in range(TEAM):
        for i in range(6):
            table[i : i + 1, team * SHARE : (team + 1) * SHARE] = extras[
                team, 0:1, i * SHARE : (i + 1) * SHARE
            ]
    for half in range(2):
        line = extras[2 * chip + half, 1:2, :]
        lo = half * SHARE
        table[BIAS_QKV : BIAS_QKV + 1, lo : lo + SHARE] = line[:, :SHARE]
        table[BIAS_QKV : BIAS_QKV + 1, 2 * D_CHIP + lo : 2 * D_CHIP + lo + SHARE] = line[
            :, SHARE : 2 * SHARE
        ]
        table[BIAS_UP : BIAS_UP + 1, half * FF_SHARE : (half + 1) * FF_SHARE] = line[:, 2 * SHARE :]
    for i in range(CHIPS):
        code = extras[2 * (chip ^ i) + core, 2:3, :rows]
        of_key = jnp.broadcast_to(code, (rows, rows))
        cell_of_key = jnp.floor(of_key * 0.5)
        open_key = of_key - 2.0 * cell_of_key
        keep = jnp.where(cell_of_key == cell_of_key.T, open_key, 0.0)
        mask[i * rows : (i + 1) * rows, :] = keep.astype(bf16)


def token_norm_kernel(x0, x1, x2, x3, normed):
    rows = x0.shape[0]
    for i, x in enumerate((x0, x1, x2, x3)):
        normed[i * rows : (i + 1) * rows, :] = normalize(x[...].astype(f32))[0]


def token_norm(blocks):
    rows, width = blocks[0].shape
    return call(token_norm_kernel, "token_norm", "vvvv", [((CHIPS * rows, width), f32)])(*blocks)[0]


def enter_kernel(spot, normed, *refs):
    mine, other, refs = refs[:3], refs[3:6], refs[6:]
    out_mine, out_other, refs = *refs[:2], refs[2:]
    table, mask, qkv, out, first_low, projected, context = refs[:7]
    partials = refs[7 : 7 + CHIPS]
    extras, out_sems = refs[7 + CHIPS :]
    rows = mask.shape[1]
    out_copies = by_core_copies(spot[1], out_mine, out_other, out, out_sems)
    start_all(out_copies)
    for of_core, lines in ((spot[1], mine[2]), (1 - spot[1], other[2])):
        for i in range(CHIPS):
            extras[2 * (spot[0] ^ i) + of_core] = lines[i * EXTRA : (i + 1) * EXTRA, :].astype(f32)
    fill_table(spot, extras, table, mask)
    columns = [(near, near.at[SHARE:], far) for near, far, _ in (mine, other)]
    stack_columns(spot, *columns, qkv)
    gain = table[GAIN1 : GAIN1 + 1, :]
    bias = table[BIAS1 : BIAS1 + 1, :]
    first_low[...] = (normed[...] * gain + bias).astype(bf16)
    for lo, hi in ((0, 384), (384, 768), (768, 960)):
        shift = table[BIAS_QKV : BIAS_QKV + 1, lo:hi]
        projected[:, lo:hi] = (mm(first_low[...], qkv[:, lo:hi]) + shift).astype(bf16)

    @pl.loop(0, CHIPS)
    def _(i):
        at = row_at(i, rows)
        context[at, :] = attend(projected[at, :], mask[at, :])

    wait_all(out_copies)

    def partial(at):
        whole = mm(context[...], out[:, at]).astype(bf16)
        for i, part in enumerate(partials):
            part[:, at] = whole[i * rows : (i + 1) * rows]

    tiled(D, 256, partial)


def enter(spot, normed, mine, other, out_mine, out_other):
    total = normed.shape[0]
    rows = total // CHIPS
    outs = call(
        enter_kernel,
        "enter",
        "sv" + "v" * 6 + "hv",
        [
            ((TABLE_ROWS, D), f32),
            ((total, rows), bf16),
            ((D, 3 * D_CHIP), bf16),
            ((D_CHIP, D), bf16),
            ((total, D), bf16),
            ((total, 3 * D_CHIP), bf16),
            ((total, D_CHIP), bf16),
        ]
        + [((rows, D), bf16)] * CHIPS,
        [pltpu.VMEM((TEAM, EXTRA, 3 * D_CHIP), f32), sems(2)],
    )(spot, normed, *mine, *other, out_mine, out_other)
    return outs[:7], outs[7:]


def leave_kernel(
    b0, b1, b2, b3, qkv, out, projected, mask, branch, grad_projected, bias_sum, *refs
):
    partials, grad_context = refs[:CHIPS], refs[CHIPS]
    rows = b0.shape[0]
    stack_blocks((b0, b1, b2, b3), branch)
    grad_context[...] = mm_t(branch[...], out[...]).astype(bf16)
    bias_sum[...] = jnp.zeros_like(bias_sum)

    @pl.loop(0, CHIPS)
    def _(i):
        at = row_at(i, rows)
        grad = attend_back(projected[at, :], mask[at, :], grad_context[at, :])
        grad_projected[at, :] = grad
        bias_sum[...] += jnp.sum(grad.astype(f32), axis=0, keepdims=True)

    def partial(at):
        whole = mm_t(grad_projected[...], qkv[at, :]).astype(bf16)
        for i, part in enumerate(partials):
            part[:, at] = whole[i * rows : (i + 1) * rows]

    tiled(D, 256, partial)


def leave(blocks, qkv, out, projected, mask):
    rows = blocks[0].shape[0]
    total = CHIPS * rows
    outs = call(
        leave_kernel,
        "leave",
        "v" * 8,
        [((total, D), bf16), ((total, 3 * D_CHIP), bf16), ((1, 3 * D_CHIP), f32)]
        + [((rows, D), bf16)] * CHIPS,
        [pltpu.VMEM((total, D_CHIP), bf16)],
    )(*blocks, qkv, out, projected, mask)
    return outs[:3], outs[3:]


def total_of(parts):
    total = parts[0][...].astype(f32)
    for part in parts[1:]:
        total = total + part[...].astype(f32)
    return total


def mix_kernel(p0, p1, p2, p3, tokens, table, mixed, second):
    total = total_of((p0, p1, p2, p3)) + tokens[...].astype(f32)
    total = total + table[BIAS_OUT : BIAS_OUT + 1, :]
    mixed[...] = total
    normed, _ = normalize(total)
    second[...] = (normed * table[GAIN2 : GAIN2 + 1, :] + table[BIAS2 : BIAS2 + 1, :]).astype(bf16)


def mix(parts, tokens, table):
    shape = tokens.shape
    return call(mix_kernel, "mix", "v" * 6, [(shape, f32), (shape, bf16)])(*parts, tokens, table)


def unmix_kernel(p0, p1, p2, p3, mixed, table, cotangent, grad_mixed, branch, sums):
    grad = total_of((p0, p1, p2, p3))
    normed, inverse = normalize(mixed[...])
    grad_in, gain_sum, bias_sum = norm_backward(grad, normed, inverse, table[GAIN2 : GAIN2 + 1, :])
    grad_out = cotangent[...].astype(f32)
    grad_in = grad_in + grad_out
    grad_mixed[...] = grad_in
    low = grad_in.astype(bf16)
    branch[...] = low
    sums[...] = jnp.zeros_like(sums)
    sums[0:1, :] = jnp.sum(low.astype(f32), axis=0, keepdims=True)
    sums[1:2, :] = gain_sum
    sums[2:3, :] = bias_sum
    sums[3:4, :] = jnp.sum(grad_out, axis=0, keepdims=True)


def unmix(parts, mixed, table, cotangent):
    shape = cotangent.shape
    return call(
        unmix_kernel, "unmix", "v" * 7, [(shape, f32), (shape, bf16), ((8, D), f32)]
    )(*parts, mixed, table, cotangent)


def act_grad_kernel(spot, whole, mine, other, grad_act, down, down_sems):
    copies = by_core_copies(spot[1], mine, other, down, down_sems)
    start_all(copies)
    wait_all(copies)

    def columns(at):
        grad_act[:, at] = mm_t(whole[...], down[at, :])

    tiled(FF_CHIP, 256, columns)


def act_grad(spot, cotangent, down_mine, down_other):
    return call(
        act_grad_kernel,
        "act_grad",
        "svhv",
        [((cotangent.shape[0], FF_CHIP), f32), ((FF_CHIP, D), bf16)],
        [sems(2)],
    )(spot, cotangent, down_mine, down_other)


def hidden_rows(at, second, up, table, grad_act, pre_act, act, grad_pre, bias_sum):
    size = at.stop - at.start

    def columns(tile):
        pre_act[at, tile] = mm(second[at, :], up[:, tile]) + table[BIAS_UP : BIAS_UP + 1, tile]

    tiled(FF_CHIP, 256, columns)

    @pl.loop(0, size // 64)
    def _(i):
        rows = pl.ds(pl.multiple_of(at.start + i * 64, 64), 64)
        pre = pre_act[rows, :]
        below = 0.5 * (1.0 + lax.erf(pre * (0.5**0.5)))
        bell = jnp.exp(-0.5 * pre * pre) * 0.3989422804014327
        act[rows, :] = (pre * below).astype(bf16)
        grad = (grad_act[rows, :] * (below + pre * bell)).astype(bf16)
        grad_pre[rows, :] = grad
        bias_sum[...] += jnp.sum(grad.astype(f32), axis=0, keepdims=True)


def hidden_first_kernel(spot, s0, s1, s2, grad_act, table, *refs):
    columns = [(own, rest, rest.at[3 * HALF :]) for own, rest in (refs[:2], refs[2:4])]
    second, act, grad_pre, bias_sum, up, pre_act = refs[4:]
    rows = s0.shape[0]
    stack_columns(spot, *columns, up)
    stack_blocks((s0, s1, s2), second)
    bias_sum[...] = jnp.zeros_like(bias_sum)
    hidden_rows(
        slice(0, 3 * rows), second, up, table, grad_act, pre_act, act, grad_pre, bias_sum
    )


def hidden_first(spot, blocks, grad_act, table, mine, other):
    total = grad_act.shape[0]
    return call(
        hidden_first_kernel,
        "hidden_first",
        "svvvvv" + "v" * 4,
        [
            ((total, D), bf16),
            ((total, FF_CHIP), bf16),
            ((total, FF_CHIP), bf16),
            ((1, FF_CHIP), f32),
            ((D, FF_CHIP), bf16),
        ],
        [pltpu.VMEM((total, FF_CHIP), f32)],
    )(spot, *blocks, grad_act, table, *mine, *other)


def hidden_last_kernel(
    spot,
    s3,
    grad_act,
    table,
    cotangent,
    up,
    second_in,
    act_in,
    grad_pre_in,
    bias_in,
    second,
    act,
    grad_pre,
    bias_sum,
    down_sent,
    pre_act,
):
    del second_in, act_in, grad_pre_in
    rows = s3.shape[0]
    at = slice(3 * rows, 4 * rows)
    second[at, :] = s3[...]
    bias_sum[...] = bias_in[...]
    hidden_rows(at, second, up, table, grad_act, pre_act, act, grad_pre, bias_sum)
    down_product(act, cotangent, 1 - spot[1], 0, down_sent)


def down_product(act, cotangent, of_core, half, target):
    low = half * ROWS_Z
    aligned = low // 128 * 128
    if half == 0:
        units = pl.ds(pl.multiple_of(of_core * FF_SHARE, 128), ROWS_Z)
        target[...] = t_mm(act[:, units], cotangent[...]).astype(target.dtype)
    else:
        units = pl.ds(pl.multiple_of(of_core * FF_SHARE + aligned, 128), FF_SHARE - aligned)
        window = act[:, units][:, low - aligned :]
        target[...] = t_mm(window, cotangent[...]).astype(target.dtype)


def up_product(second, grad_pre, pair, of_core, target, work):
    for i in range(2):
        first = (2 * (2 * pair + i) + of_core) * SHARE
        aligned = pl.multiple_of(first // 128 * 128, 128)
        work[...] = t_mm(second[:, pl.ds(aligned, 256)], grad_pre[...])
        start = pl.multiple_of(lax.rem(first, 128), 32)
        target[i * SHARE : (i + 1) * SHARE, :] = work[pl.ds(start, SHARE), :].astype(target.dtype)


def hidden_last(spot, block, grad_act, table, cotangent, up, second, act, grad_pre, bias_sum):
    total = second.shape[0]
    return pl.pallas_call(
        hidden_last_kernel,
        in_specs=[SMEM] + [VMEM] * 9,
        out_specs=[VMEM] * 5,
        out_shape=[
            jax.ShapeDtypeStruct(second.shape, bf16),
            jax.ShapeDtypeStruct(act.shape, bf16),
            jax.ShapeDtypeStruct(grad_pre.shape, bf16),
            jax.ShapeDtypeStruct(bias_sum.shape, f32),
            jax.ShapeDtypeStruct((ROWS_Z, D), bf16),
        ],
        scratch_shapes=[pltpu.VMEM((total, FF_CHIP), f32)],
        input_output_aliases={6: 0, 7: 1, 8: 2},
        compiler_params=pltpu.CompilerParams(vmem_limit_bytes=16 * 2**20),
        cost_estimate=COST,
        name="hidden_last",
    )(spot, block, grad_act, table, cotangent, up, second, act, grad_pre, bias_sum)


def second_grad_kernel(spot, grad_pre, up, second, *refs):
    partials, up_sent, work = refs[:CHIPS], refs[CHIPS], refs[CHIPS + 1]
    rows = partials[0].shape[0]

    def partial(at):
        whole = mm_t(grad_pre[...], up[at, :]).astype(bf16)
        for i, part in enumerate(partials):
            part[:, at] = whole[i * rows : (i + 1) * rows]

    tiled(D, 256, partial)
    up_product(second, grad_pre, 0, 1 - spot[1], up_sent, work)


def second_grad(spot, grad_pre, up, second):
    rows = grad_pre.shape[0] // CHIPS
    outs = call(
        second_grad_kernel,
        "second_grad",
        "svvv",
        [((rows, D), bf16)] * CHIPS + [((ROWS_Z, FF_CHIP), bf16)],
        [pltpu.VMEM((256, FF_CHIP), f32)],
    )(spot, grad_pre, up, second)
    return outs[:CHIPS], outs[CHIPS]


def split_rows(core, whole, sent, kept):
    for k in range(CHIPS):
        targets = ((sent[k // 2], k % 2, 1 - core), (kept, k, core))
        for target, at, of_core in targets:
            start = pl.multiple_of((2 * k + of_core) * SHARE, SHARE)
            target[at] = whole[pl.ds(start, SHARE), :].astype(bf16)


def down_grad_kernel(spot, act, cotangent, got, total):
    down_product(act, cotangent, spot[1], 0, total)
    total[...] = (total[...].astype(f32) + got[...].astype(f32)).astype(bf16)


def down_grad_of(spot, act, cotangent, got):
    return call(down_grad_kernel, "down_grad", "svvv", [((ROWS_Z, D), bf16)])(
        spot, act, cotangent, got
    )[0]


def rest_kernel(
    spot, second, grad_pre, act, cotangent, up_a, up_b, up_sent, down_b, down_sent, work
):
    core = spot[1]
    up_product(second, grad_pre, 0, core, up_a, work)
    up_product(second, grad_pre, 1, 1 - core, up_sent, work)
    up_product(second, grad_pre, 1, core, up_b, work)
    down_product(act, cotangent, 1 - core, 1, down_sent)
    down_product(act, cotangent, core, 1, down_b)


def rest_of_grads(spot, second, grad_pre, act, cotangent):
    return call(
        rest_kernel,
        "rest",
        "svvvv",
        [((ROWS_Z, D), bf16)] * 5,
        [pltpu.VMEM((256, FF_CHIP), f32)],
    )(spot, second, grad_pre, act, cotangent)


def result_kernel(act, down, *partials):
    rows = partials[0].shape[0]

    def columns(at):
        whole = mm(act[...], down[:, at]).astype(bf16)
        for i, part in enumerate(partials):
            part[:, at] = whole[i * rows : (i + 1) * rows]

    tiled(D, 256, columns)


def result_of(act, down):
    rows = act.shape[0] // CHIPS
    return call(result_kernel, "result", "vv", [((rows, D), bf16)] * CHIPS)(act, down)


def qkv_grad_kernel(
    spot,
    first_low,
    grad_projected,
    context,
    branch,
    sent_a,
    sent_b,
    kept,
    out_sent,
    out_kept,
    whole,
    out,
):
    core = spot[1]

    def columns(at):
        whole[at, :] = t_mm(first_low[:, at], grad_projected[...])

    tiled(D, 256, columns)
    split_rows(core, whole, (sent_a, sent_b), kept)
    out[...] = t_mm(context[...], branch[...])
    for target, of_core in ((out_sent, 1 - core), (out_kept, core)):
        target[...] = out[row_at(of_core, SHARE), :].astype(bf16)


def qkv_grad_of(spot, first_low, grad_projected, context, branch):
    half = ((CHIPS // 2, SHARE, 3 * D_CHIP), bf16)
    rows = ((SHARE, D), bf16)
    return call(
        qkv_grad_kernel,
        "qkv_grad",
        "svvvv",
        [half, half, ((CHIPS, SHARE, 3 * D_CHIP), bf16), rows, rows],
        [pltpu.VMEM((D, 3 * D_CHIP), f32), pltpu.VMEM((D_CHIP, D), f32)],
    )(spot, first_low, grad_projected, context, branch)


def add_kernel(*refs):
    count = len(refs) // 3
    for a, b, c in zip(refs[:count], refs[count : 2 * count], refs[2 * count :]):
        c[...] = (a[...].astype(f32) + b[...].astype(f32)).astype(c.dtype)


def add_all(left, right):
    shapes = [(a.shape, a.dtype) for a in left]
    return call(add_kernel, "add", "v" * (2 * len(left)), shapes)(*left, *right)


PACKED = SHARE * 3 // 4
STEP = SHARE // 4


def sum_all_kernel(a, b, c, d, total):
    total[...] = (a[...] + b[...]) + (c[...] + d[...])


def sum_all(parts):
    shape = (parts[0].shape, parts[0].dtype)
    return call(sum_all_kernel, "sum_all", "vvvv", [shape])(*parts)[0]


def pack_kernel(kept, got_a, got_b, out_kept, out_got, *chunks):
    for i, chunk in enumerate(chunks):
        for j in range(2):
            got = got_b if i else got_a
            total = (kept[2 * i + j].astype(f32) + got[j].astype(f32)).astype(bf16)
            lo = j * PACKED
            chunk[lo : lo + PACKED, : 3 * D_CHIP] = total[:PACKED]
            for part in range(3):
                at = lo + part * STEP
                chunk[at : at + STEP, 3 * D_CHIP :] = total[
                    PACKED:, part * D_CHIP : (part + 1) * D_CHIP
                ]
        rows = slice(i * HALF, (i + 1) * HALF)
        total = out_kept[rows, :].astype(f32) + out_got[rows, :].astype(f32)
        chunk[2 * PACKED :, :] = total.astype(bf16)


def pack(kept, got_a, got_b, out_kept, out_got):
    return call(pack_kernel, "pack", "vvvvv", [((ROWS_Z, D), bf16)] * 2)(
        kept, got_a, got_b, out_kept, out_got
    )


def unpacked(chunk, j):
    lo = j * PACKED
    tail = [
        chunk[lo + part * STEP : lo + (part + 1) * STEP, 3 * D_CHIP :] for part in range(3)
    ]
    return jnp.concatenate(
        [chunk[lo : lo + PACKED, : 3 * D_CHIP], jnp.concatenate(tail, axis=1)], axis=0
    )


def z_half(low, got_side):
    return add_all([low], [got_side])[0]


def z_send_kernel(spot, half, got_middle, low, sent):
    whole = (half[...].astype(f32) + got_middle[...].astype(f32)).astype(bf16)
    sent[...] = jnp.where(spot[3] > 0, whole, low[...])


def z_send(spot, half, got_middle, low):
    return call(z_send_kernel, "z_send", "svvv", [(low.shape, bf16)])(spot, half, got_middle, low)[0]


def z_final_kernel(spot, sent, got_side, final):
    final[...] = jnp.where(spot[3] > 0, sent[...], got_side[...])


def z_final(spot, sent, got_side):
    return call(z_final_kernel, "z_final", "svv", [(sent.shape, bf16)])(spot, sent, got_side)[0]


def first_down_kernel(spot, sent, got, down, here, sem):
    here[...] = jnp.where(spot[3] > 0, sent[...], got[...]).astype(f32)
    copy = pltpu.make_async_copy(here, down.at[:ROWS_Z], sem.at[0])
    copy.start()
    copy.wait()


def first_down(spot, sent, got):
    return pl.pallas_call(
        first_down_kernel,
        in_specs=[SMEM, VMEM, VMEM],
        out_specs=HBM,
        out_shape=pltpu.HBM((2 * ROWS_Z, D), f32),
        scratch_shapes=[pltpu.VMEM((ROWS_Z, D), f32), sems(1)],
        compiler_params=pltpu.CompilerParams(vmem_limit_bytes=16 * 2**20),
        cost_estimate=COST,
        name="first_down",
    )(spot, sent, got)


def second_down_kernel(spot, sent, got, before, down, here, sem):
    del before
    here[...] = jnp.where(spot[3] > 0, sent[...], got[...]).astype(f32)
    copy = pltpu.make_async_copy(here, down.at[ROWS_Z:], sem.at[0])
    copy.start()
    copy.wait()


def second_down(spot, sent, got, down):
    return pl.pallas_call(
        second_down_kernel,
        in_specs=[SMEM, VMEM, VMEM, HBM],
        out_specs=HBM,
        out_shape=pltpu.HBM((2 * ROWS_Z, D), f32),
        scratch_shapes=[pltpu.VMEM((ROWS_Z, D), f32), sems(1)],
        input_output_aliases={3: 0},
        compiler_params=pltpu.CompilerParams(vmem_limit_bytes=16 * 2**20),
        cost_estimate=COST,
        name="second_down",
    )(spot, sent, got, pltpu.with_memory_space_constraint(down, pltpu.HBM))


def qkv_rows_kernel(spot, b0, b1, b2, b3, qkv, rows, stack, sem):
    for i, block in enumerate((b0, b1, b2, b3)):
        stack[spot[0] ^ i] = block[...]
    copies = []
    for kind in range(3):
        for chip in range(CHIPS):
            lo = kind * D + chip * D_CHIP
            rows[:, lo : lo + D_CHIP] = stack[
                chip, :, kind * D_CHIP : (kind + 1) * D_CHIP
            ].astype(f32)
        at = slice(kind * D, (kind + 1) * D)
        copies.append(pltpu.make_async_copy(rows.at[:, at], qkv.at[:, at], sem.at[kind]))
        copies[-1].start()
    wait_all(copies)


def qkv_rows(spot, blocks):
    shape = blocks[0].shape
    return pl.pallas_call(
        qkv_rows_kernel,
        in_specs=[SMEM] + [VMEM] * 4,
        out_specs=HBM,
        out_shape=pltpu.HBM((shape[0], 3 * D), f32),
        scratch_shapes=[
            pltpu.VMEM((shape[0], 3 * D), f32),
            pltpu.VMEM((CHIPS,) + shape, bf16),
            sems(3),
        ],
        compiler_params=pltpu.CompilerParams(vmem_limit_bytes=16 * 2**20),
        cost_estimate=COST,
        name="qkv_rows",
    )(spot, *blocks)


def owned_kernel(count, place, sums, got, *outs):
    total = sums[...] + got[...]
    index = place[0]
    size = outs[0].shape[0]
    mine = pltpu.roll(total, D - index * size, 1)
    for i, row in enumerate((0, 1, 2, 3, 4, 5, 8, 9)):
        outs[i][...] = mine[row : row + 1, :size].reshape(size)
    wide = outs[8].shape[0]
    first = index * wide
    row = first // D
    line = total[10:11, :]
    for k in range(1, CHIPS):
        line = jnp.where(row == k, total[10 + k : 11 + k, :], line)
    line = pltpu.roll(jnp.broadcast_to(line, (8, D)), D - lax.rem(first, D), 1)
    outs[8][...] = line[0:1, :wide].reshape(wide)
    mean = total[6:7, :] / count
    outs[9][...] = mean.reshape(D)
    outs[10][...] = (total[7:8, :] / count - mean * mean).reshape(D)


def owned(place, count, fsdp_count, sums, got):
    sizes = [D // fsdp_count] * 8 + [FF // fsdp_count, D, D]

    def kernel(*refs):
        owned_kernel(count, *refs)

    return call(kernel, "owned", "svv", [((size,), f32) for size in sizes])(place, sums, got)


def up_exchange_kernel(spot, a, b, *blocks):
    chunks = (a, b)
    for i, block in enumerate(blocks):
        chip = spot[0] ^ i
        at = row_at(lax.rem(chip, 2), SHARE)
        block[...] = jnp.where(chip >= 2, chunks[1][at, :], chunks[0][at, :])


def up_exchange(spot, a, b):
    return call(up_exchange_kernel, "up_exchange", "svv", [((SHARE, FF_CHIP), bf16)] * CHIPS)(
        spot, a, b
    )


def qkv_unpack_kernel(spot, sent, got_side, blocks, out_rows):
    chunk = jnp.where(spot[3] > 0, sent[...], got_side[...])
    for j in range(2):
        blocks[j] = unpacked(chunk, j)
    out_rows[...] = chunk[2 * PACKED :, :].astype(f32)


def qkv_unpack(spot, sent, got_side):
    return call(
        qkv_unpack_kernel,
        "qkv_unpack",
        "svv",
        [((2, SHARE, 3 * D_CHIP), bf16), ((HALF, D), f32)],
    )(spot, sent, got_side)


def qkv_exchange_kernel(spot, blocks_a, rows_a, sent, got_side, *refs):
    blocks, out_rows, stack = refs[:CHIPS], refs[CHIPS], refs[CHIPS + 1]
    chunk = jnp.where(spot[3] > 0, sent[...], got_side[...])
    stack[:2] = blocks_a[...]
    for j in range(2):
        stack[2 + j] = unpacked(chunk, j)
    out_rows[:HALF, :] = rows_a[...]
    out_rows[HALF:, :] = chunk[2 * PACKED :, :].astype(f32)
    for i, block in enumerate(blocks):
        block[...] = stack[spot[0] ^ i]


def qkv_exchange(spot, blocks_a, rows_a, sent, got_side):
    shape = (SHARE, 3 * D_CHIP)
    outs = call(
        qkv_exchange_kernel,
        "qkv_exchange",
        "svvvv",
        [(shape, bf16)] * CHIPS + [((SHARE, D), f32)],
        [pltpu.VMEM((CHIPS,) + shape, bf16)],
    )(spot, blocks_a, rows_a, sent, got_side)
    return outs[:CHIPS], outs[CHIPS]


def up_rows_kernel(spot, b0, b1, b2, b3, weights):
    for i, block in enumerate((b0, b1, b2, b3)):
        start = pl.multiple_of((spot[0] ^ i) * FF_CHIP, FF_CHIP)
        weights[:, pl.ds(start, FF_CHIP)] = block[...].astype(f32)


def up_rows(spot, blocks):
    return call(up_rows_kernel, "up_rows", "svvvv", [((SHARE, FF), f32)])(spot, *blocks)[0]


def end_kernel(
    spot,
    lengths,
    p0,
    p1,
    p2,
    p3,
    r0,
    r1,
    r2,
    r3,
    grad_mixed,
    tokens,
    table,
    mixed,
    mix_sums,
    qkv_sum,
    up_sum,
    layer_out,
    grad_tokens,
    sums,
):
    grad = total_of((p0, p1, p2, p3))
    normed, inverse = normalize(tokens[...].astype(f32))
    grad_in, gain_sum, bias_sum = norm_backward(grad, normed, inverse, table[GAIN1 : GAIN1 + 1, :])
    grad_tokens[...] = grad_mixed[...] + grad_in
    result = mixed[...] + total_of((r0, r1, r2, r3)) + table[BIAS_DOWN : BIAS_DOWN + 1, :]
    layer_out[...] = result.astype(bf16)
    place = lax.broadcasted_iota(jnp.int32, (result.shape[0], 1), 0)
    picked = jnp.where((place == 0) | (place == lengths[0, 0]), result, 0.0)
    sums[...] = jnp.zeros_like(sums)
    sums[0:1, :] = gain_sum
    sums[1:2, :] = bias_sum
    sums[2:6, :] = mix_sums[0:4, :]
    sums[6:7, :] = jnp.sum(picked, axis=0, keepdims=True)
    sums[7:8, :] = jnp.sum(picked * picked, axis=0, keepdims=True)
    for k in range(CHIPS):
        here = spot[0] == k
        lo = k * D_CHIP
        sums[8:9, lo : lo + D_CHIP] = jnp.where(here, qkv_sum[:, :D_CHIP], 0.0)
        sums[9:10, lo : lo + D_CHIP] = jnp.where(here, qkv_sum[:, 2 * D_CHIP :], 0.0)
        sums[10 + k : 11 + k, :] = jnp.where(here, up_sum[...], 0.0)


def end(spot, lengths, parts, results, *rest):
    shape = parts[0].shape
    return call(
        end_kernel,
        "end",
        "ss" + "v" * 15,
        [(shape, bf16), (shape, f32), ((SUM_ROWS, D), f32)],
    )(spot, lengths, *parts, *results, *rest)


def fence(*values):
    return lax.optimization_barrier(values)


def local(
    tokens,
    lengths,
    padding,
    ln1_gain,
    ln1_bias,
    w_qkv,
    b_query,
    b_value,
    w_out,
    b_out,
    ln2_gain,
    ln2_bias,
    w_up,
    b_up,
    w_down,
    b_down,
    cotangent,
):
    fsdp_count = lax.axis_size("fsdp")
    dp_count = lax.axis_size("dp")
    groups = fsdp_count // TEAM
    place = lax.axis_index("fsdp") // groups
    chip = place // 2
    core = place % 2
    depth = lax.axis_index("dp")
    middle = (depth == 1) | (depth == 2)
    spot = jnp.stack([chip, core, depth % 2, middle.astype(jnp.int32)]).astype(jnp.int32)

    def swap(value, mask):
        pairs = [
            (team * groups + group, (team ^ mask) * groups + group)
            for team in range(TEAM)
            for group in range(groups)
        ]
        return lax.ppermute(value, "fsdp", pairs)

    shard_groups = [[team * groups + group for group in range(groups)] for team in range(TEAM)]
    def gather_shards(value):
        if groups == 1:
            return value
        return lax.all_gather(value, "fsdp", axis=0, tiled=True, axis_index_groups=shard_groups)

    def scatter_shards(value):
        if groups == 1:
            return value
        return lax.psum_scatter(
            value, "fsdp", scatter_dimension=0, tiled=True, axis_index_groups=shard_groups
        )

    def along_z(pairs, value):
        return lax.ppermute(value, "dp", pairs)

    def z_swap(value):
        return along_z([(0, 1), (1, 0), (2, 3), (3, 2)], value)

    def z_middle(value):
        return along_z([(1, 2), (2, 1)], value)

    def from_chips(blocks):
        return [blocks[0]] + [swap(block, 2 * i) for i, block in enumerate(blocks) if i > 0]

    def fence_list(first, *others):
        done = fence(*first, *others)
        return list(done[: len(first)]), *done[len(first) :]

    w_qkv, w_out, w_up, w_down = (gather_shards(w) for w in (w_qkv, w_out, w_up, w_down))
    given = (ln1_gain, ln1_bias, b_out, ln2_gain, ln2_bias, b_down, b_query, b_value, b_up)
    qkv_sent = qkv_blocks(spot, lengths, padding, w_qkv, [gather_shards(v) for v in given])
    qkv_got = from_chips(qkv_sent)
    x1, x2, *qkv_got = fence(swap(tokens, 2), swap(tokens, 4), *qkv_got)
    qkv_near, qkv_half, extras = qkv_join(qkv_got)
    qkv_far = z_swap(qkv_half)
    qkv_near_other, extras_other = swap(qkv_near, 1), swap(extras, 1)
    tokens_sent, extras = fence(tokens, extras)
    blocks = [tokens, x1, x2, swap(tokens_sent, 6)]
    normed = token_norm(blocks)
    out_sent, _ = fence(w_out, extras)
    out_other = swap(out_sent, 1)
    up_own, *up_sent = up_blocks(spot, w_up, cotangent)
    up_own, *up_sent = fence(up_own, *up_sent, extras)[:-1]
    up_own_other = swap(up_own, 1)
    loads = [swap(block, 2 * i + 2) for i, block in enumerate(up_sent)]
    normed, qkv_far, extras_other, qkv_near_other, out_other, up_own_other = fence(
        normed, qkv_far, extras_other, qkv_near_other, out_other, up_own_other
    )
    qkv_far_other = join([swap(half, 1) for half in halves(qkv_far)])

    (table, mask, qkv, out, first_low, projected, context), partial_out = enter(
        spot,
        normed,
        [qkv_near, qkv_far, extras],
        [qkv_near_other, qkv_far_other, extras_other],
        w_out,
        out_other,
    )
    out_parts = from_chips(partial_out)
    cotangent_late, _ = fence(cotangent, partial_out[0])
    up_half_a, up_half_b, whole_cotangent = up_join(cotangent_late, loads)
    up_far = [z_swap(up_half_a), z_swap(up_half_b)]
    up_far, *out_parts = fence_list(up_far, *out_parts)
    mixed, second_own = mix(out_parts, tokens, table)
    second_blocks = from_chips([second_own] * CHIPS)
    up_far, _ = fence_list(up_far, second_own)
    up_rest = join([up_half_a, up_half_b] + up_far)
    up_other = [up_own_other, swap(up_rest, 1)]
    down_sent, _ = fence(w_down, second_own)
    down_other = swap(down_sent, 1)
    whole_cotangent, down_other = fence(whole_cotangent, down_other)
    grad_act, down = act_grad(spot, whole_cotangent, w_down, down_other)

    second_low, act_low, grad_pre, up_bias_sum, up = hidden_first(
        spot,
        second_blocks[:3],
        grad_act,
        table,
        [up_own, up_rest],
        up_other,
    )
    block, up_bias_sum = fence(second_blocks[3], up_bias_sum)
    second_low, act_low, grad_pre, up_bias_sum, down_sent = hidden_last(
        spot, block, grad_act, table, whole_cotangent, up, second_low, act_low, grad_pre, up_bias_sum
    )
    down_got = swap(down_sent, 1)
    partial_second, up_sent = second_grad(spot, grad_pre, up, second_low)
    up_got = swap(up_sent, 1)
    act_low, up_sent = fence(act_low, up_sent)
    down_a = down_grad_of(spot, act_low, whole_cotangent, down_got)
    side0 = z_swap(down_a)
    *partial_second, down_a = fence(*partial_second, down_a)
    second_parts = from_chips(partial_second)
    second_low, down_a = fence(second_low, down_a)
    up_a, up_b, up_sent, down_b, down_sent = rest_of_grads(
        spot, second_low, grad_pre, act_low, whole_cotangent
    )
    up_got, up_sent = fence(up_got, up_sent)
    (up_a,) = add_all([up_a], [up_got])
    up_got = swap(up_sent, 1)

    second_parts, side0, up_a = fence_list(second_parts, side0, up_a)
    half0, send1 = z_half(down_a, side0), up_a
    send1, _ = fence(send1, half0)
    side1, middle1 = z_swap(send1), z_middle(half0)
    second_parts, half0 = fence_list(second_parts, half0)
    grad_mixed, branch_own, mix_sums = unmix(second_parts, mixed, table, cotangent)
    branch_blocks = from_chips([branch_own] * CHIPS)
    act_low, branch_own = fence(act_low, branch_own)
    partial_result = list(result_of(act_low, down))

    up_got, partial_result[0] = fence(up_got, partial_result[0])
    (up_b,) = add_all([up_b], [up_got])
    branch_blocks, side1, middle1, *partial_result, up_b = fence_list(
        branch_blocks, side1, middle1, *partial_result, up_b
    )
    half1 = z_half(up_a, side1)
    middle1, _ = fence(middle1, half1)
    send2 = z_send(spot, half0, middle1, up_b)
    side2, middle2 = z_swap(send2), z_middle(half1)
    branch_blocks, half1 = fence_list(branch_blocks, half1)
    (whole_branch, grad_projected, qkv_bias_sum), partial_first = leave(
        branch_blocks, qkv, out, projected, mask
    )
    first_low, grad_projected = fence(first_low, grad_projected)
    qkv_sent_a, qkv_sent_b, qkv_kept, out_sent, out_kept = qkv_grad_of(
        spot, first_low, grad_projected, context, whole_branch
    )
    qkv_a, qkv_b = pack(
        qkv_kept, swap(qkv_sent_a, 1), swap(qkv_sent_b, 1), out_kept, swap(out_sent, 1)
    )

    side2, middle2, qkv_a = fence(side2, middle2, qkv_a)
    half2 = z_half(up_b, side2)
    middle2, _ = fence(middle2, half2)
    send3 = z_send(spot, half1, middle2, qkv_a)
    side3, middle3 = z_swap(send3), z_middle(half2)
    down_sent, _ = fence(down_sent, send3)
    (down_b,) = add_all([down_b], [swap(down_sent, 1)])
    *partial_first, down_b = fence(*partial_first, down_b)
    first_parts = from_chips(partial_first)
    down_grad = first_down(spot, send2, side2)

    first_parts, side3, middle3 = fence_list(first_parts, side3, middle3)
    half3 = z_half(qkv_a, side3)
    middle3, _ = fence(middle3, half3)
    send4 = z_send(spot, half2, middle3, qkv_b)
    sent, _ = fence(send3, send4)
    up_a_final = z_final(spot, sent, side3)
    side4, middle4 = z_swap(send4), z_middle(half3)
    *partial_result, half3 = fence(*partial_result, half3)
    result_parts = from_chips(partial_result)

    result_parts, side4, middle4 = fence_list(result_parts, side4, middle4)
    half4 = z_half(qkv_b, side4)
    middle4, _ = fence(middle4, half4)
    send5 = z_send(spot, half3, middle4, down_b)
    sent, _ = fence(send4, send5)
    up_b_final = z_final(spot, sent, side4)
    side5, middle5 = z_swap(send5), z_middle(half4)
    result_parts, half4 = fence_list(result_parts, half4)
    layer_out, grad_tokens, sums = end(
        spot,
        lengths,
        first_parts,
        result_parts,
        grad_mixed,
        tokens,
        table,
        mixed,
        mix_sums,
        qkv_bias_sum,
        up_bias_sum,
    )
    (sums,) = add_all([sums], [swap(sums, 1)])
    sums = sum_all(from_chips([sums] * CHIPS))
    if groups > 1:
        sums = lax.psum(sums, "fsdp", axis_index_groups=shard_groups)
    sums_got = z_swap(sums)
    up_a_final, _ = fence(up_a_final, sums)
    up_ready = up_exchange(spot, up_a_final, up_b_final)

    side5, middle5, sums_got, _ = fence(side5, middle5, sums_got, up_ready[0])
    half5 = z_half(down_b, side5)
    middle5, _ = fence(middle5, half5)
    send6 = z_half(half4, middle5)
    sent, _ = fence(send5, send6)
    qkv_ready, rows_ready = qkv_unpack(spot, sent, side5)
    side6, middle6 = z_swap(send6), z_middle(half5)
    up_ready, _ = fence_list(up_ready, send6)
    up_total = from_chips(up_ready)
    (sums,) = add_all([sums], [sums_got])

    up_total, side6, middle6, sums = fence_list(up_total, side6, middle6, sums)
    middle6, _ = fence(middle6, side6)
    send7 = z_half(half5, middle6)
    side7 = along_z([(1, 0), (2, 3)], send7)
    sent, send7, sums = fence(send6, send7, sums)
    qkv_last, out_grad = qkv_exchange(spot, qkv_ready, rows_ready, sent, side6)
    qkv_total = from_chips(qkv_last)
    sums_got = along_z([(z, z ^ 2) for z in range(4)], sums)
    up_grad = up_rows(spot, up_total)
    place_in = jnp.stack([lax.axis_index("fsdp")]).astype(jnp.int32)
    vectors = list(owned(place_in, CELLS_DEV * dp_count * fsdp_count, fsdp_count, sums, sums_got))
    qkv_total, up_grad, vectors[0] = fence_list(qkv_total, up_grad, vectors[0])
    qkv_grad = qkv_rows(spot, qkv_total)
    side7, qkv_grad = fence(side7, qkv_grad)
    down_grad = second_down(spot, send7, side7, down_grad)

    return (
        layer_out,
        grad_tokens,
        vectors[0],
        vectors[1],
        scatter_shards(qkv_grad),
        vectors[6],
        vectors[7],
        scatter_shards(out_grad),
        vectors[2],
        vectors[3],
        vectors[4],
        scatter_shards(up_grad),
        vectors[8],
        scatter_shards(down_grad),
        vectors[5],
        vectors[9],
        vectors[10],
    )


def solution(mesh):
    tokens_spec = P(("dp", "fsdp"), None)
    vector = P("fsdp")
    matrix = P("fsdp", None)
    in_specs = (
        tokens_spec,
        P(("dp", "fsdp"), None),
        P(("dp", "fsdp")),
        vector,
        vector,
        matrix,
        vector,
        vector,
        matrix,
        vector,
        vector,
        vector,
        matrix,
        vector,
        matrix,
        vector,
        tokens_spec,
    )
    out_specs = (
        tokens_spec,
        tokens_spec,
        vector,
        vector,
        matrix,
        vector,
        vector,
        matrix,
        vector,
        vector,
        vector,
        matrix,
        vector,
        matrix,
        vector,
        P(),
        P(),
    )
    return jax.shard_map(local, mesh=mesh, in_specs=in_specs, out_specs=out_specs, check_vma=False)
```

```python
import jax
import jax.numpy as jnp
from jax import lax
from jax.experimental import pallas as pl
from jax.experimental.pallas import tpu as pltpu
from jax.sharding import PartitionSpec as P

D = 1280
HEADS = 20
HEAD_DIM = 64
FF = 5120
CELLS_DEV = 2
EPS = 1e-05

TEAM = 8
CHIPS = 4
HEADS_CHIP = HEADS // CHIPS
D_CHIP = D // CHIPS
FF_CHIP = FF // CHIPS
SHARE = D // TEAM
FF_SHARE = FF // TEAM
SCALE = HEAD_DIM ** (-0.5)

GAIN1, BIAS1, BIAS_OUT, GAIN2, BIAS2, BIAS_DOWN, BIAS_UP, BIAS_QKV = range(8)
TABLE_ROWS = 8
SUM_ROWS = 16

COST = pl.CostEstimate(flops=1, bytes_accessed=1, transcendentals=0)
SMEM = pl.BlockSpec(memory_space=pltpu.SMEM)
HBM = pl.BlockSpec(memory_space=pltpu.HBM)
VMEM = pl.BlockSpec(memory_space=pltpu.VMEM)

f32 = jnp.float32
bf16 = jnp.bfloat16


def dot(a, b, dims):
    return lax.dot_general(a, b, (dims, ((), ())), preferred_element_type=f32)


def mm(a, b):
    return dot(a, b, ((1,), (0,)))


def mm_t(a, b):
    return dot(a, b, ((1,), (1,)))


def t_mm(a, b):
    return dot(a, b, ((0,), (0,)))


def normalize(values):
    center = jnp.mean(values, axis=-1, keepdims=True)
    centred = values - center
    spread = jnp.mean(centred * centred, axis=-1, keepdims=True)
    inverse = lax.rsqrt(spread + EPS)
    return centred * inverse, inverse


def norm_backward(grad_out, normed, inverse, norm_gain):
    grad_normed = grad_out * norm_gain
    first_mean = jnp.mean(grad_normed, axis=-1, keepdims=True)
    second_mean = jnp.mean(grad_normed * normed, axis=-1, keepdims=True)
    grad_in = inverse * (grad_normed - first_mean - normed * second_mean)
    gain_sum = jnp.sum(grad_out * normed, axis=0, keepdims=True)
    return grad_in, gain_sum, jnp.sum(grad_out, axis=0, keepdims=True)


def heads_of(projected, offset):
    return [
        projected[:, offset + i * HEAD_DIM : offset + (i + 1) * HEAD_DIM] for i in range(HEADS_CHIP)
    ]


def softmax_rows(queries, keys, keep):
    raw = jnp.concatenate([mm_t(q, k) for q, k in zip(queries, keys)], axis=0)
    masked = jnp.where(keep, raw * SCALE, -1e30)
    grown = jnp.exp(masked - jnp.max(masked, axis=-1, keepdims=True))
    return grown * (1.0 / jnp.sum(grown, axis=-1, keepdims=True))


def keep_of(mask):
    return jnp.concatenate([mask.astype(f32)] * HEADS_CHIP, axis=0) > 0.5


def attend(projected, mask):
    rows = mask.shape[0]
    probs = softmax_rows(heads_of(projected, 0), heads_of(projected, D_CHIP), keep_of(mask))
    probs = probs.astype(bf16)
    out = [
        mm(probs[i * rows : (i + 1) * rows], value)
        for i, value in enumerate(heads_of(projected, 2 * D_CHIP))
    ]
    return jnp.concatenate(out, axis=1).astype(bf16)


def attend_back(projected, mask, grad_context):
    rows = mask.shape[0]
    queries, keys, values = (heads_of(projected, i * D_CHIP) for i in range(3))
    grads = heads_of(grad_context, 0)
    probs = softmax_rows(queries, keys, keep_of(mask))
    grad_probs = jnp.concatenate([mm_t(g, v) for g, v in zip(grads, values)], axis=0)
    along = jnp.sum(grad_probs * probs, axis=-1, keepdims=True)
    grad_scores = (probs * (grad_probs - along) * SCALE).astype(bf16)
    probs = probs.astype(bf16)

    def cut(stack, i):
        return stack[i * rows : (i + 1) * rows]

    out = (
        [mm(cut(grad_scores, i), keys[i]) for i in range(HEADS_CHIP)]
        + [t_mm(cut(grad_scores, i), queries[i]) for i in range(HEADS_CHIP)]
        + [t_mm(cut(probs, i), grads[i]) for i in range(HEADS_CHIP)]
    )
    return jnp.concatenate(out, axis=1).astype(bf16)


HALF = SHARE // 2
EXTRA = 8
ROWS_Z = 2 * SHARE


def call(kernel, name, kinds, out_shapes, scratch=(), vmem=16):
    specs = {"s": SMEM, "h": HBM, "v": VMEM}
    made = pl.pallas_call(
        kernel,
        in_specs=[specs[kind] for kind in kinds],
        out_specs=[VMEM] * len(out_shapes),
        out_shape=[jax.ShapeDtypeStruct(shape, kind) for shape, kind in out_shapes],
        scratch_shapes=list(scratch),
        compiler_params=pltpu.CompilerParams(vmem_limit_bytes=vmem * 2**20),
        cost_estimate=COST,
        name=name,
    )

    def run(*args):
        placed = [
            pltpu.with_memory_space_constraint(arg, pltpu.HBM) if kind == "h" else arg
            for kind, arg in zip(kinds, args, strict=True)
        ]
        return made(*placed)

    return run


def sems(count):
    return pltpu.SemaphoreType.DMA((count,))


def row_at(i, size):
    return pl.ds(pl.multiple_of(i * size, size), size)


def tiled(width, tile, body):
    @pl.loop(0, width // tile)
    def _(i):
        body(row_at(i, tile))


def stack_blocks(blocks, whole):
    rows = blocks[0].shape[0]
    for i, block in enumerate(blocks):
        whole[i * rows : (i + 1) * rows, :] = block[...]


def row_of(spot, i, of_core, half=None):
    row = (2 * (spot[0] ^ i) + of_core) * SHARE
    if half is None:
        return pl.ds(pl.multiple_of(row, SHARE), SHARE)
    return pl.ds(pl.multiple_of(row + half * HALF, HALF), HALF)


def stack_columns(spot, mine, other, whole):
    core, side = spot[1], spot[2]
    for of_core, (own, near, far) in ((core, mine), (1 - core, other)):
        whole[row_of(spot, 0, of_core), :] = own[:SHARE, :]
        for i in range(1, CHIPS):
            rows = slice((i - 1) * HALF, i * HALF)
            whole[row_of(spot, i, of_core, side), :] = near[rows, :]
            whole[row_of(spot, i, of_core, 1 - side), :] = far[rows, :]


def by_core_copies(core, mine, other, whole, sem):
    size = mine.shape[0]
    return [
        pltpu.make_async_copy(mine, whole.at[row_at(core, size)], sem.at[0]),
        pltpu.make_async_copy(other, whole.at[row_at(1 - core, size)], sem.at[1]),
    ]


def start_all(copies):
    for copy in copies:
        copy.start()


def wait_all(copies):
    for copy in copies:
        copy.wait()


def chip_columns(weights, rows, chip):
    start = pl.multiple_of((chip * 5 // 2) * 128, 128)
    odd = lax.rem(chip, 2) == 1
    out = []
    for kind in range(3):
        window = weights[rows, pl.ds(kind * D + start, 384)]
        out.append(jnp.where(odd, window[:, 64 : 64 + D_CHIP], window[:, :D_CHIP]))
    return jnp.concatenate(out, axis=1)


def qkv_blocks_kernel(spot, lengths, padding, weights, *refs):
    vectors, own, sent = refs[:9], refs[9], refs[10 : 9 + CHIPS]
    held, marks, whole, vector_sems, sem = refs[9 + CHIPS : 18 + CHIPS], *refs[18 + CHIPS :]
    copies = [
        pltpu.make_async_copy(vector, here, vector_sems.at[i])
        for i, (vector, here) in enumerate(zip(vectors, held))
    ]
    copies.append(pltpu.make_async_copy(padding, marks, sem.at[0]))
    copies.append(pltpu.make_async_copy(weights, whole, sem.at[1]))
    start_all(copies)
    wait_all(copies)
    rows = padding.shape[-1]
    place = lax.broadcasted_iota(jnp.int32, (1, rows), 1)
    first = lengths[0, 0]
    member = (place >= first).astype(f32)
    leading = (place == 0) | (place == first)
    usable = jnp.where(leading | (marks[...].reshape(1, rows) > 0), 1.0, 0.0)
    code = 2.0 * member + usable
    width = 3 * D_CHIP
    lines = [v[...].astype(f32).reshape(1, -1) for v in held]
    extra = jnp.concatenate(
        [
            jnp.concatenate(lines[:6], axis=1),
            jnp.concatenate(lines[6:], axis=1),
            jnp.concatenate([code, jnp.zeros((1, width - rows), f32)], axis=1),
            jnp.zeros((EXTRA - 3, width), f32),
        ],
        axis=0,
    ).astype(bf16)
    own[:SHARE, :] = chip_columns(whole, slice(None), spot[0])
    own[SHARE:, :] = extra
    for i, block in enumerate(sent):
        block[:HALF, :] = chip_columns(whole, row_at(spot[2], HALF), spot[0] ^ (i + 1))
        block[HALF:, :] = extra


def qkv_blocks(spot, lengths, padding, weights, vectors):
    half = ((HALF + EXTRA, 3 * D_CHIP), bf16)
    return call(
        qkv_blocks_kernel,
        "qkv_blocks",
        "ss" + "h" * 11,
        [((SHARE + EXTRA, 3 * D_CHIP), bf16)] + [half] * (CHIPS - 1),
        [pltpu.VMEM(v.shape, v.dtype) for v in vectors]
        + [
            pltpu.VMEM(padding.shape, padding.dtype),
            pltpu.VMEM(weights.shape, weights.dtype),
            sems(9),
            sems(2),
        ],
    )(spot, lengths, padding, weights, *vectors)


def qkv_join_kernel(own, q1, q2, q3, x1, x2, near, near_half, first, second):
    size = first.shape[0]
    first[...] = x1[:size, :]
    second[...] = x2[size:, :]
    near[:SHARE, :] = own[:SHARE, :]
    low = SHARE + 3 * HALF
    near[low : low + EXTRA, :] = own[SHARE:, :]
    for i, block in enumerate((q1, q2, q3)):
        near[SHARE + i * HALF : SHARE + (i + 1) * HALF, :] = block[:HALF, :]
        near_half[i * HALF : (i + 1) * HALF, :] = block[:HALF, :]
        low += EXTRA
        near[low : low + EXTRA, :] = block[HALF:, :]


def qkv_join(blocks, x1, x2):
    width = blocks[0].shape[-1]
    half = ((x1.shape[0] // 2, x1.shape[1]), x1.dtype)
    return call(
        qkv_join_kernel,
        "qkv_join",
        "v" * 6,
        [
            ((SHARE + 3 * HALF + CHIPS * EXTRA, width), bf16),
            ((3 * HALF, width), bf16),
            half,
            half,
        ],
    )(*blocks, x1, x2)


def up_blocks_kernel(spot, weights, cotangent, own, *sent):
    def columns(chip):
        return pl.ds(pl.multiple_of(chip * FF_CHIP, FF_CHIP), FF_CHIP)

    own[...] = weights[:, columns(spot[0])]
    for i, block in enumerate(sent):
        block[:HALF, :] = weights[row_at(spot[2], HALF), columns(spot[0] ^ (i + 1))]
    for block in sent[:2]:
        block[HALF:, :] = cotangent[...]


def up_blocks(spot, weights, cotangent):
    both = HALF + cotangent.shape[0]
    sizes = (SHARE, both, both, HALF)
    return call(up_blocks_kernel, "up_blocks", "svv", [((size, FF_CHIP), bf16) for size in sizes])(
        spot, weights, cotangent
    )


def up_join_kernel(cotangent, u1, u2, u3, half_a, half_b, whole, first, second):
    rows = cotangent.shape[0]
    for i, block in enumerate((cotangent, u1.at[HALF:], u2.at[HALF:])):
        whole[i * rows : (i + 1) * rows, :] = block[...]
    near = jnp.concatenate([block[:HALF, :] for block in (u1, u2, u3)], axis=0)
    size = half_a.shape[0]
    half_a[...] = near[:size]
    half_b[...] = near[size:]
    half = rows // 2
    first[...] = u1[HALF : HALF + half, :]
    second[...] = u2[HALF + half :, :]


def up_join(cotangent, blocks):
    rows = cotangent.shape[0]
    half = ((3 * HALF // 2, FF_CHIP), bf16)
    passed = ((rows // 2, D), bf16)
    return call(
        up_join_kernel,
        "up_join",
        "vvvv",
        [half, half, (((CHIPS - 1) * rows, D), bf16), passed, passed],
    )(cotangent, *blocks)


def halves_kernel(whole, first, second):
    size = first.shape[0]
    first[...] = whole[:size, :]
    second[...] = whole[size:, :]


def halves(whole):
    shape = (whole.shape[0] // 2, whole.shape[1])
    return call(halves_kernel, "halves", "v", [(shape, whole.dtype)] * 2)(whole)


def join_kernel(*refs):
    stack_blocks(refs[:-1], refs[-1])


def join(blocks):
    rows, width = blocks[0].shape
    count = len(blocks)
    return call(join_kernel, "join", "v" * count, [((count * rows, width), blocks[0].dtype)])(
        *blocks
    )[0]


def fill_table(spot, extras, table, mask):
    chip, core = spot[0], spot[1]
    rows = mask.shape[1]
    table[...] = jnp.zeros_like(table)
    for team in range(TEAM):
        for i in range(6):
            table[i : i + 1, team * SHARE : (team + 1) * SHARE] = extras[
                team, 0:1, i * SHARE : (i + 1) * SHARE
            ]
    for half in range(2):
        line = extras[2 * chip + half, 1:2, :]
        lo = half * SHARE
        table[BIAS_QKV : BIAS_QKV + 1, lo : lo + SHARE] = line[:, :SHARE]
        table[BIAS_QKV : BIAS_QKV + 1, 2 * D_CHIP + lo : 2 * D_CHIP + lo + SHARE] = line[
            :, SHARE : 2 * SHARE
        ]
        table[BIAS_UP : BIAS_UP + 1, half * FF_SHARE : (half + 1) * FF_SHARE] = line[:, 2 * SHARE :]
    for i in range(CHIPS):
        code = extras[2 * (chip ^ i) + core, 2:3, :rows]
        of_key = jnp.broadcast_to(code, (rows, rows))
        cell_of_key = jnp.floor(of_key * 0.5)
        open_key = of_key - 2.0 * cell_of_key
        keep = jnp.where(cell_of_key == cell_of_key.T, open_key, 0.0)
        mask[i * rows : (i + 1) * rows, :] = keep.astype(bf16)


def token_norm_kernel(*refs):
    blocks, normed = refs[:-1], refs[-1]
    at = 0
    for x in blocks:
        rows = x.shape[0]
        normed[at : at + rows, :] = normalize(x[...].astype(f32))[0]
        at += rows


def token_norm(blocks):
    rows, width = blocks[0].shape
    shape = (CHIPS * rows, width)
    return call(token_norm_kernel, "token_norm", "v" * len(blocks), [(shape, f32)])(*blocks)[0]


def enter_kernel(spot, normed, *refs):
    mine, other, refs = refs[:2], refs[2:4], refs[4:]
    out_mine, out_other, refs = *refs[:2], refs[2:]
    table, mask, qkv, out, first_low, projected, context = refs[:7]
    partials = refs[7 : 7 + CHIPS]
    extras, out_sems = refs[7 + CHIPS :]
    rows = mask.shape[1]
    out_copies = by_core_copies(spot[1], out_mine, out_other, out, out_sems)
    start_all(out_copies)
    low = SHARE + 3 * HALF
    for of_core, lines in ((spot[1], mine[0]), (1 - spot[1], other[0])):
        for i in range(CHIPS):
            at = slice(low + i * EXTRA, low + (i + 1) * EXTRA)
            extras[2 * (spot[0] ^ i) + of_core] = lines[at, :].astype(f32)
    fill_table(spot, extras, table, mask)
    columns = [(near, near.at[SHARE:], far) for near, far in (mine, other)]
    stack_columns(spot, *columns, qkv)
    gain = table[GAIN1 : GAIN1 + 1, :]
    bias = table[BIAS1 : BIAS1 + 1, :]
    first_low[...] = (normed[...] * gain + bias).astype(bf16)
    for lo, hi in ((0, 384), (384, 768), (768, 960)):
        shift = table[BIAS_QKV : BIAS_QKV + 1, lo:hi]
        projected[:, lo:hi] = (mm(first_low[...], qkv[:, lo:hi]) + shift).astype(bf16)

    @pl.loop(0, CHIPS)
    def _(i):
        at = row_at(i, rows)
        context[at, :] = attend(projected[at, :], mask[at, :])

    wait_all(out_copies)

    def partial(at):
        whole = mm(context[...], out[:, at]).astype(bf16)
        for i, part in enumerate(partials):
            part[:, at] = whole[i * rows : (i + 1) * rows]

    tiled(D, 256, partial)


def enter(spot, normed, mine, other, out_mine, out_other):
    total = normed.shape[0]
    rows = total // CHIPS
    outs = call(
        enter_kernel,
        "enter",
        "sv" + "v" * 4 + "hv",
        [
            ((TABLE_ROWS, D), f32),
            ((total, rows), bf16),
            ((D, 3 * D_CHIP), bf16),
            ((D_CHIP, D), bf16),
            ((total, D), bf16),
            ((total, 3 * D_CHIP), bf16),
            ((total, D_CHIP), bf16),
        ]
        + [((rows, D), bf16)] * CHIPS,
        [pltpu.VMEM((TEAM, EXTRA, 3 * D_CHIP), f32), sems(2)],
    )(spot, normed, *mine, *other, out_mine, out_other)
    return outs[:7], outs[7:]


def leave_kernel(
    b0, b1, b2, b3, qkv, out, projected, mask, branch, grad_projected, bias_sum, *refs
):
    partials, grad_context = refs[:CHIPS], refs[CHIPS]
    rows = b0.shape[0]
    stack_blocks((b0, b1, b2, b3), branch)
    grad_context[...] = mm_t(branch[...], out[...]).astype(bf16)
    bias_sum[...] = jnp.zeros_like(bias_sum)

    @pl.loop(0, CHIPS)
    def _(i):
        at = row_at(i, rows)
        grad = attend_back(projected[at, :], mask[at, :], grad_context[at, :])
        grad_projected[at, :] = grad
        bias_sum[...] += jnp.sum(grad.astype(f32), axis=0, keepdims=True)

    def partial(at):
        whole = mm_t(grad_projected[...], qkv[at, :]).astype(bf16)
        for i, part in enumerate(partials):
            part[:, at] = whole[i * rows : (i + 1) * rows]

    tiled(D, 256, partial)


def leave(blocks, qkv, out, projected, mask):
    rows = blocks[0].shape[0]
    total = CHIPS * rows
    outs = call(
        leave_kernel,
        "leave",
        "v" * 8,
        [((total, D), bf16), ((total, 3 * D_CHIP), bf16), ((1, 3 * D_CHIP), f32)]
        + [((rows, D), bf16)] * CHIPS,
        [pltpu.VMEM((total, D_CHIP), bf16)],
    )(*blocks, qkv, out, projected, mask)
    return outs[:3], outs[3:]


def total_of(parts):
    total = parts[0][...].astype(f32)
    for part in parts[1:]:
        total = total + part[...].astype(f32)
    return total


def mix_kernel(p0, p1, p2, p3, tokens, table, mixed, second):
    total = total_of((p0, p1, p2, p3)) + tokens[...].astype(f32)
    total = total + table[BIAS_OUT : BIAS_OUT + 1, :]
    mixed[...] = total
    normed, _ = normalize(total)
    second[...] = (normed * table[GAIN2 : GAIN2 + 1, :] + table[BIAS2 : BIAS2 + 1, :]).astype(bf16)


def mix(parts, tokens, table):
    shape = tokens.shape
    return call(mix_kernel, "mix", "v" * 6, [(shape, f32), (shape, bf16)])(*parts, tokens, table)


def unmix_kernel(p0, p1, p2, p3, mixed, table, cotangent, grad_mixed, branch, sums):
    grad = total_of((p0, p1, p2, p3))
    normed, inverse = normalize(mixed[...])
    grad_in, gain_sum, bias_sum = norm_backward(grad, normed, inverse, table[GAIN2 : GAIN2 + 1, :])
    grad_out = cotangent[...].astype(f32)
    grad_in = grad_in + grad_out
    grad_mixed[...] = grad_in
    low = grad_in.astype(bf16)
    branch[...] = low
    sums[...] = jnp.zeros_like(sums)
    sums[0:1, :] = jnp.sum(low.astype(f32), axis=0, keepdims=True)
    sums[1:2, :] = gain_sum
    sums[2:3, :] = bias_sum
    sums[3:4, :] = jnp.sum(grad_out, axis=0, keepdims=True)


def unmix(parts, mixed, table, cotangent):
    shape = cotangent.shape
    return call(
        unmix_kernel, "unmix", "v" * 7, [(shape, f32), (shape, bf16), ((8, D), f32)]
    )(*parts, mixed, table, cotangent)


def act_grad_kernel(spot, part, g1, g2, mine, other, grad_act, down, whole, down_sems):
    copies = by_core_copies(spot[1], mine, other, down, down_sems)
    start_all(copies)
    at = 0
    for block in (part, g1, g2):
        whole[at : at + block.shape[0], :] = block[...]
        at += block.shape[0]
    wait_all(copies)

    def columns(at):
        grad_act[:, at] = mm_t(whole[...], down[at, :])

    tiled(FF_CHIP, 256, columns)


def act_grad(spot, part, passed, down_mine, down_other):
    total = part.shape[0] // (CHIPS - 1) * CHIPS
    return call(
        act_grad_kernel,
        "act_grad",
        "svvvhv",
        [((total, FF_CHIP), f32), ((FF_CHIP, D), bf16), ((total, D), bf16)],
        [sems(2)],
    )(spot, part, *passed, down_mine, down_other)


def hidden_rows(at, second, up, table, grad_act, pre_act, act, grad_pre, bias_sum):
    size = at.stop - at.start

    def columns(tile):
        pre_act[at, tile] = mm(second[at, :], up[:, tile]) + table[BIAS_UP : BIAS_UP + 1, tile]

    tiled(FF_CHIP, 256, columns)

    @pl.loop(0, size // 64)
    def _(i):
        rows = pl.ds(pl.multiple_of(at.start + i * 64, 64), 64)
        pre = pre_act[rows, :]
        below = 0.5 * (1.0 + lax.erf(pre * (0.5**0.5)))
        bell = jnp.exp(-0.5 * pre * pre) * 0.3989422804014327
        act[rows, :] = (pre * below).astype(bf16)
        grad = (grad_act[rows, :] * (below + pre * bell)).astype(bf16)
        grad_pre[rows, :] = grad
        bias_sum[...] += jnp.sum(grad.astype(f32), axis=0, keepdims=True)


def hidden_first_kernel(spot, s0, s1, s2, grad_act, table, *refs):
    columns = [(own, rest, rest.at[3 * HALF :]) for own, rest in (refs[:2], refs[2:4])]
    second, act, grad_pre, bias_sum, up, pre_act = refs[4:]
    rows = s0.shape[0]
    stack_columns(spot, *columns, up)
    stack_blocks((s0, s1, s2), second)
    bias_sum[...] = jnp.zeros_like(bias_sum)
    hidden_rows(
        slice(0, 3 * rows), second, up, table, grad_act, pre_act, act, grad_pre, bias_sum
    )


def hidden_first(spot, blocks, grad_act, table, mine, other):
    total = grad_act.shape[0]
    return call(
        hidden_first_kernel,
        "hidden_first",
        "svvvvv" + "v" * 4,
        [
            ((total, D), bf16),
            ((total, FF_CHIP), bf16),
            ((total, FF_CHIP), bf16),
            ((1, FF_CHIP), f32),
            ((D, FF_CHIP), bf16),
        ],
        [pltpu.VMEM((total, FF_CHIP), f32)],
    )(spot, *blocks, grad_act, table, *mine, *other)


def hidden_last_kernel(
    spot,
    s3,
    grad_act,
    table,
    cotangent,
    up,
    second_in,
    act_in,
    grad_pre_in,
    bias_in,
    second,
    act,
    grad_pre,
    bias_sum,
    down_sent,
    pre_act,
):
    del second_in, act_in, grad_pre_in
    rows = s3.shape[0]
    at = slice(3 * rows, 4 * rows)
    second[at, :] = s3[...]
    bias_sum[...] = bias_in[...]
    hidden_rows(at, second, up, table, grad_act, pre_act, act, grad_pre, bias_sum)
    down_product(act, cotangent, 1 - spot[1], 0, down_sent)


def down_product(act, cotangent, of_core, half, target):
    low = half * ROWS_Z
    aligned = low // 128 * 128
    if half == 0:
        units = pl.ds(pl.multiple_of(of_core * FF_SHARE, 128), ROWS_Z)
        target[...] = t_mm(act[:, units], cotangent[...]).astype(target.dtype)
    else:
        units = pl.ds(pl.multiple_of(of_core * FF_SHARE + aligned, 128), FF_SHARE - aligned)
        window = act[:, units][:, low - aligned :]
        target[...] = t_mm(window, cotangent[...]).astype(target.dtype)


def up_product(second, grad_pre, pair, of_core, target, work):
    for i in range(2):
        first = (2 * (2 * pair + i) + of_core) * SHARE
        aligned = pl.multiple_of(first // 128 * 128, 128)
        work[...] = t_mm(second[:, pl.ds(aligned, 256)], grad_pre[...])
        start = pl.multiple_of(lax.rem(first, 128), 32)
        target[i * SHARE : (i + 1) * SHARE, :] = work[pl.ds(start, SHARE), :].astype(target.dtype)


def hidden_last(spot, block, grad_act, table, cotangent, up, second, act, grad_pre, bias_sum):
    total = second.shape[0]
    return pl.pallas_call(
        hidden_last_kernel,
        in_specs=[SMEM] + [VMEM] * 9,
        out_specs=[VMEM] * 5,
        out_shape=[
            jax.ShapeDtypeStruct(second.shape, bf16),
            jax.ShapeDtypeStruct(act.shape, bf16),
            jax.ShapeDtypeStruct(grad_pre.shape, bf16),
            jax.ShapeDtypeStruct(bias_sum.shape, f32),
            jax.ShapeDtypeStruct((ROWS_Z, D), bf16),
        ],
        scratch_shapes=[pltpu.VMEM((total, FF_CHIP), f32)],
        input_output_aliases={6: 0, 7: 1, 8: 2},
        compiler_params=pltpu.CompilerParams(vmem_limit_bytes=16 * 2**20),
        cost_estimate=COST,
        name="hidden_last",
    )(spot, block, grad_act, table, cotangent, up, second, act, grad_pre, bias_sum)


def second_grad_kernel(spot, grad_pre, up, second, *refs):
    partials, up_sent, work = refs[:CHIPS], refs[CHIPS], refs[CHIPS + 1]
    rows = partials[0].shape[0]

    def partial(at):
        whole = mm_t(grad_pre[...], up[at, :]).astype(bf16)
        for i, part in enumerate(partials):
            part[:, at] = whole[i * rows : (i + 1) * rows]

    tiled(D, 256, partial)
    up_product(second, grad_pre, 0, 1 - spot[1], up_sent, work)


def second_grad(spot, grad_pre, up, second):
    rows = grad_pre.shape[0] // CHIPS
    outs = call(
        second_grad_kernel,
        "second_grad",
        "svvv",
        [((rows, D), bf16)] * CHIPS + [((ROWS_Z, FF_CHIP), bf16)],
        [pltpu.VMEM((256, FF_CHIP), f32)],
    )(spot, grad_pre, up, second)
    return outs[:CHIPS], outs[CHIPS]


def split_rows(core, whole, sent, kept):
    for k in range(CHIPS):
        targets = ((sent[k // 2], k % 2, 1 - core), (kept, k, core))
        for target, at, of_core in targets:
            start = pl.multiple_of((2 * k + of_core) * SHARE, SHARE)
            target[at] = whole[pl.ds(start, SHARE), :].astype(bf16)


def down_grad_kernel(spot, act, cotangent, got, total):
    down_product(act, cotangent, spot[1], 0, total)
    total[...] = (total[...].astype(f32) + got[...].astype(f32)).astype(bf16)


def down_grad_of(spot, act, cotangent, got):
    return call(down_grad_kernel, "down_grad", "svvv", [((ROWS_Z, D), bf16)])(
        spot, act, cotangent, got
    )[0]


def rest_kernel(
    spot, second, grad_pre, act, cotangent, up_a, up_b, up_sent, down_b, down_sent, work
):
    core = spot[1]
    up_product(second, grad_pre, 0, core, up_a, work)
    up_product(second, grad_pre, 1, 1 - core, up_sent, work)
    up_product(second, grad_pre, 1, core, up_b, work)
    down_product(act, cotangent, 1 - core, 1, down_sent)
    down_product(act, cotangent, core, 1, down_b)


def rest_of_grads(spot, second, grad_pre, act, cotangent):
    return call(
        rest_kernel,
        "rest",
        "svvvv",
        [((ROWS_Z, D), bf16)] * 5,
        [pltpu.VMEM((256, FF_CHIP), f32)],
    )(spot, second, grad_pre, act, cotangent)


def result_kernel(act, down, *partials):
    rows = partials[0].shape[0]

    def columns(at):
        whole = mm(act[...], down[:, at]).astype(bf16)
        for i, part in enumerate(partials):
            part[:, at] = whole[i * rows : (i + 1) * rows]

    tiled(D, 256, columns)


def result_of(act, down):
    rows = act.shape[0] // CHIPS
    return call(result_kernel, "result", "vv", [((rows, D), bf16)] * CHIPS)(act, down)


def qkv_grad_kernel(
    spot,
    first_low,
    grad_projected,
    context,
    branch,
    sent_a,
    sent_b,
    kept,
    out_sent,
    out_kept,
    whole,
    out,
):
    core = spot[1]

    def columns(at):
        whole[at, :] = t_mm(first_low[:, at], grad_projected[...])

    tiled(D, 256, columns)
    split_rows(core, whole, (sent_a, sent_b), kept)
    out[...] = t_mm(context[...], branch[...])
    for target, of_core in ((out_sent, 1 - core), (out_kept, core)):
        target[...] = out[row_at(of_core, SHARE), :].astype(bf16)


def qkv_grad_of(spot, first_low, grad_projected, context, branch):
    half = ((CHIPS // 2, SHARE, 3 * D_CHIP), bf16)
    rows = ((SHARE, D), bf16)
    return call(
        qkv_grad_kernel,
        "qkv_grad",
        "svvvv",
        [half, half, ((CHIPS, SHARE, 3 * D_CHIP), bf16), rows, rows],
        [pltpu.VMEM((D, 3 * D_CHIP), f32), pltpu.VMEM((D_CHIP, D), f32)],
    )(spot, first_low, grad_projected, context, branch)


def add_kernel(*refs):
    count = len(refs) // 3
    for a, b, c in zip(refs[:count], refs[count : 2 * count], refs[2 * count :]):
        c[...] = (a[...].astype(f32) + b[...].astype(f32)).astype(c.dtype)


def add_all(left, right):
    shapes = [(a.shape, a.dtype) for a in left]
    return call(add_kernel, "add", "v" * (2 * len(left)), shapes)(*left, *right)


PACKED = SHARE * 3 // 4
STEP = SHARE // 4


def sum_all_kernel(a, b, c, d, total):
    total[...] = (a[...] + b[...]) + (c[...] + d[...])


def sum_all(parts):
    shape = (parts[0].shape, parts[0].dtype)
    return call(sum_all_kernel, "sum_all", "vvvv", [shape])(*parts)[0]


def pack_kernel(kept, got_a, got_b, out_kept, out_got, *chunks):
    for i, chunk in enumerate(chunks):
        for j in range(2):
            got = got_b if i else got_a
            total = (kept[2 * i + j].astype(f32) + got[j].astype(f32)).astype(bf16)
            lo = j * PACKED
            chunk[lo : lo + PACKED, : 3 * D_CHIP] = total[:PACKED]
            for part in range(3):
                at = lo + part * STEP
                chunk[at : at + STEP, 3 * D_CHIP :] = total[
                    PACKED:, part * D_CHIP : (part + 1) * D_CHIP
                ]
        rows = slice(i * HALF, (i + 1) * HALF)
        total = out_kept[rows, :].astype(f32) + out_got[rows, :].astype(f32)
        chunk[2 * PACKED :, :] = total.astype(bf16)


def pack(kept, got_a, got_b, out_kept, out_got):
    return call(pack_kernel, "pack", "vvvvv", [((ROWS_Z, D), bf16)] * 2)(
        kept, got_a, got_b, out_kept, out_got
    )


def unpacked(chunk, j):
    lo = j * PACKED
    tail = [
        chunk[lo + part * STEP : lo + (part + 1) * STEP, 3 * D_CHIP :] for part in range(3)
    ]
    return jnp.concatenate(
        [chunk[lo : lo + PACKED, : 3 * D_CHIP], jnp.concatenate(tail, axis=1)], axis=0
    )


def z_half(low, got_side):
    return add_all([low], [got_side])[0]


def z_send_kernel(spot, half, got_middle, low, sent):
    middle = spot[3] > 0

    @pl.when(middle)
    def _():
        whole = half[...].astype(f32) + got_middle[...].astype(f32)
        sent[...] = whole.astype(bf16)

    @pl.when(jnp.logical_not(middle))
    def _():
        sent[...] = low[...]


def z_send(spot, half, got_middle, low):
    return call(z_send_kernel, "z_send", "svvv", [(low.shape, bf16)])(spot, half, got_middle, low)[0]


def z_final_kernel(spot, sent, got_side, final):
    final[...] = jnp.where(spot[3] > 0, sent[...], got_side[...])


def z_final(spot, sent, got_side):
    return call(z_final_kernel, "z_final", "svv", [(sent.shape, bf16)])(spot, sent, got_side)[0]


def first_down_kernel(spot, sent, got, down, here, sem):
    here[...] = jnp.where(spot[3] > 0, sent[...], got[...]).astype(f32)
    copy = pltpu.make_async_copy(here, down.at[:ROWS_Z], sem.at[0])
    copy.start()
    copy.wait()


def first_down(spot, sent, got):
    return pl.pallas_call(
        first_down_kernel,
        in_specs=[SMEM, VMEM, VMEM],
        out_specs=HBM,
        out_shape=pltpu.HBM((2 * ROWS_Z, D), f32),
        scratch_shapes=[pltpu.VMEM((ROWS_Z, D), f32), sems(1)],
        compiler_params=pltpu.CompilerParams(vmem_limit_bytes=16 * 2**20),
        cost_estimate=COST,
        name="first_down",
    )(spot, sent, got)


def second_down_kernel(spot, sent, got, before, down, here, sem):
    del before
    here[...] = jnp.where(spot[3] > 0, sent[...], got[...]).astype(f32)
    copy = pltpu.make_async_copy(here, down.at[ROWS_Z:], sem.at[0])
    copy.start()
    copy.wait()


def second_down(spot, sent, got, down):
    return pl.pallas_call(
        second_down_kernel,
        in_specs=[SMEM, VMEM, VMEM, HBM],
        out_specs=HBM,
        out_shape=pltpu.HBM((2 * ROWS_Z, D), f32),
        scratch_shapes=[pltpu.VMEM((ROWS_Z, D), f32), sems(1)],
        input_output_aliases={3: 0},
        compiler_params=pltpu.CompilerParams(vmem_limit_bytes=16 * 2**20),
        cost_estimate=COST,
        name="second_down",
    )(spot, sent, got, pltpu.with_memory_space_constraint(down, pltpu.HBM))


def qkv_rows_kernel(spot, b0, b1, b2, b3, qkv, rows, stack, sem):
    for i, block in enumerate((b0, b1, b2, b3)):
        stack[spot[0] ^ i] = block[...]
    copies = []
    for kind in range(3):
        for chip in range(CHIPS):
            lo = kind * D + chip * D_CHIP
            rows[:, lo : lo + D_CHIP] = stack[
                chip, :, kind * D_CHIP : (kind + 1) * D_CHIP
            ].astype(f32)
        at = slice(kind * D, (kind + 1) * D)
        copies.append(pltpu.make_async_copy(rows.at[:, at], qkv.at[:, at], sem.at[kind]))
        copies[-1].start()
    wait_all(copies)


def qkv_rows(spot, blocks):
    shape = blocks[0].shape
    return pl.pallas_call(
        qkv_rows_kernel,
        in_specs=[SMEM] + [VMEM] * 4,
        out_specs=HBM,
        out_shape=pltpu.HBM((shape[0], 3 * D), f32),
        scratch_shapes=[
            pltpu.VMEM((shape[0], 3 * D), f32),
            pltpu.VMEM((CHIPS,) + shape, bf16),
            sems(3),
        ],
        compiler_params=pltpu.CompilerParams(vmem_limit_bytes=16 * 2**20),
        cost_estimate=COST,
        name="qkv_rows",
    )(spot, *blocks)


def owned_kernel(count, place, sums, got, *outs):
    total = sums[...] + got[...]
    index = place[0]
    size = outs[0].shape[0]
    mine = pltpu.roll(total, D - index * size, 1)
    for i, row in enumerate((0, 1, 2, 3, 4, 5, 8, 9)):
        outs[i][...] = mine[row : row + 1, :size].reshape(size)
    wide = outs[8].shape[0]
    first = index * wide
    row = first // D
    line = total[10:11, :]
    for k in range(1, CHIPS):
        line = jnp.where(row == k, total[10 + k : 11 + k, :], line)
    line = pltpu.roll(jnp.broadcast_to(line, (8, D)), D - lax.rem(first, D), 1)
    outs[8][...] = line[0:1, :wide].reshape(wide)
    mean = total[6:7, :] / count
    outs[9][...] = mean.reshape(D)
    outs[10][...] = (total[7:8, :] / count - mean * mean).reshape(D)


def owned(place, count, fsdp_count, sums, got):
    sizes = [D // fsdp_count] * 8 + [FF // fsdp_count, D, D]

    def kernel(*refs):
        owned_kernel(count, *refs)

    return call(kernel, "owned", "svv", [((size,), f32) for size in sizes])(place, sums, got)


def up_exchange_kernel(spot, a, b, *blocks):
    chunks = (a, b)
    for i, block in enumerate(blocks):
        chip = spot[0] ^ i
        at = row_at(lax.rem(chip, 2), SHARE)
        block[...] = jnp.where(chip >= 2, chunks[1][at, :], chunks[0][at, :])


def up_exchange(spot, a, b):
    return call(up_exchange_kernel, "up_exchange", "svv", [((SHARE, FF_CHIP), bf16)] * CHIPS)(
        spot, a, b
    )


def qkv_unpack_kernel(spot, sent, got_side, blocks, out_rows):
    chunk = jnp.where(spot[3] > 0, sent[...], got_side[...])
    for j in range(2):
        blocks[j] = unpacked(chunk, j)
    out_rows[...] = chunk[2 * PACKED :, :].astype(f32)


def qkv_unpack(spot, sent, got_side):
    return call(
        qkv_unpack_kernel,
        "qkv_unpack",
        "svv",
        [((2, SHARE, 3 * D_CHIP), bf16), ((HALF, D), f32)],
    )(spot, sent, got_side)


def qkv_exchange_kernel(spot, blocks_a, rows_a, sent, got_side, *refs):
    blocks, out_rows, stack = refs[:CHIPS], refs[CHIPS], refs[CHIPS + 1]
    chunk = jnp.where(spot[3] > 0, sent[...], got_side[...])
    stack[:2] = blocks_a[...]
    for j in range(2):
        stack[2 + j] = unpacked(chunk, j)
    out_rows[:HALF, :] = rows_a[...]
    out_rows[HALF:, :] = chunk[2 * PACKED :, :].astype(f32)
    for i, block in enumerate(blocks):
        block[...] = stack[spot[0] ^ i]


def qkv_exchange(spot, blocks_a, rows_a, sent, got_side):
    shape = (SHARE, 3 * D_CHIP)
    outs = call(
        qkv_exchange_kernel,
        "qkv_exchange",
        "svvvv",
        [(shape, bf16)] * CHIPS + [((SHARE, D), f32)],
        [pltpu.VMEM((CHIPS,) + shape, bf16)],
    )(spot, blocks_a, rows_a, sent, got_side)
    return outs[:CHIPS], outs[CHIPS]


def up_rows_kernel(spot, b0, b1, b2, b3, weights):
    for i, block in enumerate((b0, b1, b2, b3)):
        start = pl.multiple_of((spot[0] ^ i) * FF_CHIP, FF_CHIP)
        weights[:, pl.ds(start, FF_CHIP)] = block[...].astype(f32)


def up_rows(spot, blocks):
    return call(up_rows_kernel, "up_rows", "svvvv", [((SHARE, FF), f32)])(spot, *blocks)[0]


def end_kernel(
    spot,
    lengths,
    p0,
    p1,
    p2,
    p3,
    r0,
    r1,
    r2,
    r3,
    grad_mixed,
    tokens,
    table,
    mixed,
    mix_sums,
    qkv_sum,
    up_sum,
    layer_out,
    grad_tokens,
    sums,
):
    grad = total_of((p0, p1, p2, p3))
    normed, inverse = normalize(tokens[...].astype(f32))
    grad_in, gain_sum, bias_sum = norm_backward(grad, normed, inverse, table[GAIN1 : GAIN1 + 1, :])
    grad_tokens[...] = grad_mixed[...] + grad_in
    result = mixed[...] + total_of((r0, r1, r2, r3)) + table[BIAS_DOWN : BIAS_DOWN + 1, :]
    layer_out[...] = result.astype(bf16)
    place = lax.broadcasted_iota(jnp.int32, (result.shape[0], 1), 0)
    picked = jnp.where((place == 0) | (place == lengths[0, 0]), result, 0.0)
    sums[...] = jnp.zeros_like(sums)
    sums[0:1, :] = gain_sum
    sums[1:2, :] = bias_sum
    sums[2:6, :] = mix_sums[0:4, :]
    sums[6:7, :] = jnp.sum(picked, axis=0, keepdims=True)
    sums[7:8, :] = jnp.sum(picked * picked, axis=0, keepdims=True)
    for k in range(CHIPS):
        here = spot[0] == k
        lo = k * D_CHIP
        sums[8:9, lo : lo + D_CHIP] = jnp.where(here, qkv_sum[:, :D_CHIP], 0.0)
        sums[9:10, lo : lo + D_CHIP] = jnp.where(here, qkv_sum[:, 2 * D_CHIP :], 0.0)
        sums[10 + k : 11 + k, :] = jnp.where(here, up_sum[...], 0.0)


def end(spot, lengths, parts, results, *rest):
    shape = parts[0].shape
    return call(
        end_kernel,
        "end",
        "ss" + "v" * 15,
        [(shape, bf16), (shape, f32), ((SUM_ROWS, D), f32)],
    )(spot, lengths, *parts, *results, *rest)


def fence(*values):
    return lax.optimization_barrier(values)


def local(
    tokens,
    lengths,
    padding,
    ln1_gain,
    ln1_bias,
    w_qkv,
    b_query,
    b_value,
    w_out,
    b_out,
    ln2_gain,
    ln2_bias,
    w_up,
    b_up,
    w_down,
    b_down,
    cotangent,
):
    fsdp_count = lax.axis_size("fsdp")
    dp_count = lax.axis_size("dp")
    groups = fsdp_count // TEAM
    place = lax.axis_index("fsdp") // groups
    chip = place // 2
    core = place % 2
    depth = lax.axis_index("dp")
    middle = (depth == 1) | (depth == 2)
    spot = jnp.stack([chip, core, depth % 2, middle.astype(jnp.int32)]).astype(jnp.int32)

    def swap(value, mask):
        pairs = [
            (team * groups + group, (team ^ mask) * groups + group)
            for team in range(TEAM)
            for group in range(groups)
        ]
        return lax.ppermute(value, "fsdp", pairs)

    shard_groups = [[team * groups + group for group in range(groups)] for team in range(TEAM)]
    def gather_shards(value):
        if groups == 1:
            return value
        return lax.all_gather(value, "fsdp", axis=0, tiled=True, axis_index_groups=shard_groups)

    def scatter_shards(value):
        if groups == 1:
            return value
        return lax.psum_scatter(
            value, "fsdp", scatter_dimension=0, tiled=True, axis_index_groups=shard_groups
        )

    def along_z(pairs, value):
        return lax.ppermute(value, "dp", pairs)

    def z_swap(value):
        return along_z([(0, 1), (1, 0), (2, 3), (3, 2)], value)

    def z_middle(value):
        return along_z([(1, 2), (2, 1)], value)

    def from_chips(blocks):
        return [blocks[0]] + [swap(block, 2 * i) for i, block in enumerate(blocks) if i > 0]

    def fence_list(first, *others):
        done = fence(*first, *others)
        return list(done[: len(first)]), *done[len(first) :]

    w_qkv, w_out, w_up, w_down = (gather_shards(w) for w in (w_qkv, w_out, w_up, w_down))
    given = (ln1_gain, ln1_bias, b_out, ln2_gain, ln2_bias, b_down, b_query, b_value, b_up)
    qkv_sent = qkv_blocks(spot, lengths, padding, w_qkv, [gather_shards(v) for v in given])
    qkv_got = from_chips(qkv_sent)
    x1, x2, *qkv_got = fence(swap(tokens, 2), swap(tokens, 4), *qkv_got)
    qkv_near, qkv_half, x1_half, x2_half = qkv_join(qkv_got, x1, x2)
    qkv_far = z_swap(qkv_half)
    qkv_near_other = swap(qkv_near, 1)
    blocks = [tokens, x1, x2, swap(x1_half, 4), swap(x2_half, 2)]
    normed = token_norm(blocks)
    out_sent, _ = fence(w_out, qkv_near)
    out_other = swap(out_sent, 1)
    up_own, *up_sent = up_blocks(spot, w_up, cotangent)
    up_own, *up_sent = fence(up_own, *up_sent, qkv_near)[:-1]
    loads = [swap(block, 2 * i + 2) for i, block in enumerate(up_sent)]
    normed, qkv_far, qkv_near_other, out_other = fence(normed, qkv_far, qkv_near_other, out_other)
    qkv_far_other = join([swap(half, 1) for half in halves(qkv_far)])

    (table, mask, qkv, out, first_low, projected, context), partial_out = enter(
        spot,
        normed,
        [qkv_near, qkv_far],
        [qkv_near_other, qkv_far_other],
        w_out,
        out_other,
    )
    out_parts = from_chips(partial_out)
    cotangent_late, _ = fence(cotangent, partial_out[0])
    up_half_a, up_half_b, part, first, second = up_join(cotangent_late, loads)
    up_far = [z_swap(up_half_a), z_swap(up_half_b)]
    passed = [swap(first, 4), swap(second, 2)]
    passed, up_far[0], up_far[1], *out_parts = fence_list(passed, *up_far, *out_parts)
    mixed, second_own = mix(out_parts, tokens, table)
    second_blocks = from_chips([second_own] * CHIPS)
    up_far, _ = fence_list(up_far, second_own)
    up_rest = join([up_half_a, up_half_b] + up_far)
    up_own_sent, _ = fence(up_own, second_own)
    up_other = [swap(up_own_sent, 1), swap(up_rest, 1)]
    down_sent, _ = fence(w_down, second_own)
    down_other = swap(down_sent, 1)
    part, down_other = fence(part, down_other)
    grad_act, down, whole_cotangent = act_grad(spot, part, passed, w_down, down_other)

    second_low, act_low, grad_pre, up_bias_sum, up = hidden_first(
        spot,
        second_blocks[:3],
        grad_act,
        table,
        [up_own, up_rest],
        up_other,
    )
    block, up_bias_sum = fence(second_blocks[3], up_bias_sum)
    second_low, act_low, grad_pre, up_bias_sum, down_sent = hidden_last(
        spot, block, grad_act, table, whole_cotangent, up, second_low, act_low, grad_pre, up_bias_sum
    )
    down_got = swap(down_sent, 1)
    partial_second, up_sent = second_grad(spot, grad_pre, up, second_low)
    up_got = swap(up_sent, 1)
    act_low, up_sent = fence(act_low, up_sent)
    down_a = down_grad_of(spot, act_low, whole_cotangent, down_got)
    side0 = z_swap(down_a)
    *partial_second, down_a = fence(*partial_second, down_a)
    second_parts = from_chips(partial_second)
    second_low, down_a = fence(second_low, down_a)
    up_a, up_b, up_sent, down_b, down_sent = rest_of_grads(
        spot, second_low, grad_pre, act_low, whole_cotangent
    )
    up_got, up_sent = fence(up_got, up_sent)
    (up_a,) = add_all([up_a], [up_got])
    up_got = swap(up_sent, 1)

    second_parts, side0, up_a = fence_list(second_parts, side0, up_a)
    half0, send1 = z_half(down_a, side0), up_a
    send1, _ = fence(send1, half0)
    side1, middle1 = z_swap(send1), z_middle(half0)
    second_parts, half0 = fence_list(second_parts, half0)
    grad_mixed, branch_own, mix_sums = unmix(second_parts, mixed, table, cotangent)
    branch_blocks = from_chips([branch_own] * CHIPS)
    act_low, branch_own = fence(act_low, branch_own)
    partial_result = list(result_of(act_low, down))

    up_got, partial_result[0] = fence(up_got, partial_result[0])
    (up_b,) = add_all([up_b], [up_got])
    branch_blocks, side1, middle1, *partial_result, up_b = fence_list(
        branch_blocks, side1, middle1, *partial_result, up_b
    )
    half1 = z_half(up_a, side1)
    middle1, _ = fence(middle1, half1)
    send2 = z_send(spot, half0, middle1, up_b)
    side2, middle2 = z_swap(send2), z_middle(half1)
    branch_blocks, half1 = fence_list(branch_blocks, half1)
    (whole_branch, grad_projected, qkv_bias_sum), partial_first = leave(
        branch_blocks, qkv, out, projected, mask
    )
    first_low, grad_projected = fence(first_low, grad_projected)
    qkv_sent_a, qkv_sent_b, qkv_kept, out_sent, out_kept = qkv_grad_of(
        spot, first_low, grad_projected, context, whole_branch
    )
    qkv_a, qkv_b = pack(
        qkv_kept, swap(qkv_sent_a, 1), swap(qkv_sent_b, 1), out_kept, swap(out_sent, 1)
    )

    side2, middle2, qkv_a = fence(side2, middle2, qkv_a)
    half2 = z_half(up_b, side2)
    middle2, _ = fence(middle2, half2)
    send3 = z_send(spot, half1, middle2, qkv_a)
    side3, middle3 = z_swap(send3), z_middle(half2)
    down_sent, _ = fence(down_sent, send3)
    (down_b,) = add_all([down_b], [swap(down_sent, 1)])
    *partial_first, down_b = fence(*partial_first, down_b)
    first_parts = from_chips(partial_first)
    down_grad = first_down(spot, send2, side2)

    first_parts, side3, middle3 = fence_list(first_parts, side3, middle3)
    half3 = z_half(qkv_a, side3)
    middle3, _ = fence(middle3, half3)
    send4 = z_send(spot, half2, middle3, qkv_b)
    sent, _ = fence(send3, send4)
    up_a_final = z_final(spot, sent, side3)
    side4, middle4 = z_swap(send4), z_middle(half3)
    *partial_result, half3 = fence(*partial_result, half3)
    result_parts = from_chips(partial_result)

    result_parts, side4, middle4 = fence_list(result_parts, side4, middle4)
    half4 = z_half(qkv_b, side4)
    middle4, _ = fence(middle4, half4)
    send5 = z_send(spot, half3, middle4, down_b)
    sent, _ = fence(send4, send5)
    up_b_final = z_final(spot, sent, side4)
    side5, middle5 = z_swap(send5), z_middle(half4)
    result_parts, half4 = fence_list(result_parts, half4)
    layer_out, grad_tokens, sums = end(
        spot,
        lengths,
        first_parts,
        result_parts,
        grad_mixed,
        tokens,
        table,
        mixed,
        mix_sums,
        qkv_bias_sum,
        up_bias_sum,
    )
    (sums,) = add_all([sums], [swap(sums, 1)])
    sums = sum_all(from_chips([sums] * CHIPS))
    if groups > 1:
        sums = lax.psum(sums, "fsdp", axis_index_groups=shard_groups)
    sums_got = z_swap(sums)
    up_a_final, _ = fence(up_a_final, sums)
    up_ready = up_exchange(spot, up_a_final, up_b_final)

    side5, middle5, sums_got, _ = fence(side5, middle5, sums_got, up_ready[0])
    half5 = z_half(down_b, side5)
    middle5, _ = fence(middle5, half5)
    send6 = z_half(half4, middle5)
    sent, _ = fence(send5, send6)
    qkv_ready, rows_ready = qkv_unpack(spot, sent, side5)
    side6, middle6 = z_swap(send6), z_middle(half5)
    up_ready, _ = fence_list(up_ready, send6)
    up_total = from_chips(up_ready)
    (sums,) = add_all([sums], [sums_got])

    up_total, side6, middle6, sums = fence_list(up_total, side6, middle6, sums)
    middle6, _ = fence(middle6, side6)
    send7 = z_half(half5, middle6)
    side7 = along_z([(1, 0), (2, 3)], send7)
    sent, send7, sums = fence(send6, send7, sums)
    qkv_last, out_grad = qkv_exchange(spot, qkv_ready, rows_ready, sent, side6)
    qkv_total = from_chips(qkv_last)
    sums_got = along_z([(z, z ^ 2) for z in range(4)], sums)
    up_grad = up_rows(spot, up_total)
    place_in = jnp.stack([lax.axis_index("fsdp")]).astype(jnp.int32)
    vectors = list(owned(place_in, CELLS_DEV * dp_count * fsdp_count, fsdp_count, sums, sums_got))
    qkv_total, up_grad, vectors[0] = fence_list(qkv_total, up_grad, vectors[0])
    qkv_grad = qkv_rows(spot, qkv_total)
    side7, qkv_grad = fence(side7, qkv_grad)
    down_grad = second_down(spot, send7, side7, down_grad)

    return (
        layer_out,
        grad_tokens,
        vectors[0],
        vectors[1],
        scatter_shards(qkv_grad),
        vectors[6],
        vectors[7],
        scatter_shards(out_grad),
        vectors[2],
        vectors[3],
        vectors[4],
        scatter_shards(up_grad),
        vectors[8],
        scatter_shards(down_grad),
        vectors[5],
        vectors[9],
        vectors[10],
    )


def solution(mesh):
    tokens_spec = P(("dp", "fsdp"), None)
    vector = P("fsdp")
    matrix = P("fsdp", None)
    in_specs = (
        tokens_spec,
        P(("dp", "fsdp"), None),
        P(("dp", "fsdp")),
        vector,
        vector,
        matrix,
        vector,
        vector,
        matrix,
        vector,
        vector,
        vector,
        matrix,
        vector,
        matrix,
        vector,
        tokens_spec,
    )
    out_specs = (
        tokens_spec,
        tokens_spec,
        vector,
        vector,
        matrix,
        vector,
        vector,
        matrix,
        vector,
        vector,
        vector,
        matrix,
        vector,
        matrix,
        vector,
        P(),
        P(),
    )
    return jax.shard_map(local, mesh=mesh, in_specs=in_specs, out_specs=out_specs, check_vma=False)
```

```python
import jax
import jax.numpy as jnp
from jax import lax
from jax.experimental import pallas as pl
from jax.experimental.pallas import tpu as pltpu
from jax.sharding import PartitionSpec as P

D = 1280
HEADS = 20
HEAD_DIM = 64
FF = 5120
CELLS_DEV = 2
EPS = 1e-05

TEAM = 8
CHIPS = 4
HEADS_CHIP = HEADS // CHIPS
D_CHIP = D // CHIPS
FF_CHIP = FF // CHIPS
SHARE = D // TEAM
FF_SHARE = FF // TEAM
SCALE = HEAD_DIM ** (-0.5)

GAIN1, BIAS1, BIAS_OUT, GAIN2, BIAS2, BIAS_DOWN, BIAS_UP, BIAS_QKV = range(8)
TABLE_ROWS = 8
SUM_ROWS = 16

COST = pl.CostEstimate(flops=1, bytes_accessed=1, transcendentals=0)
SMEM = pl.BlockSpec(memory_space=pltpu.SMEM)
HBM = pl.BlockSpec(memory_space=pltpu.HBM)
VMEM = pl.BlockSpec(memory_space=pltpu.VMEM)

f32 = jnp.float32
bf16 = jnp.bfloat16


def dot(a, b, dims):
    return lax.dot_general(a, b, (dims, ((), ())), preferred_element_type=f32)


def mm(a, b):
    return dot(a, b, ((1,), (0,)))


def mm_t(a, b):
    return dot(a, b, ((1,), (1,)))


def t_mm(a, b):
    return dot(a, b, ((0,), (0,)))


def normalize(values):
    center = jnp.mean(values, axis=-1, keepdims=True)
    centred = values - center
    spread = jnp.mean(centred * centred, axis=-1, keepdims=True)
    inverse = lax.rsqrt(spread + EPS)
    return centred * inverse, inverse


def norm_backward(grad_out, normed, inverse, norm_gain):
    grad_normed = grad_out * norm_gain
    first_mean = jnp.mean(grad_normed, axis=-1, keepdims=True)
    second_mean = jnp.mean(grad_normed * normed, axis=-1, keepdims=True)
    grad_in = inverse * (grad_normed - first_mean - normed * second_mean)
    gain_sum = jnp.sum(grad_out * normed, axis=0, keepdims=True)
    return grad_in, gain_sum, jnp.sum(grad_out, axis=0, keepdims=True)


def heads_of(projected, offset):
    return [
        projected[:, offset + i * HEAD_DIM : offset + (i + 1) * HEAD_DIM] for i in range(HEADS_CHIP)
    ]


def softmax_rows(queries, keys, keep):
    raw = jnp.concatenate([mm_t(q, k) for q, k in zip(queries, keys)], axis=0)
    masked = jnp.where(keep, raw * SCALE, -1e30)
    grown = jnp.exp(masked - jnp.max(masked, axis=-1, keepdims=True))
    return grown * (1.0 / jnp.sum(grown, axis=-1, keepdims=True))


def keep_of(mask):
    return jnp.concatenate([mask.astype(f32)] * HEADS_CHIP, axis=0) > 0.5


def attend(projected, mask):
    rows = mask.shape[0]
    probs = softmax_rows(heads_of(projected, 0), heads_of(projected, D_CHIP), keep_of(mask))
    probs = probs.astype(bf16)
    out = [
        mm(probs[i * rows : (i + 1) * rows], value)
        for i, value in enumerate(heads_of(projected, 2 * D_CHIP))
    ]
    return jnp.concatenate(out, axis=1).astype(bf16)


def attend_back(projected, mask, grad_context):
    rows = mask.shape[0]
    queries, keys, values = (heads_of(projected, i * D_CHIP) for i in range(3))
    grads = heads_of(grad_context, 0)
    probs = softmax_rows(queries, keys, keep_of(mask))
    grad_probs = jnp.concatenate([mm_t(g, v) for g, v in zip(grads, values)], axis=0)
    along = jnp.sum(grad_probs * probs, axis=-1, keepdims=True)
    grad_scores = (probs * (grad_probs - along) * SCALE).astype(bf16)
    probs = probs.astype(bf16)

    def cut(stack, i):
        return stack[i * rows : (i + 1) * rows]

    out = (
        [mm(cut(grad_scores, i), keys[i]) for i in range(HEADS_CHIP)]
        + [t_mm(cut(grad_scores, i), queries[i]) for i in range(HEADS_CHIP)]
        + [t_mm(cut(probs, i), grads[i]) for i in range(HEADS_CHIP)]
    )
    return jnp.concatenate(out, axis=1).astype(bf16)


HALF = SHARE // 2
EXTRA = 8
ROWS_Z = 2 * SHARE


def call(kernel, name, kinds, out_shapes, scratch=(), vmem=16):
    specs = {"s": SMEM, "h": HBM, "v": VMEM}
    made = pl.pallas_call(
        kernel,
        in_specs=[specs[kind] for kind in kinds],
        out_specs=[VMEM] * len(out_shapes),
        out_shape=[jax.ShapeDtypeStruct(shape, kind) for shape, kind in out_shapes],
        scratch_shapes=list(scratch),
        compiler_params=pltpu.CompilerParams(vmem_limit_bytes=vmem * 2**20),
        cost_estimate=COST,
        name=name,
    )

    def run(*args):
        placed = [
            pltpu.with_memory_space_constraint(arg, pltpu.HBM) if kind == "h" else arg
            for kind, arg in zip(kinds, args, strict=True)
        ]
        return made(*placed)

    return run


def sems(count):
    return pltpu.SemaphoreType.DMA((count,))


def row_at(i, size):
    return pl.ds(pl.multiple_of(i * size, size), size)


def tiled(width, tile, body):
    @pl.loop(0, width // tile)
    def _(i):
        body(row_at(i, tile))


def stack_blocks(blocks, whole):
    rows = blocks[0].shape[0]
    for i, block in enumerate(blocks):
        whole[i * rows : (i + 1) * rows, :] = block[...]


def row_of(spot, i, of_core, half=None):
    row = (2 * (spot[0] ^ i) + of_core) * SHARE
    if half is None:
        return pl.ds(pl.multiple_of(row, SHARE), SHARE)
    return pl.ds(pl.multiple_of(row + half * HALF, HALF), HALF)


def stack_columns(spot, mine, other, whole):
    core, side = spot[1], spot[2]
    for of_core, (own, near, far) in ((core, mine), (1 - core, other)):
        whole[row_of(spot, 0, of_core), :] = own[:SHARE, :]
        for i in range(1, CHIPS):
            rows = slice((i - 1) * HALF, i * HALF)
            whole[row_of(spot, i, of_core, side), :] = near[rows, :]
            whole[row_of(spot, i, of_core, 1 - side), :] = far[rows, :]


def by_core_copies(core, mine, other, whole, sem):
    size = mine.shape[0]
    return [
        pltpu.make_async_copy(mine, whole.at[row_at(core, size)], sem.at[0]),
        pltpu.make_async_copy(other, whole.at[row_at(1 - core, size)], sem.at[1]),
    ]


def start_all(copies):
    for copy in copies:
        copy.start()


def wait_all(copies):
    for copy in copies:
        copy.wait()


def chip_columns(weights, rows, chip):
    start = pl.multiple_of((chip * 5 // 2) * 128, 128)
    odd = lax.rem(chip, 2) == 1
    out = []
    for kind in range(3):
        window = weights[rows, pl.ds(kind * D + start, 384)]
        out.append(jnp.where(odd, window[:, 64 : 64 + D_CHIP], window[:, :D_CHIP]))
    return jnp.concatenate(out, axis=1)


def qkv_blocks_kernel(spot, lengths, padding, weights, *refs):
    vectors, own, sent = refs[:9], refs[9], refs[10 : 9 + CHIPS]
    held, marks, whole, vector_sems, sem = refs[9 + CHIPS : 18 + CHIPS], *refs[18 + CHIPS :]
    copies = [
        pltpu.make_async_copy(vector, here, vector_sems.at[i])
        for i, (vector, here) in enumerate(zip(vectors, held))
    ]
    copies.append(pltpu.make_async_copy(padding, marks, sem.at[0]))
    copies.append(pltpu.make_async_copy(weights, whole, sem.at[1]))
    start_all(copies)
    wait_all(copies)
    rows = padding.shape[-1]
    place = lax.broadcasted_iota(jnp.int32, (1, rows), 1)
    first = lengths[0, 0]
    member = (place >= first).astype(f32)
    leading = (place == 0) | (place == first)
    usable = jnp.where(leading | (marks[...].reshape(1, rows) > 0), 1.0, 0.0)
    code = 2.0 * member + usable
    width = 3 * D_CHIP
    lines = [v[...].astype(f32).reshape(1, -1) for v in held]
    extra = jnp.concatenate(
        [
            jnp.concatenate(lines[:6], axis=1),
            jnp.concatenate(lines[6:], axis=1),
            jnp.concatenate([code, jnp.zeros((1, width - rows), f32)], axis=1),
            jnp.zeros((EXTRA - 3, width), f32),
        ],
        axis=0,
    ).astype(bf16)
    own[:SHARE, :] = chip_columns(whole, slice(None), spot[0])
    own[SHARE:, :] = extra
    for i, block in enumerate(sent):
        block[:HALF, :] = chip_columns(whole, row_at(spot[2], HALF), spot[0] ^ (i + 1))
        block[HALF:, :] = extra


def qkv_blocks(spot, lengths, padding, weights, vectors):
    half = ((HALF + EXTRA, 3 * D_CHIP), bf16)
    return call(
        qkv_blocks_kernel,
        "qkv_blocks",
        "ss" + "h" * 11,
        [((SHARE + EXTRA, 3 * D_CHIP), bf16)] + [half] * (CHIPS - 1),
        [pltpu.VMEM(v.shape, v.dtype) for v in vectors]
        + [
            pltpu.VMEM(padding.shape, padding.dtype),
            pltpu.VMEM(weights.shape, weights.dtype),
            sems(9),
            sems(2),
        ],
    )(spot, lengths, padding, weights, *vectors)


def qkv_join_kernel(own, q1, q2, q3, x1, x2, near, near_half, first, second):
    size = first.shape[0]
    first[...] = x1[:size, :]
    second[...] = x2[size:, :]
    near[:SHARE, :] = own[:SHARE, :]
    low = SHARE + 3 * HALF
    near[low : low + EXTRA, :] = own[SHARE:, :]
    for i, block in enumerate((q1, q2, q3)):
        near[SHARE + i * HALF : SHARE + (i + 1) * HALF, :] = block[:HALF, :]
        near_half[i * HALF : (i + 1) * HALF, :] = block[:HALF, :]
        low += EXTRA
        near[low : low + EXTRA, :] = block[HALF:, :]


def qkv_join(blocks, x1, x2):
    width = blocks[0].shape[-1]
    half = ((x1.shape[0] // 2, x1.shape[1]), x1.dtype)
    return call(
        qkv_join_kernel,
        "qkv_join",
        "v" * 6,
        [
            ((SHARE + 3 * HALF + CHIPS * EXTRA, width), bf16),
            ((3 * HALF, width), bf16),
            half,
            half,
        ],
    )(*blocks, x1, x2)


def up_blocks_kernel(spot, weights, cotangent, own, *sent):
    def columns(chip):
        return pl.ds(pl.multiple_of(chip * FF_CHIP, FF_CHIP), FF_CHIP)

    own[...] = weights[:, columns(spot[0])]
    for i, block in enumerate(sent):
        block[:HALF, :] = weights[row_at(spot[2], HALF), columns(spot[0] ^ (i + 1))]
    for block in sent[:2]:
        block[HALF:, :] = cotangent[...]


def up_blocks(spot, weights, cotangent):
    both = HALF + cotangent.shape[0]
    sizes = (SHARE, both, both, HALF)
    return call(up_blocks_kernel, "up_blocks", "svv", [((size, FF_CHIP), bf16) for size in sizes])(
        spot, weights, cotangent
    )


def up_join_kernel(cotangent, u1, u2, u3, near, whole, first, second):
    rows = cotangent.shape[0]
    for i, block in enumerate((cotangent, u1.at[HALF:], u2.at[HALF:])):
        whole[i * rows : (i + 1) * rows, :] = block[...]
    for i, block in enumerate((u1, u2, u3)):
        near[i * HALF : (i + 1) * HALF, :] = block[:HALF, :]
    half = rows // 2
    first[...] = u1[HALF : HALF + half, :]
    second[...] = u2[HALF + half :, :]


def up_join(cotangent, blocks):
    rows = cotangent.shape[0]
    near = ((3 * HALF, FF_CHIP), bf16)
    passed = ((rows // 2, D), bf16)
    return call(
        up_join_kernel,
        "up_join",
        "vvvv",
        [near, (((CHIPS - 1) * rows, D), bf16), passed, passed],
    )(cotangent, *blocks)


def halves_kernel(whole, first, second):
    size = first.shape[0]
    first[...] = whole[:size, :]
    second[...] = whole[size:, :]


def halves(whole):
    shape = (whole.shape[0] // 2, whole.shape[1])
    return call(halves_kernel, "halves", "v", [(shape, whole.dtype)] * 2)(whole)


def join_kernel(*refs):
    stack_blocks(refs[:-1], refs[-1])


def join(blocks):
    rows, width = blocks[0].shape
    count = len(blocks)
    return call(join_kernel, "join", "v" * count, [((count * rows, width), blocks[0].dtype)])(
        *blocks
    )[0]


def fill_table(spot, extras, table, mask):
    chip, core = spot[0], spot[1]
    rows = mask.shape[1]
    table[...] = jnp.zeros_like(table)
    for team in range(TEAM):
        for i in range(6):
            table[i : i + 1, team * SHARE : (team + 1) * SHARE] = extras[
                team, 0:1, i * SHARE : (i + 1) * SHARE
            ]
    for half in range(2):
        line = extras[2 * chip + half, 1:2, :]
        lo = half * SHARE
        table[BIAS_QKV : BIAS_QKV + 1, lo : lo + SHARE] = line[:, :SHARE]
        table[BIAS_QKV : BIAS_QKV + 1, 2 * D_CHIP + lo : 2 * D_CHIP + lo + SHARE] = line[
            :, SHARE : 2 * SHARE
        ]
        table[BIAS_UP : BIAS_UP + 1, half * FF_SHARE : (half + 1) * FF_SHARE] = line[:, 2 * SHARE :]
    for i in range(CHIPS):
        code = extras[2 * (chip ^ i) + core, 2:3, :rows]
        of_key = jnp.broadcast_to(code, (rows, rows))
        cell_of_key = jnp.floor(of_key * 0.5)
        open_key = of_key - 2.0 * cell_of_key
        keep = jnp.where(cell_of_key == cell_of_key.T, open_key, 0.0)
        mask[i * rows : (i + 1) * rows, :] = keep.astype(bf16)


def token_norm_kernel(*refs):
    blocks, normed = refs[:-1], refs[-1]
    at = 0
    for x in blocks:
        rows = x.shape[0]
        normed[at : at + rows, :] = normalize(x[...].astype(f32))[0]
        at += rows


def token_norm(blocks):
    rows, width = blocks[0].shape
    shape = (CHIPS * rows, width)
    return call(token_norm_kernel, "token_norm", "v" * len(blocks), [(shape, f32)])(*blocks)[0]


def enter_kernel(spot, normed, *refs):
    mine, other, refs = refs[:2], refs[2:4], refs[4:]
    out_mine, out_other, refs = *refs[:2], refs[2:]
    table, mask, qkv, out, first_low, projected, context = refs[:7]
    partials = refs[7 : 8 + CHIPS]
    extras, out_sems = refs[8 + CHIPS :]
    rows = mask.shape[1]
    out_copies = by_core_copies(spot[1], out_mine, out_other, out, out_sems)
    start_all(out_copies)
    low = SHARE + 3 * HALF
    for of_core, lines in ((spot[1], mine[0]), (1 - spot[1], other[0])):
        for i in range(CHIPS):
            at = slice(low + i * EXTRA, low + (i + 1) * EXTRA)
            extras[2 * (spot[0] ^ i) + of_core] = lines[at, :].astype(f32)
    fill_table(spot, extras, table, mask)
    columns = [(near, near.at[SHARE:], far) for near, far in (mine, other)]
    stack_columns(spot, *columns, qkv)
    gain = table[GAIN1 : GAIN1 + 1, :]
    bias = table[BIAS1 : BIAS1 + 1, :]
    first_low[...] = (normed[...] * gain + bias).astype(bf16)
    for lo, hi in ((0, 384), (384, 768), (768, 960)):
        shift = table[BIAS_QKV : BIAS_QKV + 1, lo:hi]
        projected[:, lo:hi] = (mm(first_low[...], qkv[:, lo:hi]) + shift).astype(bf16)

    @pl.loop(0, CHIPS)
    def _(i):
        at = row_at(i, rows)
        context[at, :] = attend(projected[at, :], mask[at, :])

    wait_all(out_copies)

    def partial(at):
        whole = mm(context[...], out[:, at]).astype(bf16)
        lo = 0
        for part in partials:
            part[:, at] = whole[lo : lo + part.shape[0]]
            lo += part.shape[0]

    tiled(D, 256, partial)


def enter(spot, normed, mine, other, out_mine, out_other):
    total = normed.shape[0]
    rows = total // CHIPS
    outs = call(
        enter_kernel,
        "enter",
        "sv" + "v" * 4 + "hv",
        [
            ((TABLE_ROWS, D), f32),
            ((total, rows), bf16),
            ((D, 3 * D_CHIP), bf16),
            ((D_CHIP, D), bf16),
            ((total, D), bf16),
            ((total, 3 * D_CHIP), bf16),
            ((total, D_CHIP), bf16),
        ]
        + [((rows, D), bf16)] * (CHIPS - 1)
        + [((rows // 2, D), bf16)] * 2,
        [pltpu.VMEM((TEAM, EXTRA, 3 * D_CHIP), f32), sems(2)],
    )(spot, normed, *mine, *other, out_mine, out_other)
    return outs[:7], outs[7:]


def leave_kernel(
    b0, b1, b2, b3, qkv, out, projected, mask, branch, grad_projected, bias_sum, *refs
):
    partials, grad_context = refs[:CHIPS], refs[CHIPS]
    rows = b0.shape[0]
    stack_blocks((b0, b1, b2, b3), branch)
    grad_context[...] = mm_t(branch[...], out[...]).astype(bf16)
    bias_sum[...] = jnp.zeros_like(bias_sum)

    @pl.loop(0, CHIPS)
    def _(i):
        at = row_at(i, rows)
        grad = attend_back(projected[at, :], mask[at, :], grad_context[at, :])
        grad_projected[at, :] = grad
        bias_sum[...] += jnp.sum(grad.astype(f32), axis=0, keepdims=True)

    def partial(at):
        whole = mm_t(grad_projected[...], qkv[at, :]).astype(bf16)
        for i, part in enumerate(partials):
            part[:, at] = whole[i * rows : (i + 1) * rows]

    tiled(D, 256, partial)


def leave(blocks, qkv, out, projected, mask):
    rows = blocks[0].shape[0]
    total = CHIPS * rows
    outs = call(
        leave_kernel,
        "leave",
        "v" * 8,
        [((total, D), bf16), ((total, 3 * D_CHIP), bf16), ((1, 3 * D_CHIP), f32)]
        + [((rows, D), bf16)] * CHIPS,
        [pltpu.VMEM((total, D_CHIP), bf16)],
    )(*blocks, qkv, out, projected, mask)
    return outs[:3], outs[3:]


def total_of(parts):
    total = parts[0][...].astype(f32)
    for part in parts[1:]:
        total = total + part[...].astype(f32)
    return total


def pass_on_kernel(p1, p2, h1, h2, sum1, sum2):
    size = h1.shape[0]
    sum1[:size, :] = (p1[:size, :].astype(f32) + h1[...].astype(f32)).astype(bf16)
    sum1[size:, :] = p1[size:, :]
    sum2[:size, :] = p2[:size, :]
    sum2[size:, :] = (p2[size:, :].astype(f32) + h2[...].astype(f32)).astype(bf16)


def pass_on(p1, p2, h1, h2):
    return call(pass_on_kernel, "pass_on", "vvvv", [(p1.shape, bf16)] * 2)(p1, p2, h1, h2)


def mix_kernel(p0, p1, p2, tokens, table, mixed, second):
    total = total_of((p0, p1, p2)) + tokens[...].astype(f32)
    total = total + table[BIAS_OUT : BIAS_OUT + 1, :]
    mixed[...] = total
    normed, _ = normalize(total)
    second[...] = (normed * table[GAIN2 : GAIN2 + 1, :] + table[BIAS2 : BIAS2 + 1, :]).astype(bf16)


def mix(parts, tokens, table):
    shape = tokens.shape
    return call(mix_kernel, "mix", "v" * 5, [(shape, f32), (shape, bf16)])(*parts, tokens, table)


def unmix_kernel(p0, p1, p2, p3, mixed, table, cotangent, grad_mixed, branch, sums):
    grad = total_of((p0, p1, p2, p3))
    normed, inverse = normalize(mixed[...])
    grad_in, gain_sum, bias_sum = norm_backward(grad, normed, inverse, table[GAIN2 : GAIN2 + 1, :])
    grad_out = cotangent[...].astype(f32)
    grad_in = grad_in + grad_out
    grad_mixed[...] = grad_in
    low = grad_in.astype(bf16)
    branch[...] = low
    sums[...] = jnp.zeros_like(sums)
    sums[0:1, :] = jnp.sum(low.astype(f32), axis=0, keepdims=True)
    sums[1:2, :] = gain_sum
    sums[2:3, :] = bias_sum
    sums[3:4, :] = jnp.sum(grad_out, axis=0, keepdims=True)


def unmix(parts, mixed, table, cotangent):
    shape = cotangent.shape
    return call(
        unmix_kernel, "unmix", "v" * 7, [(shape, f32), (shape, bf16), ((8, D), f32)]
    )(*parts, mixed, table, cotangent)


def act_grad_kernel(spot, part, g1, g2, mine, other, grad_act, down, whole, down_sems):
    copies = by_core_copies(spot[1], mine, other, down, down_sems)
    start_all(copies)
    at = 0
    for block in (part, g1, g2):
        whole[at : at + block.shape[0], :] = block[...]
        at += block.shape[0]
    wait_all(copies)

    def columns(at):
        grad_act[:, at] = mm_t(whole[...], down[at, :])

    tiled(FF_CHIP, 256, columns)


def act_grad(spot, part, passed, down_mine, down_other):
    total = part.shape[0] // (CHIPS - 1) * CHIPS
    return call(
        act_grad_kernel,
        "act_grad",
        "svvvhv",
        [((total, FF_CHIP), f32), ((FF_CHIP, D), bf16), ((total, D), bf16)],
        [sems(2)],
    )(spot, part, *passed, down_mine, down_other)


def hidden_rows(at, second, up, table, grad_act, pre_act, act, grad_pre, bias_sum):
    size = at.stop - at.start

    def columns(tile):
        pre_act[at, tile] = mm(second[at, :], up[:, tile]) + table[BIAS_UP : BIAS_UP + 1, tile]

    tiled(FF_CHIP, 256, columns)

    @pl.loop(0, size // 64)
    def _(i):
        rows = pl.ds(pl.multiple_of(at.start + i * 64, 64), 64)
        pre = pre_act[rows, :]
        below = 0.5 * (1.0 + lax.erf(pre * (0.5**0.5)))
        bell = jnp.exp(-0.5 * pre * pre) * 0.3989422804014327
        act[rows, :] = (pre * below).astype(bf16)
        grad = (grad_act[rows, :] * (below + pre * bell)).astype(bf16)
        grad_pre[rows, :] = grad
        bias_sum[...] += jnp.sum(grad.astype(f32), axis=0, keepdims=True)


def hidden_first_kernel(spot, s0, s1, s2, grad_act, table, *refs):
    columns = [(own, rest, rest.at[3 * HALF :]) for own, rest in (refs[:2], refs[2:4])]
    second, act, grad_pre, bias_sum, up = refs[4:9]
    partials, pre_act = refs[9:12], refs[12]
    rows = s0.shape[0]
    stack_columns(spot, *columns, up)
    stack_blocks((s0, s1, s2), second)
    bias_sum[...] = jnp.zeros_like(bias_sum)
    hidden_rows(
        slice(0, 3 * rows), second, up, table, grad_act, pre_act, act, grad_pre, bias_sum
    )
    second_partials(slice(0, 3 * rows), grad_pre, up, partials)


def second_partials(at, grad_pre, up, partials):
    rows = partials[0].shape[0]

    def columns(tile):
        whole = mm_t(grad_pre[at, :], up[tile, :]).astype(bf16)
        for i, part in enumerate(partials):
            part[:, tile] = whole[i * rows : (i + 1) * rows]

    tiled(D, 256, columns)


def hidden_first(spot, blocks, grad_act, table, mine, other):
    total = grad_act.shape[0]
    return call(
        hidden_first_kernel,
        "hidden_first",
        "svvvvv" + "v" * 4,
        [
            ((total, D), bf16),
            ((total, FF_CHIP), bf16),
            ((total, FF_CHIP), bf16),
            ((1, FF_CHIP), f32),
            ((D, FF_CHIP), bf16),
        ]
        + [((total // CHIPS, D), bf16)] * 3,
        [pltpu.VMEM((total, FF_CHIP), f32)],
    )(spot, *blocks, grad_act, table, *mine, *other)


def hidden_last_kernel(
    spot,
    s3,
    grad_act,
    table,
    cotangent,
    up,
    second_in,
    act_in,
    grad_pre_in,
    bias_in,
    second,
    act,
    grad_pre,
    bias_sum,
    down_sent,
    pre_act,
):
    del second_in, act_in, grad_pre_in
    rows = s3.shape[0]
    at = slice(3 * rows, 4 * rows)
    second[at, :] = s3[...]
    bias_sum[...] = bias_in[...]
    hidden_rows(at, second, up, table, grad_act, pre_act, act, grad_pre, bias_sum)
    down_product(act, cotangent, 1 - spot[1], 0, down_sent)


def down_product(act, cotangent, of_core, half, target):
    low = half * ROWS_Z
    aligned = low // 128 * 128
    if half == 0:
        units = pl.ds(pl.multiple_of(of_core * FF_SHARE, 128), ROWS_Z)
        target[...] = t_mm(act[:, units], cotangent[...]).astype(target.dtype)
    else:
        units = pl.ds(pl.multiple_of(of_core * FF_SHARE + aligned, 128), FF_SHARE - aligned)
        window = act[:, units][:, low - aligned :]
        target[...] = t_mm(window, cotangent[...]).astype(target.dtype)


def up_product(second, grad_pre, pair, of_core, target, work):
    for i in range(2):
        first = (2 * (2 * pair + i) + of_core) * SHARE
        aligned = pl.multiple_of(first // 128 * 128, 128)
        work[...] = t_mm(second[:, pl.ds(aligned, 256)], grad_pre[...])
        start = pl.multiple_of(lax.rem(first, 128), 32)
        target[i * SHARE : (i + 1) * SHARE, :] = work[pl.ds(start, SHARE), :].astype(target.dtype)


def hidden_last(spot, block, grad_act, table, cotangent, up, second, act, grad_pre, bias_sum):
    total = second.shape[0]
    return pl.pallas_call(
        hidden_last_kernel,
        in_specs=[SMEM] + [VMEM] * 9,
        out_specs=[VMEM] * 5,
        out_shape=[
            jax.ShapeDtypeStruct(second.shape, bf16),
            jax.ShapeDtypeStruct(act.shape, bf16),
            jax.ShapeDtypeStruct(grad_pre.shape, bf16),
            jax.ShapeDtypeStruct(bias_sum.shape, f32),
            jax.ShapeDtypeStruct((ROWS_Z, D), bf16),
        ],
        scratch_shapes=[pltpu.VMEM((total, FF_CHIP), f32)],
        input_output_aliases={6: 0, 7: 1, 8: 2},
        compiler_params=pltpu.CompilerParams(vmem_limit_bytes=16 * 2**20),
        cost_estimate=COST,
        name="hidden_last",
    )(spot, block, grad_act, table, cotangent, up, second, act, grad_pre, bias_sum)


def second_last_kernel(grad_pre, up, partial):
    rows = partial.shape[0]
    second_partials(slice(grad_pre.shape[0] - rows, grad_pre.shape[0]), grad_pre, up, (partial,))


def second_last(grad_pre, up):
    rows = grad_pre.shape[0] // CHIPS
    return call(second_last_kernel, "second_last", "vv", [((rows, D), bf16)])(grad_pre, up)[0]


def up_sent_kernel(spot, grad_pre, second, up_sent, work):
    up_product(second, grad_pre, 0, 1 - spot[1], up_sent, work)


def up_sent_of(spot, grad_pre, second):
    return call(
        up_sent_kernel,
        "up_sent",
        "svv",
        [((ROWS_Z, FF_CHIP), bf16)],
        [pltpu.VMEM((256, FF_CHIP), f32)],
    )(spot, grad_pre, second)[0]


def split_rows(core, whole, sent, kept):
    for k in range(CHIPS):
        targets = ((sent[k // 2], k % 2, 1 - core), (kept, k, core))
        for target, at, of_core in targets:
            start = pl.multiple_of((2 * k + of_core) * SHARE, SHARE)
            target[at] = whole[pl.ds(start, SHARE), :].astype(bf16)


def down_grad_kernel(spot, act, cotangent, got, total):
    down_product(act, cotangent, spot[1], 0, total)
    total[...] = (total[...].astype(f32) + got[...].astype(f32)).astype(bf16)


def down_grad_of(spot, act, cotangent, got):
    return call(down_grad_kernel, "down_grad", "svvv", [((ROWS_Z, D), bf16)])(
        spot, act, cotangent, got
    )[0]


def rest_kernel(
    spot, second, grad_pre, act, cotangent, up_a, up_b, up_sent, down_b, down_sent, work
):
    core = spot[1]
    up_product(second, grad_pre, 0, core, up_a, work)
    up_product(second, grad_pre, 1, 1 - core, up_sent, work)
    up_product(second, grad_pre, 1, core, up_b, work)
    down_product(act, cotangent, 1 - core, 1, down_sent)
    down_product(act, cotangent, core, 1, down_b)


def rest_of_grads(spot, second, grad_pre, act, cotangent):
    return call(
        rest_kernel,
        "rest",
        "svvvv",
        [((ROWS_Z, D), bf16)] * 5,
        [pltpu.VMEM((256, FF_CHIP), f32)],
    )(spot, second, grad_pre, act, cotangent)


def result_kernel(act, down, *partials):
    rows = partials[0].shape[0]

    def columns(at):
        whole = mm(act[...], down[:, at]).astype(bf16)
        for i, part in enumerate(partials):
            part[:, at] = whole[i * rows : (i + 1) * rows]

    tiled(D, 256, columns)


def result_of(act, down):
    rows = act.shape[0] // CHIPS
    return call(result_kernel, "result", "vv", [((rows, D), bf16)] * CHIPS)(act, down)


def qkv_grad_kernel(
    spot,
    first_low,
    grad_projected,
    context,
    branch,
    sent_a,
    sent_b,
    kept,
    out_sent,
    out_kept,
    whole,
    out,
):
    core = spot[1]

    def columns(at):
        whole[at, :] = t_mm(first_low[:, at], grad_projected[...])

    tiled(D, 256, columns)
    split_rows(core, whole, (sent_a, sent_b), kept)
    out[...] = t_mm(context[...], branch[...])
    for target, of_core in ((out_sent, 1 - core), (out_kept, core)):
        target[...] = out[row_at(of_core, SHARE), :].astype(bf16)


def qkv_grad_of(spot, first_low, grad_projected, context, branch):
    half = ((CHIPS // 2, SHARE, 3 * D_CHIP), bf16)
    rows = ((SHARE, D), bf16)
    return call(
        qkv_grad_kernel,
        "qkv_grad",
        "svvvv",
        [half, half, ((CHIPS, SHARE, 3 * D_CHIP), bf16), rows, rows],
        [pltpu.VMEM((D, 3 * D_CHIP), f32), pltpu.VMEM((D_CHIP, D), f32)],
    )(spot, first_low, grad_projected, context, branch)


def add_kernel(*refs):
    count = len(refs) // 3
    for a, b, c in zip(refs[:count], refs[count : 2 * count], refs[2 * count :]):
        c[...] = (a[...].astype(f32) + b[...].astype(f32)).astype(c.dtype)


def add_all(left, right):
    shapes = [(a.shape, a.dtype) for a in left]
    return call(add_kernel, "add", "v" * (2 * len(left)), shapes)(*left, *right)


PACKED = SHARE * 3 // 4
STEP = SHARE // 4


def sum_all_kernel(a, b, c, d, total):
    total[...] = (a[...] + b[...]) + (c[...] + d[...])


def sum_all(parts):
    shape = (parts[0].shape, parts[0].dtype)
    return call(sum_all_kernel, "sum_all", "vvvv", [shape])(*parts)[0]


def pack_kernel(kept, got_a, got_b, out_kept, out_got, *chunks):
    for i, chunk in enumerate(chunks):
        for j in range(2):
            got = got_b if i else got_a
            total = (kept[2 * i + j].astype(f32) + got[j].astype(f32)).astype(bf16)
            lo = j * PACKED
            chunk[lo : lo + PACKED, : 3 * D_CHIP] = total[:PACKED]
            for part in range(3):
                at = lo + part * STEP
                chunk[at : at + STEP, 3 * D_CHIP :] = total[
                    PACKED:, part * D_CHIP : (part + 1) * D_CHIP
                ]
        rows = slice(i * HALF, (i + 1) * HALF)
        total = out_kept[rows, :].astype(f32) + out_got[rows, :].astype(f32)
        chunk[2 * PACKED :, :] = total.astype(bf16)


def pack(kept, got_a, got_b, out_kept, out_got):
    return call(pack_kernel, "pack", "vvvvv", [((ROWS_Z, D), bf16)] * 2)(
        kept, got_a, got_b, out_kept, out_got
    )


def unpacked(chunk, j):
    lo = j * PACKED
    tail = [
        chunk[lo + part * STEP : lo + (part + 1) * STEP, 3 * D_CHIP :] for part in range(3)
    ]
    return jnp.concatenate(
        [chunk[lo : lo + PACKED, : 3 * D_CHIP], jnp.concatenate(tail, axis=1)], axis=0
    )


def z_half(low, got_side):
    return add_all([low], [got_side])[0]


def z_send_kernel(spot, half, got_middle, low, sent):
    middle = spot[3] > 0

    @pl.when(middle)
    def _():
        whole = half[...].astype(f32) + got_middle[...].astype(f32)
        sent[...] = whole.astype(bf16)

    @pl.when(jnp.logical_not(middle))
    def _():
        sent[...] = low[...]


def z_send(spot, half, got_middle, low):
    return call(z_send_kernel, "z_send", "svvv", [(low.shape, bf16)])(spot, half, got_middle, low)[0]


def z_final_kernel(spot, sent, got_side, final):
    final[...] = jnp.where(spot[3] > 0, sent[...], got_side[...])


def z_final(spot, sent, got_side):
    return call(z_final_kernel, "z_final", "svv", [(sent.shape, bf16)])(spot, sent, got_side)[0]


def first_down_kernel(spot, sent, got, down, here, sem):
    here[...] = jnp.where(spot[3] > 0, sent[...], got[...]).astype(f32)
    copy = pltpu.make_async_copy(here, down.at[:ROWS_Z], sem.at[0])
    copy.start()
    copy.wait()


def first_down(spot, sent, got):
    return pl.pallas_call(
        first_down_kernel,
        in_specs=[SMEM, VMEM, VMEM],
        out_specs=HBM,
        out_shape=pltpu.HBM((2 * ROWS_Z, D), f32),
        scratch_shapes=[pltpu.VMEM((ROWS_Z, D), f32), sems(1)],
        compiler_params=pltpu.CompilerParams(vmem_limit_bytes=16 * 2**20),
        cost_estimate=COST,
        name="first_down",
    )(spot, sent, got)


def second_down_kernel(spot, sent, got, before, down, here, sem):
    del before
    here[...] = jnp.where(spot[3] > 0, sent[...], got[...]).astype(f32)
    copy = pltpu.make_async_copy(here, down.at[ROWS_Z:], sem.at[0])
    copy.start()
    copy.wait()


def second_down(spot, sent, got, down):
    return pl.pallas_call(
        second_down_kernel,
        in_specs=[SMEM, VMEM, VMEM, HBM],
        out_specs=HBM,
        out_shape=pltpu.HBM((2 * ROWS_Z, D), f32),
        scratch_shapes=[pltpu.VMEM((ROWS_Z, D), f32), sems(1)],
        input_output_aliases={3: 0},
        compiler_params=pltpu.CompilerParams(vmem_limit_bytes=16 * 2**20),
        cost_estimate=COST,
        name="second_down",
    )(spot, sent, got, pltpu.with_memory_space_constraint(down, pltpu.HBM))


def qkv_rows_kernel(spot, b0, b1, b2, b3, qkv, rows, stack, sem):
    for i, block in enumerate((b0, b1, b2, b3)):
        stack[spot[0] ^ i] = block[...]
    copies = []
    for kind in range(3):
        for chip in range(CHIPS):
            lo = kind * D + chip * D_CHIP
            rows[:, lo : lo + D_CHIP] = stack[
                chip, :, kind * D_CHIP : (kind + 1) * D_CHIP
            ].astype(f32)
        at = slice(kind * D, (kind + 1) * D)
        copies.append(pltpu.make_async_copy(rows.at[:, at], qkv.at[:, at], sem.at[kind]))
        copies[-1].start()
    wait_all(copies)


def qkv_rows(spot, blocks):
    shape = blocks[0].shape
    return pl.pallas_call(
        qkv_rows_kernel,
        in_specs=[SMEM] + [VMEM] * 4,
        out_specs=HBM,
        out_shape=pltpu.HBM((shape[0], 3 * D), f32),
        scratch_shapes=[
            pltpu.VMEM((shape[0], 3 * D), f32),
            pltpu.VMEM((CHIPS,) + shape, bf16),
            sems(3),
        ],
        compiler_params=pltpu.CompilerParams(vmem_limit_bytes=16 * 2**20),
        cost_estimate=COST,
        name="qkv_rows",
    )(spot, *blocks)


def owned_kernel(count, place, sums, got, *outs):
    total = sums[...] + got[...]
    index = place[0]
    size = outs[0].shape[0]
    mine = pltpu.roll(total, D - index * size, 1)
    for i, row in enumerate((0, 1, 2, 3, 4, 5, 8, 9)):
        outs[i][...] = mine[row : row + 1, :size].reshape(size)
    wide = outs[8].shape[0]
    first = index * wide
    row = first // D
    line = total[10:11, :]
    for k in range(1, CHIPS):
        line = jnp.where(row == k, total[10 + k : 11 + k, :], line)
    line = pltpu.roll(jnp.broadcast_to(line, (8, D)), D - lax.rem(first, D), 1)
    outs[8][...] = line[0:1, :wide].reshape(wide)
    mean = total[6:7, :] / count
    outs[9][...] = mean.reshape(D)
    outs[10][...] = (total[7:8, :] / count - mean * mean).reshape(D)


def owned(place, count, fsdp_count, sums, got):
    sizes = [D // fsdp_count] * 8 + [FF // fsdp_count, D, D]

    def kernel(*refs):
        owned_kernel(count, *refs)

    return call(kernel, "owned", "svv", [((size,), f32) for size in sizes])(place, sums, got)


def up_exchange_kernel(spot, a, b, *blocks):
    chunks = (a, b)
    for i, block in enumerate(blocks):
        chip = spot[0] ^ i
        at = row_at(lax.rem(chip, 2), SHARE)
        block[...] = jnp.where(chip >= 2, chunks[1][at, :], chunks[0][at, :])


def up_exchange(spot, a, b):
    return call(up_exchange_kernel, "up_exchange", "svv", [((SHARE, FF_CHIP), bf16)] * CHIPS)(
        spot, a, b
    )


def qkv_unpack_kernel(spot, sent, got_side, blocks, out_rows):
    chunk = jnp.where(spot[3] > 0, sent[...], got_side[...])
    for j in range(2):
        blocks[j] = unpacked(chunk, j)
    out_rows[...] = chunk[2 * PACKED :, :].astype(f32)


def qkv_unpack(spot, sent, got_side):
    return call(
        qkv_unpack_kernel,
        "qkv_unpack",
        "svv",
        [((2, SHARE, 3 * D_CHIP), bf16), ((HALF, D), f32)],
    )(spot, sent, got_side)


def qkv_exchange_kernel(spot, blocks_a, rows_a, sent, got_side, *refs):
    blocks, out_rows, stack = refs[:CHIPS], refs[CHIPS], refs[CHIPS + 1]
    chunk = jnp.where(spot[3] > 0, sent[...], got_side[...])
    stack[:2] = blocks_a[...]
    for j in range(2):
        stack[2 + j] = unpacked(chunk, j)
    out_rows[:HALF, :] = rows_a[...]
    out_rows[HALF:, :] = chunk[2 * PACKED :, :].astype(f32)
    for i, block in enumerate(blocks):
        block[...] = stack[spot[0] ^ i]


def qkv_exchange(spot, blocks_a, rows_a, sent, got_side):
    shape = (SHARE, 3 * D_CHIP)
    outs = call(
        qkv_exchange_kernel,
        "qkv_exchange",
        "svvvv",
        [(shape, bf16)] * CHIPS + [((SHARE, D), f32)],
        [pltpu.VMEM((CHIPS,) + shape, bf16)],
    )(spot, blocks_a, rows_a, sent, got_side)
    return outs[:CHIPS], outs[CHIPS]


def up_rows_kernel(spot, b0, b1, b2, b3, weights):
    for i, block in enumerate((b0, b1, b2, b3)):
        start = pl.multiple_of((spot[0] ^ i) * FF_CHIP, FF_CHIP)
        weights[:, pl.ds(start, FF_CHIP)] = block[...].astype(f32)


def up_rows(spot, blocks):
    return call(up_rows_kernel, "up_rows", "svvvv", [((SHARE, FF), f32)])(spot, *blocks)[0]


def end_kernel(
    spot,
    lengths,
    p0,
    p1,
    p2,
    p3,
    r0,
    r1,
    r2,
    r3,
    grad_mixed,
    tokens,
    table,
    mixed,
    mix_sums,
    qkv_sum,
    up_sum,
    layer_out,
    grad_tokens,
    sums,
):
    grad = total_of((p0, p1, p2, p3))
    normed, inverse = normalize(tokens[...].astype(f32))
    grad_in, gain_sum, bias_sum = norm_backward(grad, normed, inverse, table[GAIN1 : GAIN1 + 1, :])
    grad_tokens[...] = grad_mixed[...] + grad_in
    result = mixed[...] + total_of((r0, r1, r2, r3)) + table[BIAS_DOWN : BIAS_DOWN + 1, :]
    layer_out[...] = result.astype(bf16)
    place = lax.broadcasted_iota(jnp.int32, (result.shape[0], 1), 0)
    picked = jnp.where((place == 0) | (place == lengths[0, 0]), result, 0.0)
    sums[...] = jnp.zeros_like(sums)
    sums[0:1, :] = gain_sum
    sums[1:2, :] = bias_sum
    sums[2:6, :] = mix_sums[0:4, :]
    sums[6:7, :] = jnp.sum(picked, axis=0, keepdims=True)
    sums[7:8, :] = jnp.sum(picked * picked, axis=0, keepdims=True)
    for k in range(CHIPS):
        here = spot[0] == k
        lo = k * D_CHIP
        sums[8:9, lo : lo + D_CHIP] = jnp.where(here, qkv_sum[:, :D_CHIP], 0.0)
        sums[9:10, lo : lo + D_CHIP] = jnp.where(here, qkv_sum[:, 2 * D_CHIP :], 0.0)
        sums[10 + k : 11 + k, :] = jnp.where(here, up_sum[...], 0.0)


def end(spot, lengths, parts, results, *rest):
    shape = parts[0].shape
    return call(
        end_kernel,
        "end",
        "ss" + "v" * 15,
        [(shape, bf16), (shape, f32), ((SUM_ROWS, D), f32)],
    )(spot, lengths, *parts, *results, *rest)


def fence(*values):
    return lax.optimization_barrier(values)


def local(
    tokens,
    lengths,
    padding,
    ln1_gain,
    ln1_bias,
    w_qkv,
    b_query,
    b_value,
    w_out,
    b_out,
    ln2_gain,
    ln2_bias,
    w_up,
    b_up,
    w_down,
    b_down,
    cotangent,
):
    fsdp_count = lax.axis_size("fsdp")
    dp_count = lax.axis_size("dp")
    groups = fsdp_count // TEAM
    place = lax.axis_index("fsdp") // groups
    chip = place // 2
    core = place % 2
    depth = lax.axis_index("dp")
    middle = (depth == 1) | (depth == 2)
    spot = jnp.stack([chip, core, depth % 2, middle.astype(jnp.int32)]).astype(jnp.int32)

    def swap(value, mask):
        pairs = [
            (team * groups + group, (team ^ mask) * groups + group)
            for team in range(TEAM)
            for group in range(groups)
        ]
        return lax.ppermute(value, "fsdp", pairs)

    shard_groups = [[team * groups + group for group in range(groups)] for team in range(TEAM)]
    def gather_shards(value):
        if groups == 1:
            return value
        return lax.all_gather(value, "fsdp", axis=0, tiled=True, axis_index_groups=shard_groups)

    def scatter_shards(value):
        if groups == 1:
            return value
        return lax.psum_scatter(
            value, "fsdp", scatter_dimension=0, tiled=True, axis_index_groups=shard_groups
        )

    def along_z(pairs, value):
        return lax.ppermute(value, "dp", pairs)

    def z_swap(value):
        return along_z([(0, 1), (1, 0), (2, 3), (3, 2)], value)

    def z_middle(value):
        return along_z([(1, 2), (2, 1)], value)

    def from_chips(blocks):
        return [blocks[0]] + [swap(block, 2 * i) for i, block in enumerate(blocks) if i > 0]

    def fence_list(first, *others):
        done = fence(*first, *others)
        return list(done[: len(first)]), *done[len(first) :]

    w_qkv, w_out, w_up, w_down = (gather_shards(w) for w in (w_qkv, w_out, w_up, w_down))
    given = (ln1_gain, ln1_bias, b_out, ln2_gain, ln2_bias, b_down, b_query, b_value, b_up)
    qkv_sent = qkv_blocks(spot, lengths, padding, w_qkv, [gather_shards(v) for v in given])
    qkv_got = from_chips(qkv_sent)
    x1, x2, *qkv_got = fence(swap(tokens, 2), swap(tokens, 4), *qkv_got)
    qkv_near, qkv_half, x1_half, x2_half = qkv_join(qkv_got, x1, x2)
    qkv_far = z_swap(qkv_half)
    qkv_near_other = swap(qkv_near, 1)
    blocks = [tokens, x1, x2, swap(x1_half, 4), swap(x2_half, 2)]
    normed = token_norm(blocks)
    out_sent, _ = fence(w_out, qkv_near)
    out_other = swap(out_sent, 1)
    up_own, *up_sent = up_blocks(spot, w_up, cotangent)
    up_own, *up_sent = fence(up_own, *up_sent, qkv_near)[:-1]
    loads = [swap(block, 2 * i + 2) for i, block in enumerate(up_sent)]
    normed, qkv_far, qkv_near_other, out_other = fence(normed, qkv_far, qkv_near_other, out_other)
    qkv_far_other = join([swap(half, 1) for half in halves(qkv_far)])

    (table, mask, qkv, out, first_low, projected, context), partial_out = enter(
        spot,
        normed,
        [qkv_near, qkv_far],
        [qkv_near_other, qkv_far_other],
        w_out,
        out_other,
    )
    p0, p1, p2, h1, h2 = partial_out
    p1, p2 = pass_on(p1, p2, swap(h1, 4), swap(h2, 2))
    out_parts = [p0, swap(p1, 2), swap(p2, 4)]
    cotangent_late, _ = fence(cotangent, partial_out[0])
    up_near, part, first, second = up_join(cotangent_late, loads)
    up_far = z_swap(up_near)
    passed = [swap(first, 4), swap(second, 2)]
    passed, up_far, *out_parts = fence_list(passed, up_far, *out_parts)
    mixed, second_own = mix(out_parts, tokens, table)
    second_blocks = from_chips([second_own] * CHIPS)
    up_far, _ = fence(up_far, second_own)
    up_rest = join([up_near, up_far])
    up_own_sent, _ = fence(up_own, second_own)
    up_other = [swap(up_own_sent, 1), swap(up_rest, 1)]
    down_sent, _ = fence(w_down, second_own)
    down_other = swap(down_sent, 1)
    part, down_other = fence(part, down_other)
    grad_act, down, whole_cotangent = act_grad(spot, part, passed, w_down, down_other)

    second_low, act_low, grad_pre, up_bias_sum, up, *partial_second = hidden_first(
        spot,
        second_blocks[:3],
        grad_act,
        table,
        [up_own, up_rest],
        up_other,
    )
    block, up_bias_sum = fence(second_blocks[3], up_bias_sum)
    second_low, act_low, grad_pre, up_bias_sum, down_sent = hidden_last(
        spot, block, grad_act, table, whole_cotangent, up, second_low, act_low, grad_pre, up_bias_sum
    )
    down_got = swap(down_sent, 1)
    up_sent = up_sent_of(spot, grad_pre, second_low)
    up_got = swap(up_sent, 1)
    act_low, up_sent = fence(act_low, up_sent)
    down_a = down_grad_of(spot, act_low, whole_cotangent, down_got)
    side0 = z_swap(down_a)
    up_late, _ = fence(up, down_a)
    partial_second = partial_second + [second_last(grad_pre, up_late)]
    second_parts = from_chips(partial_second)
    second_low, _ = fence(second_low, partial_second[3])
    up_a, up_b, up_sent, down_b, down_sent = rest_of_grads(
        spot, second_low, grad_pre, act_low, whole_cotangent
    )
    up_got, up_sent = fence(up_got, up_sent)
    (up_a,) = add_all([up_a], [up_got])
    up_got = swap(up_sent, 1)

    second_parts, side0, up_a = fence_list(second_parts, side0, up_a)
    half0, send1 = z_half(down_a, side0), up_a
    send1, _ = fence(send1, half0)
    side1, middle1 = z_swap(send1), z_middle(half0)
    second_parts, half0 = fence_list(second_parts, half0)
    grad_mixed, branch_own, mix_sums = unmix(second_parts, mixed, table, cotangent)
    branch_blocks = from_chips([branch_own] * CHIPS)
    act_low, branch_own = fence(act_low, branch_own)
    partial_result = list(result_of(act_low, down))

    up_got, partial_result[0] = fence(up_got, partial_result[0])
    (up_b,) = add_all([up_b], [up_got])
    branch_blocks, side1, middle1, *partial_result, up_b = fence_list(
        branch_blocks, side1, middle1, *partial_result, up_b
    )
    half1 = z_half(up_a, side1)
    middle1, _ = fence(middle1, half1)
    send2 = z_send(spot, half0, middle1, up_b)
    side2, middle2 = z_swap(send2), z_middle(half1)
    branch_blocks, half1 = fence_list(branch_blocks, half1)
    (whole_branch, grad_projected, qkv_bias_sum), partial_first = leave(
        branch_blocks, qkv, out, projected, mask
    )
    first_low, grad_projected = fence(first_low, grad_projected)
    qkv_sent_a, qkv_sent_b, qkv_kept, out_sent, out_kept = qkv_grad_of(
        spot, first_low, grad_projected, context, whole_branch
    )
    qkv_a, qkv_b = pack(
        qkv_kept, swap(qkv_sent_a, 1), swap(qkv_sent_b, 1), out_kept, swap(out_sent, 1)
    )

    side2, middle2, qkv_a = fence(side2, middle2, qkv_a)
    half2 = z_half(up_b, side2)
    middle2, _ = fence(middle2, half2)
    send3 = z_send(spot, half1, middle2, qkv_a)
    side3, middle3 = z_swap(send3), z_middle(half2)
    down_sent, _ = fence(down_sent, send3)
    (down_b,) = add_all([down_b], [swap(down_sent, 1)])
    *partial_first, down_b = fence(*partial_first, down_b)
    first_parts = from_chips(partial_first)
    down_grad = first_down(spot, send2, side2)

    first_parts, side3, middle3 = fence_list(first_parts, side3, middle3)
    half3 = z_half(qkv_a, side3)
    middle3, _ = fence(middle3, half3)
    send4 = z_send(spot, half2, middle3, qkv_b)
    sent, _ = fence(send3, send4)
    up_a_final = z_final(spot, sent, side3)
    side4, middle4 = z_swap(send4), z_middle(half3)
    *partial_result, half3 = fence(*partial_result, half3)
    result_parts = from_chips(partial_result)

    result_parts, side4, middle4 = fence_list(result_parts, side4, middle4)
    half4 = z_half(qkv_b, side4)
    middle4, _ = fence(middle4, half4)
    send5 = z_send(spot, half3, middle4, down_b)
    sent, _ = fence(send4, send5)
    up_b_final = z_final(spot, sent, side4)
    side5, middle5 = z_swap(send5), z_middle(half4)
    result_parts, half4 = fence_list(result_parts, half4)
    layer_out, grad_tokens, sums = end(
        spot,
        lengths,
        first_parts,
        result_parts,
        grad_mixed,
        tokens,
        table,
        mixed,
        mix_sums,
        qkv_bias_sum,
        up_bias_sum,
    )
    (sums,) = add_all([sums], [swap(sums, 1)])
    sums = sum_all(from_chips([sums] * CHIPS))
    if groups > 1:
        sums = lax.psum(sums, "fsdp", axis_index_groups=shard_groups)
    sums_got = z_swap(sums)
    up_a_final, _ = fence(up_a_final, sums)
    up_ready = up_exchange(spot, up_a_final, up_b_final)

    side5, middle5, sums_got, _ = fence(side5, middle5, sums_got, up_ready[0])
    half5 = z_half(down_b, side5)
    middle5, _ = fence(middle5, half5)
    send6 = z_half(half4, middle5)
    sent, _ = fence(send5, send6)
    qkv_ready, rows_ready = qkv_unpack(spot, sent, side5)
    side6, middle6 = z_swap(send6), z_middle(half5)
    up_ready, _ = fence_list(up_ready, send6)
    up_total = from_chips(up_ready)
    (sums,) = add_all([sums], [sums_got])

    up_total, side6, middle6, sums, qkv_ready = fence_list(
        up_total, side6, middle6, sums, qkv_ready
    )
    middle6, _ = fence(middle6, side6)
    send7 = z_half(half5, middle6)
    side7 = along_z([(1, 0), (2, 3)], send7)
    sent, send7, sums = fence(send6, send7, sums)
    qkv_last, out_grad = qkv_exchange(spot, qkv_ready, rows_ready, sent, side6)
    qkv_total = from_chips(qkv_last)
    sums_got = along_z([(z, z ^ 2) for z in range(4)], sums)
    up_grad = up_rows(spot, up_total)
    place_in = jnp.stack([lax.axis_index("fsdp")]).astype(jnp.int32)
    vectors = list(owned(place_in, CELLS_DEV * dp_count * fsdp_count, fsdp_count, sums, sums_got))
    qkv_total, up_grad, vectors[0] = fence_list(qkv_total, up_grad, vectors[0])
    qkv_grad = qkv_rows(spot, qkv_total)
    side7, qkv_grad = fence(side7, qkv_grad)
    down_grad = second_down(spot, send7, side7, down_grad)

    return (
        layer_out,
        grad_tokens,
        vectors[0],
        vectors[1],
        scatter_shards(qkv_grad),
        vectors[6],
        vectors[7],
        scatter_shards(out_grad),
        vectors[2],
        vectors[3],
        vectors[4],
        scatter_shards(up_grad),
        vectors[8],
        scatter_shards(down_grad),
        vectors[5],
        vectors[9],
        vectors[10],
    )


def solution(mesh):
    tokens_spec = P(("dp", "fsdp"), None)
    vector = P("fsdp")
    matrix = P("fsdp", None)
    in_specs = (
        tokens_spec,
        P(("dp", "fsdp"), None),
        P(("dp", "fsdp")),
        vector,
        vector,
        matrix,
        vector,
        vector,
        matrix,
        vector,
        vector,
        vector,
        matrix,
        vector,
        matrix,
        vector,
        tokens_spec,
    )
    out_specs = (
        tokens_spec,
        tokens_spec,
        vector,
        vector,
        matrix,
        vector,
        vector,
        matrix,
        vector,
        vector,
        vector,
        matrix,
        vector,
        matrix,
        vector,
        P(),
        P(),
    )
    return jax.shard_map(local, mesh=mesh, in_specs=in_specs, out_specs=out_specs, check_vma=False)
```

```python
import jax
import jax.numpy as jnp
from jax import lax
from jax.experimental import pallas as pl
from jax.experimental.pallas import tpu as pltpu
from jax.sharding import PartitionSpec as P

D = 1280
HEADS = 20
HEAD_DIM = 64
FF = 5120
CELLS_DEV = 2
EPS = 1e-05

TEAM = 8
CHIPS = 4
HEADS_CHIP = HEADS // CHIPS
D_CHIP = D // CHIPS
FF_CHIP = FF // CHIPS
SHARE = D // TEAM
FF_SHARE = FF // TEAM
SCALE = HEAD_DIM ** (-0.5)

GAIN1, BIAS1, BIAS_OUT, GAIN2, BIAS2, BIAS_DOWN, BIAS_UP, BIAS_QKV = range(8)
TABLE_ROWS = 8
SUM_ROWS = 16

COST = pl.CostEstimate(flops=1, bytes_accessed=1, transcendentals=0)
SMEM = pl.BlockSpec(memory_space=pltpu.SMEM)
HBM = pl.BlockSpec(memory_space=pltpu.HBM)
VMEM = pl.BlockSpec(memory_space=pltpu.VMEM)

f32 = jnp.float32
bf16 = jnp.bfloat16


def dot(a, b, dims):
    return lax.dot_general(a, b, (dims, ((), ())), preferred_element_type=f32)


def mm(a, b):
    return dot(a, b, ((1,), (0,)))


def mm_t(a, b):
    return dot(a, b, ((1,), (1,)))


def t_mm(a, b):
    return dot(a, b, ((0,), (0,)))


def normalize(values):
    center = jnp.mean(values, axis=-1, keepdims=True)
    centred = values - center
    spread = jnp.mean(centred * centred, axis=-1, keepdims=True)
    inverse = lax.rsqrt(spread + EPS)
    return centred * inverse, inverse


def norm_backward(grad_out, normed, inverse, norm_gain):
    grad_normed = grad_out * norm_gain
    first_mean = jnp.mean(grad_normed, axis=-1, keepdims=True)
    second_mean = jnp.mean(grad_normed * normed, axis=-1, keepdims=True)
    grad_in = inverse * (grad_normed - first_mean - normed * second_mean)
    gain_sum = jnp.sum(grad_out * normed, axis=0, keepdims=True)
    return grad_in, gain_sum, jnp.sum(grad_out, axis=0, keepdims=True)


def heads_of(projected, offset):
    return [
        projected[:, offset + i * HEAD_DIM : offset + (i + 1) * HEAD_DIM] for i in range(HEADS_CHIP)
    ]


def softmax_rows(queries, keys, keep):
    raw = jnp.concatenate([mm_t(q, k) for q, k in zip(queries, keys)], axis=0)
    masked = jnp.where(keep, raw * SCALE, -1e30)
    grown = jnp.exp(masked - jnp.max(masked, axis=-1, keepdims=True))
    return grown * (1.0 / jnp.sum(grown, axis=-1, keepdims=True))


def keep_of(mask):
    return jnp.concatenate([mask.astype(f32)] * HEADS_CHIP, axis=0) > 0.5


def attend(projected, mask):
    rows = mask.shape[0]
    probs = softmax_rows(heads_of(projected, 0), heads_of(projected, D_CHIP), keep_of(mask))
    probs = probs.astype(bf16)
    out = [
        mm(probs[i * rows : (i + 1) * rows], value)
        for i, value in enumerate(heads_of(projected, 2 * D_CHIP))
    ]
    return jnp.concatenate(out, axis=1).astype(bf16)


def attend_back(projected, mask, grad_context):
    rows = mask.shape[0]
    queries, keys, values = (heads_of(projected, i * D_CHIP) for i in range(3))
    grads = heads_of(grad_context, 0)
    probs = softmax_rows(queries, keys, keep_of(mask))
    grad_probs = jnp.concatenate([mm_t(g, v) for g, v in zip(grads, values)], axis=0)
    along = jnp.sum(grad_probs * probs, axis=-1, keepdims=True)
    grad_scores = (probs * (grad_probs - along) * SCALE).astype(bf16)
    probs = probs.astype(bf16)

    def cut(stack, i):
        return stack[i * rows : (i + 1) * rows]

    out = (
        [mm(cut(grad_scores, i), keys[i]) for i in range(HEADS_CHIP)]
        + [t_mm(cut(grad_scores, i), queries[i]) for i in range(HEADS_CHIP)]
        + [t_mm(cut(probs, i), grads[i]) for i in range(HEADS_CHIP)]
    )
    return jnp.concatenate(out, axis=1).astype(bf16)


HALF = SHARE // 2
EXTRA = 8
ROWS_Z = 2 * SHARE


def call(kernel, name, kinds, out_shapes, scratch=(), vmem=16):
    specs = {"s": SMEM, "h": HBM, "v": VMEM}
    made = pl.pallas_call(
        kernel,
        in_specs=[specs[kind] for kind in kinds],
        out_specs=[VMEM] * len(out_shapes),
        out_shape=[jax.ShapeDtypeStruct(shape, kind) for shape, kind in out_shapes],
        scratch_shapes=list(scratch),
        compiler_params=pltpu.CompilerParams(vmem_limit_bytes=vmem * 2**20),
        cost_estimate=COST,
        name=name,
    )

    def run(*args):
        placed = [
            pltpu.with_memory_space_constraint(arg, pltpu.HBM) if kind == "h" else arg
            for kind, arg in zip(kinds, args, strict=True)
        ]
        return made(*placed)

    return run


def sems(count):
    return pltpu.SemaphoreType.DMA((count,))


def row_at(i, size):
    return pl.ds(pl.multiple_of(i * size, size), size)


def tiled(width, tile, body):
    @pl.loop(0, width // tile)
    def _(i):
        body(row_at(i, tile))


def stack_blocks(blocks, whole):
    rows = blocks[0].shape[0]
    for i, block in enumerate(blocks):
        whole[i * rows : (i + 1) * rows, :] = block[...]


def row_of(spot, i, of_core, half=None):
    row = (2 * (spot[0] ^ i) + of_core) * SHARE
    if half is None:
        return pl.ds(pl.multiple_of(row, SHARE), SHARE)
    return pl.ds(pl.multiple_of(row + half * HALF, HALF), HALF)


def stack_columns(spot, mine, other, whole):
    core, side = spot[1], spot[2]
    for of_core, (own, near, far) in ((core, mine), (1 - core, other)):
        whole[row_of(spot, 0, of_core), :] = own[:SHARE, :]
        for i in range(1, CHIPS):
            rows = slice((i - 1) * HALF, i * HALF)
            whole[row_of(spot, i, of_core, side), :] = near[rows, :]
            whole[row_of(spot, i, of_core, 1 - side), :] = far[rows, :]


def by_core_copies(core, mine, other, whole, sem):
    size = mine.shape[0]
    return [
        pltpu.make_async_copy(mine, whole.at[row_at(core, size)], sem.at[0]),
        pltpu.make_async_copy(other, whole.at[row_at(1 - core, size)], sem.at[1]),
    ]


def start_all(copies):
    for copy in copies:
        copy.start()


def wait_all(copies):
    for copy in copies:
        copy.wait()


def chip_columns(weights, rows, chip):
    start = pl.multiple_of((chip * 5 // 2) * 128, 128)
    odd = lax.rem(chip, 2) == 1
    out = []
    for kind in range(3):
        window = weights[rows, pl.ds(kind * D + start, 384)]
        out.append(jnp.where(odd, window[:, 64 : 64 + D_CHIP], window[:, :D_CHIP]))
    return jnp.concatenate(out, axis=1)


def qkv_blocks_kernel(spot, lengths, padding, weights, *refs):
    vectors, own, sent = refs[:9], refs[9], refs[10 : 9 + CHIPS]
    held, marks, whole, vector_sems, sem = refs[9 + CHIPS : 18 + CHIPS], *refs[18 + CHIPS :]
    copies = [
        pltpu.make_async_copy(vector, here, vector_sems.at[i])
        for i, (vector, here) in enumerate(zip(vectors, held))
    ]
    copies.append(pltpu.make_async_copy(padding, marks, sem.at[0]))
    copies.append(pltpu.make_async_copy(weights, whole, sem.at[1]))
    start_all(copies)
    wait_all(copies)
    rows = padding.shape[-1]
    place = lax.broadcasted_iota(jnp.int32, (1, rows), 1)
    first = lengths[0, 0]
    member = (place >= first).astype(f32)
    leading = (place == 0) | (place == first)
    usable = jnp.where(leading | (marks[...].reshape(1, rows) > 0), 1.0, 0.0)
    code = 2.0 * member + usable
    width = 3 * D_CHIP
    lines = [v[...].astype(f32).reshape(1, -1) for v in held]
    extra = jnp.concatenate(
        [
            jnp.concatenate(lines[:6], axis=1),
            jnp.concatenate(lines[6:], axis=1),
            jnp.concatenate([code, jnp.zeros((1, width - rows), f32)], axis=1),
            jnp.zeros((EXTRA - 3, width), f32),
        ],
        axis=0,
    ).astype(bf16)
    own[:SHARE, :] = chip_columns(whole, slice(None), spot[0])
    own[SHARE:, :] = extra
    for i, block in enumerate(sent):
        block[:HALF, :] = chip_columns(whole, row_at(spot[2], HALF), spot[0] ^ (i + 1))
        block[HALF:, :] = extra


def qkv_blocks(spot, lengths, padding, weights, vectors):
    half = ((HALF + EXTRA, 3 * D_CHIP), bf16)
    return call(
        qkv_blocks_kernel,
        "qkv_blocks",
        "ss" + "h" * 11,
        [((SHARE + EXTRA, 3 * D_CHIP), bf16)] + [half] * (CHIPS - 1),
        [pltpu.VMEM(v.shape, v.dtype) for v in vectors]
        + [
            pltpu.VMEM(padding.shape, padding.dtype),
            pltpu.VMEM(weights.shape, weights.dtype),
            sems(9),
            sems(2),
        ],
    )(spot, lengths, padding, weights, *vectors)


def qkv_join_kernel(own, q1, q2, q3, x1, x2, near, near_half, first, second):
    size = first.shape[0]
    first[...] = x1[:size, :]
    second[...] = x2[size:, :]
    near[:SHARE, :] = own[:SHARE, :]
    low = SHARE + 3 * HALF
    near[low : low + EXTRA, :] = own[SHARE:, :]
    for i, block in enumerate((q1, q2, q3)):
        near[SHARE + i * HALF : SHARE + (i + 1) * HALF, :] = block[:HALF, :]
        near_half[i * HALF : (i + 1) * HALF, :] = block[:HALF, :]
        low += EXTRA
        near[low : low + EXTRA, :] = block[HALF:, :]


def qkv_join(blocks, x1, x2):
    width = blocks[0].shape[-1]
    half = ((x1.shape[0] // 2, x1.shape[1]), x1.dtype)
    return call(
        qkv_join_kernel,
        "qkv_join",
        "v" * 6,
        [
            ((SHARE + 3 * HALF + CHIPS * EXTRA, width), bf16),
            ((3 * HALF, width), bf16),
            half,
            half,
        ],
    )(*blocks, x1, x2)


def up_blocks_kernel(spot, weights, cotangent, own, *sent):
    def columns(chip):
        return pl.ds(pl.multiple_of(chip * FF_CHIP, FF_CHIP), FF_CHIP)

    own[...] = weights[:, columns(spot[0])]
    for i, block in enumerate(sent):
        block[:HALF, :] = weights[row_at(spot[2], HALF), columns(spot[0] ^ (i + 1))]
    for block in sent[:2]:
        block[HALF:, :] = cotangent[...]


def up_blocks(spot, weights, cotangent):
    both = HALF + cotangent.shape[0]
    sizes = (SHARE, both, both, HALF)
    return call(up_blocks_kernel, "up_blocks", "svv", [((size, FF_CHIP), bf16) for size in sizes])(
        spot, weights, cotangent
    )


def up_join_kernel(cotangent, u1, u2, u3, near, whole, first, second):
    rows = cotangent.shape[0]
    for i, block in enumerate((cotangent, u1.at[HALF:], u2.at[HALF:])):
        whole[i * rows : (i + 1) * rows, :] = block[...]
    for i, block in enumerate((u1, u2, u3)):
        near[i * HALF : (i + 1) * HALF, :] = block[:HALF, :]
    half = rows // 2
    first[...] = u1[HALF : HALF + half, :]
    second[...] = u2[HALF + half :, :]


def up_join(cotangent, blocks):
    rows = cotangent.shape[0]
    near = ((3 * HALF, FF_CHIP), bf16)
    passed = ((rows // 2, D), bf16)
    return call(
        up_join_kernel,
        "up_join",
        "vvvv",
        [near, (((CHIPS - 1) * rows, D), bf16), passed, passed],
    )(cotangent, *blocks)


def halves_kernel(whole, first, second):
    size = first.shape[0]
    first[...] = whole[:size, :]
    second[...] = whole[size:, :]


def halves(whole):
    shape = (whole.shape[0] // 2, whole.shape[1])
    return call(halves_kernel, "halves", "v", [(shape, whole.dtype)] * 2)(whole)


def join_kernel(*refs):
    stack_blocks(refs[:-1], refs[-1])


def join(blocks):
    rows, width = blocks[0].shape
    count = len(blocks)
    return call(join_kernel, "join", "v" * count, [((count * rows, width), blocks[0].dtype)])(
        *blocks
    )[0]


def fill_table(spot, extras, table, mask):
    chip, core = spot[0], spot[1]
    rows = mask.shape[1]
    table[...] = jnp.zeros_like(table)
    for team in range(TEAM):
        for i in range(6):
            table[i : i + 1, team * SHARE : (team + 1) * SHARE] = extras[
                team, 0:1, i * SHARE : (i + 1) * SHARE
            ]
    for half in range(2):
        line = extras[2 * chip + half, 1:2, :]
        lo = half * SHARE
        table[BIAS_QKV : BIAS_QKV + 1, lo : lo + SHARE] = line[:, :SHARE]
        table[BIAS_QKV : BIAS_QKV + 1, 2 * D_CHIP + lo : 2 * D_CHIP + lo + SHARE] = line[
            :, SHARE : 2 * SHARE
        ]
        table[BIAS_UP : BIAS_UP + 1, half * FF_SHARE : (half + 1) * FF_SHARE] = line[:, 2 * SHARE :]
    for i in range(CHIPS):
        code = extras[2 * (chip ^ i) + core, 2:3, :rows]
        of_key = jnp.broadcast_to(code, (rows, rows))
        cell_of_key = jnp.floor(of_key * 0.5)
        open_key = of_key - 2.0 * cell_of_key
        keep = jnp.where(cell_of_key == cell_of_key.T, open_key, 0.0)
        mask[i * rows : (i + 1) * rows, :] = keep.astype(bf16)


def token_norm_kernel(*refs):
    blocks, normed = refs[:-1], refs[-1]
    at = 0
    for x in blocks:
        rows = x.shape[0]
        normed[at : at + rows, :] = normalize(x[...].astype(f32))[0]
        at += rows


def token_norm(blocks):
    rows, width = blocks[0].shape
    shape = (CHIPS * rows, width)
    return call(token_norm_kernel, "token_norm", "v" * len(blocks), [(shape, f32)])(*blocks)[0]


def enter_kernel(spot, normed, *refs):
    mine, other, refs = refs[:2], refs[2:4], refs[4:]
    out_mine, out_other, refs = *refs[:2], refs[2:]
    table, mask, qkv, out, first_low, projected, context = refs[:7]
    partials = refs[7 : 8 + CHIPS]
    extras, out_sems = refs[8 + CHIPS :]
    rows = mask.shape[1]
    out_copies = by_core_copies(spot[1], out_mine, out_other, out, out_sems)
    start_all(out_copies)
    low = SHARE + 3 * HALF
    for of_core, lines in ((spot[1], mine[0]), (1 - spot[1], other[0])):
        for i in range(CHIPS):
            at = slice(low + i * EXTRA, low + (i + 1) * EXTRA)
            extras[2 * (spot[0] ^ i) + of_core] = lines[at, :].astype(f32)
    fill_table(spot, extras, table, mask)
    columns = [(near, near.at[SHARE:], far) for near, far in (mine, other)]
    stack_columns(spot, *columns, qkv)
    gain = table[GAIN1 : GAIN1 + 1, :]
    bias = table[BIAS1 : BIAS1 + 1, :]
    first_low[...] = (normed[...] * gain + bias).astype(bf16)
    for lo, hi in ((0, 384), (384, 768), (768, 960)):
        shift = table[BIAS_QKV : BIAS_QKV + 1, lo:hi]
        projected[:, lo:hi] = (mm(first_low[...], qkv[:, lo:hi]) + shift).astype(bf16)

    @pl.loop(0, CHIPS)
    def _(i):
        at = row_at(i, rows)
        context[at, :] = attend(projected[at, :], mask[at, :])

    wait_all(out_copies)

    def partial(at):
        whole = mm(context[...], out[:, at]).astype(bf16)
        lo = 0
        for part in partials:
            part[:, at] = whole[lo : lo + part.shape[0]]
            lo += part.shape[0]

    tiled(D, 256, partial)


def enter(spot, normed, mine, other, out_mine, out_other):
    total = normed.shape[0]
    rows = total // CHIPS
    outs = call(
        enter_kernel,
        "enter",
        "sv" + "v" * 4 + "hv",
        [
            ((TABLE_ROWS, D), f32),
            ((total, rows), bf16),
            ((D, 3 * D_CHIP), bf16),
            ((D_CHIP, D), bf16),
            ((total, D), bf16),
            ((total, 3 * D_CHIP), bf16),
            ((total, D_CHIP), bf16),
        ]
        + [((rows, D), bf16)] * (CHIPS - 1)
        + [((rows // 2, D), bf16)] * 2,
        [pltpu.VMEM((TEAM, EXTRA, 3 * D_CHIP), f32), sems(2)],
    )(spot, normed, *mine, *other, out_mine, out_other)
    return outs[:7], outs[7:]


def leave_kernel(
    b0, b1, b2, b3, qkv, out, projected, mask, branch, grad_projected, bias_sum, *refs
):
    partials, grad_context = refs[:CHIPS], refs[CHIPS]
    rows = b0.shape[0]
    stack_blocks((b0, b1, b2, b3), branch)
    grad_context[...] = mm_t(branch[...], out[...]).astype(bf16)
    bias_sum[...] = jnp.zeros_like(bias_sum)

    @pl.loop(0, CHIPS)
    def _(i):
        at = row_at(i, rows)
        grad = attend_back(projected[at, :], mask[at, :], grad_context[at, :])
        grad_projected[at, :] = grad
        bias_sum[...] += jnp.sum(grad.astype(f32), axis=0, keepdims=True)

    def partial(at):
        whole = mm_t(grad_projected[...], qkv[at, :]).astype(bf16)
        for i, part in enumerate(partials):
            part[:, at] = whole[i * rows : (i + 1) * rows]

    tiled(D, 256, partial)


def leave(blocks, qkv, out, projected, mask):
    rows = blocks[0].shape[0]
    total = CHIPS * rows
    outs = call(
        leave_kernel,
        "leave",
        "v" * 8,
        [((total, D), bf16), ((total, 3 * D_CHIP), bf16), ((1, 3 * D_CHIP), f32)]
        + [((rows, D), bf16)] * CHIPS,
        [pltpu.VMEM((total, D_CHIP), bf16)],
    )(*blocks, qkv, out, projected, mask)
    return outs[:3], outs[3:]


def total_of(parts):
    total = parts[0][...].astype(f32)
    for part in parts[1:]:
        total = total + part[...].astype(f32)
    return total


def pass_on_kernel(p1, p2, h1, h2, sum1, sum2):
    size = h1.shape[0]
    sum1[:size, :] = (p1[:size, :].astype(f32) + h1[...].astype(f32)).astype(bf16)
    sum1[size:, :] = p1[size:, :]
    sum2[:size, :] = p2[:size, :]
    sum2[size:, :] = (p2[size:, :].astype(f32) + h2[...].astype(f32)).astype(bf16)


def pass_on(p1, p2, h1, h2):
    return call(pass_on_kernel, "pass_on", "vvvv", [(p1.shape, bf16)] * 2)(p1, p2, h1, h2)


def mix_kernel(p0, p1, p2, tokens, table, mixed, second):
    total = total_of((p0, p1, p2)) + tokens[...].astype(f32)
    total = total + table[BIAS_OUT : BIAS_OUT + 1, :]
    mixed[...] = total
    normed, _ = normalize(total)
    second[...] = (normed * table[GAIN2 : GAIN2 + 1, :] + table[BIAS2 : BIAS2 + 1, :]).astype(bf16)


def mix(parts, tokens, table):
    shape = tokens.shape
    return call(mix_kernel, "mix", "v" * 5, [(shape, f32), (shape, bf16)])(*parts, tokens, table)


def unmix_kernel(p0, p1, p2, p3, mixed, table, cotangent, grad_mixed, branch, sums):
    grad = total_of((p0, p1, p2, p3))
    normed, inverse = normalize(mixed[...])
    grad_in, gain_sum, bias_sum = norm_backward(grad, normed, inverse, table[GAIN2 : GAIN2 + 1, :])
    grad_out = cotangent[...].astype(f32)
    grad_in = grad_in + grad_out
    grad_mixed[...] = grad_in
    low = grad_in.astype(bf16)
    branch[...] = low
    sums[...] = jnp.zeros_like(sums)
    sums[0:1, :] = jnp.sum(low.astype(f32), axis=0, keepdims=True)
    sums[1:2, :] = gain_sum
    sums[2:3, :] = bias_sum
    sums[3:4, :] = jnp.sum(grad_out, axis=0, keepdims=True)


def unmix(parts, mixed, table, cotangent):
    shape = cotangent.shape
    return call(
        unmix_kernel, "unmix", "v" * 7, [(shape, f32), (shape, bf16), ((8, D), f32)]
    )(*parts, mixed, table, cotangent)


def act_grad_kernel(spot, part, g1, g2, mine, other, grad_act, down, whole, down_sems):
    copies = by_core_copies(spot[1], mine, other, down, down_sems)
    start_all(copies)
    at = 0
    for block in (part, g1, g2):
        whole[at : at + block.shape[0], :] = block[...]
        at += block.shape[0]
    wait_all(copies)

    def columns(at):
        grad_act[:, at] = mm_t(whole[...], down[at, :])

    tiled(FF_CHIP, 256, columns)


def act_grad(spot, part, passed, down_mine, down_other):
    total = part.shape[0] // (CHIPS - 1) * CHIPS
    return call(
        act_grad_kernel,
        "act_grad",
        "svvvhv",
        [((total, FF_CHIP), f32), ((FF_CHIP, D), bf16), ((total, D), bf16)],
        [sems(2)],
    )(spot, part, *passed, down_mine, down_other)


def hidden_rows(at, second, up, table, grad_act, pre_act, act, grad_pre, bias_sum):
    size = at.stop - at.start

    def columns(tile):
        pre_act[at, tile] = mm(second[at, :], up[:, tile]) + table[BIAS_UP : BIAS_UP + 1, tile]

    tiled(FF_CHIP, 256, columns)

    @pl.loop(0, size // 64)
    def _(i):
        rows = pl.ds(pl.multiple_of(at.start + i * 64, 64), 64)
        pre = pre_act[rows, :]
        below = 0.5 * (1.0 + lax.erf(pre * (0.5**0.5)))
        bell = jnp.exp(-0.5 * pre * pre) * 0.3989422804014327
        act[rows, :] = (pre * below).astype(bf16)
        grad = (grad_act[rows, :] * (below + pre * bell)).astype(bf16)
        grad_pre[rows, :] = grad
        bias_sum[...] += jnp.sum(grad.astype(f32), axis=0, keepdims=True)


def hidden_first_kernel(spot, s0, s1, s2, grad_act, table, *refs):
    columns = [(own, rest, rest.at[3 * HALF :]) for own, rest in (refs[:2], refs[2:4])]
    second, act, grad_pre, bias_sum, up = refs[4:9]
    partials, pre_act = refs[9:12], refs[12]
    rows = s0.shape[0]
    stack_columns(spot, *columns, up)
    stack_blocks((s0, s1, s2), second)
    bias_sum[...] = jnp.zeros_like(bias_sum)
    hidden_rows(
        slice(0, 3 * rows), second, up, table, grad_act, pre_act, act, grad_pre, bias_sum
    )
    second_partials(slice(0, 3 * rows), grad_pre, up, partials)


def second_partials(at, grad_pre, up, partials):
    rows = partials[0].shape[0]

    def columns(tile):
        whole = mm_t(grad_pre[at, :], up[tile, :]).astype(bf16)
        for i, part in enumerate(partials):
            part[:, tile] = whole[i * rows : (i + 1) * rows]

    tiled(D, 256, columns)


def hidden_first(spot, blocks, grad_act, table, mine, other):
    total = grad_act.shape[0]
    return call(
        hidden_first_kernel,
        "hidden_first",
        "svvvvv" + "v" * 4,
        [
            ((total, D), bf16),
            ((total, FF_CHIP), bf16),
            ((total, FF_CHIP), bf16),
            ((1, FF_CHIP), f32),
            ((D, FF_CHIP), bf16),
        ]
        + [((total // CHIPS, D), bf16)] * 3,
        [pltpu.VMEM((total, FF_CHIP), f32)],
    )(spot, *blocks, grad_act, table, *mine, *other)


def hidden_last_kernel(
    spot,
    s3,
    grad_act,
    table,
    cotangent,
    up,
    second_in,
    act_in,
    grad_pre_in,
    bias_in,
    second,
    act,
    grad_pre,
    bias_sum,
    down_sent,
    pre_act,
):
    del second_in, act_in, grad_pre_in
    rows = s3.shape[0]
    at = slice(3 * rows, 4 * rows)
    second[at, :] = s3[...]
    bias_sum[...] = bias_in[...]
    hidden_rows(at, second, up, table, grad_act, pre_act, act, grad_pre, bias_sum)
    down_product(act, cotangent, 1 - spot[1], 0, down_sent)


def down_product(act, cotangent, of_core, half, target):
    low = half * ROWS_Z
    aligned = low // 128 * 128
    if half == 0:
        units = pl.ds(pl.multiple_of(of_core * FF_SHARE, 128), ROWS_Z)
        target[...] = t_mm(act[:, units], cotangent[...]).astype(target.dtype)
    else:
        units = pl.ds(pl.multiple_of(of_core * FF_SHARE + aligned, 128), FF_SHARE - aligned)
        window = act[:, units][:, low - aligned :]
        target[...] = t_mm(window, cotangent[...]).astype(target.dtype)


def up_product(second, grad_pre, pair, of_core, target, work):
    for i in range(2):
        first = (2 * (2 * pair + i) + of_core) * SHARE
        aligned = pl.multiple_of(first // 128 * 128, 128)
        work[...] = t_mm(second[:, pl.ds(aligned, 256)], grad_pre[...])
        start = pl.multiple_of(lax.rem(first, 128), 32)
        target[i * SHARE : (i + 1) * SHARE, :] = work[pl.ds(start, SHARE), :].astype(target.dtype)


def hidden_last(spot, block, grad_act, table, cotangent, up, second, act, grad_pre, bias_sum):
    total = second.shape[0]
    return pl.pallas_call(
        hidden_last_kernel,
        in_specs=[SMEM] + [VMEM] * 9,
        out_specs=[VMEM] * 5,
        out_shape=[
            jax.ShapeDtypeStruct(second.shape, bf16),
            jax.ShapeDtypeStruct(act.shape, bf16),
            jax.ShapeDtypeStruct(grad_pre.shape, bf16),
            jax.ShapeDtypeStruct(bias_sum.shape, f32),
            jax.ShapeDtypeStruct((ROWS_Z, D), bf16),
        ],
        scratch_shapes=[pltpu.VMEM((total, FF_CHIP), f32)],
        input_output_aliases={6: 0, 7: 1, 8: 2},
        compiler_params=pltpu.CompilerParams(vmem_limit_bytes=16 * 2**20),
        cost_estimate=COST,
        name="hidden_last",
    )(spot, block, grad_act, table, cotangent, up, second, act, grad_pre, bias_sum)


def second_last_kernel(grad_pre, up, partial):
    rows = partial.shape[0]
    second_partials(slice(grad_pre.shape[0] - rows, grad_pre.shape[0]), grad_pre, up, (partial,))


def second_last(grad_pre, up):
    rows = grad_pre.shape[0] // CHIPS
    return call(second_last_kernel, "second_last", "vv", [((rows, D), bf16)])(grad_pre, up)[0]


def up_sent_kernel(spot, grad_pre, second, up_sent, work):
    up_product(second, grad_pre, 0, 1 - spot[1], up_sent, work)


def up_sent_of(spot, grad_pre, second):
    return call(
        up_sent_kernel,
        "up_sent",
        "svv",
        [((ROWS_Z, FF_CHIP), bf16)],
        [pltpu.VMEM((256, FF_CHIP), f32)],
    )(spot, grad_pre, second)[0]


def split_rows(core, whole, sent, kept):
    for k in range(CHIPS):
        targets = ((sent[k // 2], k % 2, 1 - core), (kept, k, core))
        for target, at, of_core in targets:
            start = pl.multiple_of((2 * k + of_core) * SHARE, SHARE)
            target[at] = whole[pl.ds(start, SHARE), :].astype(bf16)


def down_grad_kernel(spot, act, cotangent, got, total):
    down_product(act, cotangent, spot[1], 0, total)
    total[...] = (total[...].astype(f32) + got[...].astype(f32)).astype(bf16)


def down_grad_of(spot, act, cotangent, got):
    return call(down_grad_kernel, "down_grad", "svvv", [((ROWS_Z, D), bf16)])(
        spot, act, cotangent, got
    )[0]


def rest_kernel(
    spot, second, grad_pre, act, cotangent, up_a, up_b, up_sent, down_b, down_sent, work
):
    core = spot[1]
    up_product(second, grad_pre, 0, core, up_a, work)
    up_product(second, grad_pre, 1, 1 - core, up_sent, work)
    up_product(second, grad_pre, 1, core, up_b, work)
    down_product(act, cotangent, 1 - core, 1, down_sent)
    down_product(act, cotangent, core, 1, down_b)


def rest_of_grads(spot, second, grad_pre, act, cotangent):
    return call(
        rest_kernel,
        "rest",
        "svvvv",
        [((ROWS_Z, D), bf16)] * 5,
        [pltpu.VMEM((256, FF_CHIP), f32)],
    )(spot, second, grad_pre, act, cotangent)


def result_kernel(act, down, *partials):
    rows = partials[0].shape[0]

    def columns(at):
        whole = mm(act[...], down[:, at]).astype(bf16)
        for i, part in enumerate(partials):
            part[:, at] = whole[i * rows : (i + 1) * rows]

    tiled(D, 256, columns)


def result_of(act, down):
    rows = act.shape[0] // CHIPS
    return call(result_kernel, "result", "vv", [((rows, D), bf16)] * CHIPS)(act, down)


def qkv_grad_kernel(
    spot,
    first_low,
    grad_projected,
    context,
    branch,
    sent_a,
    sent_b,
    kept,
    out_sent,
    out_kept,
    whole,
    out,
):
    core = spot[1]

    def columns(at):
        whole[at, :] = t_mm(first_low[:, at], grad_projected[...])

    tiled(D, 256, columns)
    split_rows(core, whole, (sent_a, sent_b), kept)
    out[...] = t_mm(context[...], branch[...])
    for target, of_core in ((out_sent, 1 - core), (out_kept, core)):
        target[...] = out[row_at(of_core, SHARE), :].astype(bf16)


def qkv_grad_of(spot, first_low, grad_projected, context, branch):
    half = ((CHIPS // 2, SHARE, 3 * D_CHIP), bf16)
    rows = ((SHARE, D), bf16)
    return call(
        qkv_grad_kernel,
        "qkv_grad",
        "svvvv",
        [half, half, ((CHIPS, SHARE, 3 * D_CHIP), bf16), rows, rows],
        [pltpu.VMEM((D, 3 * D_CHIP), f32), pltpu.VMEM((D_CHIP, D), f32)],
    )(spot, first_low, grad_projected, context, branch)


def add_kernel(*refs):
    count = len(refs) // 3
    for a, b, c in zip(refs[:count], refs[count : 2 * count], refs[2 * count :]):
        c[...] = (a[...].astype(f32) + b[...].astype(f32)).astype(c.dtype)


def add_all(left, right):
    shapes = [(a.shape, a.dtype) for a in left]
    return call(add_kernel, "add", "v" * (2 * len(left)), shapes)(*left, *right)


PACKED = SHARE * 3 // 4
STEP = SHARE // 4


def sum_all_kernel(a, b, c, d, total):
    total[...] = (a[...] + b[...]) + (c[...] + d[...])


def sum_all(parts):
    shape = (parts[0].shape, parts[0].dtype)
    return call(sum_all_kernel, "sum_all", "vvvv", [shape])(*parts)[0]


def pack_kernel(kept, got_a, got_b, out_kept, out_got, *chunks):
    for i, chunk in enumerate(chunks):
        for j in range(2):
            got = got_b if i else got_a
            total = (kept[2 * i + j].astype(f32) + got[j].astype(f32)).astype(bf16)
            lo = j * PACKED
            chunk[lo : lo + PACKED, : 3 * D_CHIP] = total[:PACKED]
            for part in range(3):
                at = lo + part * STEP
                chunk[at : at + STEP, 3 * D_CHIP :] = total[
                    PACKED:, part * D_CHIP : (part + 1) * D_CHIP
                ]
        rows = slice(i * HALF, (i + 1) * HALF)
        total = out_kept[rows, :].astype(f32) + out_got[rows, :].astype(f32)
        chunk[2 * PACKED :, :] = total.astype(bf16)


def pack(kept, got_a, got_b, out_kept, out_got):
    return call(pack_kernel, "pack", "vvvvv", [((ROWS_Z, D), bf16)] * 2)(
        kept, got_a, got_b, out_kept, out_got
    )


def unpacked(chunk, j):
    lo = j * PACKED
    tail = [
        chunk[lo + part * STEP : lo + (part + 1) * STEP, 3 * D_CHIP :] for part in range(3)
    ]
    return jnp.concatenate(
        [chunk[lo : lo + PACKED, : 3 * D_CHIP], jnp.concatenate(tail, axis=1)], axis=0
    )


def z_half(low, got_side):
    return add_all([low], [got_side])[0]


def z_send_kernel(spot, half, got_middle, low, sent):
    middle = spot[3] > 0

    @pl.when(middle)
    def _():
        whole = half[...].astype(f32) + got_middle[...].astype(f32)
        sent[...] = whole.astype(bf16)

    @pl.when(jnp.logical_not(middle))
    def _():
        sent[...] = low[...]


def z_send(spot, half, got_middle, low):
    return call(z_send_kernel, "z_send", "svvv", [(low.shape, bf16)])(spot, half, got_middle, low)[0]


def z_final_kernel(spot, sent, got_side, final):
    final[...] = jnp.where(spot[3] > 0, sent[...], got_side[...])


def z_final(spot, sent, got_side):
    return call(z_final_kernel, "z_final", "svv", [(sent.shape, bf16)])(spot, sent, got_side)[0]


def first_down_kernel(spot, sent, got, down, here, sem):
    here[...] = jnp.where(spot[3] > 0, sent[...], got[...]).astype(f32)
    copy = pltpu.make_async_copy(here, down.at[:ROWS_Z], sem.at[0])
    copy.start()
    copy.wait()


def first_down(spot, sent, got):
    return pl.pallas_call(
        first_down_kernel,
        in_specs=[SMEM, VMEM, VMEM],
        out_specs=HBM,
        out_shape=pltpu.HBM((2 * ROWS_Z, D), f32),
        scratch_shapes=[pltpu.VMEM((ROWS_Z, D), f32), sems(1)],
        compiler_params=pltpu.CompilerParams(vmem_limit_bytes=16 * 2**20),
        cost_estimate=COST,
        name="first_down",
    )(spot, sent, got)


def second_down_kernel(spot, sent, got, before, down, here, sem):
    del before
    copies = []
    for i in range(2):
        rows = slice(i * SHARE, (i + 1) * SHARE)
        here[rows, :] = jnp.where(spot[3] > 0, sent[rows, :], got[rows, :]).astype(f32)
        target = down.at[ROWS_Z + i * SHARE : ROWS_Z + (i + 1) * SHARE]
        copies.append(pltpu.make_async_copy(here.at[rows], target, sem.at[i]))
        copies[-1].start()
    wait_all(copies)


def second_down(spot, sent, got, down):
    return pl.pallas_call(
        second_down_kernel,
        in_specs=[SMEM, VMEM, VMEM, HBM],
        out_specs=HBM,
        out_shape=pltpu.HBM((2 * ROWS_Z, D), f32),
        scratch_shapes=[pltpu.VMEM((ROWS_Z, D), f32), sems(2)],
        input_output_aliases={3: 0},
        compiler_params=pltpu.CompilerParams(vmem_limit_bytes=16 * 2**20),
        cost_estimate=COST,
        name="second_down",
    )(spot, sent, got, pltpu.with_memory_space_constraint(down, pltpu.HBM))


def qkv_rows_kernel(spot, b0, b1, b2, b3, qkv, rows, stack, sem):
    for i, block in enumerate((b0, b1, b2, b3)):
        stack[spot[0] ^ i] = block[...]
    copies = []
    for kind in range(3):
        for chip in range(CHIPS):
            lo = kind * D + chip * D_CHIP
            rows[:, lo : lo + D_CHIP] = stack[
                chip, :, kind * D_CHIP : (kind + 1) * D_CHIP
            ].astype(f32)
        at = slice(kind * D, (kind + 1) * D)
        copies.append(pltpu.make_async_copy(rows.at[:, at], qkv.at[:, at], sem.at[kind]))
        copies[-1].start()
    wait_all(copies)


def qkv_rows(spot, blocks):
    shape = blocks[0].shape
    return pl.pallas_call(
        qkv_rows_kernel,
        in_specs=[SMEM] + [VMEM] * 4,
        out_specs=HBM,
        out_shape=pltpu.HBM((shape[0], 3 * D), f32),
        scratch_shapes=[
            pltpu.VMEM((shape[0], 3 * D), f32),
            pltpu.VMEM((CHIPS,) + shape, bf16),
            sems(3),
        ],
        compiler_params=pltpu.CompilerParams(vmem_limit_bytes=16 * 2**20),
        cost_estimate=COST,
        name="qkv_rows",
    )(spot, *blocks)


def owned_kernel(count, place, sums, got, *outs):
    total = sums[...] + got[...]
    index = place[0]
    size = outs[0].shape[0]
    mine = pltpu.roll(total, D - index * size, 1)
    for i, row in enumerate((0, 1, 2, 3, 4, 5, 8, 9)):
        outs[i][...] = mine[row : row + 1, :size].reshape(size)
    wide = outs[8].shape[0]
    first = index * wide
    row = first // D
    line = total[10:11, :]
    for k in range(1, CHIPS):
        line = jnp.where(row == k, total[10 + k : 11 + k, :], line)
    line = pltpu.roll(jnp.broadcast_to(line, (8, D)), D - lax.rem(first, D), 1)
    outs[8][...] = line[0:1, :wide].reshape(wide)
    mean = total[6:7, :] / count
    outs[9][...] = mean.reshape(D)
    outs[10][...] = (total[7:8, :] / count - mean * mean).reshape(D)


def owned(place, count, fsdp_count, sums, got):
    sizes = [D // fsdp_count] * 8 + [FF // fsdp_count, D, D]

    def kernel(*refs):
        owned_kernel(count, *refs)

    return call(kernel, "owned", "svv", [((size,), f32) for size in sizes])(place, sums, got)


def up_exchange_kernel(spot, a, b, *blocks):
    chunks = (a, b)
    for i, block in enumerate(blocks):
        chip = spot[0] ^ i
        at = row_at(lax.rem(chip, 2), SHARE)
        block[...] = jnp.where(chip >= 2, chunks[1][at, :], chunks[0][at, :])


def up_exchange(spot, a, b):
    return call(up_exchange_kernel, "up_exchange", "svv", [((SHARE, FF_CHIP), bf16)] * CHIPS)(
        spot, a, b
    )


def qkv_unpack_kernel(spot, sent, got_side, blocks, out_rows):
    chunk = jnp.where(spot[3] > 0, sent[...], got_side[...])
    for j in range(2):
        blocks[j] = unpacked(chunk, j)
    out_rows[...] = chunk[2 * PACKED :, :].astype(f32)


def qkv_unpack(spot, sent, got_side):
    return call(
        qkv_unpack_kernel,
        "qkv_unpack",
        "svv",
        [((2, SHARE, 3 * D_CHIP), bf16), ((HALF, D), f32)],
    )(spot, sent, got_side)


def qkv_exchange_kernel(spot, blocks_a, rows_a, sent, got_side, *refs):
    blocks, out_rows, stack = refs[:CHIPS], refs[CHIPS], refs[CHIPS + 1]
    chunk = jnp.where(spot[3] > 0, sent[...], got_side[...])
    stack[:2] = blocks_a[...]
    for j in range(2):
        stack[2 + j] = unpacked(chunk, j)
    out_rows[:HALF, :] = rows_a[...]
    out_rows[HALF:, :] = chunk[2 * PACKED :, :].astype(f32)
    for i, block in enumerate(blocks):
        block[...] = stack[spot[0] ^ i]


def qkv_exchange(spot, blocks_a, rows_a, sent, got_side):
    shape = (SHARE, 3 * D_CHIP)
    outs = call(
        qkv_exchange_kernel,
        "qkv_exchange",
        "svvvv",
        [(shape, bf16)] * CHIPS + [((SHARE, D), f32)],
        [pltpu.VMEM((CHIPS,) + shape, bf16)],
    )(spot, blocks_a, rows_a, sent, got_side)
    return outs[:CHIPS], outs[CHIPS]


def up_rows_kernel(spot, b0, b1, b2, b3, weights):
    for i, block in enumerate((b0, b1, b2, b3)):
        start = pl.multiple_of((spot[0] ^ i) * FF_CHIP, FF_CHIP)
        weights[:, pl.ds(start, FF_CHIP)] = block[...].astype(f32)


def up_rows(spot, blocks):
    return call(up_rows_kernel, "up_rows", "svvvv", [((SHARE, FF), f32)])(spot, *blocks)[0]


def end_kernel(
    spot,
    lengths,
    p0,
    p1,
    p2,
    p3,
    r0,
    r1,
    r2,
    r3,
    grad_mixed,
    tokens,
    table,
    mixed,
    mix_sums,
    qkv_sum,
    up_sum,
    layer_out,
    grad_tokens,
    sums,
):
    grad = total_of((p0, p1, p2, p3))
    normed, inverse = normalize(tokens[...].astype(f32))
    grad_in, gain_sum, bias_sum = norm_backward(grad, normed, inverse, table[GAIN1 : GAIN1 + 1, :])
    grad_tokens[...] = grad_mixed[...] + grad_in
    result = mixed[...] + total_of((r0, r1, r2, r3)) + table[BIAS_DOWN : BIAS_DOWN + 1, :]
    layer_out[...] = result.astype(bf16)
    place = lax.broadcasted_iota(jnp.int32, (result.shape[0], 1), 0)
    picked = jnp.where((place == 0) | (place == lengths[0, 0]), result, 0.0)
    sums[...] = jnp.zeros_like(sums)
    sums[0:1, :] = gain_sum
    sums[1:2, :] = bias_sum
    sums[2:6, :] = mix_sums[0:4, :]
    sums[6:7, :] = jnp.sum(picked, axis=0, keepdims=True)
    sums[7:8, :] = jnp.sum(picked * picked, axis=0, keepdims=True)
    for k in range(CHIPS):
        here = spot[0] == k
        lo = k * D_CHIP
        sums[8:9, lo : lo + D_CHIP] = jnp.where(here, qkv_sum[:, :D_CHIP], 0.0)
        sums[9:10, lo : lo + D_CHIP] = jnp.where(here, qkv_sum[:, 2 * D_CHIP :], 0.0)
        sums[10 + k : 11 + k, :] = jnp.where(here, up_sum[...], 0.0)


def end(spot, lengths, parts, results, *rest):
    shape = parts[0].shape
    return call(
        end_kernel,
        "end",
        "ss" + "v" * 15,
        [(shape, bf16), (shape, f32), ((SUM_ROWS, D), f32)],
    )(spot, lengths, *parts, *results, *rest)


def fence(*values):
    return lax.optimization_barrier(values)


def local(
    tokens,
    lengths,
    padding,
    ln1_gain,
    ln1_bias,
    w_qkv,
    b_query,
    b_value,
    w_out,
    b_out,
    ln2_gain,
    ln2_bias,
    w_up,
    b_up,
    w_down,
    b_down,
    cotangent,
):
    fsdp_count = lax.axis_size("fsdp")
    dp_count = lax.axis_size("dp")
    groups = fsdp_count // TEAM
    place = lax.axis_index("fsdp") // groups
    chip = place // 2
    core = place % 2
    depth = lax.axis_index("dp")
    middle = (depth == 1) | (depth == 2)
    spot = jnp.stack([chip, core, depth % 2, middle.astype(jnp.int32)]).astype(jnp.int32)

    def swap(value, mask):
        pairs = [
            (team * groups + group, (team ^ mask) * groups + group)
            for team in range(TEAM)
            for group in range(groups)
        ]
        return lax.ppermute(value, "fsdp", pairs)

    shard_groups = [[team * groups + group for group in range(groups)] for team in range(TEAM)]
    def gather_shards(value):
        if groups == 1:
            return value
        return lax.all_gather(value, "fsdp", axis=0, tiled=True, axis_index_groups=shard_groups)

    def scatter_shards(value):
        if groups == 1:
            return value
        return lax.psum_scatter(
            value, "fsdp", scatter_dimension=0, tiled=True, axis_index_groups=shard_groups
        )

    def along_z(pairs, value):
        return lax.ppermute(value, "dp", pairs)

    def z_swap(value):
        return along_z([(0, 1), (1, 0), (2, 3), (3, 2)], value)

    def z_middle(value):
        return along_z([(1, 2), (2, 1)], value)

    def from_chips(blocks):
        return [blocks[0]] + [swap(block, 2 * i) for i, block in enumerate(blocks) if i > 0]

    def fence_list(first, *others):
        done = fence(*first, *others)
        return list(done[: len(first)]), *done[len(first) :]

    w_qkv, w_out, w_up, w_down = (gather_shards(w) for w in (w_qkv, w_out, w_up, w_down))
    given = (ln1_gain, ln1_bias, b_out, ln2_gain, ln2_bias, b_down, b_query, b_value, b_up)
    qkv_sent = qkv_blocks(spot, lengths, padding, w_qkv, [gather_shards(v) for v in given])
    qkv_got = from_chips(qkv_sent)
    x1, x2, *qkv_got = fence(swap(tokens, 2), swap(tokens, 4), *qkv_got)
    qkv_near, qkv_half, x1_half, x2_half = qkv_join(qkv_got, x1, x2)
    qkv_far = z_swap(qkv_half)
    qkv_near_other = swap(qkv_near, 1)
    blocks = [tokens, x1, x2, swap(x1_half, 4), swap(x2_half, 2)]
    normed = token_norm(blocks)
    out_sent, _ = fence(w_out, qkv_near)
    out_other = swap(out_sent, 1)
    up_own, *up_sent = up_blocks(spot, w_up, cotangent)
    up_own, *up_sent = fence(up_own, *up_sent, qkv_near)[:-1]
    loads = [swap(block, 2 * i + 2) for i, block in enumerate(up_sent)]
    normed, qkv_far, qkv_near_other, out_other = fence(normed, qkv_far, qkv_near_other, out_other)
    qkv_far_other = join([swap(half, 1) for half in halves(qkv_far)])

    (table, mask, qkv, out, first_low, projected, context), partial_out = enter(
        spot,
        normed,
        [qkv_near, qkv_far],
        [qkv_near_other, qkv_far_other],
        w_out,
        out_other,
    )
    p0, p1, p2, h1, h2 = partial_out
    h1, h2 = swap(h1, 4), swap(h2, 2)
    cotangent_late, _ = fence(cotangent, partial_out[0])
    up_near, part, first, second = up_join(cotangent_late, loads)
    up_far = z_swap(up_near)
    passed = [swap(first, 4), swap(second, 2)]
    passed, h1, h2 = fence_list(passed, h1, h2)
    p1, p2 = pass_on(p1, p2, h1, h2)
    out_parts = [p0, swap(p1, 2), swap(p2, 4)]
    up_far, *out_parts = fence(up_far, *out_parts)
    mixed, second_own = mix(out_parts, tokens, table)
    second_blocks = from_chips([second_own] * CHIPS)
    up_far, _ = fence(up_far, second_own)
    up_rest = join([up_near, up_far])
    up_own_sent, _ = fence(up_own, second_own)
    up_other = [swap(up_own_sent, 1), swap(up_rest, 1)]
    down_sent, _ = fence(w_down, second_own)
    down_other = swap(down_sent, 1)
    part, down_other = fence(part, down_other)
    grad_act, down, whole_cotangent = act_grad(spot, part, passed, w_down, down_other)

    second_low, act_low, grad_pre, up_bias_sum, up, *partial_second = hidden_first(
        spot,
        second_blocks[:3],
        grad_act,
        table,
        [up_own, up_rest],
        up_other,
    )
    block, up_bias_sum = fence(second_blocks[3], up_bias_sum)
    second_low, act_low, grad_pre, up_bias_sum, down_sent = hidden_last(
        spot, block, grad_act, table, whole_cotangent, up, second_low, act_low, grad_pre, up_bias_sum
    )
    down_got = swap(down_sent, 1)
    up_sent = up_sent_of(spot, grad_pre, second_low)
    up_got = swap(up_sent, 1)
    act_low, up_sent = fence(act_low, up_sent)
    down_a = down_grad_of(spot, act_low, whole_cotangent, down_got)
    side0 = z_swap(down_a)
    up_late, _ = fence(up, down_a)
    partial_second = partial_second + [second_last(grad_pre, up_late)]
    second_parts = from_chips(partial_second)
    second_low, _ = fence(second_low, partial_second[3])
    up_a, up_b, up_sent, down_b, down_sent = rest_of_grads(
        spot, second_low, grad_pre, act_low, whole_cotangent
    )
    up_got, up_sent = fence(up_got, up_sent)
    (up_a,) = add_all([up_a], [up_got])
    up_got = swap(up_sent, 1)

    second_parts, up_a = fence_list(second_parts, up_a)
    grad_mixed, branch_own, mix_sums = unmix(second_parts, mixed, table, cotangent)
    side0, _ = fence(side0, branch_own)
    half0 = z_half(down_a, side0)
    send1, _ = fence(up_a, half0)
    side1, middle1 = z_swap(send1), z_middle(half0)
    branch_blocks = from_chips([branch_own] * CHIPS)
    act_low, branch_own = fence(act_low, branch_own)
    partial_result = list(result_of(act_low, down))

    up_got, partial_result[0] = fence(up_got, partial_result[0])
    (up_b,) = add_all([up_b], [up_got])
    branch_blocks, side1, middle1, *partial_result, up_b = fence_list(
        branch_blocks, side1, middle1, *partial_result, up_b
    )
    half1 = z_half(up_a, side1)
    middle1, _ = fence(middle1, half1)
    send2 = z_send(spot, half0, middle1, up_b)
    side2, middle2 = z_swap(send2), z_middle(half1)
    branch_blocks, half1 = fence_list(branch_blocks, half1)
    (whole_branch, grad_projected, qkv_bias_sum), partial_first = leave(
        branch_blocks, qkv, out, projected, mask
    )
    first_low, grad_projected = fence(first_low, grad_projected)
    qkv_sent_a, qkv_sent_b, qkv_kept, out_sent, out_kept = qkv_grad_of(
        spot, first_low, grad_projected, context, whole_branch
    )
    qkv_a, qkv_b = pack(
        qkv_kept, swap(qkv_sent_a, 1), swap(qkv_sent_b, 1), out_kept, swap(out_sent, 1)
    )

    side2, middle2, qkv_a = fence(side2, middle2, qkv_a)
    half2 = z_half(up_b, side2)
    middle2, _ = fence(middle2, half2)
    send3 = z_send(spot, half1, middle2, qkv_a)
    side3, middle3 = z_swap(send3), z_middle(half2)
    down_sent, _ = fence(down_sent, send3)
    (down_b,) = add_all([down_b], [swap(down_sent, 1)])
    *partial_first, down_b = fence(*partial_first, down_b)
    first_parts = from_chips(partial_first)
    down_grad = first_down(spot, send2, side2)

    first_parts, side3, middle3 = fence_list(first_parts, side3, middle3)
    half3 = z_half(qkv_a, side3)
    middle3, _ = fence(middle3, half3)
    send4 = z_send(spot, half2, middle3, qkv_b)
    sent, _ = fence(send3, send4)
    up_a_final = z_final(spot, sent, side3)
    side4, middle4 = z_swap(send4), z_middle(half3)
    *partial_result, half3 = fence(*partial_result, half3)
    result_parts = from_chips(partial_result)

    result_parts, side4, middle4 = fence_list(result_parts, side4, middle4)
    half4 = z_half(qkv_b, side4)
    middle4, _ = fence(middle4, half4)
    send5 = z_send(spot, half3, middle4, down_b)
    sent, _ = fence(send4, send5)
    up_b_final = z_final(spot, sent, side4)
    side5, middle5 = z_swap(send5), z_middle(half4)
    result_parts, half4 = fence_list(result_parts, half4)
    layer_out, grad_tokens, sums = end(
        spot,
        lengths,
        first_parts,
        result_parts,
        grad_mixed,
        tokens,
        table,
        mixed,
        mix_sums,
        qkv_bias_sum,
        up_bias_sum,
    )
    (sums,) = add_all([sums], [swap(sums, 1)])
    sums = sum_all(from_chips([sums] * CHIPS))
    if groups > 1:
        sums = lax.psum(sums, "fsdp", axis_index_groups=shard_groups)
    sums_got = z_swap(sums)
    up_a_final, _ = fence(up_a_final, sums)
    up_ready = up_exchange(spot, up_a_final, up_b_final)

    side5, middle5, sums_got, _ = fence(side5, middle5, sums_got, up_ready[0])
    half5 = z_half(down_b, side5)
    middle5, _ = fence(middle5, half5)
    send6 = z_half(half4, middle5)
    sent, _ = fence(send5, send6)
    qkv_ready, rows_ready = qkv_unpack(spot, sent, side5)
    side6, middle6 = z_swap(send6), z_middle(half5)
    up_ready, _ = fence_list(up_ready, send6)
    up_total = from_chips(up_ready)
    (sums,) = add_all([sums], [sums_got])

    up_total, side6, middle6, sums, qkv_ready = fence_list(
        up_total, side6, middle6, sums, qkv_ready
    )
    middle6, _ = fence(middle6, side6)
    send7 = z_half(half5, middle6)
    side7 = along_z([(1, 0), (2, 3)], send7)
    sent, send7, sums = fence(send6, send7, sums)
    qkv_last, out_grad = qkv_exchange(spot, qkv_ready, rows_ready, sent, side6)
    qkv_total = from_chips(qkv_last)
    sums_got = along_z([(z, z ^ 2) for z in range(4)], sums)
    up_grad = up_rows(spot, up_total)
    place_in = jnp.stack([lax.axis_index("fsdp")]).astype(jnp.int32)
    vectors = list(owned(place_in, CELLS_DEV * dp_count * fsdp_count, fsdp_count, sums, sums_got))
    qkv_total, up_grad, vectors[0] = fence_list(qkv_total, up_grad, vectors[0])
    qkv_grad = qkv_rows(spot, qkv_total)
    side7, qkv_grad = fence(side7, qkv_grad)
    down_grad = second_down(spot, send7, side7, down_grad)

    return (
        layer_out,
        grad_tokens,
        vectors[0],
        vectors[1],
        scatter_shards(qkv_grad),
        vectors[6],
        vectors[7],
        scatter_shards(out_grad),
        vectors[2],
        vectors[3],
        vectors[4],
        scatter_shards(up_grad),
        vectors[8],
        scatter_shards(down_grad),
        vectors[5],
        vectors[9],
        vectors[10],
    )


def solution(mesh):
    tokens_spec = P(("dp", "fsdp"), None)
    vector = P("fsdp")
    matrix = P("fsdp", None)
    in_specs = (
        tokens_spec,
        P(("dp", "fsdp"), None),
        P(("dp", "fsdp")),
        vector,
        vector,
        matrix,
        vector,
        vector,
        matrix,
        vector,
        vector,
        vector,
        matrix,
        vector,
        matrix,
        vector,
        tokens_spec,
    )
    out_specs = (
        tokens_spec,
        tokens_spec,
        vector,
        vector,
        matrix,
        vector,
        vector,
        matrix,
        vector,
        vector,
        vector,
        matrix,
        vector,
        matrix,
        vector,
        P(),
        P(),
    )
    return jax.shard_map(local, mesh=mesh, in_specs=in_specs, out_specs=out_specs, check_vma=False)
```

```python
import jax
import jax.numpy as jnp
from jax import lax
from jax.experimental import pallas as pl
from jax.experimental.pallas import tpu as pltpu
from jax.sharding import PartitionSpec as P

D = 1280
HEADS = 20
HEAD_DIM = 64
FF = 5120
CELLS_DEV = 2
EPS = 1e-05

TEAM = 8
CHIPS = 4
HEADS_CHIP = HEADS // CHIPS
D_CHIP = D // CHIPS
FF_CHIP = FF // CHIPS
SHARE = D // TEAM
FF_SHARE = FF // TEAM
SCALE = HEAD_DIM ** (-0.5)

GAIN1, BIAS1, BIAS_OUT, GAIN2, BIAS2, BIAS_DOWN, BIAS_UP, BIAS_QKV = range(8)
TABLE_ROWS = 8
SUM_ROWS = 16

COST = pl.CostEstimate(flops=1, bytes_accessed=1, transcendentals=0)
SMEM = pl.BlockSpec(memory_space=pltpu.SMEM)
HBM = pl.BlockSpec(memory_space=pltpu.HBM)
VMEM = pl.BlockSpec(memory_space=pltpu.VMEM)

f32 = jnp.float32
bf16 = jnp.bfloat16


def dot(a, b, dims):
    return lax.dot_general(a, b, (dims, ((), ())), preferred_element_type=f32)


def mm(a, b):
    return dot(a, b, ((1,), (0,)))


def mm_t(a, b):
    return dot(a, b, ((1,), (1,)))


def t_mm(a, b):
    return dot(a, b, ((0,), (0,)))


def normalize(values):
    center = jnp.mean(values, axis=-1, keepdims=True)
    centred = values - center
    spread = jnp.mean(centred * centred, axis=-1, keepdims=True)
    inverse = lax.rsqrt(spread + EPS)
    return centred * inverse, inverse


def norm_backward(grad_out, normed, inverse, norm_gain):
    grad_normed = grad_out * norm_gain
    first_mean = jnp.mean(grad_normed, axis=-1, keepdims=True)
    second_mean = jnp.mean(grad_normed * normed, axis=-1, keepdims=True)
    grad_in = inverse * (grad_normed - first_mean - normed * second_mean)
    gain_sum = jnp.sum(grad_out * normed, axis=0, keepdims=True)
    return grad_in, gain_sum, jnp.sum(grad_out, axis=0, keepdims=True)


def heads_of(projected, offset):
    return [
        projected[:, offset + i * HEAD_DIM : offset + (i + 1) * HEAD_DIM] for i in range(HEADS_CHIP)
    ]


def softmax_rows(queries, keys, keep):
    raw = jnp.concatenate([mm_t(q, k) for q, k in zip(queries, keys)], axis=0)
    masked = jnp.where(keep, raw * SCALE, -1e30)
    grown = jnp.exp(masked - jnp.max(masked, axis=-1, keepdims=True))
    return grown * (1.0 / jnp.sum(grown, axis=-1, keepdims=True))


def keep_of(mask):
    return jnp.concatenate([mask.astype(f32)] * HEADS_CHIP, axis=0) > 0.5


def attend(projected, mask):
    rows = mask.shape[0]
    probs = softmax_rows(heads_of(projected, 0), heads_of(projected, D_CHIP), keep_of(mask))
    probs = probs.astype(bf16)
    out = [
        mm(probs[i * rows : (i + 1) * rows], value)
        for i, value in enumerate(heads_of(projected, 2 * D_CHIP))
    ]
    return jnp.concatenate(out, axis=1).astype(bf16)


def attend_back(projected, mask, grad_context):
    rows = mask.shape[0]
    queries, keys, values = (heads_of(projected, i * D_CHIP) for i in range(3))
    grads = heads_of(grad_context, 0)
    probs = softmax_rows(queries, keys, keep_of(mask))
    grad_probs = jnp.concatenate([mm_t(g, v) for g, v in zip(grads, values)], axis=0)
    along = jnp.sum(grad_probs * probs, axis=-1, keepdims=True)
    grad_scores = (probs * (grad_probs - along) * SCALE).astype(bf16)
    probs = probs.astype(bf16)

    def cut(stack, i):
        return stack[i * rows : (i + 1) * rows]

    out = (
        [mm(cut(grad_scores, i), keys[i]) for i in range(HEADS_CHIP)]
        + [t_mm(cut(grad_scores, i), queries[i]) for i in range(HEADS_CHIP)]
        + [t_mm(cut(probs, i), grads[i]) for i in range(HEADS_CHIP)]
    )
    return jnp.concatenate(out, axis=1).astype(bf16)


HALF = SHARE // 2
EXTRA = 8
FLAG_ROWS = 16
ROWS_Z = 2 * SHARE


def call(kernel, name, kinds, out_shapes, scratch=(), vmem=16):
    specs = {"s": SMEM, "h": HBM, "v": VMEM}
    made = pl.pallas_call(
        kernel,
        in_specs=[specs[kind] for kind in kinds],
        out_specs=[VMEM] * len(out_shapes),
        out_shape=[jax.ShapeDtypeStruct(shape, kind) for shape, kind in out_shapes],
        scratch_shapes=list(scratch),
        compiler_params=pltpu.CompilerParams(vmem_limit_bytes=vmem * 2**20),
        cost_estimate=COST,
        name=name,
    )

    def run(*args):
        placed = [
            pltpu.with_memory_space_constraint(arg, pltpu.HBM) if kind == "h" else arg
            for kind, arg in zip(kinds, args, strict=True)
        ]
        return made(*placed)

    return run


def sems(count):
    return pltpu.SemaphoreType.DMA((count,))


def row_at(i, size):
    return pl.ds(pl.multiple_of(i * size, size), size)


def tiled(width, tile, body):
    @pl.loop(0, width // tile)
    def _(i):
        body(row_at(i, tile))


def stack_blocks(blocks, whole):
    rows = blocks[0].shape[0]
    for i, block in enumerate(blocks):
        whole[i * rows : (i + 1) * rows, :] = block[...]


def row_of(spot, i, of_core, half=None):
    row = (2 * (spot[0] ^ i) + of_core) * SHARE
    if half is None:
        return pl.ds(pl.multiple_of(row, SHARE), SHARE)
    return pl.ds(pl.multiple_of(row + half * HALF, HALF), HALF)


def stack_columns(spot, mine, other, whole):
    core, side = spot[1], spot[2]
    for of_core, (own, near, far) in ((core, mine), (1 - core, other)):
        whole[row_of(spot, 0, of_core), :] = own[:SHARE, :]
        for i in range(1, CHIPS):
            rows = slice((i - 1) * HALF, i * HALF)
            whole[row_of(spot, i, of_core, side), :] = near[rows, :]
            whole[row_of(spot, i, of_core, 1 - side), :] = far[rows, :]


def by_core_copies(core, mine, other, whole, sem):
    size = mine.shape[0]
    return [
        pltpu.make_async_copy(mine, whole.at[row_at(core, size)], sem.at[0]),
        pltpu.make_async_copy(other, whole.at[row_at(1 - core, size)], sem.at[1]),
    ]


def start_all(copies):
    for copy in copies:
        copy.start()


def wait_all(copies):
    for copy in copies:
        copy.wait()


def chip_columns(weights, rows, chip):
    start = pl.multiple_of((chip * 5 // 2) * 128, 128)
    odd = lax.rem(chip, 2) == 1
    out = []
    for kind in range(3):
        window = weights[rows, pl.ds(kind * D + start, 384)]
        out.append(jnp.where(odd, window[:, 64 : 64 + D_CHIP], window[:, :D_CHIP]))
    return jnp.concatenate(out, axis=1)


def qkv_blocks_kernel(spot, lengths, padding, weights, *refs):
    vectors, own, sent, flag = refs[:9], refs[9], refs[10 : 9 + CHIPS], refs[9 + CHIPS]
    held, marks, whole, vector_sems, sem = refs[10 + CHIPS : 19 + CHIPS], *refs[19 + CHIPS :]
    flag[...] = jnp.full(flag.shape, spot[3].astype(f32), f32).astype(bf16)
    copies = [
        pltpu.make_async_copy(vector, here, vector_sems.at[i])
        for i, (vector, here) in enumerate(zip(vectors, held))
    ]
    copies.append(pltpu.make_async_copy(padding, marks, sem.at[0]))
    copies.append(pltpu.make_async_copy(weights, whole, sem.at[1]))
    start_all(copies)
    wait_all(copies)
    rows = padding.shape[-1]
    place = lax.broadcasted_iota(jnp.int32, (1, rows), 1)
    first = lengths[0, 0]
    member = (place >= first).astype(f32)
    leading = (place == 0) | (place == first)
    usable = jnp.where(leading | (marks[...].reshape(1, rows) > 0), 1.0, 0.0)
    code = 2.0 * member + usable
    width = 3 * D_CHIP
    lines = [v[...].astype(f32).reshape(1, -1) for v in held]
    extra = jnp.concatenate(
        [
            jnp.concatenate(lines[:6], axis=1),
            jnp.concatenate(lines[6:], axis=1),
            jnp.concatenate([code, jnp.zeros((1, width - rows), f32)], axis=1),
            jnp.zeros((EXTRA - 3, width), f32),
        ],
        axis=0,
    ).astype(bf16)
    own[:SHARE, :] = chip_columns(whole, slice(None), spot[0])
    own[SHARE:, :] = extra
    for i, block in enumerate(sent):
        block[:HALF, :] = chip_columns(whole, row_at(spot[2], HALF), spot[0] ^ (i + 1))
        block[HALF:, :] = extra


def qkv_blocks(spot, lengths, padding, weights, vectors):
    half = ((HALF + EXTRA, 3 * D_CHIP), bf16)
    return call(
        qkv_blocks_kernel,
        "qkv_blocks",
        "ss" + "h" * 11,
        [((SHARE + EXTRA, 3 * D_CHIP), bf16)] + [half] * (CHIPS - 1) + [((FLAG_ROWS, D), bf16)],
        [pltpu.VMEM(v.shape, v.dtype) for v in vectors]
        + [
            pltpu.VMEM(padding.shape, padding.dtype),
            pltpu.VMEM(weights.shape, weights.dtype),
            sems(9),
            sems(2),
        ],
    )(spot, lengths, padding, weights, *vectors)


def qkv_join_kernel(own, q1, q2, q3, x1, x2, near, near_half, first, second):
    size = first.shape[0]
    first[...] = x1[:size, :]
    second[...] = x2[size:, :]
    near[:SHARE, :] = own[:SHARE, :]
    low = SHARE + 3 * HALF
    near[low : low + EXTRA, :] = own[SHARE:, :]
    for i, block in enumerate((q1, q2, q3)):
        near[SHARE + i * HALF : SHARE + (i + 1) * HALF, :] = block[:HALF, :]
        near_half[i * HALF : (i + 1) * HALF, :] = block[:HALF, :]
        low += EXTRA
        near[low : low + EXTRA, :] = block[HALF:, :]


def qkv_join(blocks, x1, x2):
    width = blocks[0].shape[-1]
    half = ((x1.shape[0] // 2, x1.shape[1]), x1.dtype)
    return call(
        qkv_join_kernel,
        "qkv_join",
        "v" * 6,
        [
            ((SHARE + 3 * HALF + CHIPS * EXTRA, width), bf16),
            ((3 * HALF, width), bf16),
            half,
            half,
        ],
    )(*blocks, x1, x2)


def up_blocks_kernel(spot, weights, cotangent, own, *sent):
    def columns(chip):
        return pl.ds(pl.multiple_of(chip * FF_CHIP, FF_CHIP), FF_CHIP)

    own[...] = weights[:, columns(spot[0])]
    for i, block in enumerate(sent):
        block[:HALF, :] = weights[row_at(spot[2], HALF), columns(spot[0] ^ (i + 1))]
    for block in sent[:2]:
        block[HALF:, :] = cotangent[...]


def up_blocks(spot, weights, cotangent):
    both = HALF + cotangent.shape[0]
    sizes = (SHARE, both, both, HALF)
    return call(up_blocks_kernel, "up_blocks", "svv", [((size, FF_CHIP), bf16) for size in sizes])(
        spot, weights, cotangent
    )


def up_join_kernel(cotangent, u1, u2, u3, near, whole, first, second):
    rows = cotangent.shape[0]
    for i, block in enumerate((cotangent, u1.at[HALF:], u2.at[HALF:])):
        whole[i * rows : (i + 1) * rows, :] = block[...]
    for i, block in enumerate((u1, u2, u3)):
        near[i * HALF : (i + 1) * HALF, :] = block[:HALF, :]
    half = rows // 2
    first[...] = u1[HALF : HALF + half, :]
    second[...] = u2[HALF + half :, :]


def up_join(cotangent, blocks):
    rows = cotangent.shape[0]
    near = ((3 * HALF, FF_CHIP), bf16)
    passed = ((rows // 2, D), bf16)
    return call(
        up_join_kernel,
        "up_join",
        "vvvv",
        [near, (((CHIPS - 1) * rows, D), bf16), passed, passed],
    )(cotangent, *blocks)


def halves_kernel(whole, first, second):
    size = first.shape[0]
    first[...] = whole[:size, :]
    second[...] = whole[size:, :]


def halves(whole):
    shape = (whole.shape[0] // 2, whole.shape[1])
    return call(halves_kernel, "halves", "v", [(shape, whole.dtype)] * 2)(whole)


def join_kernel(*refs):
    stack_blocks(refs[:-1], refs[-1])


def join(blocks):
    rows, width = blocks[0].shape
    count = len(blocks)
    return call(join_kernel, "join", "v" * count, [((count * rows, width), blocks[0].dtype)])(
        *blocks
    )[0]


def fill_table(spot, extras, table, mask):
    chip, core = spot[0], spot[1]
    rows = mask.shape[1]
    table[...] = jnp.zeros_like(table)
    for team in range(TEAM):
        for i in range(6):
            table[i : i + 1, team * SHARE : (team + 1) * SHARE] = extras[
                team, 0:1, i * SHARE : (i + 1) * SHARE
            ]
    for half in range(2):
        line = extras[2 * chip + half, 1:2, :]
        lo = half * SHARE
        table[BIAS_QKV : BIAS_QKV + 1, lo : lo + SHARE] = line[:, :SHARE]
        table[BIAS_QKV : BIAS_QKV + 1, 2 * D_CHIP + lo : 2 * D_CHIP + lo + SHARE] = line[
            :, SHARE : 2 * SHARE
        ]
        table[BIAS_UP : BIAS_UP + 1, half * FF_SHARE : (half + 1) * FF_SHARE] = line[:, 2 * SHARE :]
    for i in range(CHIPS):
        code = extras[2 * (chip ^ i) + core, 2:3, :rows]
        of_key = jnp.broadcast_to(code, (rows, rows))
        cell_of_key = jnp.floor(of_key * 0.5)
        open_key = of_key - 2.0 * cell_of_key
        keep = jnp.where(cell_of_key == cell_of_key.T, open_key, 0.0)
        mask[i * rows : (i + 1) * rows, :] = keep.astype(bf16)


def token_norm_kernel(*refs):
    blocks, normed = refs[:-1], refs[-1]
    at = 0
    for x in blocks:
        rows = x.shape[0]
        normed[at : at + rows, :] = normalize(x[...].astype(f32))[0]
        at += rows


def token_norm(blocks):
    rows, width = blocks[0].shape
    shape = (CHIPS * rows, width)
    return call(token_norm_kernel, "token_norm", "v" * len(blocks), [(shape, f32)])(*blocks)[0]


def enter_kernel(spot, normed, *refs):
    mine, other, refs = refs[:2], refs[2:4], refs[4:]
    out_mine, out_other, refs = *refs[:2], refs[2:]
    table, mask, qkv, out, first_low, projected, context = refs[:7]
    partials = refs[7 : 8 + CHIPS]
    extras, out_sems = refs[8 + CHIPS :]
    rows = mask.shape[1]
    out_copies = by_core_copies(spot[1], out_mine, out_other, out, out_sems)
    start_all(out_copies)
    low = SHARE + 3 * HALF
    for of_core, lines in ((spot[1], mine[0]), (1 - spot[1], other[0])):
        for i in range(CHIPS):
            at = slice(low + i * EXTRA, low + (i + 1) * EXTRA)
            extras[2 * (spot[0] ^ i) + of_core] = lines[at, :].astype(f32)
    fill_table(spot, extras, table, mask)
    columns = [(near, near.at[SHARE:], far) for near, far in (mine, other)]
    stack_columns(spot, *columns, qkv)
    gain = table[GAIN1 : GAIN1 + 1, :]
    bias = table[BIAS1 : BIAS1 + 1, :]
    first_low[...] = (normed[...] * gain + bias).astype(bf16)
    for lo, hi in ((0, 384), (384, 768), (768, 960)):
        shift = table[BIAS_QKV : BIAS_QKV + 1, lo:hi]
        projected[:, lo:hi] = (mm(first_low[...], qkv[:, lo:hi]) + shift).astype(bf16)

    @pl.loop(0, CHIPS)
    def _(i):
        at = row_at(i, rows)
        context[at, :] = attend(projected[at, :], mask[at, :])

    wait_all(out_copies)

    def partial(at):
        whole = mm(context[...], out[:, at]).astype(bf16)
        lo = 0
        for part in partials:
            part[:, at] = whole[lo : lo + part.shape[0]]
            lo += part.shape[0]

    tiled(D, 256, partial)


def enter(spot, normed, mine, other, out_mine, out_other):
    total = normed.shape[0]
    rows = total // CHIPS
    outs = call(
        enter_kernel,
        "enter",
        "sv" + "v" * 4 + "hv",
        [
            ((TABLE_ROWS, D), f32),
            ((total, rows), bf16),
            ((D, 3 * D_CHIP), bf16),
            ((D_CHIP, D), bf16),
            ((total, D), bf16),
            ((total, 3 * D_CHIP), bf16),
            ((total, D_CHIP), bf16),
        ]
        + [((rows, D), bf16)] * (CHIPS - 1)
        + [((rows // 2, D), bf16)] * 2,
        [pltpu.VMEM((TEAM, EXTRA, 3 * D_CHIP), f32), sems(2)],
    )(spot, normed, *mine, *other, out_mine, out_other)
    return outs[:7], outs[7:]


def leave_kernel(
    b0, b1, b2, b3, qkv, out, projected, mask, branch, grad_projected, bias_sum, *refs
):
    partials, grad_context = refs[:CHIPS], refs[CHIPS]
    rows = b0.shape[0]
    stack_blocks((b0, b1, b2, b3), branch)
    grad_context[...] = mm_t(branch[...], out[...]).astype(bf16)
    bias_sum[...] = jnp.zeros_like(bias_sum)

    @pl.loop(0, CHIPS)
    def _(i):
        at = row_at(i, rows)
        grad = attend_back(projected[at, :], mask[at, :], grad_context[at, :])
        grad_projected[at, :] = grad
        bias_sum[...] += jnp.sum(grad.astype(f32), axis=0, keepdims=True)

    def partial(at):
        whole = mm_t(grad_projected[...], qkv[at, :]).astype(bf16)
        for i, part in enumerate(partials):
            part[:, at] = whole[i * rows : (i + 1) * rows]

    tiled(D, 256, partial)


def leave(blocks, qkv, out, projected, mask):
    rows = blocks[0].shape[0]
    total = CHIPS * rows
    outs = call(
        leave_kernel,
        "leave",
        "v" * 8,
        [((total, D), bf16), ((total, 3 * D_CHIP), bf16), ((1, 3 * D_CHIP), f32)]
        + [((rows, D), bf16)] * CHIPS,
        [pltpu.VMEM((total, D_CHIP), bf16)],
    )(*blocks, qkv, out, projected, mask)
    return outs[:3], outs[3:]


def total_of(parts):
    total = parts[0][...].astype(f32)
    for part in parts[1:]:
        total = total + part[...].astype(f32)
    return total


def pass_on_kernel(p1, p2, h1, h2, sum1, sum2):
    size = h1.shape[0]
    sum1[:size, :] = (p1[:size, :].astype(f32) + h1[...].astype(f32)).astype(bf16)
    sum1[size:, :] = p1[size:, :]
    sum2[:size, :] = p2[:size, :]
    sum2[size:, :] = (p2[size:, :].astype(f32) + h2[...].astype(f32)).astype(bf16)


def pass_on(p1, p2, h1, h2):
    return call(pass_on_kernel, "pass_on", "vvvv", [(p1.shape, bf16)] * 2)(p1, p2, h1, h2)


def mix_kernel(p0, p1, p2, tokens, table, mixed, second):
    total = total_of((p0, p1, p2)) + tokens[...].astype(f32)
    total = total + table[BIAS_OUT : BIAS_OUT + 1, :]
    mixed[...] = total
    normed, _ = normalize(total)
    second[...] = (normed * table[GAIN2 : GAIN2 + 1, :] + table[BIAS2 : BIAS2 + 1, :]).astype(bf16)


def mix(parts, tokens, table):
    shape = tokens.shape
    return call(mix_kernel, "mix", "v" * 5, [(shape, f32), (shape, bf16)])(*parts, tokens, table)


def unmix_kernel(p0, p1, p2, p3, mixed, table, cotangent, grad_mixed, branch, sums):
    grad = total_of((p0, p1, p2, p3))
    normed, inverse = normalize(mixed[...])
    grad_in, gain_sum, bias_sum = norm_backward(grad, normed, inverse, table[GAIN2 : GAIN2 + 1, :])
    grad_out = cotangent[...].astype(f32)
    grad_in = grad_in + grad_out
    grad_mixed[...] = grad_in
    low = grad_in.astype(bf16)
    branch[...] = low
    sums[...] = jnp.zeros_like(sums)
    sums[0:1, :] = jnp.sum(low.astype(f32), axis=0, keepdims=True)
    sums[1:2, :] = gain_sum
    sums[2:3, :] = bias_sum
    sums[3:4, :] = jnp.sum(grad_out, axis=0, keepdims=True)


def unmix(parts, mixed, table, cotangent):
    shape = cotangent.shape
    return call(
        unmix_kernel, "unmix", "v" * 7, [(shape, f32), (shape, bf16), ((8, D), f32)]
    )(*parts, mixed, table, cotangent)


def act_grad_kernel(spot, part, g1, g2, mine, other, grad_act, down, whole, down_sems):
    copies = by_core_copies(spot[1], mine, other, down, down_sems)
    start_all(copies)
    at = 0
    for block in (part, g1, g2):
        whole[at : at + block.shape[0], :] = block[...]
        at += block.shape[0]
    wait_all(copies)

    def columns(at):
        grad_act[:, at] = mm_t(whole[...], down[at, :])

    tiled(FF_CHIP, 256, columns)


def act_grad(spot, part, passed, down_mine, down_other):
    total = part.shape[0] // (CHIPS - 1) * CHIPS
    return call(
        act_grad_kernel,
        "act_grad",
        "svvvhv",
        [((total, FF_CHIP), f32), ((FF_CHIP, D), bf16), ((total, D), bf16)],
        [sems(2)],
    )(spot, part, *passed, down_mine, down_other)


def hidden_rows(at, second, up, table, grad_act, pre_act, act, grad_pre, bias_sum):
    size = at.stop - at.start

    def columns(tile):
        pre_act[at, tile] = mm(second[at, :], up[:, tile]) + table[BIAS_UP : BIAS_UP + 1, tile]

    tiled(FF_CHIP, 640, columns)

    @pl.loop(0, size // 64)
    def _(i):
        rows = pl.ds(pl.multiple_of(at.start + i * 64, 64), 64)
        pre = pre_act[rows, :]
        below = 0.5 * (1.0 + lax.erf(pre * (0.5**0.5)))
        bell = jnp.exp(-0.5 * pre * pre) * 0.3989422804014327
        act[rows, :] = (pre * below).astype(bf16)
        grad = (grad_act[rows, :] * (below + pre * bell)).astype(bf16)
        grad_pre[rows, :] = grad
        bias_sum[...] += jnp.sum(grad.astype(f32), axis=0, keepdims=True)


def hidden_first_kernel(spot, s0, s1, s2, grad_act, table, *refs):
    columns = [(own, rest, rest.at[3 * HALF :]) for own, rest in (refs[:2], refs[2:4])]
    second, act, grad_pre, bias_sum, up = refs[4:9]
    partials, pre_act = refs[9:12], refs[12]
    rows = s0.shape[0]
    stack_columns(spot, *columns, up)
    stack_blocks((s0, s1, s2), second)
    bias_sum[...] = jnp.zeros_like(bias_sum)
    hidden_rows(
        slice(0, 3 * rows), second, up, table, grad_act, pre_act, act, grad_pre, bias_sum
    )
    second_partials(slice(0, 3 * rows), grad_pre, up, partials)


def second_partials(at, grad_pre, up, partials):
    rows = partials[0].shape[0]

    def columns(tile):
        whole = mm_t(grad_pre[at, :], up[tile, :]).astype(bf16)
        for i, part in enumerate(partials):
            part[:, tile] = whole[i * rows : (i + 1) * rows]

    tiled(D, 640, columns)


def hidden_first(spot, blocks, grad_act, table, mine, other):
    total = grad_act.shape[0]
    return call(
        hidden_first_kernel,
        "hidden_first",
        "svvvvv" + "v" * 4,
        [
            ((total, D), bf16),
            ((total, FF_CHIP), bf16),
            ((total, FF_CHIP), bf16),
            ((1, FF_CHIP), f32),
            ((D, FF_CHIP), bf16),
        ]
        + [((total // CHIPS, D), bf16)] * 3,
        [pltpu.VMEM((total, FF_CHIP), f32)],
    )(spot, *blocks, grad_act, table, *mine, *other)


def hidden_last_kernel(
    spot,
    s3,
    grad_act,
    table,
    cotangent,
    up,
    second_in,
    act_in,
    grad_pre_in,
    bias_in,
    second,
    act,
    grad_pre,
    bias_sum,
    down_sent,
    pre_act,
):
    del second_in, act_in, grad_pre_in
    rows = s3.shape[0]
    at = slice(3 * rows, 4 * rows)
    second[at, :] = s3[...]
    bias_sum[...] = bias_in[...]
    hidden_rows(at, second, up, table, grad_act, pre_act, act, grad_pre, bias_sum)
    down_product(act, cotangent, 1 - spot[1], 0, down_sent)


def down_product(act, cotangent, of_core, half, target):
    low = half * ROWS_Z
    aligned = low // 128 * 128
    if half == 0:
        units = pl.ds(pl.multiple_of(of_core * FF_SHARE, 128), ROWS_Z)
        target[...] = t_mm(act[:, units], cotangent[...]).astype(target.dtype)
    else:
        units = pl.ds(pl.multiple_of(of_core * FF_SHARE + aligned, 128), FF_SHARE - aligned)
        window = act[:, units][:, low - aligned :]
        target[...] = t_mm(window, cotangent[...]).astype(target.dtype)


def up_product(second, grad_pre, pair, of_core, target, work):
    for i in range(2):
        first = (2 * (2 * pair + i) + of_core) * SHARE
        aligned = pl.multiple_of(first // 128 * 128, 128)
        work[...] = t_mm(second[:, pl.ds(aligned, 256)], grad_pre[...])
        start = pl.multiple_of(lax.rem(first, 128), 32)
        target[i * SHARE : (i + 1) * SHARE, :] = work[pl.ds(start, SHARE), :].astype(target.dtype)


def hidden_last(spot, block, grad_act, table, cotangent, up, second, act, grad_pre, bias_sum):
    total = second.shape[0]
    return pl.pallas_call(
        hidden_last_kernel,
        in_specs=[SMEM] + [VMEM] * 9,
        out_specs=[VMEM] * 5,
        out_shape=[
            jax.ShapeDtypeStruct(second.shape, bf16),
            jax.ShapeDtypeStruct(act.shape, bf16),
            jax.ShapeDtypeStruct(grad_pre.shape, bf16),
            jax.ShapeDtypeStruct(bias_sum.shape, f32),
            jax.ShapeDtypeStruct((ROWS_Z, D), bf16),
        ],
        scratch_shapes=[pltpu.VMEM((total, FF_CHIP), f32)],
        input_output_aliases={6: 0, 7: 1, 8: 2},
        compiler_params=pltpu.CompilerParams(vmem_limit_bytes=16 * 2**20),
        cost_estimate=COST,
        name="hidden_last",
    )(spot, block, grad_act, table, cotangent, up, second, act, grad_pre, bias_sum)


def second_last_kernel(grad_pre, up, partial):
    rows = partial.shape[0]
    second_partials(slice(grad_pre.shape[0] - rows, grad_pre.shape[0]), grad_pre, up, (partial,))


def second_last(grad_pre, up):
    rows = grad_pre.shape[0] // CHIPS
    return call(second_last_kernel, "second_last", "vv", [((rows, D), bf16)])(grad_pre, up)[0]


def up_sent_kernel(spot, grad_pre, second, up_sent, work):
    up_product(second, grad_pre, 0, 1 - spot[1], up_sent, work)


def up_sent_of(spot, grad_pre, second):
    return call(
        up_sent_kernel,
        "up_sent",
        "svv",
        [((ROWS_Z, FF_CHIP), bf16)],
        [pltpu.VMEM((256, FF_CHIP), f32)],
    )(spot, grad_pre, second)[0]


def split_rows(core, whole, sent, kept):
    for k in range(CHIPS):
        targets = ((sent[k // 2], k % 2, 1 - core), (kept, k, core))
        for target, at, of_core in targets:
            start = pl.multiple_of((2 * k + of_core) * SHARE, SHARE)
            target[at] = whole[pl.ds(start, SHARE), :].astype(bf16)


def down_grad_kernel(spot, act, cotangent, got, total):
    down_product(act, cotangent, spot[1], 0, total)
    total[...] = (total[...].astype(f32) + got[...].astype(f32)).astype(bf16)


def down_grad_of(spot, act, cotangent, got):
    return call(down_grad_kernel, "down_grad", "svvv", [((ROWS_Z, D), bf16)])(
        spot, act, cotangent, got
    )[0]


def rest_kernel(
    spot, second, grad_pre, act, cotangent, up_a, up_b, up_sent, down_b, down_sent, work
):
    core = spot[1]
    up_product(second, grad_pre, 0, core, up_a, work)
    up_product(second, grad_pre, 1, 1 - core, up_sent, work)
    up_product(second, grad_pre, 1, core, up_b, work)
    down_product(act, cotangent, 1 - core, 1, down_sent)
    down_product(act, cotangent, core, 1, down_b)


def rest_of_grads(spot, second, grad_pre, act, cotangent):
    return call(
        rest_kernel,
        "rest",
        "svvvv",
        [((ROWS_Z, D), bf16)] * 5,
        [pltpu.VMEM((256, FF_CHIP), f32)],
    )(spot, second, grad_pre, act, cotangent)


def result_kernel(act, down, *partials):
    rows = partials[0].shape[0]

    def columns(at):
        whole = mm(act[...], down[:, at]).astype(bf16)
        for i, part in enumerate(partials):
            part[:, at] = whole[i * rows : (i + 1) * rows]

    tiled(D, 256, columns)


def result_of(act, down):
    rows = act.shape[0] // CHIPS
    return call(result_kernel, "result", "vv", [((rows, D), bf16)] * CHIPS)(act, down)


def qkv_grad_kernel(
    spot,
    first_low,
    grad_projected,
    context,
    branch,
    sent_a,
    sent_b,
    kept,
    out_sent,
    out_kept,
    whole,
    out,
):
    core = spot[1]

    def columns(at):
        whole[at, :] = t_mm(first_low[:, at], grad_projected[...])

    tiled(D, 256, columns)
    split_rows(core, whole, (sent_a, sent_b), kept)
    out[...] = t_mm(context[...], branch[...])
    for target, of_core in ((out_sent, 1 - core), (out_kept, core)):
        target[...] = out[row_at(of_core, SHARE), :].astype(bf16)


def qkv_grad_of(spot, first_low, grad_projected, context, branch):
    half = ((CHIPS // 2, SHARE, 3 * D_CHIP), bf16)
    rows = ((SHARE, D), bf16)
    return call(
        qkv_grad_kernel,
        "qkv_grad",
        "svvvv",
        [half, half, ((CHIPS, SHARE, 3 * D_CHIP), bf16), rows, rows],
        [pltpu.VMEM((D, 3 * D_CHIP), f32), pltpu.VMEM((D_CHIP, D), f32)],
    )(spot, first_low, grad_projected, context, branch)


def add_kernel(*refs):
    count = len(refs) // 3
    for a, b, c in zip(refs[:count], refs[count : 2 * count], refs[2 * count :]):
        c[...] = a[...] + b[...]


def add_all(left, right):
    shapes = [(a.shape, a.dtype) for a in left]
    return call(add_kernel, "add", "v" * (2 * len(left)), shapes)(*left, *right)


PACKED = SHARE * 3 // 4
STEP = SHARE // 4


def sum_all_kernel(a, b, c, d, total):
    total[...] = (a[...] + b[...]) + (c[...] + d[...])


def sum_all(parts):
    shape = (parts[0].shape, parts[0].dtype)
    return call(sum_all_kernel, "sum_all", "vvvv", [shape])(*parts)[0]


def pack_kernel(kept, got_a, got_b, out_kept, out_got, *chunks):
    for i, chunk in enumerate(chunks):
        for j in range(2):
            got = got_b if i else got_a
            total = (kept[2 * i + j].astype(f32) + got[j].astype(f32)).astype(bf16)
            lo = j * PACKED
            chunk[lo : lo + PACKED, : 3 * D_CHIP] = total[:PACKED]
            for part in range(3):
                at = lo + part * STEP
                chunk[at : at + STEP, 3 * D_CHIP :] = total[
                    PACKED:, part * D_CHIP : (part + 1) * D_CHIP
                ]
        rows = slice(i * HALF, (i + 1) * HALF)
        total = out_kept[rows, :].astype(f32) + out_got[rows, :].astype(f32)
        chunk[2 * PACKED :, :] = total.astype(bf16)


def pack(kept, got_a, got_b, out_kept, out_got):
    return call(pack_kernel, "pack", "vvvvv", [((ROWS_Z, D), bf16)] * 2)(
        kept, got_a, got_b, out_kept, out_got
    )


def unpacked(chunk, j):
    lo = j * PACKED
    tail = [
        chunk[lo + part * STEP : lo + (part + 1) * STEP, 3 * D_CHIP :] for part in range(3)
    ]
    return jnp.concatenate(
        [chunk[lo : lo + PACKED, : 3 * D_CHIP], jnp.concatenate(tail, axis=1)], axis=0
    )


def z_half(low, got_side):
    return add_all([low], [got_side])[0]


def z_send_kernel(flag, half, got_middle, low, sent):
    middle = flag[...] > 0.5
    for i in range(ROWS_Z // FLAG_ROWS):
        rows = slice(i * FLAG_ROWS, (i + 1) * FLAG_ROWS)
        sent[rows, :] = jnp.where(middle, half[rows, :] + got_middle[rows, :], low[rows, :])


def z_send(flag, half, got_middle, low):
    return call(z_send_kernel, "z_send", "vvvv", [(low.shape, bf16)])(flag, half, got_middle, low)[0]


def z_final_kernel(spot, sent, got_side, final):
    final[...] = jnp.where(spot[3] > 0, sent[...], got_side[...])


def z_final(spot, sent, got_side):
    return call(z_final_kernel, "z_final", "svv", [(sent.shape, bf16)])(spot, sent, got_side)[0]


def first_down_kernel(spot, sent, got, down, here, sem):
    here[...] = jnp.where(spot[3] > 0, sent[...], got[...]).astype(f32)
    copy = pltpu.make_async_copy(here, down.at[:ROWS_Z], sem.at[0])
    copy.start()
    copy.wait()


def first_down(spot, sent, got):
    return pl.pallas_call(
        first_down_kernel,
        in_specs=[SMEM, VMEM, VMEM],
        out_specs=HBM,
        out_shape=pltpu.HBM((2 * ROWS_Z, D), f32),
        scratch_shapes=[pltpu.VMEM((ROWS_Z, D), f32), sems(1)],
        compiler_params=pltpu.CompilerParams(vmem_limit_bytes=16 * 2**20),
        cost_estimate=COST,
        name="first_down",
    )(spot, sent, got)


def second_down_kernel(flag, sent, got, before, down, here, sem):
    del before
    copies = []
    middle = flag[...] > 0.5
    for i in range(2):
        for lo in range(i * SHARE, (i + 1) * SHARE, FLAG_ROWS):
            rows = slice(lo, lo + FLAG_ROWS)
            here[rows, :] = jnp.where(middle, sent[rows, :], got[rows, :]).astype(f32)
        rows = slice(i * SHARE, (i + 1) * SHARE)
        target = down.at[ROWS_Z + i * SHARE : ROWS_Z + (i + 1) * SHARE]
        copies.append(pltpu.make_async_copy(here.at[rows], target, sem.at[i]))
        copies[-1].start()
    wait_all(copies)


def second_down(flag, sent, got, down):
    return pl.pallas_call(
        second_down_kernel,
        in_specs=[VMEM, VMEM, VMEM, HBM],
        out_specs=HBM,
        out_shape=pltpu.HBM((2 * ROWS_Z, D), f32),
        scratch_shapes=[pltpu.VMEM((ROWS_Z, D), f32), sems(2)],
        input_output_aliases={3: 0},
        compiler_params=pltpu.CompilerParams(vmem_limit_bytes=16 * 2**20),
        cost_estimate=COST,
        name="second_down",
    )(flag, sent, got, pltpu.with_memory_space_constraint(down, pltpu.HBM))


def qkv_rows_kernel(spot, b0, b1, b2, b3, qkv, rows, stack, sem):
    for i, block in enumerate((b0, b1, b2, b3)):
        stack[spot[0] ^ i] = block[...]
    copies = []
    for kind in range(3):
        for chip in range(CHIPS):
            lo = kind * D + chip * D_CHIP
            rows[:, lo : lo + D_CHIP] = stack[
                chip, :, kind * D_CHIP : (kind + 1) * D_CHIP
            ].astype(f32)
        at = slice(kind * D, (kind + 1) * D)
        copies.append(pltpu.make_async_copy(rows.at[:, at], qkv.at[:, at], sem.at[kind]))
        copies[-1].start()
    wait_all(copies)


def qkv_rows(spot, blocks):
    shape = blocks[0].shape
    return pl.pallas_call(
        qkv_rows_kernel,
        in_specs=[SMEM] + [VMEM] * 4,
        out_specs=HBM,
        out_shape=pltpu.HBM((shape[0], 3 * D), f32),
        scratch_shapes=[
            pltpu.VMEM((shape[0], 3 * D), f32),
            pltpu.VMEM((CHIPS,) + shape, bf16),
            sems(3),
        ],
        compiler_params=pltpu.CompilerParams(vmem_limit_bytes=16 * 2**20),
        cost_estimate=COST,
        name="qkv_rows",
    )(spot, *blocks)


def owned_kernel(count, place, sums, got, *outs):
    total = sums[...] + got[...]
    index = place[0]
    size = outs[0].shape[0]
    mine = pltpu.roll(total, D - index * size, 1)
    for i, row in enumerate((0, 1, 2, 3, 4, 5, 8, 9)):
        outs[i][...] = mine[row : row + 1, :size].reshape(size)
    wide = outs[8].shape[0]
    first = index * wide
    row = first // D
    line = total[10:11, :]
    for k in range(1, CHIPS):
        line = jnp.where(row == k, total[10 + k : 11 + k, :], line)
    line = pltpu.roll(jnp.broadcast_to(line, (8, D)), D - lax.rem(first, D), 1)
    outs[8][...] = line[0:1, :wide].reshape(wide)
    mean = total[6:7, :] / count
    outs[9][...] = mean.reshape(D)
    outs[10][...] = (total[7:8, :] / count - mean * mean).reshape(D)


def owned(place, count, fsdp_count, sums, got):
    sizes = [D // fsdp_count] * 8 + [FF // fsdp_count, D, D]

    def kernel(*refs):
        owned_kernel(count, *refs)

    return call(kernel, "owned", "svv", [((size,), f32) for size in sizes])(place, sums, got)


def up_exchange_kernel(spot, a, b, *blocks):
    chunks = (a, b)
    for i, block in enumerate(blocks):
        chip = spot[0] ^ i
        at = row_at(lax.rem(chip, 2), SHARE)
        block[...] = jnp.where(chip >= 2, chunks[1][at, :], chunks[0][at, :])


def up_exchange(spot, a, b):
    return call(up_exchange_kernel, "up_exchange", "svv", [((SHARE, FF_CHIP), bf16)] * CHIPS)(
        spot, a, b
    )


def qkv_unpack_kernel(spot, sent, got_side, blocks, out_rows):
    chunk = jnp.where(spot[3] > 0, sent[...], got_side[...])
    for j in range(2):
        blocks[j] = unpacked(chunk, j)
    out_rows[...] = chunk[2 * PACKED :, :].astype(f32)


def qkv_unpack(spot, sent, got_side):
    return call(
        qkv_unpack_kernel,
        "qkv_unpack",
        "svv",
        [((2, SHARE, 3 * D_CHIP), bf16), ((HALF, D), f32)],
    )(spot, sent, got_side)


def qkv_exchange_kernel(spot, blocks_a, rows_a, sent, got_side, *refs):
    blocks, out_rows, stack = refs[:CHIPS], refs[CHIPS], refs[CHIPS + 1]
    chunk = jnp.where(spot[3] > 0, sent[...], got_side[...])
    stack[:2] = blocks_a[...]
    for j in range(2):
        stack[2 + j] = unpacked(chunk, j)
    out_rows[:HALF, :] = rows_a[...]
    out_rows[HALF:, :] = chunk[2 * PACKED :, :].astype(f32)
    for i, block in enumerate(blocks):
        block[...] = stack[spot[0] ^ i]


def qkv_exchange(spot, blocks_a, rows_a, sent, got_side):
    shape = (SHARE, 3 * D_CHIP)
    outs = call(
        qkv_exchange_kernel,
        "qkv_exchange",
        "svvvv",
        [(shape, bf16)] * CHIPS + [((SHARE, D), f32)],
        [pltpu.VMEM((CHIPS,) + shape, bf16)],
    )(spot, blocks_a, rows_a, sent, got_side)
    return outs[:CHIPS], outs[CHIPS]


def up_rows_kernel(spot, b0, b1, b2, b3, weights):
    for i, block in enumerate((b0, b1, b2, b3)):
        start = pl.multiple_of((spot[0] ^ i) * FF_CHIP, FF_CHIP)
        weights[:, pl.ds(start, FF_CHIP)] = block[...].astype(f32)


def up_rows(spot, blocks):
    return call(up_rows_kernel, "up_rows", "svvvv", [((SHARE, FF), f32)])(spot, *blocks)[0]


def end_kernel(
    spot,
    lengths,
    p0,
    p1,
    p2,
    p3,
    r0,
    r1,
    r2,
    r3,
    grad_mixed,
    tokens,
    table,
    mixed,
    mix_sums,
    qkv_sum,
    up_sum,
    layer_out,
    grad_tokens,
    sums,
):
    grad = total_of((p0, p1, p2, p3))
    normed, inverse = normalize(tokens[...].astype(f32))
    grad_in, gain_sum, bias_sum = norm_backward(grad, normed, inverse, table[GAIN1 : GAIN1 + 1, :])
    grad_tokens[...] = grad_mixed[...] + grad_in
    result = mixed[...] + total_of((r0, r1, r2, r3)) + table[BIAS_DOWN : BIAS_DOWN + 1, :]
    layer_out[...] = result.astype(bf16)
    place = lax.broadcasted_iota(jnp.int32, (result.shape[0], 1), 0)
    picked = jnp.where((place == 0) | (place == lengths[0, 0]), result, 0.0)
    sums[...] = jnp.zeros_like(sums)
    sums[0:1, :] = gain_sum
    sums[1:2, :] = bias_sum
    sums[2:6, :] = mix_sums[0:4, :]
    sums[6:7, :] = jnp.sum(picked, axis=0, keepdims=True)
    sums[7:8, :] = jnp.sum(picked * picked, axis=0, keepdims=True)
    for k in range(CHIPS):
        here = spot[0] == k
        lo = k * D_CHIP
        sums[8:9, lo : lo + D_CHIP] = jnp.where(here, qkv_sum[:, :D_CHIP], 0.0)
        sums[9:10, lo : lo + D_CHIP] = jnp.where(here, qkv_sum[:, 2 * D_CHIP :], 0.0)
        sums[10 + k : 11 + k, :] = jnp.where(here, up_sum[...], 0.0)


def end(spot, lengths, parts, results, *rest):
    shape = parts[0].shape
    return call(
        end_kernel,
        "end",
        "ss" + "v" * 15,
        [(shape, bf16), (shape, f32), ((SUM_ROWS, D), f32)],
    )(spot, lengths, *parts, *results, *rest)


def fence(*values):
    return lax.optimization_barrier(values)


def local(
    tokens,
    lengths,
    padding,
    ln1_gain,
    ln1_bias,
    w_qkv,
    b_query,
    b_value,
    w_out,
    b_out,
    ln2_gain,
    ln2_bias,
    w_up,
    b_up,
    w_down,
    b_down,
    cotangent,
):
    fsdp_count = lax.axis_size("fsdp")
    dp_count = lax.axis_size("dp")
    groups = fsdp_count // TEAM
    place = lax.axis_index("fsdp") // groups
    chip = place // 2
    core = place % 2
    depth = lax.axis_index("dp")
    middle = (depth == 1) | (depth == 2)
    spot = jnp.stack([chip, core, depth % 2, middle.astype(jnp.int32)]).astype(jnp.int32)

    def swap(value, mask):
        pairs = [
            (team * groups + group, (team ^ mask) * groups + group)
            for team in range(TEAM)
            for group in range(groups)
        ]
        return lax.ppermute(value, "fsdp", pairs)

    shard_groups = [[team * groups + group for group in range(groups)] for team in range(TEAM)]
    def gather_shards(value):
        if groups == 1:
            return value
        return lax.all_gather(value, "fsdp", axis=0, tiled=True, axis_index_groups=shard_groups)

    def scatter_shards(value):
        if groups == 1:
            return value
        return lax.psum_scatter(
            value, "fsdp", scatter_dimension=0, tiled=True, axis_index_groups=shard_groups
        )

    def along_z(pairs, value):
        return lax.ppermute(value, "dp", pairs)

    def z_swap(value):
        return along_z([(0, 1), (1, 0), (2, 3), (3, 2)], value)

    def z_middle(value):
        return along_z([(1, 2), (2, 1)], value)

    def from_chips(blocks):
        return [blocks[0]] + [swap(block, 2 * i) for i, block in enumerate(blocks) if i > 0]

    def fence_list(first, *others):
        done = fence(*first, *others)
        return list(done[: len(first)]), *done[len(first) :]

    w_qkv, w_out, w_up, w_down = (gather_shards(w) for w in (w_qkv, w_out, w_up, w_down))
    given = (ln1_gain, ln1_bias, b_out, ln2_gain, ln2_bias, b_down, b_query, b_value, b_up)
    *qkv_sent, flag = qkv_blocks(spot, lengths, padding, w_qkv, [gather_shards(v) for v in given])
    qkv_got = from_chips(qkv_sent)
    x1, x2, *qkv_got = fence(swap(tokens, 2), swap(tokens, 4), *qkv_got)
    qkv_near, qkv_half, x1_half, x2_half = qkv_join(qkv_got, x1, x2)
    qkv_far = z_swap(qkv_half)
    qkv_near_other = swap(qkv_near, 1)
    blocks = [tokens, x1, x2, swap(x1_half, 4), swap(x2_half, 2)]
    normed = token_norm(blocks)
    out_sent, _ = fence(w_out, qkv_near)
    out_other = swap(out_sent, 1)
    up_own, *up_sent = up_blocks(spot, w_up, cotangent)
    up_own, *up_sent = fence(up_own, *up_sent, qkv_near)[:-1]
    loads = [swap(block, 2 * i + 2) for i, block in enumerate(up_sent)]
    normed, qkv_far, qkv_near_other, out_other = fence(normed, qkv_far, qkv_near_other, out_other)
    qkv_far_other = join([swap(half, 1) for half in halves(qkv_far)])

    (table, mask, qkv, out, first_low, projected, context), partial_out = enter(
        spot,
        normed,
        [qkv_near, qkv_far],
        [qkv_near_other, qkv_far_other],
        w_out,
        out_other,
    )
    p0, p1, p2, h1, h2 = partial_out
    h1, h2 = swap(h1, 4), swap(h2, 2)
    cotangent_late, _ = fence(cotangent, partial_out[0])
    up_near, part, first, second = up_join(cotangent_late, loads)
    up_far = z_swap(up_near)
    passed = [swap(first, 4), swap(second, 2)]
    passed, h1, h2 = fence_list(passed, h1, h2)
    p1, p2 = pass_on(p1, p2, h1, h2)
    out_parts = [p0, swap(p1, 2), swap(p2, 4)]
    up_far, *out_parts = fence(up_far, *out_parts)
    mixed, second_own = mix(out_parts, tokens, table)
    second_blocks = from_chips([second_own] * CHIPS)
    up_far, _ = fence(up_far, second_own)
    up_rest = join([up_near, up_far])
    up_own_sent, _ = fence(up_own, second_own)
    up_other = [swap(up_own_sent, 1), swap(up_rest, 1)]
    down_sent, _ = fence(w_down, second_own)
    down_other = swap(down_sent, 1)
    part, down_other = fence(part, down_other)
    grad_act, down, whole_cotangent = act_grad(spot, part, passed, w_down, down_other)

    second_low, act_low, grad_pre, up_bias_sum, up, *partial_second = hidden_first(
        spot,
        second_blocks[:3],
        grad_act,
        table,
        [up_own, up_rest],
        up_other,
    )
    block, up_bias_sum = fence(second_blocks[3], up_bias_sum)
    second_low, act_low, grad_pre, up_bias_sum, down_sent = hidden_last(
        spot, block, grad_act, table, whole_cotangent, up, second_low, act_low, grad_pre, up_bias_sum
    )
    down_got = swap(down_sent, 1)
    up_sent = up_sent_of(spot, grad_pre, second_low)
    up_got = swap(up_sent, 1)
    act_low, up_sent = fence(act_low, up_sent)
    down_a = down_grad_of(spot, act_low, whole_cotangent, down_got)
    side0 = z_swap(down_a)
    up_late, _ = fence(up, down_a)
    partial_second = partial_second + [second_last(grad_pre, up_late)]
    second_parts = from_chips(partial_second)
    second_low, _ = fence(second_low, partial_second[3])
    up_a, up_b, up_sent, down_b, down_sent = rest_of_grads(
        spot, second_low, grad_pre, act_low, whole_cotangent
    )
    up_got, up_sent = fence(up_got, up_sent)
    (up_a,) = add_all([up_a], [up_got])
    up_got = swap(up_sent, 1)

    second_parts, up_a = fence_list(second_parts, up_a)
    grad_mixed, branch_own, mix_sums = unmix(second_parts, mixed, table, cotangent)
    side0, _ = fence(side0, branch_own)
    half0 = z_half(down_a, side0)
    send1, _ = fence(up_a, half0)
    side1, middle1 = z_swap(send1), z_middle(half0)
    branch_blocks = from_chips([branch_own] * CHIPS)
    act_low, branch_own = fence(act_low, branch_own)
    partial_result = list(result_of(act_low, down))

    up_got, partial_result[0] = fence(up_got, partial_result[0])
    (up_b,) = add_all([up_b], [up_got])
    branch_blocks, side1, middle1, *partial_result, up_b = fence_list(
        branch_blocks, side1, middle1, *partial_result, up_b
    )
    half1 = z_half(up_a, side1)
    middle1, _ = fence(middle1, half1)
    send2 = z_send(flag, half0, middle1, up_b)
    side2, middle2 = z_swap(send2), z_middle(half1)
    branch_blocks, half1 = fence_list(branch_blocks, half1)
    (whole_branch, grad_projected, qkv_bias_sum), partial_first = leave(
        branch_blocks, qkv, out, projected, mask
    )
    first_low, grad_projected = fence(first_low, grad_projected)
    qkv_sent_a, qkv_sent_b, qkv_kept, out_sent, out_kept = qkv_grad_of(
        spot, first_low, grad_projected, context, whole_branch
    )
    qkv_a, qkv_b = pack(
        qkv_kept, swap(qkv_sent_a, 1), swap(qkv_sent_b, 1), out_kept, swap(out_sent, 1)
    )

    side2, middle2, qkv_a = fence(side2, middle2, qkv_a)
    half2 = z_half(up_b, side2)
    middle2, _ = fence(middle2, half2)
    send3 = z_send(flag, half1, middle2, qkv_a)
    side3, middle3 = z_swap(send3), z_middle(half2)
    down_sent, _ = fence(down_sent, send3)
    (down_b,) = add_all([down_b], [swap(down_sent, 1)])
    *partial_first, down_b = fence(*partial_first, down_b)
    first_parts = from_chips(partial_first)
    down_grad = first_down(spot, send2, side2)

    first_parts, side3, middle3 = fence_list(first_parts, side3, middle3)
    half3 = z_half(qkv_a, side3)
    middle3, _ = fence(middle3, half3)
    send4 = z_send(flag, half2, middle3, qkv_b)
    sent, _ = fence(send3, send4)
    up_a_final = z_final(spot, sent, side3)
    side4, middle4 = z_swap(send4), z_middle(half3)
    *partial_result, half3 = fence(*partial_result, half3)
    result_parts = from_chips(partial_result)

    result_parts, side4, middle4 = fence_list(result_parts, side4, middle4)
    half4 = z_half(qkv_b, side4)
    middle4, _ = fence(middle4, half4)
    send5 = z_send(flag, half3, middle4, down_b)
    sent, _ = fence(send4, send5)
    up_b_final = z_final(spot, sent, side4)
    side5, middle5 = z_swap(send5), z_middle(half4)
    result_parts, half4 = fence_list(result_parts, half4)
    layer_out, grad_tokens, sums = end(
        spot,
        lengths,
        first_parts,
        result_parts,
        grad_mixed,
        tokens,
        table,
        mixed,
        mix_sums,
        qkv_bias_sum,
        up_bias_sum,
    )
    (sums,) = add_all([sums], [swap(sums, 1)])
    sums = sum_all(from_chips([sums] * CHIPS))
    if groups > 1:
        sums = lax.psum(sums, "fsdp", axis_index_groups=shard_groups)
    sums_got = z_swap(sums)
    up_a_final, _ = fence(up_a_final, sums)
    up_ready = up_exchange(spot, up_a_final, up_b_final)

    side5, middle5, sums_got, _ = fence(side5, middle5, sums_got, up_ready[0])
    half5 = z_half(down_b, side5)
    middle5, _ = fence(middle5, half5)
    send6 = z_half(half4, middle5)
    sent, _ = fence(send5, send6)
    qkv_ready, rows_ready = qkv_unpack(spot, sent, side5)
    side6, middle6 = z_swap(send6), z_middle(half5)
    up_ready, _ = fence_list(up_ready, send6)
    up_total = from_chips(up_ready)
    (sums,) = add_all([sums], [sums_got])

    up_total, side6, middle6, sums, qkv_ready = fence_list(
        up_total, side6, middle6, sums, qkv_ready
    )
    middle6, _ = fence(middle6, side6)
    send7 = z_half(half5, middle6)
    side7 = along_z([(1, 0), (2, 3)], send7)
    sent, send7, sums = fence(send6, send7, sums)
    qkv_last, out_grad = qkv_exchange(spot, qkv_ready, rows_ready, sent, side6)
    qkv_total = from_chips(qkv_last)
    sums_got = along_z([(z, z ^ 2) for z in range(4)], sums)
    up_grad = up_rows(spot, up_total)
    place_in = jnp.stack([lax.axis_index("fsdp")]).astype(jnp.int32)
    vectors = list(owned(place_in, CELLS_DEV * dp_count * fsdp_count, fsdp_count, sums, sums_got))
    qkv_total, up_grad, vectors[0] = fence_list(qkv_total, up_grad, vectors[0])
    qkv_grad = qkv_rows(spot, qkv_total)
    side7, qkv_grad = fence(side7, qkv_grad)
    down_grad = second_down(flag, send7, side7, down_grad)

    return (
        layer_out,
        grad_tokens,
        vectors[0],
        vectors[1],
        scatter_shards(qkv_grad),
        vectors[6],
        vectors[7],
        scatter_shards(out_grad),
        vectors[2],
        vectors[3],
        vectors[4],
        scatter_shards(up_grad),
        vectors[8],
        scatter_shards(down_grad),
        vectors[5],
        vectors[9],
        vectors[10],
    )


def solution(mesh):
    tokens_spec = P(("dp", "fsdp"), None)
    vector = P("fsdp")
    matrix = P("fsdp", None)
    in_specs = (
        tokens_spec,
        P(("dp", "fsdp"), None),
        P(("dp", "fsdp")),
        vector,
        vector,
        matrix,
        vector,
        vector,
        matrix,
        vector,
        vector,
        vector,
        matrix,
        vector,
        matrix,
        vector,
        tokens_spec,
    )
    out_specs = (
        tokens_spec,
        tokens_spec,
        vector,
        vector,
        matrix,
        vector,
        vector,
        matrix,
        vector,
        vector,
        vector,
        matrix,
        vector,
        matrix,
        vector,
        P(),
        P(),
    )
    return jax.shard_map(local, mesh=mesh, in_specs=in_specs, out_specs=out_specs, check_vma=False)
```

```python
import jax
import jax.numpy as jnp
from jax import lax
from jax.experimental import pallas as pl
from jax.experimental.pallas import tpu as pltpu
from jax.sharding import PartitionSpec as P

D = 1280
HEADS = 20
HEAD_DIM = 64
FF = 5120
CELLS_DEV = 2
EPS = 1e-05

TEAM = 8
CHIPS = 4
HEADS_CHIP = HEADS // CHIPS
D_CHIP = D // CHIPS
FF_CHIP = FF // CHIPS
SHARE = D // TEAM
FF_SHARE = FF // TEAM
SCALE = HEAD_DIM ** (-0.5)

GAIN1, BIAS1, BIAS_OUT, GAIN2, BIAS2, BIAS_DOWN, BIAS_UP, BIAS_QKV = range(8)
TABLE_ROWS = 8
SUM_ROWS = 16

COST = pl.CostEstimate(flops=1, bytes_accessed=1, transcendentals=0)
SMEM = pl.BlockSpec(memory_space=pltpu.SMEM)
HBM = pl.BlockSpec(memory_space=pltpu.HBM)
VMEM = pl.BlockSpec(memory_space=pltpu.VMEM)

f32 = jnp.float32
bf16 = jnp.bfloat16


def dot(a, b, dims):
    return lax.dot_general(a, b, (dims, ((), ())), preferred_element_type=f32)


def mm(a, b):
    return dot(a, b, ((1,), (0,)))


def mm_t(a, b):
    return dot(a, b, ((1,), (1,)))


def t_mm(a, b):
    return dot(a, b, ((0,), (0,)))


def normalize(values):
    center = jnp.mean(values, axis=-1, keepdims=True)
    centred = values - center
    spread = jnp.mean(centred * centred, axis=-1, keepdims=True)
    inverse = lax.rsqrt(spread + EPS)
    return centred * inverse, inverse


def norm_backward(grad_out, normed, inverse, norm_gain):
    grad_normed = grad_out * norm_gain
    first_mean = jnp.mean(grad_normed, axis=-1, keepdims=True)
    second_mean = jnp.mean(grad_normed * normed, axis=-1, keepdims=True)
    grad_in = inverse * (grad_normed - first_mean - normed * second_mean)
    gain_sum = jnp.sum(grad_out * normed, axis=0, keepdims=True)
    return grad_in, gain_sum, jnp.sum(grad_out, axis=0, keepdims=True)


def heads_of(projected, offset):
    return [
        projected[:, offset + i * HEAD_DIM : offset + (i + 1) * HEAD_DIM] for i in range(HEADS_CHIP)
    ]


def softmax_rows(queries, keys, keep):
    raw = jnp.concatenate([mm_t(q, k) for q, k in zip(queries, keys)], axis=0)
    masked = jnp.where(keep, raw * SCALE, -1e30)
    grown = jnp.exp(masked - jnp.max(masked, axis=-1, keepdims=True))
    return grown * (1.0 / jnp.sum(grown, axis=-1, keepdims=True))


def keep_of(mask):
    return jnp.concatenate([mask.astype(f32)] * HEADS_CHIP, axis=0) > 0.5


def attend(projected, mask):
    rows = mask.shape[0]
    probs = softmax_rows(heads_of(projected, 0), heads_of(projected, D_CHIP), keep_of(mask))
    probs = probs.astype(bf16)
    out = [
        mm(probs[i * rows : (i + 1) * rows], value)
        for i, value in enumerate(heads_of(projected, 2 * D_CHIP))
    ]
    return jnp.concatenate(out, axis=1).astype(bf16)


def attend_back(projected, mask, grad_context):
    rows = mask.shape[0]
    queries, keys, values = (heads_of(projected, i * D_CHIP) for i in range(3))
    grads = heads_of(grad_context, 0)
    probs = softmax_rows(queries, keys, keep_of(mask))
    grad_probs = jnp.concatenate([mm_t(g, v) for g, v in zip(grads, values)], axis=0)
    along = jnp.sum(grad_probs * probs, axis=-1, keepdims=True)
    grad_scores = (probs * (grad_probs - along) * SCALE).astype(bf16)
    probs = probs.astype(bf16)

    def cut(stack, i):
        return stack[i * rows : (i + 1) * rows]

    out = (
        [mm(cut(grad_scores, i), keys[i]) for i in range(HEADS_CHIP)]
        + [t_mm(cut(grad_scores, i), queries[i]) for i in range(HEADS_CHIP)]
        + [t_mm(cut(probs, i), grads[i]) for i in range(HEADS_CHIP)]
    )
    return jnp.concatenate(out, axis=1).astype(bf16)


HALF = SHARE // 2
EXTRA = 8
FLAG_ROWS = 16
ROWS_Z = 2 * SHARE


def call(kernel, name, kinds, out_shapes, scratch=(), vmem=16):
    specs = {"s": SMEM, "h": HBM, "v": VMEM}
    made = pl.pallas_call(
        kernel,
        in_specs=[specs[kind] for kind in kinds],
        out_specs=[VMEM] * len(out_shapes),
        out_shape=[jax.ShapeDtypeStruct(shape, kind) for shape, kind in out_shapes],
        scratch_shapes=list(scratch),
        compiler_params=pltpu.CompilerParams(vmem_limit_bytes=vmem * 2**20),
        cost_estimate=COST,
        name=name,
    )

    def run(*args):
        placed = [
            pltpu.with_memory_space_constraint(arg, pltpu.HBM) if kind == "h" else arg
            for kind, arg in zip(kinds, args, strict=True)
        ]
        return made(*placed)

    return run


def sems(count):
    return pltpu.SemaphoreType.DMA((count,))


def row_at(i, size):
    return pl.ds(pl.multiple_of(i * size, size), size)


def tiled(width, tile, body):
    @pl.loop(0, width // tile)
    def _(i):
        body(row_at(i, tile))


def stack_blocks(blocks, whole):
    rows = blocks[0].shape[0]
    for i, block in enumerate(blocks):
        whole[i * rows : (i + 1) * rows, :] = block[...]


def row_of(spot, i, of_core, half=None):
    row = (2 * (spot[0] ^ i) + of_core) * SHARE
    if half is None:
        return pl.ds(pl.multiple_of(row, SHARE), SHARE)
    return pl.ds(pl.multiple_of(row + half * HALF, HALF), HALF)


def stack_columns(spot, mine, other, whole):
    core, side = spot[1], spot[2]
    for of_core, (own, near, far) in ((core, mine), (1 - core, other)):
        whole[row_of(spot, 0, of_core), :] = own[:SHARE, :]
        for i in range(1, CHIPS):
            rows = slice((i - 1) * HALF, i * HALF)
            whole[row_of(spot, i, of_core, side), :] = near[rows, :]
            whole[row_of(spot, i, of_core, 1 - side), :] = far[rows, :]


def by_core_copies(core, mine, other, whole, sem):
    size = mine.shape[0]
    return [
        pltpu.make_async_copy(mine, whole.at[row_at(core, size)], sem.at[0]),
        pltpu.make_async_copy(other, whole.at[row_at(1 - core, size)], sem.at[1]),
    ]


def start_all(copies):
    for copy in copies:
        copy.start()


def wait_all(copies):
    for copy in copies:
        copy.wait()


def chip_columns(weights, rows, chip):
    start = pl.multiple_of((chip * 5 // 2) * 128, 128)
    odd = lax.rem(chip, 2) == 1
    out = []
    for kind in range(3):
        window = weights[rows, pl.ds(kind * D + start, 384)]
        out.append(jnp.where(odd, window[:, 64 : 64 + D_CHIP], window[:, :D_CHIP]))
    return jnp.concatenate(out, axis=1)


def qkv_blocks_kernel(spot, lengths, padding, weights, *refs):
    vectors, own, sent = refs[:9], refs[9], refs[10 : 9 + CHIPS]
    flag, role, refs = refs[9 + CHIPS], refs[10 + CHIPS], refs[11 + CHIPS :]
    held, marks, whole, vector_sems, sem = refs[:9], *refs[9:]
    flag[...] = jnp.full(flag.shape, spot[3].astype(f32), f32).astype(bf16)
    for i in range(3):
        role[i : i + 1, :] = jnp.full((1, 128), spot[i].astype(f32), f32)
    role[3:, :] = jnp.zeros((5, 128), f32)
    copies = [
        pltpu.make_async_copy(vector, here, vector_sems.at[i])
        for i, (vector, here) in enumerate(zip(vectors, held))
    ]
    copies.append(pltpu.make_async_copy(padding, marks, sem.at[0]))
    copies.append(pltpu.make_async_copy(weights, whole, sem.at[1]))
    start_all(copies)
    wait_all(copies)
    rows = padding.shape[-1]
    place = lax.broadcasted_iota(jnp.int32, (1, rows), 1)
    first = lengths[0, 0]
    member = (place >= first).astype(f32)
    leading = (place == 0) | (place == first)
    usable = jnp.where(leading | (marks[...].reshape(1, rows) > 0), 1.0, 0.0)
    code = 2.0 * member + usable
    width = 3 * D_CHIP
    lines = [v[...].astype(f32).reshape(1, -1) for v in held]
    extra = jnp.concatenate(
        [
            jnp.concatenate(lines[:6], axis=1),
            jnp.concatenate(lines[6:], axis=1),
            jnp.concatenate([code, jnp.zeros((1, width - rows), f32)], axis=1),
            jnp.zeros((EXTRA - 3, width), f32),
        ],
        axis=0,
    ).astype(bf16)
    own[:SHARE, :] = chip_columns(whole, slice(None), spot[0])
    own[SHARE:, :] = extra
    for i, block in enumerate(sent):
        block[:HALF, :] = chip_columns(whole, row_at(spot[2], HALF), spot[0] ^ (i + 1))
        block[HALF:, :] = extra


def qkv_blocks(spot, lengths, padding, weights, vectors):
    half = ((HALF + EXTRA, 3 * D_CHIP), bf16)
    return call(
        qkv_blocks_kernel,
        "qkv_blocks",
        "ss" + "h" * 11,
        [((SHARE + EXTRA, 3 * D_CHIP), bf16)] + [half] * (CHIPS - 1) + [((FLAG_ROWS, D), bf16), ((8, 128), f32)],
        [pltpu.VMEM(v.shape, v.dtype) for v in vectors]
        + [
            pltpu.VMEM(padding.shape, padding.dtype),
            pltpu.VMEM(weights.shape, weights.dtype),
            sems(9),
            sems(2),
        ],
    )(spot, lengths, padding, weights, *vectors)


def qkv_join_kernel(own, q1, q2, q3, x1, x2, near, near_half, first, second):
    size = first.shape[0]
    first[...] = x1[:size, :]
    second[...] = x2[size:, :]
    near[:SHARE, :] = own[:SHARE, :]
    low = SHARE + 3 * HALF
    near[low : low + EXTRA, :] = own[SHARE:, :]
    for i, block in enumerate((q1, q2, q3)):
        near[SHARE + i * HALF : SHARE + (i + 1) * HALF, :] = block[:HALF, :]
        near_half[i * HALF : (i + 1) * HALF, :] = block[:HALF, :]
        low += EXTRA
        near[low : low + EXTRA, :] = block[HALF:, :]


def qkv_join(blocks, x1, x2):
    width = blocks[0].shape[-1]
    half = ((x1.shape[0] // 2, x1.shape[1]), x1.dtype)
    return call(
        qkv_join_kernel,
        "qkv_join",
        "v" * 6,
        [
            ((SHARE + 3 * HALF + CHIPS * EXTRA, width), bf16),
            ((3 * HALF, width), bf16),
            half,
            half,
        ],
    )(*blocks, x1, x2)


def up_blocks_kernel(spot, weights, cotangent, own, *sent):
    def columns(chip):
        return pl.ds(pl.multiple_of(chip * FF_CHIP, FF_CHIP), FF_CHIP)

    own[...] = weights[:, columns(spot[0])]
    for i, block in enumerate(sent):
        block[:HALF, :] = weights[row_at(spot[2], HALF), columns(spot[0] ^ (i + 1))]
    for block in sent[:2]:
        block[HALF:, :] = cotangent[...]


def up_blocks(spot, weights, cotangent):
    both = HALF + cotangent.shape[0]
    sizes = (SHARE, both, both, HALF)
    return call(up_blocks_kernel, "up_blocks", "svv", [((size, FF_CHIP), bf16) for size in sizes])(
        spot, weights, cotangent
    )


def up_join_kernel(cotangent, u1, u2, u3, near, whole, first, second):
    rows = cotangent.shape[0]
    for i, block in enumerate((cotangent, u1.at[HALF:], u2.at[HALF:])):
        whole[i * rows : (i + 1) * rows, :] = block[...]
    for i, block in enumerate((u1, u2, u3)):
        near[i * HALF : (i + 1) * HALF, :] = block[:HALF, :]
    half = rows // 2
    first[...] = u1[HALF : HALF + half, :]
    second[...] = u2[HALF + half :, :]


def up_join(cotangent, blocks):
    rows = cotangent.shape[0]
    near = ((3 * HALF, FF_CHIP), bf16)
    passed = ((rows // 2, D), bf16)
    return call(
        up_join_kernel,
        "up_join",
        "vvvv",
        [near, (((CHIPS - 1) * rows, D), bf16), passed, passed],
    )(cotangent, *blocks)


def halves_kernel(whole, first, second):
    size = first.shape[0]
    first[...] = whole[:size, :]
    second[...] = whole[size:, :]


def halves(whole):
    shape = (whole.shape[0] // 2, whole.shape[1])
    return call(halves_kernel, "halves", "v", [(shape, whole.dtype)] * 2)(whole)


def join_kernel(*refs):
    stack_blocks(refs[:-1], refs[-1])


def join(blocks):
    rows, width = blocks[0].shape
    count = len(blocks)
    return call(join_kernel, "join", "v" * count, [((count * rows, width), blocks[0].dtype)])(
        *blocks
    )[0]


def fill_table(spot, extras, table, mask):
    chip, core = spot[0], spot[1]
    rows = mask.shape[1]
    table[...] = jnp.zeros_like(table)
    for team in range(TEAM):
        for i in range(6):
            table[i : i + 1, team * SHARE : (team + 1) * SHARE] = extras[
                team, 0:1, i * SHARE : (i + 1) * SHARE
            ]
    for half in range(2):
        line = extras[2 * chip + half, 1:2, :]
        lo = half * SHARE
        table[BIAS_QKV : BIAS_QKV + 1, lo : lo + SHARE] = line[:, :SHARE]
        table[BIAS_QKV : BIAS_QKV + 1, 2 * D_CHIP + lo : 2 * D_CHIP + lo + SHARE] = line[
            :, SHARE : 2 * SHARE
        ]
        table[BIAS_UP : BIAS_UP + 1, half * FF_SHARE : (half + 1) * FF_SHARE] = line[:, 2 * SHARE :]
    for i in range(CHIPS):
        code = extras[2 * (chip ^ i) + core, 2:3, :rows]
        of_key = jnp.broadcast_to(code, (rows, rows))
        cell_of_key = jnp.floor(of_key * 0.5)
        open_key = of_key - 2.0 * cell_of_key
        keep = jnp.where(cell_of_key == cell_of_key.T, open_key, 0.0)
        mask[i * rows : (i + 1) * rows, :] = keep.astype(bf16)


def token_norm_kernel(*refs):
    blocks, normed = refs[:-1], refs[-1]
    at = 0
    for x in blocks:
        rows = x.shape[0]
        normed[at : at + rows, :] = normalize(x[...].astype(f32))[0]
        at += rows


def token_norm(blocks):
    rows, width = blocks[0].shape
    shape = (CHIPS * rows, width)
    return call(token_norm_kernel, "token_norm", "v" * len(blocks), [(shape, f32)])(*blocks)[0]


def enter_kernel(spot, normed, *refs):
    mine, other, refs = refs[:2], refs[2:4], refs[4:]
    out_mine, out_other, refs = *refs[:2], refs[2:]
    table, mask, qkv, out, first_low, projected, context = refs[:7]
    partials = refs[7 : 8 + CHIPS]
    extras, out_sems = refs[8 + CHIPS :]
    rows = mask.shape[1]
    out_copies = by_core_copies(spot[1], out_mine, out_other, out, out_sems)
    start_all(out_copies)
    low = SHARE + 3 * HALF
    for of_core, lines in ((spot[1], mine[0]), (1 - spot[1], other[0])):
        for i in range(CHIPS):
            at = slice(low + i * EXTRA, low + (i + 1) * EXTRA)
            extras[2 * (spot[0] ^ i) + of_core] = lines[at, :].astype(f32)
    fill_table(spot, extras, table, mask)
    columns = [(near, near.at[SHARE:], far) for near, far in (mine, other)]
    stack_columns(spot, *columns, qkv)
    gain = table[GAIN1 : GAIN1 + 1, :]
    bias = table[BIAS1 : BIAS1 + 1, :]
    first_low[...] = (normed[...] * gain + bias).astype(bf16)
    for lo, hi in ((0, 384), (384, 768), (768, 960)):
        shift = table[BIAS_QKV : BIAS_QKV + 1, lo:hi]
        projected[:, lo:hi] = (mm(first_low[...], qkv[:, lo:hi]) + shift).astype(bf16)

    @pl.loop(0, CHIPS)
    def _(i):
        at = row_at(i, rows)
        context[at, :] = attend(projected[at, :], mask[at, :])

    wait_all(out_copies)

    def partial(at):
        whole = mm(context[...], out[:, at]).astype(bf16)
        lo = 0
        for part in partials:
            part[:, at] = whole[lo : lo + part.shape[0]]
            lo += part.shape[0]

    tiled(D, 256, partial)


def enter(spot, normed, mine, other, out_mine, out_other):
    total = normed.shape[0]
    rows = total // CHIPS
    outs = call(
        enter_kernel,
        "enter",
        "sv" + "v" * 4 + "hv",
        [
            ((TABLE_ROWS, D), f32),
            ((total, rows), bf16),
            ((D, 3 * D_CHIP), bf16),
            ((D_CHIP, D), bf16),
            ((total, D), bf16),
            ((total, 3 * D_CHIP), bf16),
            ((total, D_CHIP), bf16),
        ]
        + [((rows, D), bf16)] * (CHIPS - 1)
        + [((rows // 2, D), bf16)] * 2,
        [pltpu.VMEM((TEAM, EXTRA, 3 * D_CHIP), f32), sems(2)],
    )(spot, normed, *mine, *other, out_mine, out_other)
    return outs[:7], outs[7:]


def leave_kernel(
    b0, b1, b2, b3, qkv, out, projected, mask, branch, grad_projected, bias_sum, *refs
):
    partials, grad_context = refs[:CHIPS], refs[CHIPS]
    rows = b0.shape[0]
    stack_blocks((b0, b1, b2, b3), branch)
    grad_context[...] = mm_t(branch[...], out[...]).astype(bf16)
    bias_sum[...] = jnp.zeros_like(bias_sum)

    @pl.loop(0, CHIPS)
    def _(i):
        at = row_at(i, rows)
        grad = attend_back(projected[at, :], mask[at, :], grad_context[at, :])
        grad_projected[at, :] = grad
        bias_sum[...] += jnp.sum(grad.astype(f32), axis=0, keepdims=True)

    def partial(at):
        whole = mm_t(grad_projected[...], qkv[at, :]).astype(bf16)
        for i, part in enumerate(partials):
            part[:, at] = whole[i * rows : (i + 1) * rows]

    tiled(D, 256, partial)


def leave(blocks, qkv, out, projected, mask):
    rows = blocks[0].shape[0]
    total = CHIPS * rows
    outs = call(
        leave_kernel,
        "leave",
        "v" * 8,
        [((total, D), bf16), ((total, 3 * D_CHIP), bf16), ((1, 3 * D_CHIP), f32)]
        + [((rows, D), bf16)] * CHIPS,
        [pltpu.VMEM((total, D_CHIP), bf16)],
    )(*blocks, qkv, out, projected, mask)
    return outs[:3], outs[3:]


def total_of(parts):
    total = parts[0][...].astype(f32)
    for part in parts[1:]:
        total = total + part[...].astype(f32)
    return total


def pass_on_kernel(p1, p2, h1, h2, sum1, sum2):
    size = h1.shape[0]
    sum1[:size, :] = (p1[:size, :].astype(f32) + h1[...].astype(f32)).astype(bf16)
    sum1[size:, :] = p1[size:, :]
    sum2[:size, :] = p2[:size, :]
    sum2[size:, :] = (p2[size:, :].astype(f32) + h2[...].astype(f32)).astype(bf16)


def pass_on(p1, p2, h1, h2):
    return call(pass_on_kernel, "pass_on", "vvvv", [(p1.shape, bf16)] * 2)(p1, p2, h1, h2)


def mix_kernel(p0, p1, p2, tokens, table, mixed, second):
    total = total_of((p0, p1, p2)) + tokens[...].astype(f32)
    total = total + table[BIAS_OUT : BIAS_OUT + 1, :]
    mixed[...] = total
    normed, _ = normalize(total)
    second[...] = (normed * table[GAIN2 : GAIN2 + 1, :] + table[BIAS2 : BIAS2 + 1, :]).astype(bf16)


def mix(parts, tokens, table):
    shape = tokens.shape
    return call(mix_kernel, "mix", "v" * 5, [(shape, f32), (shape, bf16)])(*parts, tokens, table)


def unmix_kernel(p0, p1, p2, p3, mixed, table, cotangent, grad_mixed, branch, sums):
    grad = total_of((p0, p1, p2, p3))
    normed, inverse = normalize(mixed[...])
    grad_in, gain_sum, bias_sum = norm_backward(grad, normed, inverse, table[GAIN2 : GAIN2 + 1, :])
    grad_out = cotangent[...].astype(f32)
    grad_in = grad_in + grad_out
    grad_mixed[...] = grad_in
    low = grad_in.astype(bf16)
    branch[...] = low
    sums[...] = jnp.zeros_like(sums)
    sums[0:1, :] = jnp.sum(low.astype(f32), axis=0, keepdims=True)
    sums[1:2, :] = gain_sum
    sums[2:3, :] = bias_sum
    sums[3:4, :] = jnp.sum(grad_out, axis=0, keepdims=True)


def unmix(parts, mixed, table, cotangent):
    shape = cotangent.shape
    return call(
        unmix_kernel, "unmix", "v" * 7, [(shape, f32), (shape, bf16), ((8, D), f32)]
    )(*parts, mixed, table, cotangent)


def act_grad_kernel(spot, part, g1, g2, mine, other, grad_act, down, whole, down_sems):
    copies = by_core_copies(spot[1], mine, other, down, down_sems)
    start_all(copies)
    at = 0
    for block in (part, g1, g2):
        whole[at : at + block.shape[0], :] = block[...]
        at += block.shape[0]
    wait_all(copies)

    def columns(at):
        grad_act[:, at] = mm_t(whole[...], down[at, :])

    tiled(FF_CHIP, 256, columns)


def act_grad(spot, part, passed, down_mine, down_other):
    total = part.shape[0] // (CHIPS - 1) * CHIPS
    return call(
        act_grad_kernel,
        "act_grad",
        "svvvhv",
        [((total, FF_CHIP), f32), ((FF_CHIP, D), bf16), ((total, D), bf16)],
        [sems(2)],
    )(spot, part, *passed, down_mine, down_other)


def number(role, i):
    return jnp.max(role[i : i + 1, :]).astype(jnp.int32)


def hidden_rows(at, second, up, table, grad_act, pre_act, act, grad_pre, bias_sum):
    size = at.stop - at.start

    def columns(tile):
        pre_act[at, tile] = mm(second[at, :], up[:, tile]) + table[BIAS_UP : BIAS_UP + 1, tile]

    tiled(FF_CHIP, 640, columns)

    @pl.loop(0, size // 64)
    def _(i):
        rows = pl.ds(pl.multiple_of(at.start + i * 64, 64), 64)
        pre = pre_act[rows, :]
        below = 0.5 * (1.0 + lax.erf(pre * (0.5**0.5)))
        bell = jnp.exp(-0.5 * pre * pre) * 0.3989422804014327
        act[rows, :] = (pre * below).astype(bf16)
        grad = (grad_act[rows, :] * (below + pre * bell)).astype(bf16)
        grad_pre[rows, :] = grad
        bias_sum[...] += jnp.sum(grad.astype(f32), axis=0, keepdims=True)


def hidden_first_kernel(spot, s0, s1, s2, grad_act, table, *refs):
    columns = [(own, rest, rest.at[3 * HALF :]) for own, rest in (refs[:2], refs[2:4])]
    second, act, grad_pre, bias_sum, up = refs[4:9]
    partials, pre_act = refs[9:12], refs[12]
    rows = s0.shape[0]
    stack_columns(spot, *columns, up)
    stack_blocks((s0, s1, s2), second)
    bias_sum[...] = jnp.zeros_like(bias_sum)
    hidden_rows(
        slice(0, 3 * rows), second, up, table, grad_act, pre_act, act, grad_pre, bias_sum
    )
    second_partials(slice(0, 3 * rows), grad_pre, up, partials)


def second_partials(at, grad_pre, up, partials):
    rows = partials[0].shape[0]

    def columns(tile):
        whole = mm_t(grad_pre[at, :], up[tile, :]).astype(bf16)
        for i, part in enumerate(partials):
            part[:, tile] = whole[i * rows : (i + 1) * rows]

    tiled(D, 640, columns)


def hidden_first(spot, blocks, grad_act, table, mine, other):
    total = grad_act.shape[0]
    return call(
        hidden_first_kernel,
        "hidden_first",
        "svvvvv" + "v" * 4,
        [
            ((total, D), bf16),
            ((total, FF_CHIP), bf16),
            ((total, FF_CHIP), bf16),
            ((1, FF_CHIP), f32),
            ((D, FF_CHIP), bf16),
        ]
        + [((total // CHIPS, D), bf16)] * 3,
        [pltpu.VMEM((total, FF_CHIP), f32)],
    )(spot, *blocks, grad_act, table, *mine, *other)


def hidden_last_kernel(
    role,
    s3,
    grad_act,
    table,
    cotangent,
    up,
    second_in,
    act_in,
    grad_pre_in,
    bias_in,
    second,
    act,
    grad_pre,
    bias_sum,
    down_sent,
    pre_act,
):
    del second_in, act_in, grad_pre_in
    rows = s3.shape[0]
    at = slice(3 * rows, 4 * rows)
    second[at, :] = s3[...]
    bias_sum[...] = bias_in[...]
    hidden_rows(at, second, up, table, grad_act, pre_act, act, grad_pre, bias_sum)
    down_product(act, cotangent, 1 - number(role, 1), 0, down_sent)


def down_product(act, cotangent, of_core, half, target):
    low = half * ROWS_Z
    aligned = low // 128 * 128
    if half == 0:
        units = pl.ds(pl.multiple_of(of_core * FF_SHARE, 128), ROWS_Z)
        target[...] = t_mm(act[:, units], cotangent[...]).astype(target.dtype)
    else:
        units = pl.ds(pl.multiple_of(of_core * FF_SHARE + aligned, 128), FF_SHARE - aligned)
        window = act[:, units][:, low - aligned :]
        target[...] = t_mm(window, cotangent[...]).astype(target.dtype)


def up_product(second, grad_pre, pair, of_core, target, work):
    for i in range(2):
        first = (2 * (2 * pair + i) + of_core) * SHARE
        aligned = pl.multiple_of(first // 128 * 128, 128)
        work[...] = t_mm(second[:, pl.ds(aligned, 256)], grad_pre[...])
        start = pl.multiple_of(lax.rem(first, 128), 32)
        target[i * SHARE : (i + 1) * SHARE, :] = work[pl.ds(start, SHARE), :].astype(target.dtype)


def hidden_last(role, block, grad_act, table, cotangent, up, second, act, grad_pre, bias_sum):
    total = second.shape[0]
    return pl.pallas_call(
        hidden_last_kernel,
        in_specs=[VMEM] * 10,
        out_specs=[VMEM] * 5,
        out_shape=[
            jax.ShapeDtypeStruct(second.shape, bf16),
            jax.ShapeDtypeStruct(act.shape, bf16),
            jax.ShapeDtypeStruct(grad_pre.shape, bf16),
            jax.ShapeDtypeStruct(bias_sum.shape, f32),
            jax.ShapeDtypeStruct((ROWS_Z, D), bf16),
        ],
        scratch_shapes=[pltpu.VMEM((total, FF_CHIP), f32)],
        input_output_aliases={6: 0, 7: 1, 8: 2},
        compiler_params=pltpu.CompilerParams(vmem_limit_bytes=16 * 2**20),
        cost_estimate=COST,
        name="hidden_last",
    )(role, block, grad_act, table, cotangent, up, second, act, grad_pre, bias_sum)


def second_last_kernel(grad_pre, up, partial):
    rows = partial.shape[0]
    second_partials(slice(grad_pre.shape[0] - rows, grad_pre.shape[0]), grad_pre, up, (partial,))


def second_last(grad_pre, up):
    rows = grad_pre.shape[0] // CHIPS
    return call(second_last_kernel, "second_last", "vv", [((rows, D), bf16)])(grad_pre, up)[0]


def up_sent_kernel(role, grad_pre, second, up_sent, work):
    up_product(second, grad_pre, 0, 1 - number(role, 1), up_sent, work)


def up_sent_of(role, grad_pre, second):
    return call(
        up_sent_kernel,
        "up_sent",
        "vvv",
        [((ROWS_Z, FF_CHIP), bf16)],
        [pltpu.VMEM((256, FF_CHIP), f32)],
    )(role, grad_pre, second)[0]


def split_rows(core, whole, sent, kept):
    for k in range(CHIPS):
        targets = ((sent[k // 2], k % 2, 1 - core), (kept, k, core))
        for target, at, of_core in targets:
            start = pl.multiple_of((2 * k + of_core) * SHARE, SHARE)
            target[at] = whole[pl.ds(start, SHARE), :].astype(bf16)


def down_grad_kernel(role, act, cotangent, got, total):
    down_product(act, cotangent, number(role, 1), 0, total)
    total[...] = (total[...].astype(f32) + got[...].astype(f32)).astype(bf16)


def down_grad_of(role, act, cotangent, got):
    return call(down_grad_kernel, "down_grad", "vvvv", [((ROWS_Z, D), bf16)])(
        role, act, cotangent, got
    )[0]


def rest_kernel(
    spot, second, grad_pre, act, cotangent, up_a, up_b, up_sent, down_b, down_sent, work
):
    core = spot[1]
    up_product(second, grad_pre, 0, core, up_a, work)
    up_product(second, grad_pre, 1, 1 - core, up_sent, work)
    up_product(second, grad_pre, 1, core, up_b, work)
    down_product(act, cotangent, 1 - core, 1, down_sent)
    down_product(act, cotangent, core, 1, down_b)


def rest_of_grads(spot, second, grad_pre, act, cotangent):
    return call(
        rest_kernel,
        "rest",
        "svvvv",
        [((ROWS_Z, D), bf16)] * 5,
        [pltpu.VMEM((256, FF_CHIP), f32)],
    )(spot, second, grad_pre, act, cotangent)


def result_kernel(act, down, *partials):
    rows = partials[0].shape[0]

    def columns(at):
        whole = mm(act[...], down[:, at]).astype(bf16)
        for i, part in enumerate(partials):
            part[:, at] = whole[i * rows : (i + 1) * rows]

    tiled(D, 256, columns)


def result_of(act, down):
    rows = act.shape[0] // CHIPS
    return call(result_kernel, "result", "vv", [((rows, D), bf16)] * CHIPS)(act, down)


def qkv_grad_kernel(
    spot,
    first_low,
    grad_projected,
    context,
    branch,
    sent_a,
    sent_b,
    kept,
    out_sent,
    out_kept,
    whole,
    out,
):
    core = spot[1]

    def columns(at):
        whole[at, :] = t_mm(first_low[:, at], grad_projected[...])

    tiled(D, 256, columns)
    split_rows(core, whole, (sent_a, sent_b), kept)
    out[...] = t_mm(context[...], branch[...])
    for target, of_core in ((out_sent, 1 - core), (out_kept, core)):
        target[...] = out[row_at(of_core, SHARE), :].astype(bf16)


def qkv_grad_of(spot, first_low, grad_projected, context, branch):
    half = ((CHIPS // 2, SHARE, 3 * D_CHIP), bf16)
    rows = ((SHARE, D), bf16)
    return call(
        qkv_grad_kernel,
        "qkv_grad",
        "svvvv",
        [half, half, ((CHIPS, SHARE, 3 * D_CHIP), bf16), rows, rows],
        [pltpu.VMEM((D, 3 * D_CHIP), f32), pltpu.VMEM((D_CHIP, D), f32)],
    )(spot, first_low, grad_projected, context, branch)


def add_kernel(*refs):
    count = len(refs) // 3
    for a, b, c in zip(refs[:count], refs[count : 2 * count], refs[2 * count :]):
        c[...] = a[...] + b[...]


def add_all(left, right):
    shapes = [(a.shape, a.dtype) for a in left]
    return call(add_kernel, "add", "v" * (2 * len(left)), shapes)(*left, *right)


PACKED = SHARE * 3 // 4
STEP = SHARE // 4


def sum_all_kernel(a, b, c, d, total):
    total[...] = (a[...] + b[...]) + (c[...] + d[...])


def sum_all(parts):
    shape = (parts[0].shape, parts[0].dtype)
    return call(sum_all_kernel, "sum_all", "vvvv", [shape])(*parts)[0]


def pack_kernel(kept, got_a, got_b, out_kept, out_got, *chunks):
    for i, chunk in enumerate(chunks):
        for j in range(2):
            got = got_b if i else got_a
            total = (kept[2 * i + j].astype(f32) + got[j].astype(f32)).astype(bf16)
            lo = j * PACKED
            chunk[lo : lo + PACKED, : 3 * D_CHIP] = total[:PACKED]
            for part in range(3):
                at = lo + part * STEP
                chunk[at : at + STEP, 3 * D_CHIP :] = total[
                    PACKED:, part * D_CHIP : (part + 1) * D_CHIP
                ]
        rows = slice(i * HALF, (i + 1) * HALF)
        total = out_kept[rows, :].astype(f32) + out_got[rows, :].astype(f32)
        chunk[2 * PACKED :, :] = total.astype(bf16)


def pack(kept, got_a, got_b, out_kept, out_got):
    return call(pack_kernel, "pack", "vvvvv", [((ROWS_Z, D), bf16)] * 2)(
        kept, got_a, got_b, out_kept, out_got
    )


def unpacked(chunk, j):
    lo = j * PACKED
    tail = [
        chunk[lo + part * STEP : lo + (part + 1) * STEP, 3 * D_CHIP :] for part in range(3)
    ]
    return jnp.concatenate(
        [chunk[lo : lo + PACKED, : 3 * D_CHIP], jnp.concatenate(tail, axis=1)], axis=0
    )


def z_half(low, got_side):
    return add_all([low], [got_side])[0]


def z_send_kernel(flag, half, got_middle, low, sent):
    middle = flag[...] > 0.5
    for i in range(ROWS_Z // FLAG_ROWS):
        rows = slice(i * FLAG_ROWS, (i + 1) * FLAG_ROWS)
        sent[rows, :] = jnp.where(middle, half[rows, :] + got_middle[rows, :], low[rows, :])


def z_send(flag, half, got_middle, low):
    return call(z_send_kernel, "z_send", "vvvv", [(low.shape, bf16)])(flag, half, got_middle, low)[0]


def z_final_kernel(spot, sent, got_side, final):
    final[...] = jnp.where(spot[3] > 0, sent[...], got_side[...])


def z_final(spot, sent, got_side):
    return call(z_final_kernel, "z_final", "svv", [(sent.shape, bf16)])(spot, sent, got_side)[0]


def first_down_kernel(spot, sent, got, down, here, sem):
    here[...] = jnp.where(spot[3] > 0, sent[...], got[...]).astype(f32)
    copy = pltpu.make_async_copy(here, down.at[:ROWS_Z], sem.at[0])
    copy.start()
    copy.wait()


def first_down(spot, sent, got):
    return pl.pallas_call(
        first_down_kernel,
        in_specs=[SMEM, VMEM, VMEM],
        out_specs=HBM,
        out_shape=pltpu.HBM((2 * ROWS_Z, D), f32),
        scratch_shapes=[pltpu.VMEM((ROWS_Z, D), f32), sems(1)],
        compiler_params=pltpu.CompilerParams(vmem_limit_bytes=16 * 2**20),
        cost_estimate=COST,
        name="first_down",
    )(spot, sent, got)


def second_down_kernel(flag, sent, got, before, down, here, sem):
    del before
    copies = []
    middle = flag[...] > 0.5
    for i in range(2):
        for lo in range(i * SHARE, (i + 1) * SHARE, FLAG_ROWS):
            rows = slice(lo, lo + FLAG_ROWS)
            here[rows, :] = jnp.where(middle, sent[rows, :], got[rows, :]).astype(f32)
        rows = slice(i * SHARE, (i + 1) * SHARE)
        target = down.at[ROWS_Z + i * SHARE : ROWS_Z + (i + 1) * SHARE]
        copies.append(pltpu.make_async_copy(here.at[rows], target, sem.at[i]))
        copies[-1].start()
    wait_all(copies)


def second_down(flag, sent, got, down):
    return pl.pallas_call(
        second_down_kernel,
        in_specs=[VMEM, VMEM, VMEM, HBM],
        out_specs=HBM,
        out_shape=pltpu.HBM((2 * ROWS_Z, D), f32),
        scratch_shapes=[pltpu.VMEM((ROWS_Z, D), f32), sems(2)],
        input_output_aliases={3: 0},
        compiler_params=pltpu.CompilerParams(vmem_limit_bytes=16 * 2**20),
        cost_estimate=COST,
        name="second_down",
    )(flag, sent, got, pltpu.with_memory_space_constraint(down, pltpu.HBM))


def qkv_rows_kernel(spot, b0, b1, b2, b3, qkv, rows, stack, sem):
    for i, block in enumerate((b0, b1, b2, b3)):
        stack[spot[0] ^ i] = block[...]
    copies = []
    for kind in range(3):
        for chip in range(CHIPS):
            lo = kind * D + chip * D_CHIP
            rows[:, lo : lo + D_CHIP] = stack[
                chip, :, kind * D_CHIP : (kind + 1) * D_CHIP
            ].astype(f32)
        at = slice(kind * D, (kind + 1) * D)
        copies.append(pltpu.make_async_copy(rows.at[:, at], qkv.at[:, at], sem.at[kind]))
        copies[-1].start()
    wait_all(copies)


def qkv_rows(spot, blocks):
    shape = blocks[0].shape
    return pl.pallas_call(
        qkv_rows_kernel,
        in_specs=[SMEM] + [VMEM] * 4,
        out_specs=HBM,
        out_shape=pltpu.HBM((shape[0], 3 * D), f32),
        scratch_shapes=[
            pltpu.VMEM((shape[0], 3 * D), f32),
            pltpu.VMEM((CHIPS,) + shape, bf16),
            sems(3),
        ],
        compiler_params=pltpu.CompilerParams(vmem_limit_bytes=16 * 2**20),
        cost_estimate=COST,
        name="qkv_rows",
    )(spot, *blocks)


def owned_kernel(count, place, sums, got, *outs):
    total = sums[...] + got[...]
    index = place[0]
    size = outs[0].shape[0]
    mine = pltpu.roll(total, D - index * size, 1)
    for i, row in enumerate((0, 1, 2, 3, 4, 5, 8, 9)):
        outs[i][...] = mine[row : row + 1, :size].reshape(size)
    wide = outs[8].shape[0]
    first = index * wide
    row = first // D
    line = total[10:11, :]
    for k in range(1, CHIPS):
        line = jnp.where(row == k, total[10 + k : 11 + k, :], line)
    line = pltpu.roll(jnp.broadcast_to(line, (8, D)), D - lax.rem(first, D), 1)
    outs[8][...] = line[0:1, :wide].reshape(wide)
    mean = total[6:7, :] / count
    outs[9][...] = mean.reshape(D)
    outs[10][...] = (total[7:8, :] / count - mean * mean).reshape(D)


def owned(place, count, fsdp_count, sums, got):
    sizes = [D // fsdp_count] * 8 + [FF // fsdp_count, D, D]

    def kernel(*refs):
        owned_kernel(count, *refs)

    return call(kernel, "owned", "svv", [((size,), f32) for size in sizes])(place, sums, got)


def up_exchange_kernel(spot, a, b, *blocks):
    chunks = (a, b)
    for i, block in enumerate(blocks):
        chip = spot[0] ^ i
        at = row_at(lax.rem(chip, 2), SHARE)
        block[...] = jnp.where(chip >= 2, chunks[1][at, :], chunks[0][at, :])


def up_exchange(spot, a, b):
    return call(up_exchange_kernel, "up_exchange", "svv", [((SHARE, FF_CHIP), bf16)] * CHIPS)(
        spot, a, b
    )


def qkv_unpack_kernel(spot, sent, got_side, blocks, out_rows):
    chunk = jnp.where(spot[3] > 0, sent[...], got_side[...])
    for j in range(2):
        blocks[j] = unpacked(chunk, j)
    out_rows[...] = chunk[2 * PACKED :, :].astype(f32)


def qkv_unpack(spot, sent, got_side):
    return call(
        qkv_unpack_kernel,
        "qkv_unpack",
        "svv",
        [((2, SHARE, 3 * D_CHIP), bf16), ((HALF, D), f32)],
    )(spot, sent, got_side)


def qkv_exchange_kernel(spot, blocks_a, rows_a, sent, got_side, *refs):
    blocks, out_rows, stack = refs[:CHIPS], refs[CHIPS], refs[CHIPS + 1]
    chunk = jnp.where(spot[3] > 0, sent[...], got_side[...])
    stack[:2] = blocks_a[...]
    for j in range(2):
        stack[2 + j] = unpacked(chunk, j)
    out_rows[:HALF, :] = rows_a[...]
    out_rows[HALF:, :] = chunk[2 * PACKED :, :].astype(f32)
    for i, block in enumerate(blocks):
        block[...] = stack[spot[0] ^ i]


def qkv_exchange(spot, blocks_a, rows_a, sent, got_side):
    shape = (SHARE, 3 * D_CHIP)
    outs = call(
        qkv_exchange_kernel,
        "qkv_exchange",
        "svvvv",
        [(shape, bf16)] * CHIPS + [((SHARE, D), f32)],
        [pltpu.VMEM((CHIPS,) + shape, bf16)],
    )(spot, blocks_a, rows_a, sent, got_side)
    return outs[:CHIPS], outs[CHIPS]


def up_rows_kernel(spot, b0, b1, b2, b3, weights):
    for i, block in enumerate((b0, b1, b2, b3)):
        start = pl.multiple_of((spot[0] ^ i) * FF_CHIP, FF_CHIP)
        weights[:, pl.ds(start, FF_CHIP)] = block[...].astype(f32)


def up_rows(spot, blocks):
    return call(up_rows_kernel, "up_rows", "svvvv", [((SHARE, FF), f32)])(spot, *blocks)[0]


def end_kernel(
    spot,
    lengths,
    p0,
    p1,
    p2,
    p3,
    r0,
    r1,
    r2,
    r3,
    grad_mixed,
    tokens,
    table,
    mixed,
    mix_sums,
    qkv_sum,
    up_sum,
    layer_out,
    grad_tokens,
    sums,
):
    grad = total_of((p0, p1, p2, p3))
    normed, inverse = normalize(tokens[...].astype(f32))
    grad_in, gain_sum, bias_sum = norm_backward(grad, normed, inverse, table[GAIN1 : GAIN1 + 1, :])
    grad_tokens[...] = grad_mixed[...] + grad_in
    result = mixed[...] + total_of((r0, r1, r2, r3)) + table[BIAS_DOWN : BIAS_DOWN + 1, :]
    layer_out[...] = result.astype(bf16)
    place = lax.broadcasted_iota(jnp.int32, (result.shape[0], 1), 0)
    picked = jnp.where((place == 0) | (place == lengths[0, 0]), result, 0.0)
    sums[...] = jnp.zeros_like(sums)
    sums[0:1, :] = gain_sum
    sums[1:2, :] = bias_sum
    sums[2:6, :] = mix_sums[0:4, :]
    sums[6:7, :] = jnp.sum(picked, axis=0, keepdims=True)
    sums[7:8, :] = jnp.sum(picked * picked, axis=0, keepdims=True)
    for k in range(CHIPS):
        here = spot[0] == k
        lo = k * D_CHIP
        sums[8:9, lo : lo + D_CHIP] = jnp.where(here, qkv_sum[:, :D_CHIP], 0.0)
        sums[9:10, lo : lo + D_CHIP] = jnp.where(here, qkv_sum[:, 2 * D_CHIP :], 0.0)
        sums[10 + k : 11 + k, :] = jnp.where(here, up_sum[...], 0.0)


def end(spot, lengths, parts, results, *rest):
    shape = parts[0].shape
    return call(
        end_kernel,
        "end",
        "ss" + "v" * 15,
        [(shape, bf16), (shape, f32), ((SUM_ROWS, D), f32)],
    )(spot, lengths, *parts, *results, *rest)


def fence(*values):
    return lax.optimization_barrier(values)


def local(
    tokens,
    lengths,
    padding,
    ln1_gain,
    ln1_bias,
    w_qkv,
    b_query,
    b_value,
    w_out,
    b_out,
    ln2_gain,
    ln2_bias,
    w_up,
    b_up,
    w_down,
    b_down,
    cotangent,
):
    fsdp_count = lax.axis_size("fsdp")
    dp_count = lax.axis_size("dp")
    groups = fsdp_count // TEAM
    place = lax.axis_index("fsdp") // groups
    chip = place // 2
    core = place % 2
    depth = lax.axis_index("dp")
    middle = (depth == 1) | (depth == 2)
    spot = jnp.stack([chip, core, depth % 2, middle.astype(jnp.int32)]).astype(jnp.int32)

    def swap(value, mask):
        pairs = [
            (team * groups + group, (team ^ mask) * groups + group)
            for team in range(TEAM)
            for group in range(groups)
        ]
        return lax.ppermute(value, "fsdp", pairs)

    shard_groups = [[team * groups + group for group in range(groups)] for team in range(TEAM)]
    def gather_shards(value):
        if groups == 1:
            return value
        return lax.all_gather(value, "fsdp", axis=0, tiled=True, axis_index_groups=shard_groups)

    def scatter_shards(value):
        if groups == 1:
            return value
        return lax.psum_scatter(
            value, "fsdp", scatter_dimension=0, tiled=True, axis_index_groups=shard_groups
        )

    def along_z(pairs, value):
        return lax.ppermute(value, "dp", pairs)

    def z_swap(value):
        return along_z([(0, 1), (1, 0), (2, 3), (3, 2)], value)

    def z_middle(value):
        return along_z([(1, 2), (2, 1)], value)

    def from_chips(blocks):
        return [blocks[0]] + [swap(block, 2 * i) for i, block in enumerate(blocks) if i > 0]

    def fence_list(first, *others):
        done = fence(*first, *others)
        return list(done[: len(first)]), *done[len(first) :]

    w_qkv, w_out, w_up, w_down = (gather_shards(w) for w in (w_qkv, w_out, w_up, w_down))
    given = (ln1_gain, ln1_bias, b_out, ln2_gain, ln2_bias, b_down, b_query, b_value, b_up)
    *qkv_sent, flag, role = qkv_blocks(spot, lengths, padding, w_qkv, [gather_shards(v) for v in given])
    qkv_got = from_chips(qkv_sent)
    x1, x2, *qkv_got = fence(swap(tokens, 2), swap(tokens, 4), *qkv_got)
    qkv_near, qkv_half, x1_half, x2_half = qkv_join(qkv_got, x1, x2)
    qkv_far = z_swap(qkv_half)
    qkv_near_other = swap(qkv_near, 1)
    blocks = [tokens, x1, x2, swap(x1_half, 4), swap(x2_half, 2)]
    normed = token_norm(blocks)
    out_sent, _ = fence(w_out, qkv_near)
    out_other = swap(out_sent, 1)
    up_own, *up_sent = up_blocks(spot, w_up, cotangent)
    up_own, *up_sent = fence(up_own, *up_sent, qkv_near)[:-1]
    loads = [swap(block, 2 * i + 2) for i, block in enumerate(up_sent)]
    normed, qkv_far, qkv_near_other, out_other = fence(normed, qkv_far, qkv_near_other, out_other)
    qkv_far_other = join([swap(half, 1) for half in halves(qkv_far)])

    (table, mask, qkv, out, first_low, projected, context), partial_out = enter(
        spot,
        normed,
        [qkv_near, qkv_far],
        [qkv_near_other, qkv_far_other],
        w_out,
        out_other,
    )
    p0, p1, p2, h1, h2 = partial_out
    h1, h2 = swap(h1, 4), swap(h2, 2)
    cotangent_late, _ = fence(cotangent, partial_out[0])
    up_near, part, first, second = up_join(cotangent_late, loads)
    up_far = z_swap(up_near)
    passed = [swap(first, 4), swap(second, 2)]
    passed, h1, h2 = fence_list(passed, h1, h2)
    p1, p2 = pass_on(p1, p2, h1, h2)
    out_parts = [p0, swap(p1, 2), swap(p2, 4)]
    up_far, *out_parts = fence(up_far, *out_parts)
    mixed, second_own = mix(out_parts, tokens, table)
    second_blocks = from_chips([second_own] * CHIPS)
    up_far, _ = fence(up_far, second_own)
    up_rest = join([up_near, up_far])
    up_own_sent, _ = fence(up_own, second_own)
    up_other = [swap(up_own_sent, 1), swap(up_rest, 1)]
    down_sent, _ = fence(w_down, second_own)
    down_other = swap(down_sent, 1)
    part, down_other = fence(part, down_other)
    grad_act, down, whole_cotangent = act_grad(spot, part, passed, w_down, down_other)

    second_low, act_low, grad_pre, up_bias_sum, up, *partial_second = hidden_first(
        spot,
        second_blocks[:3],
        grad_act,
        table,
        [up_own, up_rest],
        up_other,
    )
    block, up_bias_sum = fence(second_blocks[3], up_bias_sum)
    second_low, act_low, grad_pre, up_bias_sum, down_sent = hidden_last(
        role, block, grad_act, table, whole_cotangent, up, second_low, act_low, grad_pre, up_bias_sum
    )
    down_got = swap(down_sent, 1)
    up_sent = up_sent_of(role, grad_pre, second_low)
    up_got = swap(up_sent, 1)
    act_low, up_sent = fence(act_low, up_sent)
    down_a = down_grad_of(role, act_low, whole_cotangent, down_got)
    side0 = z_swap(down_a)
    up_late, _ = fence(up, down_a)
    partial_second = partial_second + [second_last(grad_pre, up_late)]
    second_parts = from_chips(partial_second)
    second_low, _ = fence(second_low, partial_second[3])
    up_a, up_b, up_sent, down_b, down_sent = rest_of_grads(
        spot, second_low, grad_pre, act_low, whole_cotangent
    )
    up_got, up_sent = fence(up_got, up_sent)
    (up_a,) = add_all([up_a], [up_got])
    up_got = swap(up_sent, 1)

    second_parts, up_a = fence_list(second_parts, up_a)
    grad_mixed, branch_own, mix_sums = unmix(second_parts, mixed, table, cotangent)
    side0, _ = fence(side0, branch_own)
    half0 = z_half(down_a, side0)
    send1, _ = fence(up_a, half0)
    side1, middle1 = z_swap(send1), z_middle(half0)
    branch_blocks = from_chips([branch_own] * CHIPS)
    act_low, branch_own = fence(act_low, branch_own)
    partial_result = list(result_of(act_low, down))

    up_got, partial_result[0] = fence(up_got, partial_result[0])
    (up_b,) = add_all([up_b], [up_got])
    branch_blocks, side1, middle1, *partial_result, up_b = fence_list(
        branch_blocks, side1, middle1, *partial_result, up_b
    )
    half1 = z_half(up_a, side1)
    middle1, _ = fence(middle1, half1)
    send2 = z_send(flag, half0, middle1, up_b)
    side2, middle2 = z_swap(send2), z_middle(half1)
    branch_blocks, half1 = fence_list(branch_blocks, half1)
    (whole_branch, grad_projected, qkv_bias_sum), partial_first = leave(
        branch_blocks, qkv, out, projected, mask
    )
    first_low, grad_projected = fence(first_low, grad_projected)
    qkv_sent_a, qkv_sent_b, qkv_kept, out_sent, out_kept = qkv_grad_of(
        spot, first_low, grad_projected, context, whole_branch
    )
    qkv_a, qkv_b = pack(
        qkv_kept, swap(qkv_sent_a, 1), swap(qkv_sent_b, 1), out_kept, swap(out_sent, 1)
    )

    side2, middle2, qkv_a = fence(side2, middle2, qkv_a)
    half2 = z_half(up_b, side2)
    middle2, _ = fence(middle2, half2)
    send3 = z_send(flag, half1, middle2, qkv_a)
    side3, middle3 = z_swap(send3), z_middle(half2)
    down_sent, _ = fence(down_sent, send3)
    (down_b,) = add_all([down_b], [swap(down_sent, 1)])
    *partial_first, down_b = fence(*partial_first, down_b)
    first_parts = from_chips(partial_first)
    down_grad = first_down(spot, send2, side2)

    first_parts, side3, middle3 = fence_list(first_parts, side3, middle3)
    half3 = z_half(qkv_a, side3)
    middle3, _ = fence(middle3, half3)
    send4 = z_send(flag, half2, middle3, qkv_b)
    sent, _ = fence(send3, send4)
    up_a_final = z_final(spot, sent, side3)
    side4, middle4 = z_swap(send4), z_middle(half3)
    *partial_result, half3 = fence(*partial_result, half3)
    result_parts = from_chips(partial_result)

    result_parts, side4, middle4 = fence_list(result_parts, side4, middle4)
    half4 = z_half(qkv_b, side4)
    middle4, _ = fence(middle4, half4)
    send5 = z_send(flag, half3, middle4, down_b)
    sent, _ = fence(send4, send5)
    up_b_final = z_final(spot, sent, side4)
    side5, middle5 = z_swap(send5), z_middle(half4)
    result_parts, half4 = fence_list(result_parts, half4)
    layer_out, grad_tokens, sums = end(
        spot,
        lengths,
        first_parts,
        result_parts,
        grad_mixed,
        tokens,
        table,
        mixed,
        mix_sums,
        qkv_bias_sum,
        up_bias_sum,
    )
    (sums,) = add_all([sums], [swap(sums, 1)])
    sums = sum_all(from_chips([sums] * CHIPS))
    if groups > 1:
        sums = lax.psum(sums, "fsdp", axis_index_groups=shard_groups)
    sums_got = z_swap(sums)
    up_a_final, _ = fence(up_a_final, sums)
    up_ready = up_exchange(spot, up_a_final, up_b_final)

    side5, middle5, sums_got, _ = fence(side5, middle5, sums_got, up_ready[0])
    half5 = z_half(down_b, side5)
    middle5, _ = fence(middle5, half5)
    send6 = z_half(half4, middle5)
    sent, _ = fence(send5, send6)
    qkv_ready, rows_ready = qkv_unpack(spot, sent, side5)
    side6, middle6 = z_swap(send6), z_middle(half5)
    up_ready, _ = fence_list(up_ready, send6)
    up_total = from_chips(up_ready)
    (sums,) = add_all([sums], [sums_got])

    up_total, side6, middle6, sums, qkv_ready = fence_list(
        up_total, side6, middle6, sums, qkv_ready
    )
    middle6, _ = fence(middle6, side6)
    send7 = z_half(half5, middle6)
    side7 = along_z([(1, 0), (2, 3)], send7)
    sent, send7, sums = fence(send6, send7, sums)
    qkv_last, out_grad = qkv_exchange(spot, qkv_ready, rows_ready, sent, side6)
    qkv_total = from_chips(qkv_last)
    sums_got = along_z([(z, z ^ 2) for z in range(4)], sums)
    up_grad = up_rows(spot, up_total)
    place_in = jnp.stack([lax.axis_index("fsdp")]).astype(jnp.int32)
    vectors = list(owned(place_in, CELLS_DEV * dp_count * fsdp_count, fsdp_count, sums, sums_got))
    qkv_total, up_grad, vectors[0] = fence_list(qkv_total, up_grad, vectors[0])
    qkv_grad = qkv_rows(spot, qkv_total)
    side7, qkv_grad = fence(side7, qkv_grad)
    down_grad = second_down(flag, send7, side7, down_grad)

    return (
        layer_out,
        grad_tokens,
        vectors[0],
        vectors[1],
        scatter_shards(qkv_grad),
        vectors[6],
        vectors[7],
        scatter_shards(out_grad),
        vectors[2],
        vectors[3],
        vectors[4],
        scatter_shards(up_grad),
        vectors[8],
        scatter_shards(down_grad),
        vectors[5],
        vectors[9],
        vectors[10],
    )


def solution(mesh):
    tokens_spec = P(("dp", "fsdp"), None)
    vector = P("fsdp")
    matrix = P("fsdp", None)
    in_specs = (
        tokens_spec,
        P(("dp", "fsdp"), None),
        P(("dp", "fsdp")),
        vector,
        vector,
        matrix,
        vector,
        vector,
        matrix,
        vector,
        vector,
        vector,
        matrix,
        vector,
        matrix,
        vector,
        tokens_spec,
    )
    out_specs = (
        tokens_spec,
        tokens_spec,
        vector,
        vector,
        matrix,
        vector,
        vector,
        matrix,
        vector,
        vector,
        vector,
        matrix,
        vector,
        matrix,
        vector,
        P(),
        P(),
    )
    return jax.shard_map(local, mesh=mesh, in_specs=in_specs, out_specs=out_specs, check_vma=False)
```

```python
import jax
import jax.numpy as jnp
from jax import lax
from jax.experimental import pallas as pl
from jax.experimental.pallas import tpu as pltpu
from jax.sharding import PartitionSpec as P

D = 1280
HEADS = 20
HEAD_DIM = 64
FF = 5120
CELLS_DEV = 2
EPS = 1e-05

TEAM = 8
CHIPS = 4
HEADS_CHIP = HEADS // CHIPS
D_CHIP = D // CHIPS
FF_CHIP = FF // CHIPS
SHARE = D // TEAM
FF_SHARE = FF // TEAM
SCALE = HEAD_DIM ** (-0.5)

GAIN1, BIAS1, BIAS_OUT, GAIN2, BIAS2, BIAS_DOWN, BIAS_UP, BIAS_QKV = range(8)
TABLE_ROWS = 8
SUM_ROWS = 16

COST = pl.CostEstimate(flops=1, bytes_accessed=1, transcendentals=0)
SMEM = pl.BlockSpec(memory_space=pltpu.SMEM)
HBM = pl.BlockSpec(memory_space=pltpu.HBM)
VMEM = pl.BlockSpec(memory_space=pltpu.VMEM)

f32 = jnp.float32
bf16 = jnp.bfloat16


def dot(a, b, dims):
    return lax.dot_general(a, b, (dims, ((), ())), preferred_element_type=f32)


def mm(a, b):
    return dot(a, b, ((1,), (0,)))


def mm_t(a, b):
    return dot(a, b, ((1,), (1,)))


def t_mm(a, b):
    return dot(a, b, ((0,), (0,)))


def normalize(values):
    center = jnp.mean(values, axis=-1, keepdims=True)
    centred = values - center
    spread = jnp.mean(centred * centred, axis=-1, keepdims=True)
    inverse = lax.rsqrt(spread + EPS)
    return centred * inverse, inverse


def norm_backward(grad_out, normed, inverse, norm_gain):
    grad_normed = grad_out * norm_gain
    first_mean = jnp.mean(grad_normed, axis=-1, keepdims=True)
    second_mean = jnp.mean(grad_normed * normed, axis=-1, keepdims=True)
    grad_in = inverse * (grad_normed - first_mean - normed * second_mean)
    gain_sum = jnp.sum(grad_out * normed, axis=0, keepdims=True)
    return grad_in, gain_sum, jnp.sum(grad_out, axis=0, keepdims=True)


def heads_of(projected, offset):
    return [
        projected[:, offset + i * HEAD_DIM : offset + (i + 1) * HEAD_DIM] for i in range(HEADS_CHIP)
    ]


def softmax_rows(queries, keys, keep):
    raw = jnp.concatenate([mm_t(q, k) for q, k in zip(queries, keys)], axis=0)
    masked = jnp.where(keep, raw * SCALE, -1e30)
    grown = jnp.exp(masked - jnp.max(masked, axis=-1, keepdims=True))
    return grown * (1.0 / jnp.sum(grown, axis=-1, keepdims=True))


def keep_of(mask):
    return jnp.concatenate([mask.astype(f32)] * HEADS_CHIP, axis=0) > 0.5


def attend(projected, mask):
    rows = mask.shape[0]
    probs = softmax_rows(heads_of(projected, 0), heads_of(projected, D_CHIP), keep_of(mask))
    probs = probs.astype(bf16)
    out = [
        mm(probs[i * rows : (i + 1) * rows], value)
        for i, value in enumerate(heads_of(projected, 2 * D_CHIP))
    ]
    return jnp.concatenate(out, axis=1).astype(bf16)


def attend_back(projected, mask, grad_context):
    rows = mask.shape[0]
    queries, keys, values = (heads_of(projected, i * D_CHIP) for i in range(3))
    grads = heads_of(grad_context, 0)
    probs = softmax_rows(queries, keys, keep_of(mask))
    grad_probs = jnp.concatenate([mm_t(g, v) for g, v in zip(grads, values)], axis=0)
    along = jnp.sum(grad_probs * probs, axis=-1, keepdims=True)
    grad_scores = (probs * (grad_probs - along) * SCALE).astype(bf16)
    probs = probs.astype(bf16)

    def cut(stack, i):
        return stack[i * rows : (i + 1) * rows]

    out = (
        [mm(cut(grad_scores, i), keys[i]) for i in range(HEADS_CHIP)]
        + [t_mm(cut(grad_scores, i), queries[i]) for i in range(HEADS_CHIP)]
        + [t_mm(cut(probs, i), grads[i]) for i in range(HEADS_CHIP)]
    )
    return jnp.concatenate(out, axis=1).astype(bf16)


HALF = SHARE // 2
EXTRA = 8
FLAG_ROWS = 16
ROWS_Z = 2 * SHARE


def call(kernel, name, kinds, out_shapes, scratch=(), vmem=16):
    specs = {"s": SMEM, "h": HBM, "v": VMEM}
    made = pl.pallas_call(
        kernel,
        in_specs=[specs[kind] for kind in kinds],
        out_specs=[VMEM] * len(out_shapes),
        out_shape=[jax.ShapeDtypeStruct(shape, kind) for shape, kind in out_shapes],
        scratch_shapes=list(scratch),
        compiler_params=pltpu.CompilerParams(vmem_limit_bytes=vmem * 2**20),
        cost_estimate=COST,
        name=name,
    )

    def run(*args):
        placed = [
            pltpu.with_memory_space_constraint(arg, pltpu.HBM) if kind == "h" else arg
            for kind, arg in zip(kinds, args, strict=True)
        ]
        return made(*placed)

    return run


def sems(count):
    return pltpu.SemaphoreType.DMA((count,))


def row_at(i, size):
    return pl.ds(pl.multiple_of(i * size, size), size)


def tiled(width, tile, body):
    @pl.loop(0, width // tile)
    def _(i):
        body(row_at(i, tile))


def stack_blocks(blocks, whole):
    rows = blocks[0].shape[0]
    for i, block in enumerate(blocks):
        whole[i * rows : (i + 1) * rows, :] = block[...]


def row_of(spot, i, of_core, half=None):
    row = (2 * (spot[0] ^ i) + of_core) * SHARE
    if half is None:
        return pl.ds(pl.multiple_of(row, SHARE), SHARE)
    return pl.ds(pl.multiple_of(row + half * HALF, HALF), HALF)


def stack_columns(spot, mine, other, whole):
    core, side = spot[1], spot[2]
    for of_core, (own, near, far) in ((core, mine), (1 - core, other)):
        whole[row_of(spot, 0, of_core), :] = own[:SHARE, :]
        for i in range(1, CHIPS):
            rows = slice((i - 1) * HALF, i * HALF)
            whole[row_of(spot, i, of_core, side), :] = near[rows, :]
            whole[row_of(spot, i, of_core, 1 - side), :] = far[rows, :]


def by_core_copies(core, mine, other, whole, sem):
    size = mine.shape[0]
    return [
        pltpu.make_async_copy(mine, whole.at[row_at(core, size)], sem.at[0]),
        pltpu.make_async_copy(other, whole.at[row_at(1 - core, size)], sem.at[1]),
    ]


def start_all(copies):
    for copy in copies:
        copy.start()


def wait_all(copies):
    for copy in copies:
        copy.wait()


def chip_columns(weights, rows, chip):
    start = pl.multiple_of((chip * 5 // 2) * 128, 128)
    odd = lax.rem(chip, 2) == 1
    out = []
    for kind in range(3):
        window = weights[rows, pl.ds(kind * D + start, 384)]
        out.append(jnp.where(odd, window[:, 64 : 64 + D_CHIP], window[:, :D_CHIP]))
    return jnp.concatenate(out, axis=1)


def qkv_blocks_kernel(spot, lengths, padding, weights, *refs):
    vectors, own, sent = refs[:9], refs[9], refs[10 : 9 + CHIPS]
    flag, role, refs = refs[9 + CHIPS], refs[10 + CHIPS], refs[11 + CHIPS :]
    held, marks, whole, vector_sems, sem = refs[:9], *refs[9:]
    flag[...] = jnp.full(flag.shape, spot[3].astype(f32), f32).astype(bf16)
    for i in range(3):
        role[i : i + 1, :] = jnp.full((1, 128), spot[i].astype(f32), f32)
    role[3:, :] = jnp.zeros((5, 128), f32)
    copies = [
        pltpu.make_async_copy(vector, here, vector_sems.at[i])
        for i, (vector, here) in enumerate(zip(vectors, held))
    ]
    copies.append(pltpu.make_async_copy(padding, marks, sem.at[0]))
    copies.append(pltpu.make_async_copy(weights, whole, sem.at[1]))
    start_all(copies)
    wait_all(copies)
    rows = padding.shape[-1]
    place = lax.broadcasted_iota(jnp.int32, (1, rows), 1)
    first = lengths[0, 0]
    member = (place >= first).astype(f32)
    leading = (place == 0) | (place == first)
    usable = jnp.where(leading | (marks[...].reshape(1, rows) > 0), 1.0, 0.0)
    code = 2.0 * member + usable
    width = 3 * D_CHIP
    lines = [v[...].astype(f32).reshape(1, -1) for v in held]
    extra = jnp.concatenate(
        [
            jnp.concatenate(lines[:6], axis=1),
            jnp.concatenate(lines[6:], axis=1),
            jnp.concatenate([code, jnp.zeros((1, width - rows), f32)], axis=1),
            jnp.zeros((EXTRA - 3, width), f32),
        ],
        axis=0,
    ).astype(bf16)
    own[:SHARE, :] = chip_columns(whole, slice(None), spot[0])
    own[SHARE:, :] = extra
    for i, block in enumerate(sent):
        block[:HALF, :] = chip_columns(whole, row_at(spot[2], HALF), spot[0] ^ (i + 1))
        block[HALF:, :] = extra


def qkv_blocks(spot, lengths, padding, weights, vectors):
    half = ((HALF + EXTRA, 3 * D_CHIP), bf16)
    return call(
        qkv_blocks_kernel,
        "qkv_blocks",
        "ss" + "h" * 11,
        [((SHARE + EXTRA, 3 * D_CHIP), bf16)] + [half] * (CHIPS - 1) + [((FLAG_ROWS, D), bf16), ((8, 128), f32)],
        [pltpu.VMEM(v.shape, v.dtype) for v in vectors]
        + [
            pltpu.VMEM(padding.shape, padding.dtype),
            pltpu.VMEM(weights.shape, weights.dtype),
            sems(9),
            sems(2),
        ],
    )(spot, lengths, padding, weights, *vectors)


def qkv_join_kernel(own, q1, q2, q3, x1, x2, near, near_half, first, second):
    size = first.shape[0]
    first[...] = x1[:size, :]
    second[...] = x2[size:, :]
    near[:SHARE, :] = own[:SHARE, :]
    low = SHARE + 3 * HALF
    near[low : low + EXTRA, :] = own[SHARE:, :]
    for i, block in enumerate((q1, q2, q3)):
        near[SHARE + i * HALF : SHARE + (i + 1) * HALF, :] = block[:HALF, :]
        near_half[i * HALF : (i + 1) * HALF, :] = block[:HALF, :]
        low += EXTRA
        near[low : low + EXTRA, :] = block[HALF:, :]


def qkv_join(blocks, x1, x2):
    width = blocks[0].shape[-1]
    half = ((x1.shape[0] // 2, x1.shape[1]), x1.dtype)
    return call(
        qkv_join_kernel,
        "qkv_join",
        "v" * 6,
        [
            ((SHARE + 3 * HALF + CHIPS * EXTRA, width), bf16),
            ((3 * HALF, width), bf16),
            half,
            half,
        ],
    )(*blocks, x1, x2)


def up_blocks_kernel(spot, weights, cotangent, own, *sent):
    def columns(chip):
        return pl.ds(pl.multiple_of(chip * FF_CHIP, FF_CHIP), FF_CHIP)

    own[...] = weights[:, columns(spot[0])]
    for i, block in enumerate(sent):
        block[:HALF, :] = weights[row_at(spot[2], HALF), columns(spot[0] ^ (i + 1))]
    for block in sent[:2]:
        block[HALF:, :] = cotangent[...]


def up_blocks(spot, weights, cotangent):
    both = HALF + cotangent.shape[0]
    sizes = (SHARE, both, both, HALF)
    return call(up_blocks_kernel, "up_blocks", "svv", [((size, FF_CHIP), bf16) for size in sizes])(
        spot, weights, cotangent
    )


def up_join_kernel(cotangent, u1, u2, u3, near, whole, first, second):
    rows = cotangent.shape[0]
    for i, block in enumerate((cotangent, u1.at[HALF:], u2.at[HALF:])):
        whole[i * rows : (i + 1) * rows, :] = block[...]
    for i, block in enumerate((u1, u2, u3)):
        near[i * HALF : (i + 1) * HALF, :] = block[:HALF, :]
    half = rows // 2
    first[...] = u1[HALF : HALF + half, :]
    second[...] = u2[HALF + half :, :]


def up_join(cotangent, blocks):
    rows = cotangent.shape[0]
    near = ((3 * HALF, FF_CHIP), bf16)
    passed = ((rows // 2, D), bf16)
    return call(
        up_join_kernel,
        "up_join",
        "vvvv",
        [near, (((CHIPS - 1) * rows, D), bf16), passed, passed],
    )(cotangent, *blocks)


def halves_kernel(whole, first, second):
    size = first.shape[0]
    first[...] = whole[:size, :]
    second[...] = whole[size:, :]


def halves(whole):
    shape = (whole.shape[0] // 2, whole.shape[1])
    return call(halves_kernel, "halves", "v", [(shape, whole.dtype)] * 2)(whole)


def join_kernel(*refs):
    stack_blocks(refs[:-1], refs[-1])


def join(blocks):
    rows, width = blocks[0].shape
    count = len(blocks)
    return call(join_kernel, "join", "v" * count, [((count * rows, width), blocks[0].dtype)])(
        *blocks
    )[0]


def number(role, i):
    return jnp.max(role[i : i + 1, :]).astype(jnp.int32)


def numbers(role):
    return [number(role, i) for i in range(3)]


def fill_table(spot, extras, table, mask):
    chip, core = spot[0], spot[1]
    rows = mask.shape[1]
    table[...] = jnp.zeros_like(table)
    for team in range(TEAM):
        for i in range(6):
            table[i : i + 1, team * SHARE : (team + 1) * SHARE] = extras[
                team, 0:1, i * SHARE : (i + 1) * SHARE
            ]
    for half in range(2):
        line = extras[2 * chip + half, 1:2, :]
        lo = half * SHARE
        table[BIAS_QKV : BIAS_QKV + 1, lo : lo + SHARE] = line[:, :SHARE]
        table[BIAS_QKV : BIAS_QKV + 1, 2 * D_CHIP + lo : 2 * D_CHIP + lo + SHARE] = line[
            :, SHARE : 2 * SHARE
        ]
        table[BIAS_UP : BIAS_UP + 1, half * FF_SHARE : (half + 1) * FF_SHARE] = line[:, 2 * SHARE :]
    for i in range(CHIPS):
        code = extras[2 * (chip ^ i) + core, 2:3, :rows]
        of_key = jnp.broadcast_to(code, (rows, rows))
        cell_of_key = jnp.floor(of_key * 0.5)
        open_key = of_key - 2.0 * cell_of_key
        keep = jnp.where(cell_of_key == cell_of_key.T, open_key, 0.0)
        mask[i * rows : (i + 1) * rows, :] = keep.astype(bf16)


def token_norm_kernel(*refs):
    blocks, normed = refs[:-1], refs[-1]
    at = 0
    for x in blocks:
        rows = x.shape[0]
        normed[at : at + rows, :] = normalize(x[...].astype(f32))[0]
        at += rows


def token_norm(blocks):
    rows, width = blocks[0].shape
    shape = (CHIPS * rows, width)
    return call(token_norm_kernel, "token_norm", "v" * len(blocks), [(shape, f32)])(*blocks)[0]


def enter_kernel(role, normed, *refs):
    spot = numbers(role)
    mine, other, refs = refs[:2], refs[2:4], refs[4:]
    out_mine, out_other, refs = *refs[:2], refs[2:]
    table, mask, qkv, out, first_low, projected, context = refs[:7]
    partials = refs[7 : 8 + CHIPS]
    extras, out_sems = refs[8 + CHIPS :]
    rows = mask.shape[1]
    out_copies = by_core_copies(spot[1], out_mine, out_other, out, out_sems)
    start_all(out_copies)
    low = SHARE + 3 * HALF
    for of_core, lines in ((spot[1], mine[0]), (1 - spot[1], other[0])):
        for i in range(CHIPS):
            at = slice(low + i * EXTRA, low + (i + 1) * EXTRA)
            extras[2 * (spot[0] ^ i) + of_core] = lines[at, :].astype(f32)
    fill_table(spot, extras, table, mask)
    columns = [(near, near.at[SHARE:], far) for near, far in (mine, other)]
    stack_columns(spot, *columns, qkv)
    gain = table[GAIN1 : GAIN1 + 1, :]
    bias = table[BIAS1 : BIAS1 + 1, :]
    first_low[...] = (normed[...] * gain + bias).astype(bf16)
    for lo, hi in ((0, 384), (384, 768), (768, 960)):
        shift = table[BIAS_QKV : BIAS_QKV + 1, lo:hi]
        projected[:, lo:hi] = (mm(first_low[...], qkv[:, lo:hi]) + shift).astype(bf16)

    @pl.loop(0, CHIPS)
    def _(i):
        at = row_at(i, rows)
        context[at, :] = attend(projected[at, :], mask[at, :])

    wait_all(out_copies)

    def partial(at):
        whole = mm(context[...], out[:, at]).astype(bf16)
        lo = 0
        for part in partials:
            part[:, at] = whole[lo : lo + part.shape[0]]
            lo += part.shape[0]

    tiled(D, 256, partial)


def enter(role, normed, mine, other, out_mine, out_other):
    total = normed.shape[0]
    rows = total // CHIPS
    outs = call(
        enter_kernel,
        "enter",
        "vv" + "v" * 4 + "hv",
        [
            ((TABLE_ROWS, D), f32),
            ((total, rows), bf16),
            ((D, 3 * D_CHIP), bf16),
            ((D_CHIP, D), bf16),
            ((total, D), bf16),
            ((total, 3 * D_CHIP), bf16),
            ((total, D_CHIP), bf16),
        ]
        + [((rows, D), bf16)] * (CHIPS - 1)
        + [((rows // 2, D), bf16)] * 2,
        [pltpu.VMEM((TEAM, EXTRA, 3 * D_CHIP), f32), sems(2)],
    )(role, normed, *mine, *other, out_mine, out_other)
    return outs[:7], outs[7:]


def leave_kernel(
    b0, b1, b2, b3, qkv, out, projected, mask, branch, grad_projected, bias_sum, *refs
):
    partials, grad_context = refs[:CHIPS], refs[CHIPS]
    rows = b0.shape[0]
    stack_blocks((b0, b1, b2, b3), branch)
    grad_context[...] = mm_t(branch[...], out[...]).astype(bf16)
    bias_sum[...] = jnp.zeros_like(bias_sum)

    @pl.loop(0, CHIPS)
    def _(i):
        at = row_at(i, rows)
        grad = attend_back(projected[at, :], mask[at, :], grad_context[at, :])
        grad_projected[at, :] = grad
        bias_sum[...] += jnp.sum(grad.astype(f32), axis=0, keepdims=True)

    def partial(at):
        whole = mm_t(grad_projected[...], qkv[at, :]).astype(bf16)
        for i, part in enumerate(partials):
            part[:, at] = whole[i * rows : (i + 1) * rows]

    tiled(D, 256, partial)


def leave(blocks, qkv, out, projected, mask):
    rows = blocks[0].shape[0]
    total = CHIPS * rows
    outs = call(
        leave_kernel,
        "leave",
        "v" * 8,
        [((total, D), bf16), ((total, 3 * D_CHIP), bf16), ((1, 3 * D_CHIP), f32)]
        + [((rows, D), bf16)] * CHIPS,
        [pltpu.VMEM((total, D_CHIP), bf16)],
    )(*blocks, qkv, out, projected, mask)
    return outs[:3], outs[3:]


def total_of(parts):
    total = parts[0][...].astype(f32)
    for part in parts[1:]:
        total = total + part[...].astype(f32)
    return total


def pass_on_kernel(p1, p2, h1, h2, sum1, sum2):
    size = h1.shape[0]
    sum1[:size, :] = (p1[:size, :].astype(f32) + h1[...].astype(f32)).astype(bf16)
    sum1[size:, :] = p1[size:, :]
    sum2[:size, :] = p2[:size, :]
    sum2[size:, :] = (p2[size:, :].astype(f32) + h2[...].astype(f32)).astype(bf16)


def pass_on(p1, p2, h1, h2):
    return call(pass_on_kernel, "pass_on", "vvvv", [(p1.shape, bf16)] * 2)(p1, p2, h1, h2)


def mix_kernel(p0, p1, p2, tokens, table, mixed, second):
    total = total_of((p0, p1, p2)) + tokens[...].astype(f32)
    total = total + table[BIAS_OUT : BIAS_OUT + 1, :]
    mixed[...] = total
    normed, _ = normalize(total)
    second[...] = (normed * table[GAIN2 : GAIN2 + 1, :] + table[BIAS2 : BIAS2 + 1, :]).astype(bf16)


def mix(parts, tokens, table):
    shape = tokens.shape
    return call(mix_kernel, "mix", "v" * 5, [(shape, f32), (shape, bf16)])(*parts, tokens, table)


def unmix_kernel(p0, p1, p2, p3, mixed, table, cotangent, grad_mixed, branch, sums):
    grad = total_of((p0, p1, p2, p3))
    normed, inverse = normalize(mixed[...])
    grad_in, gain_sum, bias_sum = norm_backward(grad, normed, inverse, table[GAIN2 : GAIN2 + 1, :])
    grad_out = cotangent[...].astype(f32)
    grad_in = grad_in + grad_out
    grad_mixed[...] = grad_in
    low = grad_in.astype(bf16)
    branch[...] = low
    sums[...] = jnp.zeros_like(sums)
    sums[0:1, :] = jnp.sum(low.astype(f32), axis=0, keepdims=True)
    sums[1:2, :] = gain_sum
    sums[2:3, :] = bias_sum
    sums[3:4, :] = jnp.sum(grad_out, axis=0, keepdims=True)


def unmix(parts, mixed, table, cotangent):
    shape = cotangent.shape
    return call(
        unmix_kernel, "unmix", "v" * 7, [(shape, f32), (shape, bf16), ((8, D), f32)]
    )(*parts, mixed, table, cotangent)


def act_grad_kernel(spot, part, g1, g2, mine, other, grad_act, down, whole, down_sems):
    copies = by_core_copies(spot[1], mine, other, down, down_sems)
    start_all(copies)
    at = 0
    for block in (part, g1, g2):
        whole[at : at + block.shape[0], :] = block[...]
        at += block.shape[0]
    wait_all(copies)

    def columns(at):
        grad_act[:, at] = mm_t(whole[...], down[at, :])

    tiled(FF_CHIP, 256, columns)


def act_grad(spot, part, passed, down_mine, down_other):
    total = part.shape[0] // (CHIPS - 1) * CHIPS
    return call(
        act_grad_kernel,
        "act_grad",
        "svvvhv",
        [((total, FF_CHIP), f32), ((FF_CHIP, D), bf16), ((total, D), bf16)],
        [sems(2)],
    )(spot, part, *passed, down_mine, down_other)


def hidden_rows(at, second, up, table, grad_act, pre_act, act, grad_pre, bias_sum):
    size = at.stop - at.start

    def columns(tile):
        pre_act[at, tile] = mm(second[at, :], up[:, tile]) + table[BIAS_UP : BIAS_UP + 1, tile]

    tiled(FF_CHIP, 640, columns)

    @pl.loop(0, size // 64)
    def _(i):
        rows = pl.ds(pl.multiple_of(at.start + i * 64, 64), 64)
        pre = pre_act[rows, :]
        below = 0.5 * (1.0 + lax.erf(pre * (0.5**0.5)))
        bell = jnp.exp(-0.5 * pre * pre) * 0.3989422804014327
        act[rows, :] = (pre * below).astype(bf16)
        grad = (grad_act[rows, :] * (below + pre * bell)).astype(bf16)
        grad_pre[rows, :] = grad
        bias_sum[...] += jnp.sum(grad.astype(f32), axis=0, keepdims=True)


def hidden_first_kernel(role, s0, s1, s2, grad_act, table, *refs):
    spot = numbers(role)
    columns = [(own, rest, rest.at[3 * HALF :]) for own, rest in (refs[:2], refs[2:4])]
    second, act, grad_pre, bias_sum, up = refs[4:9]
    partials, pre_act = refs[9:12], refs[12]
    rows = s0.shape[0]
    stack_columns(spot, *columns, up)
    stack_blocks((s0, s1, s2), second)
    bias_sum[...] = jnp.zeros_like(bias_sum)
    hidden_rows(
        slice(0, 3 * rows), second, up, table, grad_act, pre_act, act, grad_pre, bias_sum
    )
    second_partials(slice(0, 3 * rows), grad_pre, up, partials)


def second_partials(at, grad_pre, up, partials):
    rows = partials[0].shape[0]

    def columns(tile):
        whole = mm_t(grad_pre[at, :], up[tile, :]).astype(bf16)
        for i, part in enumerate(partials):
            part[:, tile] = whole[i * rows : (i + 1) * rows]

    tiled(D, 640, columns)


def hidden_first(role, blocks, grad_act, table, mine, other):
    total = grad_act.shape[0]
    return call(
        hidden_first_kernel,
        "hidden_first",
        "v" * 10,
        [
            ((total, D), bf16),
            ((total, FF_CHIP), bf16),
            ((total, FF_CHIP), bf16),
            ((1, FF_CHIP), f32),
            ((D, FF_CHIP), bf16),
        ]
        + [((total // CHIPS, D), bf16)] * 3,
        [pltpu.VMEM((total, FF_CHIP), f32)],
    )(role, *blocks, grad_act, table, *mine, *other)


def hidden_last_kernel(
    role,
    s3,
    grad_act,
    table,
    cotangent,
    up,
    second_in,
    act_in,
    grad_pre_in,
    bias_in,
    second,
    act,
    grad_pre,
    bias_sum,
    down_sent,
    pre_act,
):
    del second_in, act_in, grad_pre_in
    rows = s3.shape[0]
    at = slice(3 * rows, 4 * rows)
    second[at, :] = s3[...]
    bias_sum[...] = bias_in[...]
    hidden_rows(at, second, up, table, grad_act, pre_act, act, grad_pre, bias_sum)
    down_product(act, cotangent, 1 - number(role, 1), 0, down_sent)


def down_product(act, cotangent, of_core, half, target):
    low = half * ROWS_Z
    aligned = low // 128 * 128
    if half == 0:
        units = pl.ds(pl.multiple_of(of_core * FF_SHARE, 128), ROWS_Z)
        target[...] = t_mm(act[:, units], cotangent[...]).astype(target.dtype)
    else:
        units = pl.ds(pl.multiple_of(of_core * FF_SHARE + aligned, 128), FF_SHARE - aligned)
        window = act[:, units][:, low - aligned :]
        target[...] = t_mm(window, cotangent[...]).astype(target.dtype)


def up_product(second, grad_pre, pair, of_core, target, work):
    for i in range(2):
        first = (2 * (2 * pair + i) + of_core) * SHARE
        aligned = pl.multiple_of(first // 128 * 128, 128)
        work[...] = t_mm(second[:, pl.ds(aligned, 256)], grad_pre[...])
        start = pl.multiple_of(lax.rem(first, 128), 32)
        target[i * SHARE : (i + 1) * SHARE, :] = work[pl.ds(start, SHARE), :].astype(target.dtype)


def hidden_last(role, block, grad_act, table, cotangent, up, second, act, grad_pre, bias_sum):
    total = second.shape[0]
    return pl.pallas_call(
        hidden_last_kernel,
        in_specs=[VMEM] * 10,
        out_specs=[VMEM] * 5,
        out_shape=[
            jax.ShapeDtypeStruct(second.shape, bf16),
            jax.ShapeDtypeStruct(act.shape, bf16),
            jax.ShapeDtypeStruct(grad_pre.shape, bf16),
            jax.ShapeDtypeStruct(bias_sum.shape, f32),
            jax.ShapeDtypeStruct((ROWS_Z, D), bf16),
        ],
        scratch_shapes=[pltpu.VMEM((total, FF_CHIP), f32)],
        input_output_aliases={6: 0, 7: 1, 8: 2},
        compiler_params=pltpu.CompilerParams(vmem_limit_bytes=16 * 2**20),
        cost_estimate=COST,
        name="hidden_last",
    )(role, block, grad_act, table, cotangent, up, second, act, grad_pre, bias_sum)


def second_last_kernel(grad_pre, up, partial):
    rows = partial.shape[0]
    second_partials(slice(grad_pre.shape[0] - rows, grad_pre.shape[0]), grad_pre, up, (partial,))


def second_last(grad_pre, up):
    rows = grad_pre.shape[0] // CHIPS
    return call(second_last_kernel, "second_last", "vv", [((rows, D), bf16)])(grad_pre, up)[0]


def up_sent_kernel(role, grad_pre, second, up_sent, work):
    up_product(second, grad_pre, 0, 1 - number(role, 1), up_sent, work)


def up_sent_of(role, grad_pre, second):
    return call(
        up_sent_kernel,
        "up_sent",
        "vvv",
        [((ROWS_Z, FF_CHIP), bf16)],
        [pltpu.VMEM((256, FF_CHIP), f32)],
    )(role, grad_pre, second)[0]


def split_rows(core, whole, sent, kept):
    for k in range(CHIPS):
        targets = ((sent[k // 2], k % 2, 1 - core), (kept, k, core))
        for target, at, of_core in targets:
            start = pl.multiple_of((2 * k + of_core) * SHARE, SHARE)
            target[at] = whole[pl.ds(start, SHARE), :].astype(bf16)


def down_grad_kernel(role, act, cotangent, got, total):
    down_product(act, cotangent, number(role, 1), 0, total)
    total[...] = (total[...].astype(f32) + got[...].astype(f32)).astype(bf16)


def down_grad_of(role, act, cotangent, got):
    return call(down_grad_kernel, "down_grad", "vvvv", [((ROWS_Z, D), bf16)])(
        role, act, cotangent, got
    )[0]


def rest_kernel(
    spot, second, grad_pre, act, cotangent, up_a, up_b, up_sent, down_b, down_sent, work
):
    core = spot[1]
    up_product(second, grad_pre, 0, core, up_a, work)
    up_product(second, grad_pre, 1, 1 - core, up_sent, work)
    up_product(second, grad_pre, 1, core, up_b, work)
    down_product(act, cotangent, 1 - core, 1, down_sent)
    down_product(act, cotangent, core, 1, down_b)


def rest_of_grads(spot, second, grad_pre, act, cotangent):
    return call(
        rest_kernel,
        "rest",
        "svvvv",
        [((ROWS_Z, D), bf16)] * 5,
        [pltpu.VMEM((256, FF_CHIP), f32)],
    )(spot, second, grad_pre, act, cotangent)


def result_kernel(act, down, *partials):
    rows = partials[0].shape[0]

    def columns(at):
        whole = mm(act[...], down[:, at]).astype(bf16)
        for i, part in enumerate(partials):
            part[:, at] = whole[i * rows : (i + 1) * rows]

    tiled(D, 256, columns)


def result_of(act, down):
    rows = act.shape[0] // CHIPS
    return call(result_kernel, "result", "vv", [((rows, D), bf16)] * CHIPS)(act, down)


def qkv_grad_kernel(
    spot,
    first_low,
    grad_projected,
    context,
    branch,
    sent_a,
    sent_b,
    kept,
    out_sent,
    out_kept,
    whole,
    out,
):
    core = spot[1]

    def columns(at):
        whole[at, :] = t_mm(first_low[:, at], grad_projected[...])

    tiled(D, 256, columns)
    split_rows(core, whole, (sent_a, sent_b), kept)
    out[...] = t_mm(context[...], branch[...])
    for target, of_core in ((out_sent, 1 - core), (out_kept, core)):
        target[...] = out[row_at(of_core, SHARE), :].astype(bf16)


def qkv_grad_of(spot, first_low, grad_projected, context, branch):
    half = ((CHIPS // 2, SHARE, 3 * D_CHIP), bf16)
    rows = ((SHARE, D), bf16)
    return call(
        qkv_grad_kernel,
        "qkv_grad",
        "svvvv",
        [half, half, ((CHIPS, SHARE, 3 * D_CHIP), bf16), rows, rows],
        [pltpu.VMEM((D, 3 * D_CHIP), f32), pltpu.VMEM((D_CHIP, D), f32)],
    )(spot, first_low, grad_projected, context, branch)


def add_kernel(*refs):
    count = len(refs) // 3
    for a, b, c in zip(refs[:count], refs[count : 2 * count], refs[2 * count :]):
        c[...] = a[...] + b[...]


def add_all(left, right):
    shapes = [(a.shape, a.dtype) for a in left]
    return call(add_kernel, "add", "v" * (2 * len(left)), shapes)(*left, *right)


PACKED = SHARE * 3 // 4
STEP = SHARE // 4


def sum_all_kernel(a, b, c, d, total):
    total[...] = (a[...] + b[...]) + (c[...] + d[...])


def sum_all(parts):
    shape = (parts[0].shape, parts[0].dtype)
    return call(sum_all_kernel, "sum_all", "vvvv", [shape])(*parts)[0]


def pack_kernel(kept, got_a, got_b, out_kept, out_got, *chunks):
    for i, chunk in enumerate(chunks):
        for j in range(2):
            got = got_b if i else got_a
            total = (kept[2 * i + j].astype(f32) + got[j].astype(f32)).astype(bf16)
            lo = j * PACKED
            chunk[lo : lo + PACKED, : 3 * D_CHIP] = total[:PACKED]
            for part in range(3):
                at = lo + part * STEP
                chunk[at : at + STEP, 3 * D_CHIP :] = total[
                    PACKED:, part * D_CHIP : (part + 1) * D_CHIP
                ]
        rows = slice(i * HALF, (i + 1) * HALF)
        total = out_kept[rows, :].astype(f32) + out_got[rows, :].astype(f32)
        chunk[2 * PACKED :, :] = total.astype(bf16)


def pack(kept, got_a, got_b, out_kept, out_got):
    return call(pack_kernel, "pack", "vvvvv", [((ROWS_Z, D), bf16)] * 2)(
        kept, got_a, got_b, out_kept, out_got
    )


def unpacked(chunk, j):
    lo = j * PACKED
    tail = [
        chunk[lo + part * STEP : lo + (part + 1) * STEP, 3 * D_CHIP :] for part in range(3)
    ]
    return jnp.concatenate(
        [chunk[lo : lo + PACKED, : 3 * D_CHIP], jnp.concatenate(tail, axis=1)], axis=0
    )


def z_half(low, got_side):
    return add_all([low], [got_side])[0]


def z_send_kernel(flag, half, got_middle, low, sent):
    middle = flag[...] > 0.5
    for i in range(ROWS_Z // FLAG_ROWS):
        rows = slice(i * FLAG_ROWS, (i + 1) * FLAG_ROWS)
        sent[rows, :] = jnp.where(middle, half[rows, :] + got_middle[rows, :], low[rows, :])


def z_send(flag, half, got_middle, low):
    return call(z_send_kernel, "z_send", "vvvv", [(low.shape, bf16)])(flag, half, got_middle, low)[0]


def z_final_kernel(spot, sent, got_side, final):
    final[...] = jnp.where(spot[3] > 0, sent[...], got_side[...])


def z_final(spot, sent, got_side):
    return call(z_final_kernel, "z_final", "svv", [(sent.shape, bf16)])(spot, sent, got_side)[0]


def first_down_kernel(spot, sent, got, down, here, sem):
    here[...] = jnp.where(spot[3] > 0, sent[...], got[...]).astype(f32)
    copy = pltpu.make_async_copy(here, down.at[:ROWS_Z], sem.at[0])
    copy.start()
    copy.wait()


def first_down(spot, sent, got):
    return pl.pallas_call(
        first_down_kernel,
        in_specs=[SMEM, VMEM, VMEM],
        out_specs=HBM,
        out_shape=pltpu.HBM((2 * ROWS_Z, D), f32),
        scratch_shapes=[pltpu.VMEM((ROWS_Z, D), f32), sems(1)],
        compiler_params=pltpu.CompilerParams(vmem_limit_bytes=16 * 2**20),
        cost_estimate=COST,
        name="first_down",
    )(spot, sent, got)


def second_down_kernel(flag, sent, got, before, down, here, sem):
    del before
    copies = []
    middle = flag[...] > 0.5
    for i in range(2):
        for lo in range(i * SHARE, (i + 1) * SHARE, FLAG_ROWS):
            rows = slice(lo, lo + FLAG_ROWS)
            here[rows, :] = jnp.where(middle, sent[rows, :], got[rows, :]).astype(f32)
        rows = slice(i * SHARE, (i + 1) * SHARE)
        target = down.at[ROWS_Z + i * SHARE : ROWS_Z + (i + 1) * SHARE]
        copies.append(pltpu.make_async_copy(here.at[rows], target, sem.at[i]))
        copies[-1].start()
    wait_all(copies)


def second_down(flag, sent, got, down):
    return pl.pallas_call(
        second_down_kernel,
        in_specs=[VMEM, VMEM, VMEM, HBM],
        out_specs=HBM,
        out_shape=pltpu.HBM((2 * ROWS_Z, D), f32),
        scratch_shapes=[pltpu.VMEM((ROWS_Z, D), f32), sems(2)],
        input_output_aliases={3: 0},
        compiler_params=pltpu.CompilerParams(vmem_limit_bytes=16 * 2**20),
        cost_estimate=COST,
        name="second_down",
    )(flag, sent, got, pltpu.with_memory_space_constraint(down, pltpu.HBM))


def qkv_rows_kernel(spot, b0, b1, b2, b3, qkv, rows, stack, sem):
    for i, block in enumerate((b0, b1, b2, b3)):
        stack[spot[0] ^ i] = block[...]
    copies = []
    for kind in range(3):
        for chip in range(CHIPS):
            lo = kind * D + chip * D_CHIP
            rows[:, lo : lo + D_CHIP] = stack[
                chip, :, kind * D_CHIP : (kind + 1) * D_CHIP
            ].astype(f32)
        at = slice(kind * D, (kind + 1) * D)
        copies.append(pltpu.make_async_copy(rows.at[:, at], qkv.at[:, at], sem.at[kind]))
        copies[-1].start()
    wait_all(copies)


def qkv_rows(spot, blocks):
    shape = blocks[0].shape
    return pl.pallas_call(
        qkv_rows_kernel,
        in_specs=[SMEM] + [VMEM] * 4,
        out_specs=HBM,
        out_shape=pltpu.HBM((shape[0], 3 * D), f32),
        scratch_shapes=[
            pltpu.VMEM((shape[0], 3 * D), f32),
            pltpu.VMEM((CHIPS,) + shape, bf16),
            sems(3),
        ],
        compiler_params=pltpu.CompilerParams(vmem_limit_bytes=16 * 2**20),
        cost_estimate=COST,
        name="qkv_rows",
    )(spot, *blocks)


def owned_kernel(count, place, sums, got, *outs):
    total = sums[...] + got[...]
    index = place[0]
    size = outs[0].shape[0]
    mine = pltpu.roll(total, D - index * size, 1)
    for i, row in enumerate((0, 1, 2, 3, 4, 5, 8, 9)):
        outs[i][...] = mine[row : row + 1, :size].reshape(size)
    wide = outs[8].shape[0]
    first = index * wide
    row = first // D
    line = total[10:11, :]
    for k in range(1, CHIPS):
        line = jnp.where(row == k, total[10 + k : 11 + k, :], line)
    line = pltpu.roll(jnp.broadcast_to(line, (8, D)), D - lax.rem(first, D), 1)
    outs[8][...] = line[0:1, :wide].reshape(wide)
    mean = total[6:7, :] / count
    outs[9][...] = mean.reshape(D)
    outs[10][...] = (total[7:8, :] / count - mean * mean).reshape(D)


def owned(place, count, fsdp_count, sums, got):
    sizes = [D // fsdp_count] * 8 + [FF // fsdp_count, D, D]

    def kernel(*refs):
        owned_kernel(count, *refs)

    return call(kernel, "owned", "svv", [((size,), f32) for size in sizes])(place, sums, got)


def up_exchange_kernel(spot, a, b, *blocks):
    chunks = (a, b)
    for i, block in enumerate(blocks):
        chip = spot[0] ^ i
        at = row_at(lax.rem(chip, 2), SHARE)
        block[...] = jnp.where(chip >= 2, chunks[1][at, :], chunks[0][at, :])


def up_exchange(spot, a, b):
    return call(up_exchange_kernel, "up_exchange", "svv", [((SHARE, FF_CHIP), bf16)] * CHIPS)(
        spot, a, b
    )


def qkv_unpack_kernel(spot, sent, got_side, blocks, out_rows):
    chunk = jnp.where(spot[3] > 0, sent[...], got_side[...])
    for j in range(2):
        blocks[j] = unpacked(chunk, j)
    out_rows[...] = chunk[2 * PACKED :, :].astype(f32)


def qkv_unpack(spot, sent, got_side):
    return call(
        qkv_unpack_kernel,
        "qkv_unpack",
        "svv",
        [((2, SHARE, 3 * D_CHIP), bf16), ((HALF, D), f32)],
    )(spot, sent, got_side)


def qkv_exchange_kernel(spot, blocks_a, rows_a, sent, got_side, *refs):
    blocks, out_rows, stack = refs[:CHIPS], refs[CHIPS], refs[CHIPS + 1]
    chunk = jnp.where(spot[3] > 0, sent[...], got_side[...])
    stack[:2] = blocks_a[...]
    for j in range(2):
        stack[2 + j] = unpacked(chunk, j)
    out_rows[:HALF, :] = rows_a[...]
    out_rows[HALF:, :] = chunk[2 * PACKED :, :].astype(f32)
    for i, block in enumerate(blocks):
        block[...] = stack[spot[0] ^ i]


def qkv_exchange(spot, blocks_a, rows_a, sent, got_side):
    shape = (SHARE, 3 * D_CHIP)
    outs = call(
        qkv_exchange_kernel,
        "qkv_exchange",
        "svvvv",
        [(shape, bf16)] * CHIPS + [((SHARE, D), f32)],
        [pltpu.VMEM((CHIPS,) + shape, bf16)],
    )(spot, blocks_a, rows_a, sent, got_side)
    return outs[:CHIPS], outs[CHIPS]


def up_rows_kernel(spot, b0, b1, b2, b3, weights):
    for i, block in enumerate((b0, b1, b2, b3)):
        start = pl.multiple_of((spot[0] ^ i) * FF_CHIP, FF_CHIP)
        weights[:, pl.ds(start, FF_CHIP)] = block[...].astype(f32)


def up_rows(spot, blocks):
    return call(up_rows_kernel, "up_rows", "svvvv", [((SHARE, FF), f32)])(spot, *blocks)[0]


def end_kernel(
    spot,
    lengths,
    p0,
    p1,
    p2,
    p3,
    r0,
    r1,
    r2,
    r3,
    grad_mixed,
    tokens,
    table,
    mixed,
    mix_sums,
    qkv_sum,
    up_sum,
    layer_out,
    grad_tokens,
    sums,
):
    grad = total_of((p0, p1, p2, p3))
    normed, inverse = normalize(tokens[...].astype(f32))
    grad_in, gain_sum, bias_sum = norm_backward(grad, normed, inverse, table[GAIN1 : GAIN1 + 1, :])
    grad_tokens[...] = grad_mixed[...] + grad_in
    result = mixed[...] + total_of((r0, r1, r2, r3)) + table[BIAS_DOWN : BIAS_DOWN + 1, :]
    layer_out[...] = result.astype(bf16)
    place = lax.broadcasted_iota(jnp.int32, (result.shape[0], 1), 0)
    picked = jnp.where((place == 0) | (place == lengths[0, 0]), result, 0.0)
    sums[...] = jnp.zeros_like(sums)
    sums[0:1, :] = gain_sum
    sums[1:2, :] = bias_sum
    sums[2:6, :] = mix_sums[0:4, :]
    sums[6:7, :] = jnp.sum(picked, axis=0, keepdims=True)
    sums[7:8, :] = jnp.sum(picked * picked, axis=0, keepdims=True)
    for k in range(CHIPS):
        here = spot[0] == k
        lo = k * D_CHIP
        sums[8:9, lo : lo + D_CHIP] = jnp.where(here, qkv_sum[:, :D_CHIP], 0.0)
        sums[9:10, lo : lo + D_CHIP] = jnp.where(here, qkv_sum[:, 2 * D_CHIP :], 0.0)
        sums[10 + k : 11 + k, :] = jnp.where(here, up_sum[...], 0.0)


def end(spot, lengths, parts, results, *rest):
    shape = parts[0].shape
    return call(
        end_kernel,
        "end",
        "ss" + "v" * 15,
        [(shape, bf16), (shape, f32), ((SUM_ROWS, D), f32)],
    )(spot, lengths, *parts, *results, *rest)


def fence(*values):
    return lax.optimization_barrier(values)


def local(
    tokens,
    lengths,
    padding,
    ln1_gain,
    ln1_bias,
    w_qkv,
    b_query,
    b_value,
    w_out,
    b_out,
    ln2_gain,
    ln2_bias,
    w_up,
    b_up,
    w_down,
    b_down,
    cotangent,
):
    fsdp_count = lax.axis_size("fsdp")
    dp_count = lax.axis_size("dp")
    groups = fsdp_count // TEAM
    place = lax.axis_index("fsdp") // groups
    chip = place // 2
    core = place % 2
    depth = lax.axis_index("dp")
    middle = (depth == 1) | (depth == 2)
    spot = jnp.stack([chip, core, depth % 2, middle.astype(jnp.int32)]).astype(jnp.int32)

    def swap(value, mask):
        pairs = [
            (team * groups + group, (team ^ mask) * groups + group)
            for team in range(TEAM)
            for group in range(groups)
        ]
        return lax.ppermute(value, "fsdp", pairs)

    shard_groups = [[team * groups + group for group in range(groups)] for team in range(TEAM)]
    def gather_shards(value):
        if groups == 1:
            return value
        return lax.all_gather(value, "fsdp", axis=0, tiled=True, axis_index_groups=shard_groups)

    def scatter_shards(value):
        if groups == 1:
            return value
        return lax.psum_scatter(
            value, "fsdp", scatter_dimension=0, tiled=True, axis_index_groups=shard_groups
        )

    def along_z(pairs, value):
        return lax.ppermute(value, "dp", pairs)

    def z_swap(value):
        return along_z([(0, 1), (1, 0), (2, 3), (3, 2)], value)

    def z_middle(value):
        return along_z([(1, 2), (2, 1)], value)

    def from_chips(blocks):
        return [blocks[0]] + [swap(block, 2 * i) for i, block in enumerate(blocks) if i > 0]

    def fence_list(first, *others):
        done = fence(*first, *others)
        return list(done[: len(first)]), *done[len(first) :]

    w_qkv, w_out, w_up, w_down = (gather_shards(w) for w in (w_qkv, w_out, w_up, w_down))
    given = (ln1_gain, ln1_bias, b_out, ln2_gain, ln2_bias, b_down, b_query, b_value, b_up)
    *qkv_sent, flag, role = qkv_blocks(spot, lengths, padding, w_qkv, [gather_shards(v) for v in given])
    qkv_got = from_chips(qkv_sent)
    x1, x2, *qkv_got = fence(swap(tokens, 2), swap(tokens, 4), *qkv_got)
    qkv_near, qkv_half, x1_half, x2_half = qkv_join(qkv_got, x1, x2)
    qkv_far = z_swap(qkv_half)
    qkv_near_other = swap(qkv_near, 1)
    blocks = [tokens, x1, x2, swap(x1_half, 4), swap(x2_half, 2)]
    normed = token_norm(blocks)
    out_sent, _ = fence(w_out, qkv_near)
    out_other = swap(out_sent, 1)
    up_own, *up_sent = up_blocks(spot, w_up, cotangent)
    up_own, *up_sent = fence(up_own, *up_sent, qkv_near)[:-1]
    loads = [swap(block, 2 * i + 2) for i, block in enumerate(up_sent)]
    normed, qkv_far, qkv_near_other, out_other = fence(normed, qkv_far, qkv_near_other, out_other)
    qkv_far_other = join([swap(half, 1) for half in halves(qkv_far)])

    (table, mask, qkv, out, first_low, projected, context), partial_out = enter(
        role,
        normed,
        [qkv_near, qkv_far],
        [qkv_near_other, qkv_far_other],
        w_out,
        out_other,
    )
    p0, p1, p2, h1, h2 = partial_out
    h1, h2 = swap(h1, 4), swap(h2, 2)
    cotangent_late, _ = fence(cotangent, partial_out[0])
    up_near, part, first, second = up_join(cotangent_late, loads)
    up_far = z_swap(up_near)
    passed = [swap(first, 4), swap(second, 2)]
    passed, h1, h2 = fence_list(passed, h1, h2)
    p1, p2 = pass_on(p1, p2, h1, h2)
    out_parts = [p0, swap(p1, 2), swap(p2, 4)]
    up_far, *out_parts = fence(up_far, *out_parts)
    mixed, second_own = mix(out_parts, tokens, table)
    second_blocks = from_chips([second_own] * CHIPS)
    up_far, _ = fence(up_far, second_own)
    up_rest = join([up_near, up_far])
    up_own_sent, _ = fence(up_own, second_own)
    up_other = [swap(up_own_sent, 1), swap(up_rest, 1)]
    down_sent, _ = fence(w_down, second_own)
    down_other = swap(down_sent, 1)
    part, down_other = fence(part, down_other)
    grad_act, down, whole_cotangent = act_grad(spot, part, passed, w_down, down_other)

    second_low, act_low, grad_pre, up_bias_sum, up, *partial_second = hidden_first(
        role,
        second_blocks[:3],
        grad_act,
        table,
        [up_own, up_rest],
        up_other,
    )
    block, up_bias_sum = fence(second_blocks[3], up_bias_sum)
    second_low, act_low, grad_pre, up_bias_sum, down_sent = hidden_last(
        role, block, grad_act, table, whole_cotangent, up, second_low, act_low, grad_pre, up_bias_sum
    )
    down_got = swap(down_sent, 1)
    up_sent = up_sent_of(role, grad_pre, second_low)
    up_got = swap(up_sent, 1)
    act_low, up_sent = fence(act_low, up_sent)
    down_a = down_grad_of(role, act_low, whole_cotangent, down_got)
    side0 = z_swap(down_a)
    up_late, _ = fence(up, down_a)
    partial_second = partial_second + [second_last(grad_pre, up_late)]
    second_parts = from_chips(partial_second)
    second_low, _ = fence(second_low, partial_second[3])
    up_a, up_b, up_sent, down_b, down_sent = rest_of_grads(
        spot, second_low, grad_pre, act_low, whole_cotangent
    )
    up_got, up_sent = fence(up_got, up_sent)
    (up_a,) = add_all([up_a], [up_got])
    up_got = swap(up_sent, 1)

    second_parts, up_a = fence_list(second_parts, up_a)
    grad_mixed, branch_own, mix_sums = unmix(second_parts, mixed, table, cotangent)
    side0, _ = fence(side0, branch_own)
    half0 = z_half(down_a, side0)
    send1, _ = fence(up_a, half0)
    side1, middle1 = z_swap(send1), z_middle(half0)
    branch_blocks = from_chips([branch_own] * CHIPS)
    act_low, branch_own = fence(act_low, branch_own)
    partial_result = list(result_of(act_low, down))

    up_got, partial_result[0] = fence(up_got, partial_result[0])
    (up_b,) = add_all([up_b], [up_got])
    branch_blocks, side1, middle1, *partial_result, up_b = fence_list(
        branch_blocks, side1, middle1, *partial_result, up_b
    )
    half1 = z_half(up_a, side1)
    middle1, _ = fence(middle1, half1)
    send2 = z_send(flag, half0, middle1, up_b)
    side2, middle2 = z_swap(send2), z_middle(half1)
    branch_blocks, half1 = fence_list(branch_blocks, half1)
    (whole_branch, grad_projected, qkv_bias_sum), partial_first = leave(
        branch_blocks, qkv, out, projected, mask
    )
    first_low, grad_projected = fence(first_low, grad_projected)
    qkv_sent_a, qkv_sent_b, qkv_kept, out_sent, out_kept = qkv_grad_of(
        spot, first_low, grad_projected, context, whole_branch
    )
    qkv_a, qkv_b = pack(
        qkv_kept, swap(qkv_sent_a, 1), swap(qkv_sent_b, 1), out_kept, swap(out_sent, 1)
    )

    side2, middle2, qkv_a = fence(side2, middle2, qkv_a)
    half2 = z_half(up_b, side2)
    middle2, _ = fence(middle2, half2)
    send3 = z_send(flag, half1, middle2, qkv_a)
    side3, middle3 = z_swap(send3), z_middle(half2)
    down_sent, _ = fence(down_sent, send3)
    (down_b,) = add_all([down_b], [swap(down_sent, 1)])
    *partial_first, down_b = fence(*partial_first, down_b)
    first_parts = from_chips(partial_first)
    down_grad = first_down(spot, send2, side2)

    first_parts, side3, middle3 = fence_list(first_parts, side3, middle3)
    half3 = z_half(qkv_a, side3)
    middle3, _ = fence(middle3, half3)
    send4 = z_send(flag, half2, middle3, qkv_b)
    sent, _ = fence(send3, send4)
    up_a_final = z_final(spot, sent, side3)
    side4, middle4 = z_swap(send4), z_middle(half3)
    *partial_result, half3 = fence(*partial_result, half3)
    result_parts = from_chips(partial_result)

    result_parts, side4, middle4 = fence_list(result_parts, side4, middle4)
    half4 = z_half(qkv_b, side4)
    middle4, _ = fence(middle4, half4)
    send5 = z_send(flag, half3, middle4, down_b)
    sent, _ = fence(send4, send5)
    up_b_final = z_final(spot, sent, side4)
    side5, middle5 = z_swap(send5), z_middle(half4)
    result_parts, half4 = fence_list(result_parts, half4)
    layer_out, grad_tokens, sums = end(
        spot,
        lengths,
        first_parts,
        result_parts,
        grad_mixed,
        tokens,
        table,
        mixed,
        mix_sums,
        qkv_bias_sum,
        up_bias_sum,
    )
    (sums,) = add_all([sums], [swap(sums, 1)])
    sums = sum_all(from_chips([sums] * CHIPS))
    if groups > 1:
        sums = lax.psum(sums, "fsdp", axis_index_groups=shard_groups)
    sums_got = z_swap(sums)
    up_a_final, _ = fence(up_a_final, sums)
    up_ready = up_exchange(spot, up_a_final, up_b_final)

    side5, middle5, sums_got, _ = fence(side5, middle5, sums_got, up_ready[0])
    half5 = z_half(down_b, side5)
    middle5, _ = fence(middle5, half5)
    send6 = z_half(half4, middle5)
    sent, _ = fence(send5, send6)
    qkv_ready, rows_ready = qkv_unpack(spot, sent, side5)
    side6, middle6 = z_swap(send6), z_middle(half5)
    up_ready, _ = fence_list(up_ready, send6)
    up_total = from_chips(up_ready)
    (sums,) = add_all([sums], [sums_got])

    up_total, side6, middle6, sums, qkv_ready = fence_list(
        up_total, side6, middle6, sums, qkv_ready
    )
    middle6, _ = fence(middle6, side6)
    send7 = z_half(half5, middle6)
    side7 = along_z([(1, 0), (2, 3)], send7)
    sent, send7, sums = fence(send6, send7, sums)
    qkv_last, out_grad = qkv_exchange(spot, qkv_ready, rows_ready, sent, side6)
    qkv_total = from_chips(qkv_last)
    sums_got = along_z([(z, z ^ 2) for z in range(4)], sums)
    up_grad = up_rows(spot, up_total)
    place_in = jnp.stack([lax.axis_index("fsdp")]).astype(jnp.int32)
    vectors = list(owned(place_in, CELLS_DEV * dp_count * fsdp_count, fsdp_count, sums, sums_got))
    qkv_total, up_grad, vectors[0] = fence_list(qkv_total, up_grad, vectors[0])
    qkv_grad = qkv_rows(spot, qkv_total)
    side7, qkv_grad = fence(side7, qkv_grad)
    down_grad = second_down(flag, send7, side7, down_grad)

    return (
        layer_out,
        grad_tokens,
        vectors[0],
        vectors[1],
        scatter_shards(qkv_grad),
        vectors[6],
        vectors[7],
        scatter_shards(out_grad),
        vectors[2],
        vectors[3],
        vectors[4],
        scatter_shards(up_grad),
        vectors[8],
        scatter_shards(down_grad),
        vectors[5],
        vectors[9],
        vectors[10],
    )


def solution(mesh):
    tokens_spec = P(("dp", "fsdp"), None)
    vector = P("fsdp")
    matrix = P("fsdp", None)
    in_specs = (
        tokens_spec,
        P(("dp", "fsdp"), None),
        P(("dp", "fsdp")),
        vector,
        vector,
        matrix,
        vector,
        vector,
        matrix,
        vector,
        vector,
        vector,
        matrix,
        vector,
        matrix,
        vector,
        tokens_spec,
    )
    out_specs = (
        tokens_spec,
        tokens_spec,
        vector,
        vector,
        matrix,
        vector,
        vector,
        matrix,
        vector,
        vector,
        vector,
        matrix,
        vector,
        matrix,
        vector,
        P(),
        P(),
    )
    return jax.shard_map(local, mesh=mesh, in_specs=in_specs, out_specs=out_specs, check_vma=False)
```
